32 devices in a mesh: dp: 8 (over y, x, core), tensor: 4 (over z).
Axes of the slice: x: 2, y: 2, z: 4, core: 2. Of those that a mesh axis runs over, the one named last changes fastest.
Arguments:
- layer_in: bfloat16 [8192, 2048], P(('dp', 'tensor')), may hold values from -6 to 6
- teacher: bfloat16 [8192, 2048], P(('dp', 'tensor')), may hold values from -6 to 6
- lengths: int32 [8], replicated, may hold values from 256 to 1024, as said below
- input_gain: float32 [2048], replicated, may hold values from 0.5 to 1.5
- mixer_in_weight: bfloat16 [2048, 2, 3072], P('dp', None, 'tensor'), may hold values from -0.125 to 0.125
- step_weight: bfloat16 [2048, 48], P('dp', 'tensor'), may hold values from -0.125 to 0.125
- query_weight: bfloat16 [2048, 1024], P('dp', 'tensor'), may hold values from -0.125 to 0.125
- shared_weight: bfloat16 [2048, 1024], P(('dp', 'tensor')), may hold values from -0.125 to 0.125
- conv_inner: float32 [4, 3072], P(None, 'tensor'), may hold values from -3 to 3
- conv_shared: float32 [4, 512], replicated, may hold values from -3 to 3
- step_bias: float32 [48], P('tensor'), may hold values from -4 to -1
- decay_log: float32 [48], P('tensor'), may hold values from -7 to 0
- skip_gain: float32 [48], P('tensor'), may hold values from 0.5 to 1.5
- inner_gain: float32 [3072], P('tensor'), may hold values from 0.5 to 1.5
- mixer_out_weight: bfloat16 [2048, 3072], P('dp', 'tensor'), may hold values from -0.109375 to 0.109375
- attn_out_weight: bfloat16 [2048, 1024], P('dp', 'tensor'), may hold values from -1.5 to 1.5
- middle_gain: float32 [2048], replicated, may hold values from 0.5 to 1.5
- gate_up_weight: bfloat16 [2048, 2, 4096], P('dp', None, 'tensor'), may hold values from -0.125 to 0.125
- down_weight: bfloat16 [2048, 4096], P('dp', 'tensor'), may hold values from -0.09375 to 0.09375
Outputs:
- layer_out: bfloat16 [8192, 2048], P(('dp', 'tensor'))
- loss: float32 [], replicated
- input_grad: float32 [8192, 2048], P(('dp', 'tensor'))
- input_gain_grad: float32 [2048], replicated
- mixer_in_grad: float32 [2048, 2, 3072], P('dp', None, 'tensor')
- step_weight_grad: float32 [2048, 48], P('dp', 'tensor')
- query_weight_grad: float32 [2048, 1024], P('dp', 'tensor')
- shared_weight_grad: float32 [2048, 1024], P(('dp', 'tensor'))
- conv_inner_grad: float32 [4, 3072], P(None, 'tensor')
- conv_shared_grad: float32 [4, 512], replicated
- step_bias_grad: float32 [48], P('tensor')
- decay_log_grad: float32 [48], P('tensor')
- skip_gain_grad: float32 [48], P('tensor')
- inner_gain_grad: float32 [3072], P('tensor')
- mixer_out_grad: float32 [2048, 3072], P('dp', 'tensor')
- attn_out_grad: float32 [2048, 1024], P('dp', 'tensor')
- middle_gain_grad: float32 [2048], replicated
- gate_up_grad: float32 [2048, 2, 4096], P('dp', None, 'tensor')
- down_grad: float32 [2048, 4096], P('dp', 'tensor')
The draws below stay inside these ranges and needn't reach their ends.
Inputs may be any that keep to these rules, and one draw needn't show every extreme that they name: Slot i holds one sequence of lengths[i] tokens at its start, the rest is padding; some slot is full (1024 tokens) and some holds exactly 256.
All inputs are finite; a program needn't handle non-finite values.
Results may differ from the reference program's by a relative error of at most 0.014.
Values may be sent and summed in bfloat16 or wider, within the bound.
A program may use at most 320 MiB of HBM per device.

```python
import jax
import jax.numpy as jnp
from jax import lax

D = 2048
H = 48
N = 256
KC = 4
QH = 8
KVH = 2
HD = 128
FF = 4096
NGROUPS = 4
SLOT = 1024
DI = 3072
QD = 1024
SHW = 1024
SSD_BLOCK = 256
ATT_BLOCK = 512
SEQS = 8
TOKENS = 8192


def draw_lengths(key, part):
    key_len = jax.random.fold_in(key, 11)
    key_full = jax.random.fold_in(key, 12)
    key_short = jax.random.fold_in(key, 13)
    values = jax.random.randint(key_len, (SEQS,), SLOT // 4, SLOT + 1)
    slot_ids = jnp.arange(SEQS)
    full_at = jax.random.randint(key_full, (), 0, SEQS)
    values = jnp.where(slot_ids == full_at, SLOT, values)
    short_at = (full_at + 1 + jax.random.randint(key_short, (), 0, SEQS - 1)) % SEQS
    values = jnp.where(slot_ids == short_at, SLOT // 4, values)
    return values.astype(jnp.int32)


def levels(own_key, dims, split, smallest, high):
    level = 1.0
    for position, parts in split:
        heights = jax.random.uniform(jax.random.fold_in(jax.random.fold_in(own_key, 6), position), (parts,), jnp.float32, smallest / len(split), high / len(split))
        level = level * jnp.repeat(jnp.exp(heights), dims[position] // parts).reshape((-1,) + (1,) * (len(dims) - 1 - position))
    return level


def noise(stream_key, extent, spread, most, split=(), kind=jnp.bfloat16):
    values = spread * jax.random.normal(stream_key, extent, jnp.float32)
    if split:
        values = values * levels(stream_key, extent, split, -0.22, 0.18)
    return jnp.clip(values, -most, most).astype(kind)


def setup_inputs(seed: int = 0) -> dict:
    splits = jax.random.split(jax.random.key(seed), 20)
    return {
        "layer_in": noise(splits[0], (TOKENS, D), 1.0, 6.0, ((0, 32),)),
        "teacher": noise(splits[1], (TOKENS, D), 1.0, 6.0, ((0, 32),)),
        "lengths": draw_lengths(jax.random.fold_in(splits[19], 71), 0),
        "input_gain": jnp.clip(1.0 + 0.1 * jax.random.normal(splits[3], (D,), jnp.float32), 0.5, 1.5),
        "mixer_in_weight": noise(splits[4], (D, 2, DI), D ** -0.5, 0.125, ((0, 8), (2, 4))),
        "step_weight": noise(splits[5], (D, H), D ** -0.5, 0.125, ((0, 8), (1, 4))),
        "query_weight": noise(splits[6], (D, QD), D ** -0.5, 0.125, ((0, 8), (1, 4))),
        "shared_weight": noise(splits[7], (D, SHW), D ** -0.5, 0.125, ((0, 32),)),
        "conv_inner": noise(splits[8], (KC, DI), 0.5, 3.0, ((1, 4),), jnp.float32),
        "conv_shared": noise(splits[9], (KC, 2 * N), 0.5, 3.0, (), jnp.float32),
        "step_bias": jnp.clip(-4.0 + 3.0 * jax.random.uniform(splits[10], (H,), jnp.float32) ** levels(splits[10], (H,), ((0, 4),), -0.2, 0.2), -4.0, -1.0),
        "decay_log": jnp.clip(-7.0 + 7.0 * jax.random.uniform(splits[11], (H,), jnp.float32) ** levels(splits[11], (H,), ((0, 4),), -0.2, 0.2), -7.0, 0.0),
        "skip_gain": jnp.clip(0.5 + 1.0 * jax.random.uniform(splits[12], (H,), jnp.float32) ** levels(splits[12], (H,), ((0, 4),), -0.2, 0.2), 0.5, 1.5),
        "inner_gain": jnp.clip(1.0 + 0.1 * jax.random.normal(splits[13], (DI,), jnp.float32), 0.5, 1.5),
        "mixer_out_weight": noise(splits[14], (D, DI), DI ** -0.5, 0.109375, ((0, 8), (1, 4))),
        "attn_out_weight": noise(splits[15], (D, QD), (HD // 8) ** -0.5, 1.5, ((0, 8), (1, 4))),
        "middle_gain": jnp.clip(1.0 + 0.1 * jax.random.normal(splits[16], (D,), jnp.float32), 0.5, 1.5),
        "gate_up_weight": noise(splits[17], (D, 2, FF), D ** -0.5, 0.125, ((0, 8), (2, 4))),
        "down_weight": noise(splits[18], (D, FF), FF ** -0.5, 0.09375, ((0, 8), (1, 4))),
    }


EPS = 1e-05
ROPE_BASE = 100000000000.0
NEG_FILL = -1e+30

@jax.custom_vjp
def low(v):
    return lax.optimization_barrier(v.astype(jnp.bfloat16)).astype(jnp.float32)

@jax.custom_vjp
def low_back(v):
    return v

def low_keep(v):
    return (low(v), None)

def low_pass(kept, grad):
    return (grad,)

def back_keep(v):
    return (v, None)

def back_low(kept, grad):
    return (low(grad),)
low.defvjp(low_keep, low_pass)
low_back.defvjp(back_keep, back_low)

def matmul(left, right):
    return jnp.dot(left, right, precision=lax.Precision.HIGHEST, preferred_element_type=jnp.float32)

def rms_norm(values, gain):
    return values * lax.rsqrt(lax.optimization_barrier(jnp.mean(values * values, axis=-1, keepdims=True)) + EPS) * gain

def causal_conv(values, taps):
    length = values.shape[0]
    width = taps.shape[0]
    padded = jnp.pad(values, ((width - 1, 0), (0, 0)))
    total = padded[0:length] * taps[0]
    for offset in range(1, width):
        total = total + padded[offset:offset + length] * taps[offset]
    return total

def rotary(values, positions, head_size):
    half_size = head_size // 2
    freqs = jnp.exp(-jnp.log(ROPE_BASE) * 2.0 * jnp.arange(half_size, dtype=jnp.float32) / head_size)
    angles = positions[:, None] * freqs[None, :]
    cosine = jnp.cos(angles)[:, None, :]
    sine_part = jnp.sin(angles)[:, None, :]
    front_part = values[..., :half_size]
    back_part = values[..., half_size:]
    return jnp.concatenate([front_part * cosine - back_part * sine_part, back_part * cosine + front_part * sine_part], axis=-1)

def ssd_scan(inputs, b_mat, c_mat, log_decay, step_size, skip_gain, block_len):
    length, num_heads, head_dim = inputs.shape
    state_dim = b_mat.shape[1]
    num_blocks = length // block_len
    highest = lax.Precision.HIGHEST
    row_index = jnp.arange(block_len)
    lower_mask = (row_index[:, None] >= row_index[None, :])[:, :, None]

    def block_step(carry_state, pieces):
        x_blk, b_blk, c_blk, decay_blk, step_blk = pieces
        cum_decay = jnp.cumsum(decay_blk, axis=0)
        gap_decay = jnp.where(lower_mask, cum_decay[:, None, :] - cum_decay[None, :, :], 0.0)
        kernel = jnp.where(lower_mask, jnp.exp(gap_decay), 0.0)
        cross_terms = jnp.dot(c_blk, b_blk.T, precision=highest)
        weights = cross_terms[:, :, None] * kernel * step_blk[None, :, :]
        inner_out = jnp.einsum('ijh,jhp->ihp', weights, x_blk, precision=highest)
        carried = jnp.einsum('in,hpn->ihp', c_blk, carry_state, precision=highest) * jnp.exp(cum_decay)[:, :, None]
        tail_weight = jnp.exp(cum_decay[-1][None, :] - cum_decay) * step_blk
        new_state = carry_state * jnp.exp(cum_decay[-1])[:, None, None] + jnp.einsum('jh,jhp,jn->hpn', tail_weight, x_blk, b_blk, precision=highest)
        return (new_state, inner_out + carried + skip_gain[None, :, None] * x_blk)
    start_state = jnp.zeros((num_heads, head_dim, state_dim), jnp.float32)
    pieces = (inputs.reshape(num_blocks, block_len, num_heads, head_dim), b_mat.reshape(num_blocks, block_len, state_dim), c_mat.reshape(num_blocks, block_len, state_dim), log_decay.reshape(num_blocks, block_len, num_heads), step_size.reshape(num_blocks, block_len, num_heads))
    _, results = lax.scan(jax.checkpoint(block_step), start_state, pieces)
    return results.reshape(length, num_heads, head_dim)

def attend(queries, keys_in, values_in, att_block):
    length, num_queries, head_size = queries.shape
    query_low = low(queries)
    key_low_t = low(keys_in).T
    value_low = low(values_in)
    score_scale = head_size ** (-0.5)
    key_pos = jnp.arange(length).astype(jnp.int32)

    def one_block(row_start):
        query_rows = lax.dynamic_slice_in_dim(query_low, row_start, att_block, 0).reshape(att_block * num_queries, head_size)
        raw_scores = low_back(matmul(query_rows, key_low_t))
        query_pos = row_start + (jnp.arange(att_block * num_queries) // num_queries).astype(jnp.int32)
        scores = jnp.where(key_pos[None, :] <= query_pos[:, None], raw_scores * score_scale, NEG_FILL)
        top_score = lax.optimization_barrier(jnp.max(scores, axis=1, keepdims=True))
        weights_un = jnp.exp(scores - top_score)
        probs = weights_un / lax.optimization_barrier(jnp.sum(weights_un, axis=1, keepdims=True))
        mixed_out = low_back(matmul(low(probs), value_low))
        return low(mixed_out).reshape(att_block, num_queries * head_size)
    starts = (jnp.arange(length // att_block) * att_block).astype(jnp.int32)
    results = lax.map(jax.checkpoint(one_block), starts)
    return results.reshape(length, num_queries * head_size)

def mixer_group(proj_zx, proj_dt, proj_shared, proj_query, conv_inner, conv_shared, step_bias, decay_log, skip_gain, inner_gain, kv_index, head_size, kv_heads, ssd_block, att_block):
    length = proj_zx.shape[0]
    num_heads = proj_dt.shape[1]
    inner_width = proj_zx.shape[2]
    head_dim = inner_width // num_heads
    state_dim = conv_shared.shape[1] // 2
    gate_in = proj_zx[:, 0]
    conv_out = jax.nn.silu(causal_conv(proj_zx[:, 1], conv_inner))
    bc_out = jax.nn.silu(causal_conv(proj_shared[:, :2 * state_dim], conv_shared))
    step_size = jax.nn.softplus(proj_dt + step_bias)
    log_decay = -jnp.exp(decay_log) * step_size
    scanned = ssd_scan(conv_out.reshape(length, num_heads, head_dim), bc_out[:, :state_dim], bc_out[:, state_dim:], log_decay, step_size, skip_gain, ssd_block).reshape(length, inner_width)
    mixer_normed = low(rms_norm(scanned * jax.nn.silu(gate_in), inner_gain))
    key_start = 2 * state_dim + kv_index * head_size
    keys_in = lax.dynamic_slice_in_dim(proj_shared, key_start, head_size, 1)
    values_in = lax.dynamic_slice_in_dim(proj_shared, key_start + kv_heads * head_size, head_size, 1)
    num_queries = proj_query.shape[1] // head_size
    positions = jnp.arange(length).astype(jnp.float32)
    queries = rotary(proj_query.reshape(length, num_queries, head_size), positions, head_size)
    keys_rot = rotary(keys_in.reshape(length, 1, head_size), positions, head_size).reshape(length, head_size)
    attn_heads = attend(queries, keys_rot, values_in, att_block)
    return (mixer_normed, attn_heads)

def slot_forward(inputs, targets, seq_len, params):
    gain_first, w_zx, w_dt, w_query, w_shared, w_conv_inner, w_conv_shared, bias_dt, log_rate, skip_w, gain_inner, w_mix_out, w_attn_out, gain_second, w_gate_up, w_down = params
    highest = lax.Precision.HIGHEST
    act_low = low(rms_norm(inputs, gain_first))
    inner_part = DI // NGROUPS
    heads_part = H // NGROUPS
    query_part = QD // NGROUPS
    queries_part = QH // NGROUPS
    mixed_sum = jnp.zeros((SLOT, D), jnp.float32)
    for group_idx in range(NGROUPS):
        inner_from = group_idx * inner_part
        head_from = group_idx * heads_part
        query_from = group_idx * query_part
        proj_zx = low_back(jnp.einsum('sd,dkc->skc', act_low, w_zx[:, :, inner_from:inner_from + inner_part], precision=highest))
        proj_dt = low_back(matmul(act_low, w_dt[:, head_from:head_from + heads_part]))
        proj_shared = low_back(matmul(act_low, w_shared))
        proj_query = low_back(matmul(act_low, w_query[:, query_from:query_from + query_part]))
        kv_index = group_idx * queries_part // (QH // KVH)
        mixer_normed, attn_heads = mixer_group(proj_zx, proj_dt, proj_shared, proj_query, w_conv_inner[:, inner_from:inner_from + inner_part], w_conv_shared, bias_dt[head_from:head_from + heads_part], log_rate[head_from:head_from + heads_part], skip_w[head_from:head_from + heads_part], gain_inner[inner_from:inner_from + inner_part], kv_index, HD, KVH, SSD_BLOCK, ATT_BLOCK)
        mixed_sum = mixed_sum + matmul(mixer_normed, w_mix_out[:, inner_from:inner_from + inner_part].T)
        mixed_sum = mixed_sum + matmul(attn_heads, w_attn_out[:, query_from:query_from + query_part].T)
    resid = inputs + low_back(mixed_sum)
    mid_low = low(rms_norm(resid, gain_second))
    gate_up = low_back(jnp.einsum('sd,dkf->skf', mid_low, w_gate_up, precision=highest))
    hidden = low(jax.nn.silu(gate_up[:, 0]) * gate_up[:, 1])
    outputs = resid + low_back(matmul(hidden, w_down.T))
    live = (jnp.arange(SLOT).astype(jnp.int32) < seq_len).astype(jnp.float32)
    error = (outputs - targets) * live[:, None]
    return (outputs, 0.5 * jnp.sum(error * error))

def reference(layer_in, teacher, lengths, input_gain, mixer_in_weight, step_weight, query_weight, shared_weight, conv_inner, conv_shared, step_bias, decay_log, skip_gain, inner_gain, mixer_out_weight, attn_out_weight, middle_gain, gate_up_weight, down_weight):
    params = tuple((source.astype(jnp.float32) for source in (input_gain, mixer_in_weight, step_weight, query_weight, shared_weight, conv_inner, conv_shared, step_bias, decay_log, skip_gain, inner_gain, mixer_out_weight, attn_out_weight, middle_gain, gate_up_weight, down_weight)))
    inputs = layer_in.astype(jnp.float32).reshape(SEQS, SLOT, D)
    targets = teacher.astype(jnp.float32).reshape(SEQS, SLOT, D)
    slot_pass = jax.checkpoint(slot_forward)

    def whole(inputs_all, params_all):

        def scan_step(total, pieces):
            slot_out, slot_err = slot_pass(pieces[0], pieces[1], pieces[2], params_all)
            return (total + slot_err, slot_out)
        err_sum, outputs = lax.scan(scan_step, jnp.zeros((), jnp.float32), (inputs_all, targets, lengths))
        return (outputs, err_sum)
    (outputs, err_sum), back_fn = jax.vjp(whole, inputs, params)
    grad_inputs, grad_params = back_fn((jnp.zeros_like(outputs), jnp.ones((), jnp.float32)))
    loss = err_sum / jnp.sum(lengths).astype(jnp.float32)
    return (outputs.reshape(TOKENS, D).astype(jnp.bfloat16), loss, grad_inputs.reshape(TOKENS, D), grad_params[0], grad_params[1], grad_params[2], grad_params[3], grad_params[4], grad_params[5], grad_params[6], grad_params[7], grad_params[8], grad_params[9], grad_params[10], grad_params[11], grad_params[12], grad_params[13], grad_params[14], grad_params[15])
```

```python
import jax
import jax.numpy as jnp
from jax import lax
from jax.experimental import pallas as pl
from jax.experimental.pallas import tpu as pltpu
from jax.sharding import PartitionSpec as P

H = 48
KC = 4
QH = 8
KVH = 2
HD = 128
DI = 3072

EPS = 1e-05
ROPE_BASE = 100000000000.0


def rms_norm(values, gain):
    return values * lax.rsqrt(jnp.mean(values * values, axis=-1, keepdims=True) + EPS) * gain


def low_dot(left, right, dims):
    return lax.dot_general(left, right, (dims, ((), ())), preferred_element_type=jnp.float32)


NN = ((1,), (0,))
NT = ((1,), (1,))
TN = ((0,), (0,))
CHUNK = 128
ROWS = 256
WIDE = 128
FAR = -1e30


def exact_dot(ones, values, parts=3):
    total = None
    for _ in range(parts):
        part = values.astype(jnp.bfloat16)
        values = values - part.astype(jnp.float32)
        term = low_dot(ones, part, NN)
        total = term if total is None else total + term
    return total


def split_dot(values, ones, parts=2):
    total = None
    for _ in range(parts):
        part = values.astype(jnp.bfloat16)
        values = values - part.astype(jnp.float32)
        term = low_dot(part, ones, NN)
        total = term if total is None else total + term
    return total


def sigmoid(v):
    return 1.0 / (1.0 + jnp.exp(-v))


def softplus(v):
    return jnp.maximum(v, 0.0) + jnp.log1p(jnp.exp(-jnp.abs(v)))


def iota(shape, axis):
    return lax.broadcasted_iota(jnp.int32, shape, axis)


def spin(values, cosine, sine):
    return values * cosine + pltpu.roll(values, HD // 2, 1) * sine


def unspin(values, cosine, sine):
    return values * cosine - pltpu.roll(values, HD // 2, 1) * sine


def attn_probs(query_low, key_low, first_row, scale):
    scores = low_dot(query_low, key_low, NT) * scale
    rows, keys = scores.shape
    allowed = iota((rows, keys), 1) <= iota((rows, keys), 0) + first_row
    scores = jnp.where(allowed, scores, FAR)
    top = jnp.max(scores, axis=1, keepdims=True)
    weights = jnp.exp(scores - top)
    return weights / jnp.sum(weights, axis=1, keepdims=True)


def attn_fwd_body(order, q_ref, kv_ref, cos_ref, sin_ref, out_ref, key_s, value_s):
    bf16 = jnp.bfloat16
    step = pl.program_id(0)
    cosine, sine = cos_ref[...], sin_ref[...]
    rows = pl.ds(pl.multiple_of(step * ROWS, ROWS), ROWS)
    key_s[rows, :] = spin(kv_ref[:, :HD], cosine, sine).astype(bf16)
    value_s[rows, :] = kv_ref[:, HD:].astype(bf16)
    heads = q_ref.shape[1] // HD
    blocks = key_s.shape[0] // ROWS
    for block in range(blocks):

        @pl.when(step == block)
        def _(block=block):
            keys = (block + 1) * ROWS
            for head in range(heads):
                lanes = slice(head * HD, (head + 1) * HD)
                query = spin(q_ref[:, lanes], cosine, sine).astype(bf16)
                probs = attn_probs(query, key_s[:keys, :], block * ROWS, HD**-0.5)
                out_ref[:, lanes] = low_dot(
                    probs.astype(bf16), value_s[:keys, :], NN
                ).astype(bf16)


def attn_bwd_body(
    order, q_ref, kv_ref, cos_ref, sin_ref, grad_ref, all_cos, all_sin, dq_ref, dkv_ref,
    key_s, value_s, dkey_s, dvalue_s,
):
    bf16, f32 = jnp.bfloat16, jnp.float32
    step = pl.program_id(0)

    @pl.when(step == 0)
    def _():
        dkey_s[...] = jnp.zeros_like(dkey_s)
        dvalue_s[...] = jnp.zeros_like(dvalue_s)

    cosine, sine = cos_ref[...], sin_ref[...]
    rows = pl.ds(pl.multiple_of(step * ROWS, ROWS), ROWS)
    key_s[rows, :] = spin(kv_ref[:, :HD], cosine, sine).astype(bf16)
    value_s[rows, :] = kv_ref[:, HD:].astype(bf16)
    heads = q_ref.shape[1] // HD
    blocks = key_s.shape[0] // ROWS
    scale = HD**-0.5
    for block in range(blocks):

        @pl.when(step == block)
        def _(block=block):
            keys = (block + 1) * ROWS
            for head in range(heads):
                lanes = slice(head * HD, (head + 1) * HD)
                query = spin(q_ref[:, lanes], cosine, sine).astype(bf16)
                probs = attn_probs(query, key_s[:keys, :], block * ROWS, scale)
                grad = grad_ref[:, lanes].astype(bf16)
                dprobs = low_dot(grad, value_s[:keys, :], NT)
                dvalue_s[:keys, :] += low_dot(probs.astype(bf16), grad, TN)
                inner = jnp.sum(dprobs * probs, axis=1, keepdims=True)
                dscores = (probs * (dprobs - inner) * scale).astype(bf16)
                dquery = low_dot(dscores, key_s[:keys, :], NN)
                dkey_s[:keys, :] += low_dot(dscores, query, TN)
                dq_ref[:, lanes] = unspin(dquery, cosine, sine).astype(bf16)

    @pl.when(step == blocks - 1)
    def _():
        dkv_ref[:, :HD] = unspin(dkey_s[...], all_cos[...], all_sin[...]).astype(bf16)
        dkv_ref[:, HD:] = dvalue_s[...].astype(bf16)


def conv_taps(ext, taps, first, width):
    rows = ext.shape[0] - 8
    total = None
    for tap in range(width):
        at = 8 - (width - 1) + tap
        term = ext[at : at + rows, :] * taps[first + tap : first + tap + 1, :]
        total = term if total is None else total + term
    return total


def decays(steps, head_params, tri):
    shifted = steps + head_params[0:1, :]
    dt = softplus(shifted)
    la = dt * head_params[1:2, :]
    cum = exact_dot(tri, la)
    return shifted, dt, la, cum


def spread_lanes(values, pair, first):
    rows = values.shape[0]
    a = jnp.broadcast_to(values[:, 2 * pair : 2 * pair + 1], (rows, WIDE))
    b = jnp.broadcast_to(values[:, 2 * pair + 1 : 2 * pair + 2], (rows, WIDE))
    return a, b, jnp.where(first, a, b)


def mixer_fwd_body(
    order, gate_ref, inner_ref, step_ref, bc_ref, attn_ref, lane_ref, conv_ref, head_ref,
    out_ref, y_ref, state_ref, ext_s, extbc_s, state_s, x_s,
):
    bf16, f32 = jnp.bfloat16, jnp.float32
    step = pl.program_id(0)
    width = inner_ref.shape[1]
    states = bc_ref.shape[1] // 2

    @pl.when(step == 0)
    def _():
        ext_s[0:8, :] = jnp.zeros((8, width), f32)
        extbc_s[0:8, :] = jnp.zeros((8, 2 * states), f32)
        state_s[...] = jnp.zeros_like(state_s)

    ext_s[8:, :] = inner_ref[...]
    extbc_s[8:, :] = bc_ref[...]
    pre = conv_taps(ext_s, lane_ref, 0, KC)
    x_s[...] = pre * sigmoid(pre)
    pre = conv_taps(extbc_s, conv_ref, 0, KC)
    bc = (pre * sigmoid(pre)).astype(bf16)
    ext_s[0:8, :] = ext_s[ROWS : ROWS + 8, :]
    extbc_s[0:8, :] = extbc_s[ROWS : ROWS + 8, :]
    row, col = iota((CHUNK, CHUNK), 0), iota((CHUNK, CHUNK), 1)
    causal = row >= col
    tri = jnp.where(causal, 1.0, 0.0).astype(bf16)
    first = iota((CHUNK, WIDE), 1) < WIDE // 2
    for sub in range(ROWS // CHUNK):
        lo = sub * CHUNK
        b_low = bc[lo : lo + CHUNK, :states]
        c_low = bc[lo : lo + CHUNK, states:]
        _, dt, _, cum = decays(step_ref[lo : lo + CHUNK, :], head_ref, tri)
        cum_t = cum.T
        cross = low_dot(c_low, b_low, NT)
        state_low = state_s[...].astype(bf16)
        state_ref[sub] = state_low
        b_t = b_low.T
        for pair in range(width // WIDE):
            lanes = slice(pair * WIDE, (pair + 1) * WIDE)
            cum_a, cum_b, cum_p = spread_lanes(cum, pair, first)
            _, _, dt_p = spread_lanes(dt, pair, first)
            weights = []
            for wide, head in ((cum_a, 2 * pair), (cum_b, 2 * pair + 1)):
                gap = jnp.where(causal, wide - cum_t[head : head + 1, :], FAR)
                weights.append((cross * jnp.exp(gap)).astype(bf16))
            x = x_s[lo : lo + CHUNK, lanes]
            scaled = x * dt_p
            zero = jnp.zeros_like(scaled)
            stacked = jnp.concatenate(
                [jnp.where(first, scaled, zero), jnp.where(first, zero, scaled)], axis=0
            ).astype(bf16)
            y = low_dot(jnp.concatenate(weights, axis=1), stacked, NN)
            y = y + jnp.exp(cum_p) * low_dot(c_low, state_low[:, lanes], NN)
            y_ref[lo : lo + CHUNK, lanes] = y + lane_ref[5:6, lanes] * x
            last = cum_p[CHUNK - 1 : CHUNK, :]
            ends = (scaled * jnp.exp(last - cum_p)).astype(bf16)
            state_s[:, lanes] = state_s[:, lanes] * jnp.exp(last) + low_dot(b_t, ends, NN)
    gate = gate_ref[...]
    gated = y_ref[...] * (gate * sigmoid(gate))
    scale = lax.rsqrt(jnp.mean(gated * gated, axis=1, keepdims=True) + EPS)
    out_ref[:, :width] = (gated * scale * lane_ref[4:5, :]).astype(bf16)
    out_ref[:, width:] = attn_ref[...]


def mixer_bwd_body(
    order, gate_ref, inner_ref, before_ref, step_ref, bc_ref, bcbefore_ref, y_ref, state_ref,
    grad_ref, dq_ref, dkv_ref, lane_ref, conv_ref, head_ref, seg_ref,
    low_ref, lowsh_ref, dlane_ref, dconv_ref, dhead_ref,
    ext_s, extbc_s, pre_s, prebc_s, x_s, bc_s, g_s, dx_s, dbc_s, dpre_s, dprebc_s, dstate_s,
    z_s, rows_s,
):
    bf16, f32 = jnp.bfloat16, jnp.float32
    step = pl.program_id(0)
    blocks = pl.num_programs(0)
    width = inner_ref.shape[1]
    states = bc_ref.shape[1] // 2
    query_width = dq_ref.shape[1]

    @pl.when(step == 0)
    def _():
        dlane_ref[...] = jnp.zeros_like(dlane_ref)
        dconv_ref[...] = jnp.zeros_like(dconv_ref)
        dhead_ref[...] = jnp.zeros_like(dhead_ref)
        dstate_s[...] = jnp.zeros_like(dstate_s)
        dpre_s[ROWS:, :] = jnp.zeros((8, width), f32)
        dprebc_s[ROWS:, :] = jnp.zeros((8, 2 * states), f32)
        z_s[...] = jnp.zeros_like(z_s)
        rows_s[...] = jnp.zeros_like(rows_s)

    keep = jnp.where(step == blocks - 1, 0.0, 1.0)
    ext_s[0:8, :] = before_ref[...] * keep
    extbc_s[0:8, :] = bcbefore_ref[...] * keep
    ext_s[8:, :] = inner_ref[...]
    extbc_s[8:, :] = bc_ref[...]
    pre = conv_taps(ext_s, lane_ref, 0, KC)
    pre_s[...] = pre
    x_s[...] = pre * sigmoid(pre)
    pre = conv_taps(extbc_s, conv_ref, 0, KC)
    prebc_s[...] = pre
    bc_s[...] = (pre * sigmoid(pre)).astype(bf16)

    gate = gate_ref[...]
    sig = sigmoid(gate)
    gate_act = gate * sig
    y = y_ref[...]
    gated = y * gate_act
    scale = lax.rsqrt(jnp.mean(gated * gated, axis=1, keepdims=True) + EPS)
    grad = grad_ref[...]
    dlane_ref[4:5, :] += jnp.sum(grad * gated * scale, axis=0, keepdims=True)
    grad = grad * lane_ref[4:5, :]
    mean = jnp.mean(grad * gated, axis=1, keepdims=True)
    dgated = scale * grad - gated * (scale * scale * scale * mean)
    g_s[...] = dgated * gate_act
    low_ref[:, :width] = (dgated * y * sig * (1.0 + gate * (1.0 - sig))).astype(bf16)

    row, col = iota((CHUNK, CHUNK), 0), iota((CHUNK, CHUNK), 1)
    tri = jnp.where(row >= col, 1.0, 0.0).astype(bf16)
    tri_up = jnp.where(row <= col, 1.0, 0.0).astype(bf16)
    later = row <= col
    first = iota((CHUNK, WIDE), 1) < WIDE // 2
    last_row = iota((CHUNK, WIDE), 0) == CHUNK - 1
    for sub in reversed(range(ROWS // CHUNK)):
        lo = sub * CHUNK
        b_low = bc_s[lo : lo + CHUNK, :states]
        c_low = bc_s[lo : lo + CHUNK, states:]
        shifted, dt, la, cum = decays(step_ref[lo : lo + CHUNK, :], head_ref, tri)
        cum_t = cum.T
        cross_t = low_dot(b_low, c_low, NT)
        c_t = c_low.T
        state_low = state_ref[sub]
        dstate_low = dstate_s[...].astype(bf16)
        dcross_t = jnp.zeros((CHUNK, CHUNK), f32)
        db = jnp.zeros((CHUNK, states), f32)
        dc = jnp.zeros((CHUNK, states), f32)
        for pair in range(width // WIDE):
            lanes = slice(pair * WIDE, (pair + 1) * WIDE)
            cum_a, cum_b, cum_p = spread_lanes(cum, pair, first)
            _, _, dt_p = spread_lanes(dt, pair, first)
            x = x_s[lo : lo + CHUNK, lanes]
            g = g_s[lo : lo + CHUNK, lanes]
            scaled = x * dt_p
            scaled_low = scaled.astype(bf16)
            zero = jnp.zeros_like(g)
            g_stack = jnp.concatenate(
                [jnp.where(first, g, zero), jnp.where(first, zero, g)], axis=0
            ).astype(bf16)
            dweights_t = low_dot(scaled_low, g_stack, NT)
            weights_t = []
            for place, wide, head in ((0, cum_a, 2 * pair), (1, cum_b, 2 * pair + 1)):
                gap = jnp.where(later, cum_t[head : head + 1, :] - wide, FAR)
                grow = jnp.exp(gap)
                weight = (cross_t * grow).astype(bf16)
                weights_t.append(weight)
                dweight = dweights_t[:, place * CHUNK : (place + 1) * CHUNK]
                dcross_t = dcross_t + dweight * grow
                rows_s[head : head + 1, :] = jnp.sum(
                    dweight * weight.astype(f32), axis=0, keepdims=True
                )
            dx_in = low_dot(jnp.concatenate(weights_t, axis=1), g_stack, NN)
            grown = jnp.exp(cum_p)
            last = cum_p[CHUNK - 1 : CHUNK, :]
            tail = jnp.exp(last - cum_p)
            last = jnp.exp(last)
            dx_tail = tail * low_dot(b_low, dstate_low[:, lanes], NN)
            dscaled = dx_in + dx_tail
            g_grown = g * grown
            g_low = g_grown.astype(bf16)
            ends = (scaled * tail).astype(bf16)
            carried = low_dot(c_low, state_low[:, lanes], NN)
            dc = dc + low_dot(g_low, state_low[:, lanes], NT)
            db = db + low_dot(ends, dstate_low[:, lanes], NT)
            dstate = dstate_s[:, lanes]
            kept = jnp.sum(dstate * state_low[:, lanes].astype(f32), axis=0, keepdims=True) * last
            dstate_s[:, lanes] = dstate * last + low_dot(c_t, g_low, NN)
            tails = scaled * dx_tail
            z_s[0:CHUNK, lanes] = g_grown * carried - tails - scaled_low.astype(f32) * dx_in
            z_s[CHUNK : 2 * CHUNK, lanes] = dscaled * x
            z_s[2 * CHUNK : 2 * CHUNK + 1, lanes] = (
                jnp.sum(tails, axis=0, keepdims=True) + kept
            )
            dx_s[lo : lo + CHUNK, lanes] = dscaled * dt_p + lane_ref[5:6, lanes] * g
            dlane_ref[5:6, lanes] += jnp.sum(g * x, axis=0, keepdims=True)
        sums = split_dot(z_s[...], seg_ref[...])
        dcum = sums[0:CHUNK, :] + rows_s[...].T
        dcum = dcum + jnp.where(last_row, sums[2 * CHUNK : 2 * CHUNK + 1, :], 0.0)
        dla = exact_dot(tri_up, dcum)
        ddt = sums[CHUNK : 2 * CHUNK, :] + dla * head_ref[1:2, :]
        dsteps = ddt * sigmoid(shifted)
        dhead_ref[0:1, :] += jnp.sum(dsteps, axis=0, keepdims=True)
        dhead_ref[1:2, :] += jnp.sum(dla * la, axis=0, keepdims=True)
        low_ref[lo : lo + CHUNK, 2 * width + query_width :] = dsteps.astype(bf16)
        dcross_low = dcross_t.astype(bf16)
        dbc_s[lo : lo + CHUNK, :states] = db + low_dot(dcross_low, c_low, NN)
        dbc_s[lo : lo + CHUNK, states:] = dc + low_dot(dcross_low, b_low, TN)

    def conv_back(pre_ref, dact, dpre_ref, ext, taps, dtaps_ref):
        pre = pre_ref[...]
        sig = sigmoid(pre)
        dpre = dact * (sig * (1.0 + pre * (1.0 - sig)))
        dpre_ref[0:ROWS, :] = dpre
        total = None
        for tap in range(KC):
            ahead = KC - 1 - tap
            term = dpre_ref[ahead : ahead + ROWS, :] * taps[tap : tap + 1, :]
            total = term if total is None else total + term
            at = 8 - (KC - 1) + tap
            dtaps_ref[tap : tap + 1, :] += jnp.sum(
                dpre * ext[at : at + ROWS, :], axis=0, keepdims=True
            )
        dpre_ref[ROWS:, :] = dpre_ref[0:8, :]
        return total

    dinner = conv_back(pre_s, dx_s[...], dpre_s, ext_s, lane_ref, dlane_ref)
    low_ref[:, width : 2 * width] = dinner.astype(bf16)
    dbc = conv_back(prebc_s, dbc_s[...], dprebc_s, extbc_s, conv_ref, dconv_ref)
    lowsh_ref[:, : 2 * states] = dbc.astype(bf16)
    lowsh_ref[:, 2 * states :] = dkv_ref[...]
    low_ref[:, 2 * width : 2 * width + query_width] = dq_ref[...]


def block_at(rows, cols, col):
    return pl.BlockSpec((rows, cols), lambda i, order: (order[i], col))


def whole_at(shape):
    return pl.BlockSpec(shape, lambda i, order: (0,) * len(shape))


def kernel_params():
    return pltpu.CompilerParams(
        dimension_semantics=("arbitrary",), vmem_limit_bytes=56 * 1024 * 1024
    )


def attn_forward(order, proj, proj_shared, cosine, sine, query_width, width, bc_width):
    slot = proj.shape[0]
    scratch = [pltpu.VMEM((slot, HD), jnp.bfloat16)] * 2
    return pl.pallas_call(
        attn_fwd_body,
        grid_spec=pltpu.PrefetchScalarGridSpec(
            num_scalar_prefetch=1,
            grid=(slot // ROWS,),
            in_specs=[
                block_at(ROWS, query_width, 2 * width // query_width),
                block_at(ROWS, 2 * HD, bc_width // (2 * HD)),
                pl.BlockSpec((ROWS, HD), lambda i, order: (i, 0)),
                pl.BlockSpec((ROWS, HD), lambda i, order: (i, 0)),
            ],
            out_specs=block_at(ROWS, query_width, 0),
            scratch_shapes=scratch,
        ),
        out_shape=jax.ShapeDtypeStruct((slot, query_width), jnp.bfloat16),
        compiler_params=kernel_params(),
        cost_estimate=pl.CostEstimate(
            flops=slot * slot * query_width * 3,
            bytes_accessed=slot * 4 * (query_width + 4 * HD),
            transcendentals=slot * slot * query_width // HD,
        ),
    )(order, proj, proj_shared, cosine, sine)


def attn_backward(order, proj, proj_shared, cosine, sine, grad_heads, query_width, width, bc_width):
    slot = proj.shape[0]
    return pl.pallas_call(
        attn_bwd_body,
        grid_spec=pltpu.PrefetchScalarGridSpec(
            num_scalar_prefetch=1,
            grid=(slot // ROWS,),
            in_specs=[
                block_at(ROWS, query_width, 2 * width // query_width),
                block_at(ROWS, 2 * HD, bc_width // (2 * HD)),
                pl.BlockSpec((ROWS, HD), lambda i, order: (i, 0)),
                pl.BlockSpec((ROWS, HD), lambda i, order: (i, 0)),
                block_at(ROWS, query_width, width // query_width),
                whole_at((slot, HD)),
                whole_at((slot, HD)),
            ],
            out_specs=[block_at(ROWS, query_width, 0), whole_at((slot, 2 * HD))],
            scratch_shapes=[pltpu.VMEM((slot, HD), jnp.bfloat16)] * 2
            + [pltpu.VMEM((slot, HD), jnp.float32)] * 2,
        ),
        out_shape=[
            jax.ShapeDtypeStruct((slot, query_width), jnp.bfloat16),
            jax.ShapeDtypeStruct((slot, 2 * HD), jnp.bfloat16),
        ],
        compiler_params=kernel_params(),
        cost_estimate=pl.CostEstimate(
            flops=slot * slot * query_width * 8,
            bytes_accessed=slot * 4 * (2 * query_width + 6 * HD),
            transcendentals=slot * slot * query_width // HD,
        ),
    )(order, proj, proj_shared, cosine, sine, grad_heads, cosine, sine)


def mixer_forward(order, proj, proj_shared, attn_low, lane_params, conv_shared, head_params):
    slot = proj.shape[0]
    f32, bf16 = jnp.float32, jnp.bfloat16
    width = lane_params.shape[1]
    bc_width = conv_shared.shape[1]
    query_width = attn_low.shape[1]
    chunks = ROWS // CHUNK
    return pl.pallas_call(
        mixer_fwd_body,
        grid_spec=pltpu.PrefetchScalarGridSpec(
            num_scalar_prefetch=1,
            grid=(slot // ROWS,),
            in_specs=[
                block_at(ROWS, width, 0),
                block_at(ROWS, width, 1),
                block_at(ROWS, WIDE, (2 * width + query_width) // WIDE),
                block_at(ROWS, bc_width, 0),
                block_at(ROWS, query_width, 0),
                whole_at(lane_params.shape),
                whole_at(conv_shared.shape),
                whole_at(head_params.shape),
            ],
            out_specs=[
                block_at(ROWS, width + query_width, 0),
                pl.BlockSpec((ROWS, width), lambda i, order: (i, 0)),
                pl.BlockSpec((chunks, bc_width // 2, width), lambda i, order: (i, 0, 0)),
            ],
            scratch_shapes=[
                pltpu.VMEM((ROWS + 8, width), f32),
                pltpu.VMEM((ROWS + 8, bc_width), f32),
                pltpu.VMEM((bc_width // 2, width), f32),
                pltpu.VMEM((ROWS, width), f32),
            ],
        ),
        out_shape=[
            jax.ShapeDtypeStruct((slot, width + query_width), bf16),
            jax.ShapeDtypeStruct((slot, width), f32),
            jax.ShapeDtypeStruct((slot // CHUNK, bc_width // 2, width), bf16),
        ],
        compiler_params=kernel_params(),
        cost_estimate=pl.CostEstimate(
            flops=slot * width * bc_width * 8,
            bytes_accessed=slot * width * 20,
            transcendentals=slot * width * 8,
        ),
    )(order, proj, proj, proj, proj_shared, attn_low, lane_params, conv_shared, head_params)


def mixer_backward(
    order, proj, proj_shared, y, states, grad_heads, dq, dkv, lane_params, conv_shared,
    head_params, seg, query_width,
):
    slot = proj.shape[0]
    f32, bf16 = jnp.float32, jnp.bfloat16
    width = lane_params.shape[1]
    bc_width = conv_shared.shape[1]
    blocks = slot // ROWS
    chunks = ROWS // CHUNK

    def back(rows, cols, col):
        return pl.BlockSpec((rows, cols), lambda i, order: (order[blocks - 1 - i], col))

    def straight(shape):
        return pl.BlockSpec(
            shape, lambda i, order: (blocks - 1 - i,) + (0,) * (len(shape) - 1)
        )

    def before(cols, col):
        return pl.BlockSpec(
            (8, cols),
            lambda i, order: (
                order[jnp.maximum(blocks - 2 - i, 0)] * (ROWS // 8) + ROWS // 8 - 1,
                col,
            ),
        )

    return pl.pallas_call(
        mixer_bwd_body,
        grid_spec=pltpu.PrefetchScalarGridSpec(
            num_scalar_prefetch=1,
            grid=(blocks,),
            in_specs=[
                back(ROWS, width, 0),
                back(ROWS, width, 1),
                before(width, 1),
                back(ROWS, WIDE, (2 * width + query_width) // WIDE),
                back(ROWS, bc_width, 0),
                before(bc_width, 0),
                straight((ROWS, width)),
                straight((chunks, bc_width // 2, width)),
                back(ROWS, width, 0),
                back(ROWS, query_width, 0),
                straight((ROWS, 2 * HD)),
                whole_at(lane_params.shape),
                whole_at(conv_shared.shape),
                whole_at(head_params.shape),
                whole_at(seg.shape),
            ],
            out_specs=[
                back(ROWS, 2 * width + query_width + WIDE, 0),
                back(ROWS, bc_width + 2 * HD, 0),
                whole_at((8, width)),
                whole_at((8, bc_width)),
                whole_at((8, WIDE)),
            ],
            scratch_shapes=[
                pltpu.VMEM((ROWS + 8, width), f32),
                pltpu.VMEM((ROWS + 8, bc_width), f32),
                pltpu.VMEM((ROWS, width), f32),
                pltpu.VMEM((ROWS, bc_width), f32),
                pltpu.VMEM((ROWS, width), f32),
                pltpu.VMEM((ROWS, bc_width), bf16),
                pltpu.VMEM((ROWS, width), f32),
                pltpu.VMEM((ROWS, width), f32),
                pltpu.VMEM((ROWS, bc_width), f32),
                pltpu.VMEM((ROWS + 8, width), f32),
                pltpu.VMEM((ROWS + 8, bc_width), f32),
                pltpu.VMEM((bc_width // 2, width), f32),
                pltpu.VMEM((2 * CHUNK + 8, width), f32),
                pltpu.VMEM((WIDE, CHUNK), f32),
            ],
        ),
        out_shape=[
            jax.ShapeDtypeStruct((slot, 2 * width + query_width + WIDE), bf16),
            jax.ShapeDtypeStruct((slot, bc_width + 2 * HD), bf16),
            jax.ShapeDtypeStruct((8, width), f32),
            jax.ShapeDtypeStruct((8, bc_width), f32),
            jax.ShapeDtypeStruct((8, WIDE), f32),
        ],
        compiler_params=kernel_params(),
        cost_estimate=pl.CostEstimate(
            flops=slot * width * bc_width * 20,
            bytes_accessed=slot * width * 40,
            transcendentals=slot * width * 16,
        ),
    )(
        order, proj, proj, proj, proj, proj_shared, proj_shared, y, states, grad_heads, dq, dkv,
        lane_params, conv_shared, head_params, seg,
    )


class Places:
    def __init__(self):
        self.dp = lax.axis_size("dp")
        self.tp = lax.axis_size("tensor")
        d = lax.axis_index("dp")
        t = lax.axis_index("tensor")
        self.d, self.t = d, t
        self.c = d % 2
        self.k = d // 2
        self.zq = t % 2
        self.home = self.c == t // 2
        self.quarter = 2 * self.c + self.zq
        self.column = self.zq + 2 * self.c
        self.slot = 2 * self.k + t // 2
        self.blocks = self.dp // 2
        self.bits = self.blocks.bit_length() - 1

    def pairs(self, where_to):
        out = []
        for d in range(self.dp):
            for t in range(self.tp):
                target = where_to(d, t)
                if target is not None:
                    out.append((d * self.tp + t, target[0] * self.tp + target[1]))
        return out

    def send(self, values, where_to):
        return lax.ppermute(values, ("dp", "tensor"), self.pairs(where_to))

    def over_core(self, values):
        return self.send(values, lambda d, t: (d ^ 1, t))

    def over_z(self, values):
        return self.send(values, lambda d, t: (d, t ^ 1))

    def over_far(self, values):
        return self.send(values, lambda d, t: (d, t ^ 2))

    def over_bit(self, values, bit):
        return self.send(values, lambda d, t: (d ^ (2 << bit), t))

    def swap_away(self, values):
        def where_to(d, t):
            if d % 2 == t // 2:
                return None
            return (d ^ 1, t ^ 2)

        return self.send(values, where_to)

    def column_out(self, values):
        def where_to(d, t):
            if d % 2 == t // 2:
                return (d, t ^ 2)
            return (d ^ 1, t)

        return self.send(values, where_to)

    def column_back(self, values):
        def where_to(d, t):
            if d % 2 == t // 2:
                return (d ^ 1, t)
            return (d, t ^ 2)

        return self.send(values, where_to)


def relocate(values, at):
    return jnp.where(at.home, values, at.swap_away(values))


def turn_features(values, at, axis):
    block = values.shape[axis] // at.blocks
    parts = [
        lax.slice_in_dim(values, place * block, (place + 1) * block, axis=axis)
        for place in range(at.blocks)
    ]
    for bit in range(at.bits):
        turned = (at.k >> bit) % 2 == 1
        parts = [
            jnp.where(turned, parts[place ^ (1 << bit)], parts[place])
            for place in range(at.blocks)
        ]
    return jnp.concatenate(parts, axis=axis)


def share_rows(values, at):
    far = at.over_z(values)
    core = at.over_core(values)
    both = at.over_core(far)
    return (values, core, far, both)


def sum_rows(pieces, at):
    own, core, far, both = pieces
    bf16 = jnp.bfloat16
    from_both = at.over_core(both.astype(bf16))
    passed = (far + from_both.astype(jnp.float32)).astype(bf16)
    from_far = at.over_z(passed)
    from_core = at.over_core(core.astype(bf16))
    return own + from_core.astype(jnp.float32) + from_far.astype(jnp.float32)


def spread(piece, at, upward):
    found = {0: piece}
    order = range(at.bits) if upward else reversed(range(at.bits))
    for bit in order:
        for place in sorted(found):
            found[place | (1 << bit)] = at.over_bit(found[place], bit)
    return found


def gather_weight(shard, at):
    first_in = at.column_out(shard)
    second_in = at.swap_away(shard)
    own = jnp.where(at.home, shard, first_in)
    other = jnp.where(at.home, first_in, second_in)
    low = jnp.where(at.c == 0, own, other)
    high = jnp.where(at.c == 0, other, own)
    lows = spread(low, at, True)
    highs = spread(high, at, False)
    return jnp.concatenate(
        [part for place in range(at.blocks) for part in (lows[place], highs[place])], axis=0
    )


def collect(piece_of, at, half):
    bf16 = jnp.bfloat16
    bits = list(range(at.bits))
    order = list(reversed(bits)) if half == 0 else bits
    arrived = {}
    places = list(range(at.blocks))

    def total(place):
        value = piece_of(place, half)
        for part in arrived.get(place, []):
            value = value + part.astype(jnp.float32)
        return value

    for bit in order:
        going = [place for place in places if (place >> bit) & 1]
        places = [place for place in places if not (place >> bit) & 1]
        for place in going:
            part = at.over_bit(total(place).astype(bf16), bit)
            arrived.setdefault(place ^ (1 << bit), []).append(part)
    return total(0)


def scatter_weight(piece_of, at):
    bf16 = jnp.bfloat16
    low = collect(piece_of, at, 0)
    high = collect(piece_of, at, 1)
    own = jnp.where(at.c == 0, low, high)
    other = jnp.where(at.c == 0, high, low)
    first_in = at.column_back(jnp.where(at.home, other, own).astype(bf16)).astype(jnp.float32)
    second_in = at.swap_away(other.astype(bf16)).astype(jnp.float32)
    return first_in + jnp.where(at.home, own, second_in)


def gather_shared(shard, at):
    rows, width = shard.shape
    half = width // 2
    mine = jnp.where(at.c == 0, shard[:, :half], shard[:, half:])
    theirs = jnp.where(at.c == 0, shard[:, half:], shard[:, :half])
    came = at.over_core(theirs)
    both = jnp.stack([jnp.where(at.c == 0, mine, came), jnp.where(at.c == 0, came, mine)])
    near = at.over_z(both)
    lowest = at.t % 2 == 0
    two = jnp.stack([jnp.where(lowest, both, near), jnp.where(lowest, near, both)], axis=1)
    far = at.over_far(two)
    lower = at.t // 2 == 0
    four = jnp.stack([jnp.where(lower, two, far), jnp.where(lower, far, two)], axis=1)
    line = four.reshape(2, rows * at.tp, half)
    lows = spread(line[0], at, True)
    highs = spread(line[1], at, False)
    part = jnp.concatenate(
        [piece for place in range(at.blocks) for piece in (lows[place], highs[place])], axis=0
    )
    other = at.over_core(part)
    return jnp.where(at.c == 0, part, other), jnp.where(at.c == 0, other, part)


def scatter_shared(grad_bc, grad_kv, at):
    f32, bf16 = jnp.float32, jnp.bfloat16
    first = at.c == 0
    bc_width = grad_bc.shape[1]
    going = jnp.where(
        first, jnp.pad(grad_kv, ((0, 0), (0, bc_width - grad_kv.shape[1]))), grad_bc
    )
    came = at.over_core(going.astype(bf16)).astype(f32)
    kept = jnp.concatenate(
        [came[:, :HD], grad_kv[:, :HD], came[:, HD : 2 * HD], grad_kv[:, HD:]], axis=1
    )
    total = jnp.where(first, grad_bc + came, kept)
    rows = total.shape[0] // (2 * at.blocks)
    parts = total.reshape(at.blocks, 2, rows, total.shape[1])
    low = collect(lambda place, half: parts[place, half], at, 0)
    high = collect(lambda place, half: parts[place, half], at, 1)
    piece = rows // at.tp
    line = jnp.stack([low, high]).reshape(2, 2, 2, piece, total.shape[1])
    lower = at.t // 2 == 0
    went = at.over_far(jnp.where(lower, line[:, 1], line[:, 0]).astype(bf16)).astype(f32)
    line = jnp.where(lower, line[:, 0], line[:, 1]) + went
    lowest = at.t % 2 == 0
    went = at.over_z(jnp.where(lowest, line[:, 1], line[:, 0]).astype(bf16)).astype(f32)
    line = jnp.where(lowest, line[:, 0], line[:, 1]) + went
    mine = jnp.where(first, line[0], line[1])
    came = at.over_core(jnp.where(first, line[1], line[0]).astype(bf16)).astype(f32)
    return jnp.concatenate([jnp.where(first, mine, came), jnp.where(first, came, mine)], axis=1)


def sum_everywhere(values, at):
    for bit in range(at.dp.bit_length() - 1):
        values = values + at.send(values, lambda d, t: (d ^ (1 << bit), t))
    for bit in range(at.tp.bit_length() - 1):
        values = values + at.send(values, lambda d, t: (d, t ^ (1 << bit)))
    return values


def per_device(
    layer_in,
    teacher,
    lengths,
    input_gain,
    mixer_in_weight,
    step_weight,
    query_weight,
    shared_weight,
    conv_inner,
    conv_shared,
    step_bias,
    decay_log,
    skip_gain,
    inner_gain,
    mixer_out_weight,
    attn_out_weight,
    middle_gain,
    gate_up_weight,
    down_weight,
):
    f32 = jnp.float32
    bf16 = jnp.bfloat16
    contract_last = (((1,), (1,)), ((), ()))
    contract_first = (((0,), (0,)), ((), ()))
    at = Places()
    rows_here, features = layer_in.shape
    slot_len = rows_here * at.tp
    local_heads = step_bias.shape[0]
    width = inner_gain.shape[0]
    head_dim = width // local_heads
    query_width = query_weight.shape[1]
    hidden_width = down_weight.shape[1]
    bc_width = conv_shared.shape[1]
    w_rows = step_weight.shape[0]

    inputs = turn_features(relocate(layer_in, at), at, 1).astype(f32)
    target = turn_features(relocate(teacher, at), at, 1).astype(f32)
    gain_in = turn_features(input_gain, at, 0)
    gain_mid = turn_features(middle_gain, at, 0)
    column_params = jnp.concatenate(
        [conv_inner.reshape(-1), inner_gain, step_bias, decay_log, skip_gain]
    )
    column_params = relocate(column_params, at)
    lane_params = jnp.concatenate(
        [
            column_params[: (KC + 1) * width].reshape(KC + 1, width),
            jnp.repeat(column_params[(KC + 1) * width + 2 * local_heads :], head_dim)[None],
            jnp.zeros((2, width), f32),
        ],
        axis=0,
    )
    head_rows = column_params[(KC + 1) * width :][: 2 * local_heads].reshape(2, local_heads)
    head_rows = jnp.concatenate([head_rows[:1], -jnp.exp(head_rows[1:])], axis=0)
    head_params = jnp.pad(head_rows, ((0, 6), (0, WIDE - local_heads)))
    seg = (
        lax.broadcasted_iota(jnp.int32, (width, WIDE), 0) // head_dim
        == lax.broadcasted_iota(jnp.int32, (width, WIDE), 1)
    ).astype(bf16)
    half = HD // 2
    freqs = jnp.exp(-jnp.log(ROPE_BASE) * 2.0 * jnp.arange(half, dtype=f32) / HD)
    angles = jnp.arange(slot_len).astype(f32)[:, None] * freqs[None, :]
    cosine, sine = jnp.cos(angles), jnp.sin(angles)
    cosine = jnp.concatenate([cosine, cosine], axis=1)
    sine = jnp.concatenate([-sine, sine], axis=1)
    quarters = jnp.arange(at.tp, dtype=jnp.int32)
    order = (at.c ^ (quarters // 2)) + 2 * (at.zq ^ (quarters % 2))

    left, right = gather_shared(shared_weight, at)
    kv_index = at.column * (query_width // HD) // (QH // KVH)
    second = kv_index == 1
    shared_all = jnp.concatenate(
        [
            left,
            jnp.where(second, right[:, HD : 2 * HD], right[:, :HD]),
            jnp.where(second, right[:, 3 * HD :], right[:, 2 * HD : 3 * HD]),
        ],
        axis=1,
    )
    in_pack = jnp.concatenate(
        [
            mixer_in_weight.reshape(w_rows, 2 * width),
            query_weight,
            step_weight,
            jnp.zeros((w_rows, WIDE - local_heads), bf16),
        ],
        axis=1,
    )
    in_all = gather_weight(in_pack, at)
    out_all = gather_weight(jnp.concatenate([mixer_out_weight, attn_out_weight], axis=1), at)
    gate_up_all = gather_weight(gate_up_weight.reshape(w_rows, 2 * hidden_width), at)
    down_all = gather_weight(down_weight, at)

    def row_split(values):
        return [values[i * rows_here : (i + 1) * rows_here] for i in range(at.tp)]

    normed_in, norm_in_back = jax.vjp(rms_norm, inputs, gain_in)
    act_all = jnp.concatenate(share_rows(normed_in.astype(bf16), at), axis=0)
    proj_shared = jnp.dot(act_all, shared_all, preferred_element_type=f32)
    proj = jnp.dot(act_all, in_all, preferred_element_type=f32)
    attn_low = attn_forward(order, proj, proj_shared, cosine, sine, query_width, width, bc_width)
    heads_all, y, states = mixer_forward(
        order, proj, proj_shared, attn_low, lane_params, conv_shared, head_params
    )
    mix_parts = [
        lax.dot_general(piece, out_all, contract_last, preferred_element_type=f32)
        for piece in row_split(heads_all)
    ]
    resid = inputs + sum_rows(mix_parts, at)
    normed_mid, norm_mid_back = jax.vjp(rms_norm, resid, gain_mid)
    mid_all = jnp.concatenate(share_rows(normed_mid.astype(bf16), at), axis=0)
    gate_up = jnp.dot(mid_all, gate_up_all, preferred_element_type=f32)
    gate_val = gate_up[:, :hidden_width]
    up_val = gate_up[:, hidden_width:]
    sigmoid_gate = jax.nn.sigmoid(gate_val)
    hidden = (gate_val * sigmoid_gate * up_val).astype(bf16)
    mlp_parts = [
        lax.dot_general(piece, down_all, contract_last, preferred_element_type=f32)
        for piece in row_split(hidden)
    ]
    outputs = resid + sum_rows(mlp_parts, at)
    seq_len = lax.dynamic_index_in_dim(lengths, at.slot, keepdims=False)
    positions = at.quarter * rows_here + jnp.arange(rows_here)
    live = (positions < seq_len).astype(f32)
    error = (outputs - target) * live[:, None]
    err_local = 0.5 * jnp.sum(error * error)
    layer_out = relocate(turn_features(outputs.astype(bf16), at, 1), at)

    grad_all = jnp.concatenate(share_rows(error.astype(bf16), at), axis=0)
    block = features // (2 * at.blocks)

    def columns_of(values, place, half):
        start = (2 * place + half) * block
        return values[:, start : start + block]

    def weight_grad(left, right):
        def piece_of(place, half):
            return lax.dot_general(
                columns_of(left, place, half), right, contract_first, preferred_element_type=f32
            )

        return scatter_weight(piece_of, at)

    grad_down = weight_grad(grad_all, hidden)
    grad_hidden = jnp.dot(grad_all, down_all, preferred_element_type=f32)
    grad_gate = grad_hidden * up_val * sigmoid_gate * (1.0 + gate_val * (1.0 - sigmoid_gate))
    grad_up = grad_hidden * gate_val * sigmoid_gate
    grad_gu = jnp.concatenate([grad_gate.astype(bf16), grad_up.astype(bf16)], axis=1)
    grad_mid_parts = [
        lax.dot_general(piece, gate_up_all, contract_last, preferred_element_type=f32)
        for piece in row_split(grad_gu)
    ]
    grad_gate_up = weight_grad(mid_all, grad_gu)
    grad_mid = sum_rows(grad_mid_parts, at)
    grad_resid_norm, grad_middle_gain = norm_mid_back(grad_mid)
    grad_resid = error + grad_resid_norm
    mix_grad_all = jnp.concatenate(share_rows(grad_resid.astype(bf16), at), axis=0)
    grad_heads = jnp.dot(mix_grad_all, out_all, preferred_element_type=f32)
    grad_out = weight_grad(mix_grad_all, heads_all)
    dq, dkv = attn_backward(
        order, proj, proj_shared, cosine, sine, grad_heads, query_width, width, bc_width
    )
    low_pack, low_shared, dlane, dconv, dhead = mixer_backward(
        order, proj, proj_shared, y, states, grad_heads, dq, dkv, lane_params, conv_shared,
        head_params, seg, query_width,
    )
    grad_bc = lax.dot_general(
        act_all, low_shared[:, :bc_width], contract_first, preferred_element_type=f32
    )
    grad_kv = lax.dot_general(
        act_all, low_shared[:, bc_width:], contract_first, preferred_element_type=f32
    )
    grad_shared_weight = scatter_shared(grad_bc, grad_kv, at)
    grad_in = weight_grad(act_all, low_pack)
    grad_act_parts = [
        lax.dot_general(a, in_all, contract_last, preferred_element_type=f32)
        + lax.dot_general(b, shared_all, contract_last, preferred_element_type=f32)
        for a, b in zip(row_split(low_pack), row_split(low_shared))
    ]
    grad_act = sum_rows(grad_act_parts, at)
    grad_input_norm, grad_input_gain = norm_in_back(grad_act)
    input_grad = grad_resid + grad_input_norm
    input_grad = relocate(turn_features(input_grad, at, 1), at)

    column = at.column
    convx_full = lax.dynamic_update_slice(
        jnp.zeros((KC + 1, DI), f32), dlane[: KC + 1], (0, column * width)
    )
    head_stack = jnp.concatenate(
        [dhead[:2, :local_heads], dlane[KC + 1].reshape(1, local_heads, head_dim).sum(2)], axis=0
    )
    heads_full = lax.dynamic_update_slice(
        jnp.zeros((3, H), f32), head_stack, (0, column * local_heads)
    )
    small = (
        convx_full,
        dconv[:KC],
        heads_full,
        turn_features(grad_input_gain, at, 0),
        turn_features(grad_middle_gain, at, 0),
        err_local,
    )
    flat = jnp.concatenate([part.reshape(-1) for part in small])
    length = flat.shape[0]
    padded = -(-length // 1024) * 1024
    flat = jnp.pad(flat, (0, padded - length)).reshape(-1, 128)
    flat = sum_everywhere(flat, at).reshape(-1)
    sums = []
    start = 0
    for part in small:
        sums.append(flat[start : start + part.size].reshape(part.shape))
        start += part.size
    sum_lanes, sum_convs, sum_heads, sum_input_gain, sum_middle_gain, err_total = sums
    lanes_local = lax.dynamic_slice_in_dim(sum_lanes, at.t * width, width, 1)
    heads_local = lax.dynamic_slice_in_dim(sum_heads, at.t * local_heads, local_heads, 1)
    loss = err_total / jnp.sum(lengths).astype(f32)
    query_from = 2 * width
    step_from = query_from + query_width
    return (
        layer_out,
        loss,
        input_grad,
        sum_input_gain,
        grad_in[:, :query_from].reshape(w_rows, 2, width),
        grad_in[:, step_from : step_from + local_heads],
        grad_in[:, query_from:step_from],
        grad_shared_weight,
        lanes_local[:KC],
        sum_convs,
        heads_local[0],
        heads_local[1],
        heads_local[2],
        lanes_local[KC],
        grad_out[:, :width],
        grad_out[:, width:],
        sum_middle_gain,
        grad_gate_up.reshape(w_rows, 2, hidden_width),
        grad_down,
    )


def solution(mesh):
    placed = (
        P(("dp", "tensor"), None),
        P(("dp", "tensor"), None),
        P(),
        P(),
        P("dp", None, "tensor"),
        P("dp", "tensor"),
        P("dp", "tensor"),
        P(("dp", "tensor"), None),
        P(None, "tensor"),
        P(),
        P("tensor"),
        P("tensor"),
        P("tensor"),
        P("tensor"),
        P("dp", "tensor"),
        P("dp", "tensor"),
        P(),
        P("dp", None, "tensor"),
        P("dp", "tensor"),
    )
    return jax.shard_map(
        per_device,
        mesh=mesh,
        in_specs=placed,
        out_specs=(
            P(("dp", "tensor"), None),
            P(),
            P(("dp", "tensor"), None),
            P(),
            P("dp", None, "tensor"),
            P("dp", "tensor"),
            P("dp", "tensor"),
            P(("dp", "tensor"), None),
            P(None, "tensor"),
            P(),
            P("tensor"),
            P("tensor"),
            P("tensor"),
            P("tensor"),
            P("dp", "tensor"),
            P("dp", "tensor"),
            P(),
            P("dp", None, "tensor"),
            P("dp", "tensor"),
        ),
        check_vma=False,
    )
```

```python
import functools

import jax
import jax.numpy as jnp
from jax import lax
from jax.experimental import pallas as pl
from jax.experimental.pallas import tpu as pltpu
from jax.sharding import PartitionSpec as P

H = 48
KC = 4
QH = 8
KVH = 2
HD = 128
DI = 3072

EPS = 1e-05
ROPE_BASE = 100000000000.0


def rms_norm(values, gain):
    return values * lax.rsqrt(jnp.mean(values * values, axis=-1, keepdims=True) + EPS) * gain


def low_dot(left, right, dims):
    return lax.dot_general(left, right, (dims, ((), ())), preferred_element_type=jnp.float32)


NN = ((1,), (0,))
NT = ((1,), (1,))
TN = ((0,), (0,))
CHUNK = 128
ROWS = 256
WIDE = 128
FAR = -1e30


def exact_dot(ones, values, parts=3):
    total = None
    for _ in range(parts):
        part = values.astype(jnp.bfloat16)
        values = values - part.astype(jnp.float32)
        term = low_dot(ones, part, NN)
        total = term if total is None else total + term
    return total


def split_dot(values, ones, parts=2):
    total = None
    for _ in range(parts):
        part = values.astype(jnp.bfloat16)
        values = values - part.astype(jnp.float32)
        term = low_dot(part, ones, NN)
        total = term if total is None else total + term
    return total


def sigmoid(v):
    return 1.0 / (1.0 + jnp.exp(-v))


def softplus(v):
    return jnp.maximum(v, 0.0) + jnp.log1p(jnp.exp(-jnp.abs(v)))


def iota(shape, axis):
    return lax.broadcasted_iota(jnp.int32, shape, axis)


def spin(values, cosine, sine):
    return values * cosine + pltpu.roll(values, HD // 2, 1) * sine


def unspin(values, cosine, sine):
    return values * cosine - pltpu.roll(values, HD // 2, 1) * sine


def attn_probs(query_low, key_low, first_row, scale):
    scores = low_dot(query_low, key_low, NT) * scale
    rows, keys = scores.shape
    allowed = iota((rows, keys), 1) <= iota((rows, keys), 0) + first_row
    scores = jnp.where(allowed, scores, FAR)
    top = jnp.max(scores, axis=1, keepdims=True)
    weights = jnp.exp(scores - top)
    return weights / jnp.sum(weights, axis=1, keepdims=True)


def attn_fwd_body(order, q_ref, kv_ref, cos_ref, sin_ref, out_ref, key_s, value_s):
    bf16 = jnp.bfloat16
    step = pl.program_id(0)
    cosine, sine = cos_ref[...], sin_ref[...]
    rows = pl.ds(pl.multiple_of(step * ROWS, ROWS), ROWS)
    key_s[rows, :] = spin(kv_ref[:, :HD], cosine, sine).astype(bf16)
    value_s[rows, :] = kv_ref[:, HD:].astype(bf16)
    heads = q_ref.shape[1] // HD
    blocks = key_s.shape[0] // ROWS
    for block in range(blocks):

        @pl.when(step == block)
        def _(block=block):
            keys = (block + 1) * ROWS
            for head in range(heads):
                lanes = slice(head * HD, (head + 1) * HD)
                query = spin(q_ref[:, lanes], cosine, sine).astype(bf16)
                probs = attn_probs(query, key_s[:keys, :], block * ROWS, HD**-0.5)
                out_ref[:, lanes] = low_dot(
                    probs.astype(bf16), value_s[:keys, :], NN
                ).astype(bf16)


def attn_bwd_body(
    order, q_ref, kv_ref, cos_ref, sin_ref, grad_ref, all_cos, all_sin, dq_ref, dkv_ref,
    key_s, value_s, dkey_s, dvalue_s,
):
    bf16, f32 = jnp.bfloat16, jnp.float32
    step = pl.program_id(0)

    @pl.when(step == 0)
    def _():
        dkey_s[...] = jnp.zeros_like(dkey_s)
        dvalue_s[...] = jnp.zeros_like(dvalue_s)

    cosine, sine = cos_ref[...], sin_ref[...]
    rows = pl.ds(pl.multiple_of(step * ROWS, ROWS), ROWS)
    key_s[rows, :] = spin(kv_ref[:, :HD], cosine, sine).astype(bf16)
    value_s[rows, :] = kv_ref[:, HD:].astype(bf16)
    heads = q_ref.shape[1] // HD
    blocks = key_s.shape[0] // ROWS
    scale = HD**-0.5
    for block in range(blocks):

        @pl.when(step == block)
        def _(block=block):
            keys = (block + 1) * ROWS
            for head in range(heads):
                lanes = slice(head * HD, (head + 1) * HD)
                query = spin(q_ref[:, lanes], cosine, sine).astype(bf16)
                probs = attn_probs(query, key_s[:keys, :], block * ROWS, scale)
                grad = grad_ref[:, lanes].astype(bf16)
                dprobs = low_dot(grad, value_s[:keys, :], NT)
                dvalue_s[:keys, :] += low_dot(probs.astype(bf16), grad, TN)
                inner = jnp.sum(dprobs * probs, axis=1, keepdims=True)
                dscores = (probs * (dprobs - inner) * scale).astype(bf16)
                dquery = low_dot(dscores, key_s[:keys, :], NN)
                dkey_s[:keys, :] += low_dot(dscores, query, TN)
                dq_ref[:, lanes] = unspin(dquery, cosine, sine).astype(bf16)

    @pl.when(step == blocks - 1)
    def _():
        dkv_ref[:, :HD] = unspin(dkey_s[...], all_cos[...], all_sin[...]).astype(bf16)
        dkv_ref[:, HD:] = dvalue_s[...].astype(bf16)


def conv_taps(ext, taps, first, width):
    rows = ext.shape[0] - 8
    total = None
    for tap in range(width):
        at = 8 - (width - 1) + tap
        term = ext[at : at + rows, :] * taps[first + tap : first + tap + 1, :]
        total = term if total is None else total + term
    return total


def decays(steps, head_params, tri):
    shifted = steps + head_params[0:1, :]
    dt = softplus(shifted)
    la = dt * head_params[1:2, :]
    cum = exact_dot(tri, la)
    return shifted, dt, la, cum


def spread_lanes(values, pair, first):
    rows = values.shape[0]
    a = jnp.broadcast_to(values[:, 2 * pair : 2 * pair + 1], (rows, WIDE))
    b = jnp.broadcast_to(values[:, 2 * pair + 1 : 2 * pair + 2], (rows, WIDE))
    return a, b, jnp.where(first, a, b)


def mixer_fwd_body(
    order, gate_ref, inner_ref, step_ref, bc_ref, attn_ref, lane_ref, conv_ref, head_ref,
    out_ref, y_ref, state_ref, ext_s, extbc_s, state_s, x_s,
):
    bf16, f32 = jnp.bfloat16, jnp.float32
    step = pl.program_id(0)
    width = inner_ref.shape[1]
    states = bc_ref.shape[1] // 2

    @pl.when(step == 0)
    def _():
        ext_s[0:8, :] = jnp.zeros((8, width), f32)
        extbc_s[0:8, :] = jnp.zeros((8, 2 * states), f32)
        state_s[...] = jnp.zeros_like(state_s)

    ext_s[8:, :] = inner_ref[...]
    extbc_s[8:, :] = bc_ref[...]
    pre = conv_taps(ext_s, lane_ref, 0, KC)
    x_s[...] = pre * sigmoid(pre)
    pre = conv_taps(extbc_s, conv_ref, 0, KC)
    bc = (pre * sigmoid(pre)).astype(bf16)
    ext_s[0:8, :] = ext_s[ROWS : ROWS + 8, :]
    extbc_s[0:8, :] = extbc_s[ROWS : ROWS + 8, :]
    row, col = iota((CHUNK, CHUNK), 0), iota((CHUNK, CHUNK), 1)
    causal = row >= col
    tri = jnp.where(causal, 1.0, 0.0).astype(bf16)
    first = iota((CHUNK, WIDE), 1) < WIDE // 2
    for sub in range(ROWS // CHUNK):
        lo = sub * CHUNK
        b_low = bc[lo : lo + CHUNK, :states]
        c_low = bc[lo : lo + CHUNK, states:]
        _, dt, _, cum = decays(step_ref[lo : lo + CHUNK, :], head_ref, tri)
        cum_t = cum.T
        cross = low_dot(c_low, b_low, NT)
        state_low = state_s[...].astype(bf16)
        state_ref[sub] = state_low
        b_t = b_low.T
        for pair in range(width // WIDE):
            lanes = slice(pair * WIDE, (pair + 1) * WIDE)
            cum_a, cum_b, cum_p = spread_lanes(cum, pair, first)
            _, _, dt_p = spread_lanes(dt, pair, first)
            weights = []
            for wide, head in ((cum_a, 2 * pair), (cum_b, 2 * pair + 1)):
                gap = jnp.where(causal, wide - cum_t[head : head + 1, :], FAR)
                weights.append((cross * jnp.exp(gap)).astype(bf16))
            x = x_s[lo : lo + CHUNK, lanes]
            scaled = x * dt_p
            zero = jnp.zeros_like(scaled)
            stacked = jnp.concatenate(
                [jnp.where(first, scaled, zero), jnp.where(first, zero, scaled)], axis=0
            ).astype(bf16)
            y = low_dot(jnp.concatenate(weights, axis=1), stacked, NN)
            y = y + jnp.exp(cum_p) * low_dot(c_low, state_low[:, lanes], NN)
            y_ref[lo : lo + CHUNK, lanes] = y + lane_ref[5:6, lanes] * x
            last = cum_p[CHUNK - 1 : CHUNK, :]
            ends = (scaled * jnp.exp(last - cum_p)).astype(bf16)
            state_s[:, lanes] = state_s[:, lanes] * jnp.exp(last) + low_dot(b_t, ends, NN)
    gate = gate_ref[...]
    gated = y_ref[...] * (gate * sigmoid(gate))
    scale = lax.rsqrt(jnp.mean(gated * gated, axis=1, keepdims=True) + EPS)
    out_ref[:, :width] = (gated * scale * lane_ref[4:5, :]).astype(bf16)
    out_ref[:, width:] = attn_ref[...]


def mixer_bwd_body(
    order, gate_ref, inner_ref, before_ref, step_ref, bc_ref, bcbefore_ref, y_ref, state_ref,
    grad_ref, dq_ref, dkv_ref, lane_ref, conv_ref, head_ref, seg_ref,
    low_ref, lowsh_ref, dlane_ref, dconv_ref, dhead_ref,
    ext_s, extbc_s, pre_s, prebc_s, x_s, bc_s, g_s, dx_s, dbc_s, dpre_s, dprebc_s, dstate_s,
    z_s, rows_s,
):
    bf16, f32 = jnp.bfloat16, jnp.float32
    step = pl.program_id(0)
    blocks = pl.num_programs(0)
    width = inner_ref.shape[1]
    states = bc_ref.shape[1] // 2
    query_width = dq_ref.shape[1]

    @pl.when(step == 0)
    def _():
        dlane_ref[...] = jnp.zeros_like(dlane_ref)
        dconv_ref[...] = jnp.zeros_like(dconv_ref)
        dhead_ref[...] = jnp.zeros_like(dhead_ref)
        dstate_s[...] = jnp.zeros_like(dstate_s)
        dpre_s[ROWS:, :] = jnp.zeros((8, width), f32)
        dprebc_s[ROWS:, :] = jnp.zeros((8, 2 * states), f32)
        z_s[...] = jnp.zeros_like(z_s)
        rows_s[...] = jnp.zeros_like(rows_s)

    keep = jnp.where(step == blocks - 1, 0.0, 1.0)
    ext_s[0:8, :] = before_ref[...] * keep
    extbc_s[0:8, :] = bcbefore_ref[...] * keep
    ext_s[8:, :] = inner_ref[...]
    extbc_s[8:, :] = bc_ref[...]
    pre = conv_taps(ext_s, lane_ref, 0, KC)
    pre_s[...] = pre
    x_s[...] = pre * sigmoid(pre)
    pre = conv_taps(extbc_s, conv_ref, 0, KC)
    prebc_s[...] = pre
    bc_s[...] = (pre * sigmoid(pre)).astype(bf16)

    gate = gate_ref[...]
    sig = sigmoid(gate)
    gate_act = gate * sig
    y = y_ref[...]
    gated = y * gate_act
    scale = lax.rsqrt(jnp.mean(gated * gated, axis=1, keepdims=True) + EPS)
    grad = grad_ref[...]
    dlane_ref[4:5, :] += jnp.sum(grad * gated * scale, axis=0, keepdims=True)
    grad = grad * lane_ref[4:5, :]
    mean = jnp.mean(grad * gated, axis=1, keepdims=True)
    dgated = scale * grad - gated * (scale * scale * scale * mean)
    g_s[...] = dgated * gate_act
    low_ref[:, :width] = (dgated * y * sig * (1.0 + gate * (1.0 - sig))).astype(bf16)

    row, col = iota((CHUNK, CHUNK), 0), iota((CHUNK, CHUNK), 1)
    tri = jnp.where(row >= col, 1.0, 0.0).astype(bf16)
    tri_up = jnp.where(row <= col, 1.0, 0.0).astype(bf16)
    later = row <= col
    first = iota((CHUNK, WIDE), 1) < WIDE // 2
    last_row = iota((CHUNK, WIDE), 0) == CHUNK - 1
    for sub in reversed(range(ROWS // CHUNK)):
        lo = sub * CHUNK
        b_low = bc_s[lo : lo + CHUNK, :states]
        c_low = bc_s[lo : lo + CHUNK, states:]
        shifted, dt, la, cum = decays(step_ref[lo : lo + CHUNK, :], head_ref, tri)
        cum_t = cum.T
        cross_t = low_dot(b_low, c_low, NT)
        c_t = c_low.T
        state_low = state_ref[sub]
        dstate_low = dstate_s[...].astype(bf16)
        dcross_t = jnp.zeros((CHUNK, CHUNK), f32)
        db = jnp.zeros((CHUNK, states), f32)
        dc = jnp.zeros((CHUNK, states), f32)
        for pair in range(width // WIDE):
            lanes = slice(pair * WIDE, (pair + 1) * WIDE)
            cum_a, cum_b, cum_p = spread_lanes(cum, pair, first)
            _, _, dt_p = spread_lanes(dt, pair, first)
            x = x_s[lo : lo + CHUNK, lanes]
            g = g_s[lo : lo + CHUNK, lanes]
            scaled = x * dt_p
            scaled_low = scaled.astype(bf16)
            zero = jnp.zeros_like(g)
            g_stack = jnp.concatenate(
                [jnp.where(first, g, zero), jnp.where(first, zero, g)], axis=0
            ).astype(bf16)
            dweights_t = low_dot(scaled_low, g_stack, NT)
            weights_t = []
            for place, wide, head in ((0, cum_a, 2 * pair), (1, cum_b, 2 * pair + 1)):
                gap = jnp.where(later, cum_t[head : head + 1, :] - wide, FAR)
                grow = jnp.exp(gap)
                weight = (cross_t * grow).astype(bf16)
                weights_t.append(weight)
                dweight = dweights_t[:, place * CHUNK : (place + 1) * CHUNK]
                dcross_t = dcross_t + dweight * grow
                rows_s[head : head + 1, :] = jnp.sum(
                    dweight * weight.astype(f32), axis=0, keepdims=True
                )
            dx_in = low_dot(jnp.concatenate(weights_t, axis=1), g_stack, NN)
            grown = jnp.exp(cum_p)
            last = cum_p[CHUNK - 1 : CHUNK, :]
            tail = jnp.exp(last - cum_p)
            last = jnp.exp(last)
            dx_tail = tail * low_dot(b_low, dstate_low[:, lanes], NN)
            dscaled = dx_in + dx_tail
            g_grown = g * grown
            g_low = g_grown.astype(bf16)
            ends = (scaled * tail).astype(bf16)
            carried = low_dot(c_low, state_low[:, lanes], NN)
            dc = dc + low_dot(g_low, state_low[:, lanes], NT)
            db = db + low_dot(ends, dstate_low[:, lanes], NT)
            dstate = dstate_s[:, lanes]
            kept = jnp.sum(dstate * state_low[:, lanes].astype(f32), axis=0, keepdims=True) * last
            dstate_s[:, lanes] = dstate * last + low_dot(c_t, g_low, NN)
            tails = scaled * dx_tail
            z_s[0:CHUNK, lanes] = g_grown * carried - tails - scaled_low.astype(f32) * dx_in
            z_s[CHUNK : 2 * CHUNK, lanes] = dscaled * x
            z_s[2 * CHUNK : 2 * CHUNK + 1, lanes] = (
                jnp.sum(tails, axis=0, keepdims=True) + kept
            )
            dx_s[lo : lo + CHUNK, lanes] = dscaled * dt_p + lane_ref[5:6, lanes] * g
            dlane_ref[5:6, lanes] += jnp.sum(g * x, axis=0, keepdims=True)
        sums = split_dot(z_s[...], seg_ref[...])
        dcum = sums[0:CHUNK, :] + rows_s[...].T
        dcum = dcum + jnp.where(last_row, sums[2 * CHUNK : 2 * CHUNK + 1, :], 0.0)
        dla = exact_dot(tri_up, dcum)
        ddt = sums[CHUNK : 2 * CHUNK, :] + dla * head_ref[1:2, :]
        dsteps = ddt * sigmoid(shifted)
        dhead_ref[0:1, :] += jnp.sum(dsteps, axis=0, keepdims=True)
        dhead_ref[1:2, :] += jnp.sum(dla * la, axis=0, keepdims=True)
        low_ref[lo : lo + CHUNK, 2 * width + query_width :] = dsteps.astype(bf16)
        dcross_low = dcross_t.astype(bf16)
        dbc_s[lo : lo + CHUNK, :states] = db + low_dot(dcross_low, c_low, NN)
        dbc_s[lo : lo + CHUNK, states:] = dc + low_dot(dcross_low, b_low, TN)

    def conv_back(pre_ref, dact, dpre_ref, ext, taps, dtaps_ref):
        pre = pre_ref[...]
        sig = sigmoid(pre)
        dpre = dact * (sig * (1.0 + pre * (1.0 - sig)))
        dpre_ref[0:ROWS, :] = dpre
        total = None
        for tap in range(KC):
            ahead = KC - 1 - tap
            term = dpre_ref[ahead : ahead + ROWS, :] * taps[tap : tap + 1, :]
            total = term if total is None else total + term
            at = 8 - (KC - 1) + tap
            dtaps_ref[tap : tap + 1, :] += jnp.sum(
                dpre * ext[at : at + ROWS, :], axis=0, keepdims=True
            )
        dpre_ref[ROWS:, :] = dpre_ref[0:8, :]
        return total

    dinner = conv_back(pre_s, dx_s[...], dpre_s, ext_s, lane_ref, dlane_ref)
    low_ref[:, width : 2 * width] = dinner.astype(bf16)
    dbc = conv_back(prebc_s, dbc_s[...], dprebc_s, extbc_s, conv_ref, dconv_ref)
    lowsh_ref[:, : 2 * states] = dbc.astype(bf16)
    lowsh_ref[:, 2 * states :] = dkv_ref[...]
    low_ref[:, 2 * width : 2 * width + query_width] = dq_ref[...]


def block_at(rows, cols, col):
    return pl.BlockSpec((rows, cols), lambda i, order: (order[i], col))


def whole_at(shape):
    return pl.BlockSpec(shape, lambda i, order: (0,) * len(shape))


def kernel_params():
    return pltpu.CompilerParams(
        dimension_semantics=("arbitrary",), vmem_limit_bytes=56 * 1024 * 1024
    )


def attn_forward(order, proj, proj_shared, cosine, sine, query_width, width, bc_width):
    slot = proj.shape[0]
    scratch = [pltpu.VMEM((slot, HD), jnp.bfloat16)] * 2
    return pl.pallas_call(
        attn_fwd_body,
        grid_spec=pltpu.PrefetchScalarGridSpec(
            num_scalar_prefetch=1,
            grid=(slot // ROWS,),
            in_specs=[
                block_at(ROWS, query_width, 2 * width // query_width),
                block_at(ROWS, 2 * HD, bc_width // (2 * HD)),
                pl.BlockSpec((ROWS, HD), lambda i, order: (i, 0)),
                pl.BlockSpec((ROWS, HD), lambda i, order: (i, 0)),
            ],
            out_specs=block_at(ROWS, query_width, 0),
            scratch_shapes=scratch,
        ),
        out_shape=jax.ShapeDtypeStruct((slot, query_width), jnp.bfloat16),
        compiler_params=kernel_params(),
        cost_estimate=pl.CostEstimate(
            flops=slot * slot * query_width * 3,
            bytes_accessed=slot * 4 * (query_width + 4 * HD),
            transcendentals=slot * slot * query_width // HD,
        ),
    )(order, proj, proj_shared, cosine, sine)


def attn_backward(order, proj, proj_shared, cosine, sine, grad_heads, query_width, width, bc_width):
    slot = proj.shape[0]
    return pl.pallas_call(
        attn_bwd_body,
        grid_spec=pltpu.PrefetchScalarGridSpec(
            num_scalar_prefetch=1,
            grid=(slot // ROWS,),
            in_specs=[
                block_at(ROWS, query_width, 2 * width // query_width),
                block_at(ROWS, 2 * HD, bc_width // (2 * HD)),
                pl.BlockSpec((ROWS, HD), lambda i, order: (i, 0)),
                pl.BlockSpec((ROWS, HD), lambda i, order: (i, 0)),
                block_at(ROWS, query_width, width // query_width),
                whole_at((slot, HD)),
                whole_at((slot, HD)),
            ],
            out_specs=[block_at(ROWS, query_width, 0), whole_at((slot, 2 * HD))],
            scratch_shapes=[pltpu.VMEM((slot, HD), jnp.bfloat16)] * 2
            + [pltpu.VMEM((slot, HD), jnp.float32)] * 2,
        ),
        out_shape=[
            jax.ShapeDtypeStruct((slot, query_width), jnp.bfloat16),
            jax.ShapeDtypeStruct((slot, 2 * HD), jnp.bfloat16),
        ],
        compiler_params=kernel_params(),
        cost_estimate=pl.CostEstimate(
            flops=slot * slot * query_width * 8,
            bytes_accessed=slot * 4 * (2 * query_width + 6 * HD),
            transcendentals=slot * slot * query_width // HD,
        ),
    )(order, proj, proj_shared, cosine, sine, grad_heads, cosine, sine)


def mixer_forward(order, proj, proj_shared, attn_low, lane_params, conv_shared, head_params):
    slot = proj.shape[0]
    f32, bf16 = jnp.float32, jnp.bfloat16
    width = lane_params.shape[1]
    bc_width = conv_shared.shape[1]
    query_width = attn_low.shape[1]
    chunks = ROWS // CHUNK
    return pl.pallas_call(
        mixer_fwd_body,
        grid_spec=pltpu.PrefetchScalarGridSpec(
            num_scalar_prefetch=1,
            grid=(slot // ROWS,),
            in_specs=[
                block_at(ROWS, width, 0),
                block_at(ROWS, width, 1),
                block_at(ROWS, WIDE, (2 * width + query_width) // WIDE),
                block_at(ROWS, bc_width, 0),
                block_at(ROWS, query_width, 0),
                whole_at(lane_params.shape),
                whole_at(conv_shared.shape),
                whole_at(head_params.shape),
            ],
            out_specs=[
                block_at(ROWS, width + query_width, 0),
                pl.BlockSpec((ROWS, width), lambda i, order: (i, 0)),
                pl.BlockSpec((chunks, bc_width // 2, width), lambda i, order: (i, 0, 0)),
            ],
            scratch_shapes=[
                pltpu.VMEM((ROWS + 8, width), f32),
                pltpu.VMEM((ROWS + 8, bc_width), f32),
                pltpu.VMEM((bc_width // 2, width), f32),
                pltpu.VMEM((ROWS, width), f32),
            ],
        ),
        out_shape=[
            jax.ShapeDtypeStruct((slot, width + query_width), bf16),
            jax.ShapeDtypeStruct((slot, width), f32),
            jax.ShapeDtypeStruct((slot // CHUNK, bc_width // 2, width), bf16),
        ],
        compiler_params=kernel_params(),
        cost_estimate=pl.CostEstimate(
            flops=slot * width * bc_width * 8,
            bytes_accessed=slot * width * 20,
            transcendentals=slot * width * 8,
        ),
    )(order, proj, proj, proj, proj_shared, attn_low, lane_params, conv_shared, head_params)


def mixer_backward(
    order, proj, proj_shared, y, states, grad_heads, dq, dkv, lane_params, conv_shared,
    head_params, seg, query_width,
):
    slot = proj.shape[0]
    f32, bf16 = jnp.float32, jnp.bfloat16
    width = lane_params.shape[1]
    bc_width = conv_shared.shape[1]
    blocks = slot // ROWS
    chunks = ROWS // CHUNK

    def back(rows, cols, col):
        return pl.BlockSpec((rows, cols), lambda i, order: (order[blocks - 1 - i], col))

    def straight(shape):
        return pl.BlockSpec(
            shape, lambda i, order: (blocks - 1 - i,) + (0,) * (len(shape) - 1)
        )

    def before(cols, col):
        return pl.BlockSpec(
            (8, cols),
            lambda i, order: (
                order[jnp.maximum(blocks - 2 - i, 0)] * (ROWS // 8) + ROWS // 8 - 1,
                col,
            ),
        )

    return pl.pallas_call(
        mixer_bwd_body,
        grid_spec=pltpu.PrefetchScalarGridSpec(
            num_scalar_prefetch=1,
            grid=(blocks,),
            in_specs=[
                back(ROWS, width, 0),
                back(ROWS, width, 1),
                before(width, 1),
                back(ROWS, WIDE, (2 * width + query_width) // WIDE),
                back(ROWS, bc_width, 0),
                before(bc_width, 0),
                straight((ROWS, width)),
                straight((chunks, bc_width // 2, width)),
                back(ROWS, width, 0),
                back(ROWS, query_width, 0),
                straight((ROWS, 2 * HD)),
                whole_at(lane_params.shape),
                whole_at(conv_shared.shape),
                whole_at(head_params.shape),
                whole_at(seg.shape),
            ],
            out_specs=[
                back(ROWS, 2 * width + query_width + WIDE, 0),
                back(ROWS, bc_width + 2 * HD, 0),
                whole_at((8, width)),
                whole_at((8, bc_width)),
                whole_at((8, WIDE)),
            ],
            scratch_shapes=[
                pltpu.VMEM((ROWS + 8, width), f32),
                pltpu.VMEM((ROWS + 8, bc_width), f32),
                pltpu.VMEM((ROWS, width), f32),
                pltpu.VMEM((ROWS, bc_width), f32),
                pltpu.VMEM((ROWS, width), f32),
                pltpu.VMEM((ROWS, bc_width), bf16),
                pltpu.VMEM((ROWS, width), f32),
                pltpu.VMEM((ROWS, width), f32),
                pltpu.VMEM((ROWS, bc_width), f32),
                pltpu.VMEM((ROWS + 8, width), f32),
                pltpu.VMEM((ROWS + 8, bc_width), f32),
                pltpu.VMEM((bc_width // 2, width), f32),
                pltpu.VMEM((2 * CHUNK + 8, width), f32),
                pltpu.VMEM((WIDE, CHUNK), f32),
            ],
        ),
        out_shape=[
            jax.ShapeDtypeStruct((slot, 2 * width + query_width + WIDE), bf16),
            jax.ShapeDtypeStruct((slot, bc_width + 2 * HD), bf16),
            jax.ShapeDtypeStruct((8, width), f32),
            jax.ShapeDtypeStruct((8, bc_width), f32),
            jax.ShapeDtypeStruct((8, WIDE), f32),
        ],
        compiler_params=kernel_params(),
        cost_estimate=pl.CostEstimate(
            flops=slot * width * bc_width * 20,
            bytes_accessed=slot * width * 40,
            transcendentals=slot * width * 16,
        ),
    )(
        order, proj, proj, proj, proj, proj_shared, proj_shared, y, states, grad_heads, dq, dkv,
        lane_params, conv_shared, head_params, seg,
    )


class Places:
    def __init__(self):
        self.dp = lax.axis_size("dp")
        self.tp = lax.axis_size("tensor")
        d = lax.axis_index("dp")
        t = lax.axis_index("tensor")
        self.d, self.t = d, t
        self.c = d % 2
        self.k = d // 2
        self.zq = t % 2
        self.home = self.c == t // 2
        self.quarter = 2 * self.c + self.zq
        self.column = self.zq + 2 * self.c
        self.slot = 2 * self.k + t // 2
        self.blocks = self.dp // 2
        self.bits = self.blocks.bit_length() - 1

    def pairs(self, where_to):
        out = []
        for d in range(self.dp):
            for t in range(self.tp):
                target = where_to(d, t)
                if target is not None:
                    out.append((d * self.tp + t, target[0] * self.tp + target[1]))
        return out

    def send(self, values, where_to):
        return lax.ppermute(values, ("dp", "tensor"), self.pairs(where_to))

    def over_core(self, values):
        return self.send(values, lambda d, t: (d ^ 1, t))

    def over_z(self, values):
        return self.send(values, lambda d, t: (d, t ^ 1))

    def over_far(self, values):
        return self.send(values, lambda d, t: (d, t ^ 2))

    def over_bit(self, values, bit):
        return self.send(values, lambda d, t: (d ^ (2 << bit), t))

    def swap_away(self, values):
        def where_to(d, t):
            if d % 2 == t // 2:
                return None
            return (d ^ 1, t ^ 2)

        return self.send(values, where_to)

    def column_out(self, values):
        def where_to(d, t):
            if d % 2 == t // 2:
                return (d, t ^ 2)
            return (d ^ 1, t)

        return self.send(values, where_to)

    def column_back(self, values):
        def where_to(d, t):
            if d % 2 == t // 2:
                return (d ^ 1, t)
            return (d, t ^ 2)

        return self.send(values, where_to)


def relocate(values, at):
    return jnp.where(at.home, values, at.swap_away(values))


MESH = pl.DeviceIdType.MESH


class Lanes:
    def __init__(self, blocks):
        d = lax.axis_index("dp")
        t = lax.axis_index("tensor")
        self.c = lax.rem(d, 2)
        self.k = lax.div(d, 2)
        self.d, self.t = d, t
        self.home = self.c == lax.div(t, 2)
        self.away = self.c != lax.div(t, 2)
        self.other = d + 1 - 2 * self.c
        self.near = t + 1 - 2 * lax.rem(t, 2)
        self.far = lax.rem(t + 2, 4)
        self.blocks = blocks
        self.bits = blocks.bit_length() - 1

    def block(self, place):
        value = self.k
        for bit in range(self.bits):
            if (place >> bit) & 1:
                value = value + (1 << bit) * (1 - 2 * lax.rem(lax.div(self.k, 1 << bit), 2))
        return value

    def across(self, bit):
        return (2 * self.block(1 << bit) + self.c, self.t)

    def greet(self):
        partners = [
            (self.other, self.t),
            (self.d, self.near),
            (self.d, self.far),
            (self.other, self.far),
        ] + [self.across(bit) for bit in range(self.bits)]
        barrier = pltpu.get_barrier_semaphore()
        for partner in partners:
            pl.semaphore_signal(barrier, inc=1, device_id=partner, device_id_type=MESH)
        pl.semaphore_wait(barrier, len(partners))


def remote(src, dst, send_sem, recv_sem, device):
    return pltpu.make_async_remote_copy(
        src_ref=src,
        dst_ref=dst,
        send_sem=send_sem,
        recv_sem=recv_sem,
        device_id=device,
        device_id_type=MESH,
    )


def onward(place, half, bits):
    if half == 0:
        return [bit for bit in range(bits) if place < (1 << bit)]
    return [bit for bit in reversed(range(bits)) if place % (2 << bit) == 0]


class Spread:
    def __init__(self, lanes, full, rows, chunks, send_sems, recv_sems):
        self.lanes, self.full, self.rows, self.chunks = lanes, full, rows, chunks
        self.piece = rows // chunks
        self.send_sems, self.recv_sems = send_sems, recv_sems

    def view(self, place, half, chunk):
        start = self.lanes.block(place) * (2 * self.rows) + half * self.rows + chunk * self.piece
        return self.full.at[pl.ds(pl.multiple_of(start, self.piece), self.piece), :]

    def copy(self, place, half, chunk, bit):
        view = self.view(place, half, chunk)
        to = place | (1 << bit)
        return remote(
            view,
            view,
            self.send_sems.at[half, to, chunk],
            self.recv_sems.at[half, to, chunk],
            self.lanes.across(bit),
        )

    def give(self, place, half, chunk):
        for bit in onward(place, half, self.lanes.bits):
            self.copy(place, half, chunk, bit).start()

    def take(self, place, half, chunk):
        view = self.view(place, half, chunk)
        remote(
            view,
            view,
            self.send_sems.at[half, place, chunk],
            self.recv_sems.at[half, place, chunk],
            self.lanes.across(0),
        ).wait_recv()

    def pass_on(self, chunk):
        for half in range(2):
            places = range(1, self.lanes.blocks)
            if half == 1:
                key = lambda place: [-bit for bit in reversed(range(8)) if (place >> bit) & 1]
                places = sorted(places, key=key)
            for place in places:
                if onward(place, half, self.lanes.bits):
                    self.take(place, half, chunk)
                    self.give(place, half, chunk)

    def finish(self, chunk):
        for half in range(2):
            for place in range(1, self.lanes.blocks):
                if not onward(place, half, self.lanes.bits):
                    self.take(place, half, chunk)
        for half in range(2):
            for place in range(self.lanes.blocks):
                for bit in onward(place, half, self.lanes.bits):
                    self.copy(place, half, chunk, bit).wait_send()


def front_body(
    blocks, chunks, in_ref, out_ref, x_ref, gain_ref,
    full_ref, pair_ref, act_ref, xr_ref,
    x_s, act_s, home_sems, z_send, z_recv, o_sems, o_recv, send_sems, recv_sems, x_sems, a_send,
    a_recv,
):
    lanes = Lanes(blocks)
    rows = in_ref.shape[0]
    piece = rows // chunks
    here = x_ref.shape[0]
    c, t = lanes.c, lanes.t
    lanes.greet()
    spread = Spread(lanes, full_ref, rows, chunks, send_sems, recv_sems)

    def slot(chunk):
        start = lanes.k * (2 * rows) + c * rows + chunk * piece
        return full_ref.at[pl.ds(pl.multiple_of(start, piece), piece), :]

    def first_copy(chunk, device):
        return remote(
            in_ref.at[pl.ds(chunk * piece, piece), :],
            slot(chunk),
            z_send.at[0, chunk],
            z_recv.at[c, chunk],
            device,
        )

    def second_copy(chunk):
        return remote(
            in_ref.at[pl.ds(chunk * piece, piece), :],
            slot(chunk),
            z_send.at[1, chunk],
            z_recv.at[c, chunk],
            (lanes.other, lanes.far),
        )

    def own_copy(chunk):
        return pltpu.make_async_copy(
            in_ref.at[pl.ds(chunk * piece, piece), :], slot(chunk), home_sems.at[chunk]
        )

    def out_slot():
        return pair_ref.at[pl.ds(pl.multiple_of(c * rows, rows), rows), :]

    def out_first(device):
        return remote(out_ref, out_slot(), o_sems.at[0], o_recv.at[c], device)

    def out_second():
        return remote(out_ref, out_slot(), o_sems.at[1], o_recv.at[c], (lanes.other, lanes.far))

    def x_away():
        return remote(x_ref, x_s, x_sems.at[0], x_sems.at[1], (lanes.other, lanes.far))

    def x_home():
        return pltpu.make_async_copy(x_ref, x_s, x_sems.at[2])

    def send_first(chunk):
        @pl.when(lanes.home)
        def _():
            own_copy(chunk).start()
            first_copy(chunk, (lanes.d, lanes.far)).start()

        @pl.when(lanes.away)
        def _():
            first_copy(chunk, (lanes.other, t)).start()
            second_copy(chunk).start()

    early = max(chunks // 2, 1)
    for chunk in range(early):
        send_first(chunk)

    @pl.when(lanes.home)
    def _():
        x_home().start()

    @pl.when(lanes.away)
    def _():
        x_away().start()

    for chunk in range(early, chunks):
        send_first(chunk)

    @pl.when(lanes.home)
    def _():
        out_first((lanes.d, lanes.far)).start()
        pltpu.make_async_copy(out_ref, out_slot(), o_sems.at[2]).start()

    @pl.when(lanes.away)
    def _():
        out_first((lanes.other, t)).start()
        out_second().start()

    def z_view(half, chunk):
        start = lanes.k * (2 * rows) + half * rows + chunk * piece
        return full_ref.at[pl.ds(pl.multiple_of(start, piece), piece), :]

    def came(half, chunk):
        view = z_view(half, chunk)
        return remote(
            view, view, z_send.at[0, chunk], z_recv.at[half, chunk], (lanes.other, t)
        )

    def arrive(chunk):
        @pl.when(lanes.home)
        def _():
            own_copy(chunk).wait()
            start = lanes.k * (2 * rows) + (1 - c) * rows + chunk * piece
            view = full_ref.at[pl.ds(pl.multiple_of(start, piece), piece), :]
            remote(
                view, view, z_send.at[0, chunk], z_recv.at[1 - c, chunk], (lanes.other, t)
            ).wait_recv()

        @pl.when(lanes.away)
        def _():
            for half in range(2):
                came(half, chunk).wait_recv()

        for half in range(2):
            spread.give(0, half, chunk)

    def act_slot(index):
        return act_ref.at[pl.ds(index * here, here), :]

    def act_far():
        return remote(act_s, act_slot(2), a_send.at[0], a_recv.at[0], (lanes.d, lanes.near))

    def act_core():
        return remote(act_s, act_slot(1), a_send.at[1], a_recv.at[1], (lanes.other, t))

    def act_both():
        return remote(act_slot(2), act_slot(3), a_send.at[2], a_recv.at[2], (lanes.other, t))

    def norm():
        @pl.when(lanes.home)
        def _():
            x_home().wait()

        @pl.when(lanes.away)
        def _():
            x_away().wait_recv()

        @pl.loop(0, here // 32)
        def _(step):
            part = pl.ds(pl.multiple_of(step * 32, 32), 32)
            x = x_s[part, :].astype(jnp.float32)
            scale = lax.rsqrt(jnp.mean(x * x, axis=1, keepdims=True) + EPS)
            act_s[part, :] = (x * scale * gain_ref[...]).astype(jnp.bfloat16)

        act_far().start()
        act_core().start()
        pltpu.make_async_copy(act_s, act_slot(0), a_send.at[3]).start()
        pltpu.make_async_copy(x_s, xr_ref, x_sems.at[3]).start()

    for chunk in range(chunks):
        arrive(chunk)
        if chunk >= 1:
            spread.pass_on(chunk - 1)
        if chunk == early:
            norm()
    if early >= chunks:
        norm()
    spread.pass_on(chunks - 1)
    act_far().wait_recv()
    act_both().start()
    act_core().wait_recv()
    for chunk in range(chunks):
        spread.finish(chunk)
    act_both().wait_recv()
    act_far().wait_send()
    act_core().wait_send()
    act_both().wait_send()
    pltpu.make_async_copy(act_s, act_slot(0), a_send.at[3]).wait()
    pltpu.make_async_copy(x_s, xr_ref, x_sems.at[3]).wait()

    @pl.when(lanes.home)
    def _():
        for chunk in range(chunks):
            first_copy(chunk, (lanes.d, lanes.far)).wait_send()
        out_first((lanes.d, lanes.far)).wait_send()
        pltpu.make_async_copy(out_ref, out_slot(), o_sems.at[2]).wait()
        start = (1 - c) * rows
        view = pair_ref.at[pl.ds(pl.multiple_of(start, rows), rows), :]
        remote(view, view, o_sems.at[0], o_recv.at[1 - c], (lanes.other, t)).wait_recv()

    @pl.when(lanes.away)
    def _():
        x_away().wait_send()
        for chunk in range(chunks):
            first_copy(chunk, (lanes.other, t)).wait_send()
            second_copy(chunk).wait_send()
        out_first((lanes.other, t)).wait_send()
        out_second().wait_send()
        for half in range(2):
            view = pair_ref.at[pl.ds(half * rows, rows), :]
            remote(view, view, o_sems.at[0], o_recv.at[half], (lanes.other, t)).wait_recv()


def front(in_pack, out_pack, layer_in, gain, at):
    bf16 = jnp.bfloat16
    rows = in_pack.shape[0]
    blocks = at.blocks
    chunks = 4 if rows >= 256 else 1
    dma = pltpu.SemaphoreType.DMA
    anywhere = pl.BlockSpec(memory_space=pl.ANY)
    here, features = layer_in.shape
    total = 2 * blocks * rows
    return pl.pallas_call(
        functools.partial(front_body, blocks, chunks),
        in_specs=[anywhere, anywhere, anywhere, pl.BlockSpec(memory_space=pltpu.VMEM)],
        out_specs=[anywhere] * 4,
        out_shape=[
            jax.ShapeDtypeStruct((total, in_pack.shape[1]), bf16),
            jax.ShapeDtypeStruct((2 * rows, out_pack.shape[1]), bf16),
            jax.ShapeDtypeStruct((4 * here, features), bf16),
            jax.ShapeDtypeStruct((here, features), bf16),
        ],
        scratch_shapes=[
            pltpu.VMEM((here, features), bf16),
            pltpu.VMEM((here, features), bf16),
            dma((chunks,)),
            dma((2, chunks)),
            dma((2, chunks)),
            dma((3,)),
            dma((2,)),
            dma((2, blocks, chunks)),
            dma((2, blocks, chunks)),
            dma((4,)),
            dma((4,)),
            dma((3,)),
        ],
        compiler_params=pltpu.CompilerParams(
            collective_id=1, has_side_effects=True, vmem_limit_bytes=16 * 1024 * 1024
        ),
        cost_estimate=pl.CostEstimate(
            flops=here * features * 8, bytes_accessed=300_000_000, transcendentals=0
        ),
    )(in_pack, out_pack, layer_in, gain.reshape(1, -1))


def after(values, *others):
    return lax.optimization_barrier((values,) + others)[0]


def share_rows(values, at):
    far = at.over_z(values)
    core = at.over_core(values)
    both = at.over_core(far)
    return (values, core, far, both)


def sum_rows(pieces, at):
    own, core, far, both = pieces
    bf16 = jnp.bfloat16
    from_both = at.over_core(both.astype(bf16))
    passed = (far + from_both.astype(jnp.float32)).astype(bf16)
    from_far = at.over_z(passed)
    from_core = at.over_core(core.astype(bf16))
    return own + from_core.astype(jnp.float32) + from_far.astype(jnp.float32)


def groups(at):
    return [[d for d in range(at.dp) if d % 2 == c] for c in range(2)]


def gather_blocks(block, at):
    return lax.all_gather(block, "dp", axis=0, tiled=True, axis_index_groups=groups(at))


def sum_blocks(values, at):
    return lax.psum_scatter(
        values, "dp", scatter_dimension=0, tiled=True, axis_index_groups=groups(at)
    )


def pair_up(own, other, at):
    first = at.c == 0
    return jnp.concatenate([jnp.where(first, own, other), jnp.where(first, other, own)], axis=0)


def pair_weight(shard, at):
    first_in = at.column_out(shard)
    second_in = at.swap_away(shard)
    own = jnp.where(at.home, shard, first_in)
    other = jnp.where(at.home, first_in, second_in)
    return pair_up(own, other, at)


def gather_weight(shard, at):
    return gather_blocks(pair_weight(shard, at), at)


def scatter_weight(grad, at):
    f32 = jnp.float32
    mine = sum_blocks(grad, at)
    rows = mine.shape[0] // 2
    low, high = mine[:rows], mine[rows:]
    own = jnp.where(at.c == 0, low, high)
    other = jnp.where(at.c == 0, high, low)
    first_in = at.column_back(jnp.where(at.home, other, own)).astype(f32)
    second_in = at.swap_away(other).astype(f32)
    return first_in + jnp.where(at.home, own.astype(f32), second_in)


def gather_shared(shard, at):
    rows, width = shard.shape
    half = width // 2
    mine = jnp.where(at.c == 0, shard[:, :half], shard[:, half:])
    theirs = jnp.where(at.c == 0, shard[:, half:], shard[:, :half])
    came = at.over_core(theirs)
    both = jnp.stack([jnp.where(at.c == 0, mine, came), jnp.where(at.c == 0, came, mine)])
    near = at.over_z(both)
    lowest = at.t % 2 == 0
    two = jnp.stack([jnp.where(lowest, both, near), jnp.where(lowest, near, both)], axis=1)
    far = at.over_far(two)
    lower = at.t // 2 == 0
    four = jnp.stack([jnp.where(lower, two, far), jnp.where(lower, far, two)], axis=1)
    part = gather_blocks(four.reshape(2 * rows * at.tp, half), at)
    other = at.over_core(part)
    return jnp.where(at.c == 0, part, other), jnp.where(at.c == 0, other, part)


def scatter_shared(grad_bc, grad_kv, earlier, at):
    f32, bf16 = jnp.float32, jnp.bfloat16
    first = at.c == 0
    bc_width = grad_bc.shape[1]
    going = jnp.where(
        first, jnp.pad(grad_kv, ((0, 0), (0, bc_width - grad_kv.shape[1]))), grad_bc
    )
    came = at.over_core(going.astype(bf16)).astype(f32)
    kept = jnp.concatenate(
        [came[:, :HD], grad_kv[:, :HD], came[:, HD : 2 * HD], grad_kv[:, HD:]], axis=1
    )
    total = jnp.where(first, grad_bc + came, kept)
    mine = sum_blocks(after(total.astype(bf16), earlier), at)
    piece = mine.shape[0] // (2 * at.tp)
    line = mine.astype(f32).reshape(2, 2, 2, piece, total.shape[1])
    lower = at.t // 2 == 0
    went = at.over_far(jnp.where(lower, line[:, 1], line[:, 0]).astype(bf16)).astype(f32)
    line = jnp.where(lower, line[:, 0], line[:, 1]) + went
    lowest = at.t % 2 == 0
    went = at.over_z(jnp.where(lowest, line[:, 1], line[:, 0]).astype(bf16)).astype(f32)
    line = jnp.where(lowest, line[:, 0], line[:, 1]) + went
    mine = jnp.where(first, line[0], line[1])
    came = at.over_core(jnp.where(first, line[1], line[0]).astype(bf16)).astype(f32)
    return jnp.concatenate([jnp.where(first, mine, came), jnp.where(first, came, mine)], axis=1)


def sum_tensor(values, at):
    for bit in range(at.tp.bit_length() - 1):
        values = values + at.send(values, lambda d, t: (d, t ^ (1 << bit)))
    return values


def sum_data(values, at):
    for bit in range(at.dp.bit_length() - 1):
        values = values + at.send(values, lambda d, t: (d ^ (1 << bit), t))
    return values


def per_device(
    layer_in,
    teacher,
    lengths,
    input_gain,
    mixer_in_weight,
    step_weight,
    query_weight,
    shared_weight,
    conv_inner,
    conv_shared,
    step_bias,
    decay_log,
    skip_gain,
    inner_gain,
    mixer_out_weight,
    attn_out_weight,
    middle_gain,
    gate_up_weight,
    down_weight,
):
    f32 = jnp.float32
    bf16 = jnp.bfloat16
    contract_last = (((1,), (1,)), ((), ()))
    contract_first = (((0,), (0,)), ((), ()))
    at = Places()
    rows_here = layer_in.shape[0]
    slot_len = rows_here * at.tp
    local_heads = step_bias.shape[0]
    width = inner_gain.shape[0]
    head_dim = width // local_heads
    query_width = query_weight.shape[1]
    hidden_width = down_weight.shape[1]
    bc_width = conv_shared.shape[1]
    w_rows = step_weight.shape[0]

    column_params = jnp.concatenate(
        [conv_inner.reshape(-1), inner_gain, step_bias, decay_log, skip_gain]
    )
    column_params = relocate(column_params, at)
    lane_params = jnp.concatenate(
        [
            column_params[: (KC + 1) * width].reshape(KC + 1, width),
            jnp.repeat(column_params[(KC + 1) * width + 2 * local_heads :], head_dim)[None],
            jnp.zeros((2, width), f32),
        ],
        axis=0,
    )
    head_rows = column_params[(KC + 1) * width :][: 2 * local_heads].reshape(2, local_heads)
    head_rows = jnp.concatenate([head_rows[:1], -jnp.exp(head_rows[1:])], axis=0)
    head_params = jnp.pad(head_rows, ((0, 6), (0, WIDE - local_heads)))
    seg = (
        lax.broadcasted_iota(jnp.int32, (width, WIDE), 0) // head_dim
        == lax.broadcasted_iota(jnp.int32, (width, WIDE), 1)
    ).astype(bf16)
    half = HD // 2
    freqs = jnp.exp(-jnp.log(ROPE_BASE) * 2.0 * jnp.arange(half, dtype=f32) / HD)
    angles = jnp.arange(slot_len).astype(f32)[:, None] * freqs[None, :]
    cosine, sine = jnp.cos(angles), jnp.sin(angles)
    cosine = jnp.concatenate([cosine, cosine], axis=1)
    sine = jnp.concatenate([-sine, sine], axis=1)
    quarters = jnp.arange(at.tp, dtype=jnp.int32)
    order = (at.c ^ (quarters // 2)) + 2 * (at.zq ^ (quarters % 2))

    shared_full = lax.all_gather(shared_weight, ("dp", "tensor"), axis=0, tiled=True)
    left, right = shared_full[:, :bc_width], shared_full[:, bc_width:]
    kv_index = at.column * (query_width // HD) // (QH // KVH)
    second = kv_index == 1
    shared_all = jnp.concatenate(
        [
            left,
            jnp.where(second, right[:, HD : 2 * HD], right[:, :HD]),
            jnp.where(second, right[:, 3 * HD :], right[:, 2 * HD : 3 * HD]),
        ],
        axis=1,
    )
    in_pack = jnp.concatenate(
        [
            mixer_in_weight.reshape(w_rows, 2 * width),
            query_weight,
            step_weight,
            jnp.zeros((w_rows, WIDE - local_heads), bf16),
        ],
        axis=1,
    )
    out_pack = jnp.concatenate([mixer_out_weight, attn_out_weight], axis=1)
    in_all, out_pair, act_all, inputs = front(in_pack, out_pack, layer_in, input_gain, at)
    inputs = inputs.astype(f32)

    def row_split(values):
        return [values[i * rows_here : (i + 1) * rows_here] for i in range(at.tp)]

    _, norm_in_back = jax.vjp(rms_norm, inputs, input_gain)
    out_all = gather_blocks(out_pair, at)
    rest = jnp.concatenate(
        [gate_up_weight.reshape(w_rows, 2 * hidden_width), down_weight], axis=1
    )
    rest = pair_weight(after(rest, act_all), at)
    gate_up_all = gather_blocks(rest[:, : 2 * hidden_width], at)
    down_all = gather_blocks(rest[:, 2 * hidden_width :], at)
    proj_shared = jnp.dot(act_all, shared_all, preferred_element_type=f32)
    proj = jnp.dot(act_all, in_all, preferred_element_type=f32)
    target = relocate(after(teacher, proj), at).astype(f32)
    attn_low = attn_forward(order, proj, proj_shared, cosine, sine, query_width, width, bc_width)
    heads_all, y, states = mixer_forward(
        order, proj, proj_shared, attn_low, lane_params, conv_shared, head_params
    )
    mix_parts = [
        lax.dot_general(piece, out_all, contract_last, preferred_element_type=f32)
        for piece in row_split(heads_all)
    ]
    resid = inputs + sum_rows(mix_parts, at)
    normed_mid, norm_mid_back = jax.vjp(rms_norm, resid, middle_gain)
    mid_all = jnp.concatenate(share_rows(normed_mid.astype(bf16), at), axis=0)
    gate_up = jnp.dot(mid_all, gate_up_all, preferred_element_type=f32)
    gate_val = gate_up[:, :hidden_width]
    up_val = gate_up[:, hidden_width:]
    sigmoid_gate = jax.nn.sigmoid(gate_val)
    hidden = (gate_val * sigmoid_gate * up_val).astype(bf16)
    mlp_parts = [
        lax.dot_general(piece, down_all, contract_last, preferred_element_type=f32)
        for piece in row_split(hidden)
    ]
    outputs = resid + sum_rows(mlp_parts, at)
    seq_len = lax.dynamic_index_in_dim(lengths, at.slot, keepdims=False)
    positions = at.quarter * rows_here + jnp.arange(rows_here)
    live = (positions < seq_len).astype(f32)
    error = (outputs - target) * live[:, None]
    err_local = 0.5 * jnp.sum(error * error)

    grad_all = jnp.concatenate(share_rows(error.astype(bf16), at), axis=0)
    def weight_grad(left, right):
        return lax.dot_general(left, right, contract_first, preferred_element_type=f32).astype(bf16)

    part_down = weight_grad(grad_all, hidden)
    grad_hidden = jnp.dot(grad_all, down_all, preferred_element_type=f32)
    grad_gate = grad_hidden * up_val * sigmoid_gate * (1.0 + gate_val * (1.0 - sigmoid_gate))
    grad_up = grad_hidden * gate_val * sigmoid_gate
    grad_gu = jnp.concatenate([grad_gate.astype(bf16), grad_up.astype(bf16)], axis=1)
    grad_mid_parts = [
        lax.dot_general(piece, gate_up_all, contract_last, preferred_element_type=f32)
        for piece in row_split(grad_gu)
    ]
    part_gate_up = weight_grad(mid_all, grad_gu)
    grad_mid = sum_rows(grad_mid_parts, at)
    grad_mid, part_down, part_gate_up = lax.optimization_barrier((grad_mid, part_down, part_gate_up))
    grad_down = scatter_weight(part_down, at)
    grad_gate_up = scatter_weight(part_gate_up, at)
    grad_resid_norm, grad_middle_gain = norm_mid_back(grad_mid)
    grad_resid = error + grad_resid_norm
    mix_grad_all = jnp.concatenate(share_rows(grad_resid.astype(bf16), at), axis=0)
    grad_heads = jnp.dot(mix_grad_all, out_all, preferred_element_type=f32)
    part_out = weight_grad(mix_grad_all, heads_all)
    grad_heads, part_out = lax.optimization_barrier((grad_heads, part_out))
    layer_out = relocate(after(outputs.astype(bf16), grad_heads), at)
    part_out = after(part_out, grad_down)
    grad_out = scatter_weight(part_out, at)
    dq, dkv = attn_backward(
        order, proj, proj_shared, cosine, sine, grad_heads, query_width, width, bc_width
    )
    low_pack, low_shared, dlane, dconv, dhead = mixer_backward(
        order, proj, proj_shared, y, states, grad_heads, dq, dkv, lane_params, conv_shared,
        head_params, seg, query_width,
    )
    grad_bc = lax.dot_general(
        act_all, low_shared[:, :bc_width], contract_first, preferred_element_type=f32
    )
    grad_kv = lax.dot_general(
        act_all, low_shared[:, bc_width:], contract_first, preferred_element_type=f32
    )
    part_in = weight_grad(act_all, low_pack)
    low_pack, low_shared, part_in, grad_bc, grad_kv = lax.optimization_barrier(
        (low_pack, low_shared, part_in, grad_bc, grad_kv)
    )
    grad_in = scatter_weight(after(part_in, grad_gate_up), at)
    grad_shared_weight = scatter_shared(grad_bc, grad_kv, grad_out, at)
    grad_act_parts = [
        lax.dot_general(a, in_all, contract_last, preferred_element_type=f32)
        + lax.dot_general(b, shared_all, contract_last, preferred_element_type=f32)
        for a, b in zip(row_split(low_pack), row_split(low_shared))
    ]
    grad_act = sum_rows(grad_act_parts, at)
    grad_input_norm, grad_input_gain = norm_in_back(grad_act)
    input_grad = grad_resid + grad_input_norm

    column = at.column
    convx_full = lax.dynamic_update_slice(
        jnp.zeros((KC + 1, DI), f32), dlane[: KC + 1], (0, column * width)
    )
    head_stack = jnp.concatenate(
        [dhead[:2, :local_heads], dlane[KC + 1].reshape(1, local_heads, head_dim).sum(2)], axis=0
    )
    heads_full = lax.dynamic_update_slice(
        jnp.zeros((3, H), f32), head_stack, (0, column * local_heads)
    )
    small = (
        convx_full,
        dconv[:KC],
        heads_full,
        grad_input_gain,
        grad_middle_gain,
        err_local,
    )
    flat = jnp.concatenate([part.reshape(-1) for part in small])
    length = flat.shape[0]
    padded = -(-length // 1024) * 1024
    flat = jnp.pad(flat, (0, padded - length)).reshape(-1, 128)
    flat = sum_tensor(flat, at)
    input_grad = relocate(after(input_grad.astype(bf16), flat), at).astype(f32)
    flat = sum_data(flat, at).reshape(-1)
    sums = []
    start = 0
    for part in small:
        sums.append(flat[start : start + part.size].reshape(part.shape))
        start += part.size
    sum_lanes, sum_convs, sum_heads, sum_input_gain, sum_middle_gain, err_total = sums
    lanes_local = lax.dynamic_slice_in_dim(sum_lanes, at.t * width, width, 1)
    heads_local = lax.dynamic_slice_in_dim(sum_heads, at.t * local_heads, local_heads, 1)
    loss = err_total / jnp.sum(lengths).astype(f32)
    query_from = 2 * width
    step_from = query_from + query_width
    return (
        layer_out,
        loss,
        input_grad,
        sum_input_gain,
        grad_in[:, :query_from].reshape(w_rows, 2, width),
        grad_in[:, step_from : step_from + local_heads],
        grad_in[:, query_from:step_from],
        grad_shared_weight,
        lanes_local[:KC],
        sum_convs,
        heads_local[0],
        heads_local[1],
        heads_local[2],
        lanes_local[KC],
        grad_out[:, :width],
        grad_out[:, width:],
        sum_middle_gain,
        grad_gate_up.reshape(w_rows, 2, hidden_width),
        grad_down,
    )


def solution(mesh):
    placed = (
        P(("dp", "tensor"), None),
        P(("dp", "tensor"), None),
        P(),
        P(),
        P("dp", None, "tensor"),
        P("dp", "tensor"),
        P("dp", "tensor"),
        P(("dp", "tensor"), None),
        P(None, "tensor"),
        P(),
        P("tensor"),
        P("tensor"),
        P("tensor"),
        P("tensor"),
        P("dp", "tensor"),
        P("dp", "tensor"),
        P(),
        P("dp", None, "tensor"),
        P("dp", "tensor"),
    )
    return jax.shard_map(
        per_device,
        mesh=mesh,
        in_specs=placed,
        out_specs=(
            P(("dp", "tensor"), None),
            P(),
            P(("dp", "tensor"), None),
            P(),
            P("dp", None, "tensor"),
            P("dp", "tensor"),
            P("dp", "tensor"),
            P(("dp", "tensor"), None),
            P(None, "tensor"),
            P(),
            P("tensor"),
            P("tensor"),
            P("tensor"),
            P("tensor"),
            P("dp", "tensor"),
            P("dp", "tensor"),
            P(),
            P("dp", None, "tensor"),
            P("dp", "tensor"),
        ),
        check_vma=False,
    )
```

```python
import functools

import jax
import jax.numpy as jnp
from jax import lax
from jax.experimental import pallas as pl
from jax.experimental.pallas import tpu as pltpu
from jax.sharding import PartitionSpec as P

H = 48
KC = 4
QH = 8
KVH = 2
HD = 128
DI = 3072

EPS = 1e-05
ROPE_BASE = 100000000000.0


def rms_norm(values, gain):
    return values * lax.rsqrt(jnp.mean(values * values, axis=-1, keepdims=True) + EPS) * gain


def low_dot(left, right, dims):
    return lax.dot_general(left, right, (dims, ((), ())), preferred_element_type=jnp.float32)


NN = ((1,), (0,))
NT = ((1,), (1,))
TN = ((0,), (0,))
CHUNK = 128
ROWS = 256
WIDE = 128
FAR = -1e30


def exact_dot(ones, values, parts=3):
    total = None
    for _ in range(parts):
        part = values.astype(jnp.bfloat16)
        values = values - part.astype(jnp.float32)
        term = low_dot(ones, part, NN)
        total = term if total is None else total + term
    return total


def split_dot(values, ones, parts=2):
    total = None
    for _ in range(parts):
        part = values.astype(jnp.bfloat16)
        values = values - part.astype(jnp.float32)
        term = low_dot(part, ones, NN)
        total = term if total is None else total + term
    return total


def sigmoid(v):
    return 1.0 / (1.0 + jnp.exp(-v))


def softplus(v):
    return jnp.maximum(v, 0.0) + jnp.log1p(jnp.exp(-jnp.abs(v)))


def iota(shape, axis):
    return lax.broadcasted_iota(jnp.int32, shape, axis)


def spin(values, cosine, sine):
    return values * cosine + pltpu.roll(values, HD // 2, 1) * sine


def unspin(values, cosine, sine):
    return values * cosine - pltpu.roll(values, HD // 2, 1) * sine


def attn_probs(query_low, key_low, first_row, scale):
    scores = low_dot(query_low, key_low, NT) * scale
    rows, keys = scores.shape
    allowed = iota((rows, keys), 1) <= iota((rows, keys), 0) + first_row
    scores = jnp.where(allowed, scores, FAR)
    top = jnp.max(scores, axis=1, keepdims=True)
    weights = jnp.exp(scores - top)
    return weights / jnp.sum(weights, axis=1, keepdims=True)


def attn_fwd_body(order, q_ref, kv_ref, cos_ref, sin_ref, out_ref, key_s, value_s):
    bf16 = jnp.bfloat16
    step = pl.program_id(0)
    cosine, sine = cos_ref[...], sin_ref[...]
    rows = pl.ds(pl.multiple_of(step * ROWS, ROWS), ROWS)
    key_s[rows, :] = spin(kv_ref[:, :HD], cosine, sine).astype(bf16)
    value_s[rows, :] = kv_ref[:, HD:].astype(bf16)
    heads = q_ref.shape[1] // HD
    blocks = key_s.shape[0] // ROWS
    for block in range(blocks):

        @pl.when(step == block)
        def _(block=block):
            keys = (block + 1) * ROWS
            for head in range(heads):
                lanes = slice(head * HD, (head + 1) * HD)
                query = spin(q_ref[:, lanes], cosine, sine).astype(bf16)
                probs = attn_probs(query, key_s[:keys, :], block * ROWS, HD**-0.5)
                out_ref[:, lanes] = low_dot(
                    probs.astype(bf16), value_s[:keys, :], NN
                ).astype(bf16)


def attn_bwd_body(
    order, q_ref, kv_ref, cos_ref, sin_ref, grad_ref, all_cos, all_sin, dq_ref, dkv_ref,
    key_s, value_s, dkey_s, dvalue_s,
):
    bf16, f32 = jnp.bfloat16, jnp.float32
    step = pl.program_id(0)

    @pl.when(step == 0)
    def _():
        dkey_s[...] = jnp.zeros_like(dkey_s)
        dvalue_s[...] = jnp.zeros_like(dvalue_s)

    cosine, sine = cos_ref[...], sin_ref[...]
    rows = pl.ds(pl.multiple_of(step * ROWS, ROWS), ROWS)
    key_s[rows, :] = spin(kv_ref[:, :HD], cosine, sine).astype(bf16)
    value_s[rows, :] = kv_ref[:, HD:].astype(bf16)
    heads = q_ref.shape[1] // HD
    blocks = key_s.shape[0] // ROWS
    scale = HD**-0.5
    for block in range(blocks):

        @pl.when(step == block)
        def _(block=block):
            keys = (block + 1) * ROWS
            for head in range(heads):
                lanes = slice(head * HD, (head + 1) * HD)
                query = spin(q_ref[:, lanes], cosine, sine).astype(bf16)
                probs = attn_probs(query, key_s[:keys, :], block * ROWS, scale)
                grad = grad_ref[:, lanes].astype(bf16)
                dprobs = low_dot(grad, value_s[:keys, :], NT)
                dvalue_s[:keys, :] += low_dot(probs.astype(bf16), grad, TN)
                inner = jnp.sum(dprobs * probs, axis=1, keepdims=True)
                dscores = (probs * (dprobs - inner) * scale).astype(bf16)
                dquery = low_dot(dscores, key_s[:keys, :], NN)
                dkey_s[:keys, :] += low_dot(dscores, query, TN)
                dq_ref[:, lanes] = unspin(dquery, cosine, sine).astype(bf16)

    @pl.when(step == blocks - 1)
    def _():
        dkv_ref[:, :HD] = unspin(dkey_s[...], all_cos[...], all_sin[...]).astype(bf16)
        dkv_ref[:, HD:] = dvalue_s[...].astype(bf16)


def conv_taps(ext, taps, first, width):
    rows = ext.shape[0] - 8
    total = None
    for tap in range(width):
        at = 8 - (width - 1) + tap
        term = ext[at : at + rows, :] * taps[first + tap : first + tap + 1, :]
        total = term if total is None else total + term
    return total


def decays(steps, head_params, tri):
    shifted = steps + head_params[0:1, :]
    dt = softplus(shifted)
    la = dt * head_params[1:2, :]
    cum = exact_dot(tri, la)
    return shifted, dt, la, cum


def spread_lanes(values, pair, first):
    rows = values.shape[0]
    a = jnp.broadcast_to(values[:, 2 * pair : 2 * pair + 1], (rows, WIDE))
    b = jnp.broadcast_to(values[:, 2 * pair + 1 : 2 * pair + 2], (rows, WIDE))
    return a, b, jnp.where(first, a, b)


def mixer_fwd_body(
    order, gate_ref, inner_ref, step_ref, bc_ref, attn_ref, lane_ref, conv_ref, head_ref,
    out_ref, y_ref, state_ref, ext_s, extbc_s, state_s, x_s,
):
    bf16, f32 = jnp.bfloat16, jnp.float32
    step = pl.program_id(0)
    width = inner_ref.shape[1]
    states = bc_ref.shape[1] // 2

    @pl.when(step == 0)
    def _():
        ext_s[0:8, :] = jnp.zeros((8, width), f32)
        extbc_s[0:8, :] = jnp.zeros((8, 2 * states), f32)
        state_s[...] = jnp.zeros_like(state_s)

    ext_s[8:, :] = inner_ref[...]
    extbc_s[8:, :] = bc_ref[...]
    pre = conv_taps(ext_s, lane_ref, 0, KC)
    x_s[...] = pre * sigmoid(pre)
    pre = conv_taps(extbc_s, conv_ref, 0, KC)
    bc = (pre * sigmoid(pre)).astype(bf16)
    ext_s[0:8, :] = ext_s[ROWS : ROWS + 8, :]
    extbc_s[0:8, :] = extbc_s[ROWS : ROWS + 8, :]
    row, col = iota((CHUNK, CHUNK), 0), iota((CHUNK, CHUNK), 1)
    causal = row >= col
    tri = jnp.where(causal, 1.0, 0.0).astype(bf16)
    first = iota((CHUNK, WIDE), 1) < WIDE // 2
    for sub in range(ROWS // CHUNK):
        lo = sub * CHUNK
        b_low = bc[lo : lo + CHUNK, :states]
        c_low = bc[lo : lo + CHUNK, states:]
        _, dt, _, cum = decays(step_ref[lo : lo + CHUNK, :], head_ref, tri)
        cum_t = cum.T
        cross = low_dot(c_low, b_low, NT)
        state_low = state_s[...].astype(bf16)
        state_ref[sub] = state_low
        b_t = b_low.T
        for pair in range(width // WIDE):
            lanes = slice(pair * WIDE, (pair + 1) * WIDE)
            cum_a, cum_b, cum_p = spread_lanes(cum, pair, first)
            _, _, dt_p = spread_lanes(dt, pair, first)
            weights = []
            for wide, head in ((cum_a, 2 * pair), (cum_b, 2 * pair + 1)):
                gap = jnp.where(causal, wide - cum_t[head : head + 1, :], FAR)
                weights.append((cross * jnp.exp(gap)).astype(bf16))
            x = x_s[lo : lo + CHUNK, lanes]
            scaled = x * dt_p
            zero = jnp.zeros_like(scaled)
            stacked = jnp.concatenate(
                [jnp.where(first, scaled, zero), jnp.where(first, zero, scaled)], axis=0
            ).astype(bf16)
            y = low_dot(jnp.concatenate(weights, axis=1), stacked, NN)
            y = y + jnp.exp(cum_p) * low_dot(c_low, state_low[:, lanes], NN)
            y_ref[lo : lo + CHUNK, lanes] = y + lane_ref[5:6, lanes] * x
            last = cum_p[CHUNK - 1 : CHUNK, :]
            ends = (scaled * jnp.exp(last - cum_p)).astype(bf16)
            state_s[:, lanes] = state_s[:, lanes] * jnp.exp(last) + low_dot(b_t, ends, NN)
    gate = gate_ref[...]
    gated = y_ref[...] * (gate * sigmoid(gate))
    scale = lax.rsqrt(jnp.mean(gated * gated, axis=1, keepdims=True) + EPS)
    out_ref[:, :width] = (gated * scale * lane_ref[4:5, :]).astype(bf16)
    out_ref[:, width:] = attn_ref[...]


def mixer_bwd_body(
    order, gate_ref, inner_ref, before_ref, step_ref, bc_ref, bcbefore_ref, y_ref, state_ref,
    grad_ref, dq_ref, dkv_ref, lane_ref, conv_ref, head_ref, seg_ref,
    low_ref, lowsh_ref, dlane_ref, dconv_ref, dhead_ref,
    ext_s, extbc_s, pre_s, prebc_s, x_s, bc_s, g_s, dx_s, dbc_s, dpre_s, dprebc_s, dstate_s,
    z_s, rows_s,
):
    bf16, f32 = jnp.bfloat16, jnp.float32
    step = pl.program_id(0)
    blocks = pl.num_programs(0)
    width = inner_ref.shape[1]
    states = bc_ref.shape[1] // 2
    query_width = dq_ref.shape[1]

    @pl.when(step == 0)
    def _():
        dlane_ref[...] = jnp.zeros_like(dlane_ref)
        dconv_ref[...] = jnp.zeros_like(dconv_ref)
        dhead_ref[...] = jnp.zeros_like(dhead_ref)
        dstate_s[...] = jnp.zeros_like(dstate_s)
        dpre_s[ROWS:, :] = jnp.zeros((8, width), f32)
        dprebc_s[ROWS:, :] = jnp.zeros((8, 2 * states), f32)
        z_s[...] = jnp.zeros_like(z_s)
        rows_s[...] = jnp.zeros_like(rows_s)

    keep = jnp.where(step == blocks - 1, 0.0, 1.0)
    ext_s[0:8, :] = before_ref[...] * keep
    extbc_s[0:8, :] = bcbefore_ref[...] * keep
    ext_s[8:, :] = inner_ref[...]
    extbc_s[8:, :] = bc_ref[...]
    pre = conv_taps(ext_s, lane_ref, 0, KC)
    pre_s[...] = pre
    x_s[...] = pre * sigmoid(pre)
    pre = conv_taps(extbc_s, conv_ref, 0, KC)
    prebc_s[...] = pre
    bc_s[...] = (pre * sigmoid(pre)).astype(bf16)

    gate = gate_ref[...]
    sig = sigmoid(gate)
    gate_act = gate * sig
    y = y_ref[...]
    gated = y * gate_act
    scale = lax.rsqrt(jnp.mean(gated * gated, axis=1, keepdims=True) + EPS)
    grad = grad_ref[...]
    dlane_ref[4:5, :] += jnp.sum(grad * gated * scale, axis=0, keepdims=True)
    grad = grad * lane_ref[4:5, :]
    mean = jnp.mean(grad * gated, axis=1, keepdims=True)
    dgated = scale * grad - gated * (scale * scale * scale * mean)
    g_s[...] = dgated * gate_act
    low_ref[:, :width] = (dgated * y * sig * (1.0 + gate * (1.0 - sig))).astype(bf16)

    row, col = iota((CHUNK, CHUNK), 0), iota((CHUNK, CHUNK), 1)
    tri = jnp.where(row >= col, 1.0, 0.0).astype(bf16)
    tri_up = jnp.where(row <= col, 1.0, 0.0).astype(bf16)
    later = row <= col
    first = iota((CHUNK, WIDE), 1) < WIDE // 2
    last_row = iota((CHUNK, WIDE), 0) == CHUNK - 1
    for sub in reversed(range(ROWS // CHUNK)):
        lo = sub * CHUNK
        b_low = bc_s[lo : lo + CHUNK, :states]
        c_low = bc_s[lo : lo + CHUNK, states:]
        shifted, dt, la, cum = decays(step_ref[lo : lo + CHUNK, :], head_ref, tri)
        cum_t = cum.T
        cross_t = low_dot(b_low, c_low, NT)
        c_t = c_low.T
        state_low = state_ref[sub]
        dstate_low = dstate_s[...].astype(bf16)
        dcross_t = jnp.zeros((CHUNK, CHUNK), f32)
        db = jnp.zeros((CHUNK, states), f32)
        dc = jnp.zeros((CHUNK, states), f32)
        for pair in range(width // WIDE):
            lanes = slice(pair * WIDE, (pair + 1) * WIDE)
            cum_a, cum_b, cum_p = spread_lanes(cum, pair, first)
            _, _, dt_p = spread_lanes(dt, pair, first)
            x = x_s[lo : lo + CHUNK, lanes]
            g = g_s[lo : lo + CHUNK, lanes]
            scaled = x * dt_p
            scaled_low = scaled.astype(bf16)
            zero = jnp.zeros_like(g)
            g_stack = jnp.concatenate(
                [jnp.where(first, g, zero), jnp.where(first, zero, g)], axis=0
            ).astype(bf16)
            dweights_t = low_dot(scaled_low, g_stack, NT)
            weights_t = []
            for place, wide, head in ((0, cum_a, 2 * pair), (1, cum_b, 2 * pair + 1)):
                gap = jnp.where(later, cum_t[head : head + 1, :] - wide, FAR)
                grow = jnp.exp(gap)
                weight = (cross_t * grow).astype(bf16)
                weights_t.append(weight)
                dweight = dweights_t[:, place * CHUNK : (place + 1) * CHUNK]
                dcross_t = dcross_t + dweight * grow
                rows_s[head : head + 1, :] = jnp.sum(
                    dweight * weight.astype(f32), axis=0, keepdims=True
                )
            dx_in = low_dot(jnp.concatenate(weights_t, axis=1), g_stack, NN)
            grown = jnp.exp(cum_p)
            last = cum_p[CHUNK - 1 : CHUNK, :]
            tail = jnp.exp(last - cum_p)
            last = jnp.exp(last)
            dx_tail = tail * low_dot(b_low, dstate_low[:, lanes], NN)
            dscaled = dx_in + dx_tail
            g_grown = g * grown
            g_low = g_grown.astype(bf16)
            ends = (scaled * tail).astype(bf16)
            carried = low_dot(c_low, state_low[:, lanes], NN)
            dc = dc + low_dot(g_low, state_low[:, lanes], NT)
            db = db + low_dot(ends, dstate_low[:, lanes], NT)
            dstate = dstate_s[:, lanes]
            kept = jnp.sum(dstate * state_low[:, lanes].astype(f32), axis=0, keepdims=True) * last
            dstate_s[:, lanes] = dstate * last + low_dot(c_t, g_low, NN)
            tails = scaled * dx_tail
            z_s[0:CHUNK, lanes] = g_grown * carried - tails - scaled_low.astype(f32) * dx_in
            z_s[CHUNK : 2 * CHUNK, lanes] = dscaled * x
            z_s[2 * CHUNK : 2 * CHUNK + 1, lanes] = (
                jnp.sum(tails, axis=0, keepdims=True) + kept
            )
            dx_s[lo : lo + CHUNK, lanes] = dscaled * dt_p + lane_ref[5:6, lanes] * g
            dlane_ref[5:6, lanes] += jnp.sum(g * x, axis=0, keepdims=True)
        sums = split_dot(z_s[...], seg_ref[...])
        dcum = sums[0:CHUNK, :] + rows_s[...].T
        dcum = dcum + jnp.where(last_row, sums[2 * CHUNK : 2 * CHUNK + 1, :], 0.0)
        dla = exact_dot(tri_up, dcum)
        ddt = sums[CHUNK : 2 * CHUNK, :] + dla * head_ref[1:2, :]
        dsteps = ddt * sigmoid(shifted)
        dhead_ref[0:1, :] += jnp.sum(dsteps, axis=0, keepdims=True)
        dhead_ref[1:2, :] += jnp.sum(dla * la, axis=0, keepdims=True)
        low_ref[lo : lo + CHUNK, 2 * width + query_width :] = dsteps.astype(bf16)
        dcross_low = dcross_t.astype(bf16)
        dbc_s[lo : lo + CHUNK, :states] = db + low_dot(dcross_low, c_low, NN)
        dbc_s[lo : lo + CHUNK, states:] = dc + low_dot(dcross_low, b_low, TN)

    def conv_back(pre_ref, dact, dpre_ref, ext, taps, dtaps_ref):
        pre = pre_ref[...]
        sig = sigmoid(pre)
        dpre = dact * (sig * (1.0 + pre * (1.0 - sig)))
        dpre_ref[0:ROWS, :] = dpre
        total = None
        for tap in range(KC):
            ahead = KC - 1 - tap
            term = dpre_ref[ahead : ahead + ROWS, :] * taps[tap : tap + 1, :]
            total = term if total is None else total + term
            at = 8 - (KC - 1) + tap
            dtaps_ref[tap : tap + 1, :] += jnp.sum(
                dpre * ext[at : at + ROWS, :], axis=0, keepdims=True
            )
        dpre_ref[ROWS:, :] = dpre_ref[0:8, :]
        return total

    dinner = conv_back(pre_s, dx_s[...], dpre_s, ext_s, lane_ref, dlane_ref)
    low_ref[:, width : 2 * width] = dinner.astype(bf16)
    dbc = conv_back(prebc_s, dbc_s[...], dprebc_s, extbc_s, conv_ref, dconv_ref)
    lowsh_ref[:, : 2 * states] = dbc.astype(bf16)
    lowsh_ref[:, 2 * states :] = dkv_ref[...]
    low_ref[:, 2 * width : 2 * width + query_width] = dq_ref[...]


def block_at(rows, cols, col):
    return pl.BlockSpec((rows, cols), lambda i, order: (order[i], col))


def whole_at(shape):
    return pl.BlockSpec(shape, lambda i, order: (0,) * len(shape))


def kernel_params():
    return pltpu.CompilerParams(
        dimension_semantics=("arbitrary",), vmem_limit_bytes=56 * 1024 * 1024
    )


def attn_forward(order, proj, proj_shared, cosine, sine, query_width, width, bc_width):
    slot = proj.shape[0]
    scratch = [pltpu.VMEM((slot, HD), jnp.bfloat16)] * 2
    return pl.pallas_call(
        attn_fwd_body,
        grid_spec=pltpu.PrefetchScalarGridSpec(
            num_scalar_prefetch=1,
            grid=(slot // ROWS,),
            in_specs=[
                block_at(ROWS, query_width, 2 * width // query_width),
                block_at(ROWS, 2 * HD, bc_width // (2 * HD)),
                pl.BlockSpec((ROWS, HD), lambda i, order: (i, 0)),
                pl.BlockSpec((ROWS, HD), lambda i, order: (i, 0)),
            ],
            out_specs=block_at(ROWS, query_width, 0),
            scratch_shapes=scratch,
        ),
        out_shape=jax.ShapeDtypeStruct((slot, query_width), jnp.bfloat16),
        compiler_params=kernel_params(),
        cost_estimate=pl.CostEstimate(
            flops=slot * slot * query_width * 3,
            bytes_accessed=slot * 4 * (query_width + 4 * HD),
            transcendentals=slot * slot * query_width // HD,
        ),
    )(order, proj, proj_shared, cosine, sine)


def attn_backward(order, proj, proj_shared, cosine, sine, grad_heads, query_width, width, bc_width):
    slot = proj.shape[0]
    return pl.pallas_call(
        attn_bwd_body,
        grid_spec=pltpu.PrefetchScalarGridSpec(
            num_scalar_prefetch=1,
            grid=(slot // ROWS,),
            in_specs=[
                block_at(ROWS, query_width, 2 * width // query_width),
                block_at(ROWS, 2 * HD, bc_width // (2 * HD)),
                pl.BlockSpec((ROWS, HD), lambda i, order: (i, 0)),
                pl.BlockSpec((ROWS, HD), lambda i, order: (i, 0)),
                block_at(ROWS, query_width, width // query_width),
                whole_at((slot, HD)),
                whole_at((slot, HD)),
            ],
            out_specs=[block_at(ROWS, query_width, 0), whole_at((slot, 2 * HD))],
            scratch_shapes=[pltpu.VMEM((slot, HD), jnp.bfloat16)] * 2
            + [pltpu.VMEM((slot, HD), jnp.float32)] * 2,
        ),
        out_shape=[
            jax.ShapeDtypeStruct((slot, query_width), jnp.bfloat16),
            jax.ShapeDtypeStruct((slot, 2 * HD), jnp.bfloat16),
        ],
        compiler_params=kernel_params(),
        cost_estimate=pl.CostEstimate(
            flops=slot * slot * query_width * 8,
            bytes_accessed=slot * 4 * (2 * query_width + 6 * HD),
            transcendentals=slot * slot * query_width // HD,
        ),
    )(order, proj, proj_shared, cosine, sine, grad_heads, cosine, sine)


def mixer_forward(order, proj, proj_shared, attn_low, lane_params, conv_shared, head_params):
    slot = proj.shape[0]
    f32, bf16 = jnp.float32, jnp.bfloat16
    width = lane_params.shape[1]
    bc_width = conv_shared.shape[1]
    query_width = attn_low.shape[1]
    chunks = ROWS // CHUNK
    return pl.pallas_call(
        mixer_fwd_body,
        grid_spec=pltpu.PrefetchScalarGridSpec(
            num_scalar_prefetch=1,
            grid=(slot // ROWS,),
            in_specs=[
                block_at(ROWS, width, 0),
                block_at(ROWS, width, 1),
                block_at(ROWS, WIDE, (2 * width + query_width) // WIDE),
                block_at(ROWS, bc_width, 0),
                block_at(ROWS, query_width, 0),
                whole_at(lane_params.shape),
                whole_at(conv_shared.shape),
                whole_at(head_params.shape),
            ],
            out_specs=[
                block_at(ROWS, width + query_width, 0),
                pl.BlockSpec((ROWS, width), lambda i, order: (i, 0)),
                pl.BlockSpec((chunks, bc_width // 2, width), lambda i, order: (i, 0, 0)),
            ],
            scratch_shapes=[
                pltpu.VMEM((ROWS + 8, width), f32),
                pltpu.VMEM((ROWS + 8, bc_width), f32),
                pltpu.VMEM((bc_width // 2, width), f32),
                pltpu.VMEM((ROWS, width), f32),
            ],
        ),
        out_shape=[
            jax.ShapeDtypeStruct((slot, width + query_width), bf16),
            jax.ShapeDtypeStruct((slot, width), f32),
            jax.ShapeDtypeStruct((slot // CHUNK, bc_width // 2, width), bf16),
        ],
        compiler_params=kernel_params(),
        cost_estimate=pl.CostEstimate(
            flops=slot * width * bc_width * 8,
            bytes_accessed=slot * width * 20,
            transcendentals=slot * width * 8,
        ),
    )(order, proj, proj, proj, proj_shared, attn_low, lane_params, conv_shared, head_params)


def mixer_backward(
    order, proj, proj_shared, y, states, grad_heads, dq, dkv, lane_params, conv_shared,
    head_params, seg, query_width,
):
    slot = proj.shape[0]
    f32, bf16 = jnp.float32, jnp.bfloat16
    width = lane_params.shape[1]
    bc_width = conv_shared.shape[1]
    blocks = slot // ROWS
    chunks = ROWS // CHUNK

    def back(rows, cols, col):
        return pl.BlockSpec((rows, cols), lambda i, order: (order[blocks - 1 - i], col))

    def straight(shape):
        return pl.BlockSpec(
            shape, lambda i, order: (blocks - 1 - i,) + (0,) * (len(shape) - 1)
        )

    def before(cols, col):
        return pl.BlockSpec(
            (8, cols),
            lambda i, order: (
                order[jnp.maximum(blocks - 2 - i, 0)] * (ROWS // 8) + ROWS // 8 - 1,
                col,
            ),
        )

    return pl.pallas_call(
        mixer_bwd_body,
        grid_spec=pltpu.PrefetchScalarGridSpec(
            num_scalar_prefetch=1,
            grid=(blocks,),
            in_specs=[
                back(ROWS, width, 0),
                back(ROWS, width, 1),
                before(width, 1),
                back(ROWS, WIDE, (2 * width + query_width) // WIDE),
                back(ROWS, bc_width, 0),
                before(bc_width, 0),
                straight((ROWS, width)),
                straight((chunks, bc_width // 2, width)),
                back(ROWS, width, 0),
                back(ROWS, query_width, 0),
                straight((ROWS, 2 * HD)),
                whole_at(lane_params.shape),
                whole_at(conv_shared.shape),
                whole_at(head_params.shape),
                whole_at(seg.shape),
            ],
            out_specs=[
                back(ROWS, 2 * width + query_width + WIDE, 0),
                back(ROWS, bc_width + 2 * HD, 0),
                whole_at((8, width)),
                whole_at((8, bc_width)),
                whole_at((8, WIDE)),
            ],
            scratch_shapes=[
                pltpu.VMEM((ROWS + 8, width), f32),
                pltpu.VMEM((ROWS + 8, bc_width), f32),
                pltpu.VMEM((ROWS, width), f32),
                pltpu.VMEM((ROWS, bc_width), f32),
                pltpu.VMEM((ROWS, width), f32),
                pltpu.VMEM((ROWS, bc_width), bf16),
                pltpu.VMEM((ROWS, width), f32),
                pltpu.VMEM((ROWS, width), f32),
                pltpu.VMEM((ROWS, bc_width), f32),
                pltpu.VMEM((ROWS + 8, width), f32),
                pltpu.VMEM((ROWS + 8, bc_width), f32),
                pltpu.VMEM((bc_width // 2, width), f32),
                pltpu.VMEM((2 * CHUNK + 8, width), f32),
                pltpu.VMEM((WIDE, CHUNK), f32),
            ],
        ),
        out_shape=[
            jax.ShapeDtypeStruct((slot, 2 * width + query_width + WIDE), bf16),
            jax.ShapeDtypeStruct((slot, bc_width + 2 * HD), bf16),
            jax.ShapeDtypeStruct((8, width), f32),
            jax.ShapeDtypeStruct((8, bc_width), f32),
            jax.ShapeDtypeStruct((8, WIDE), f32),
        ],
        compiler_params=kernel_params(),
        cost_estimate=pl.CostEstimate(
            flops=slot * width * bc_width * 20,
            bytes_accessed=slot * width * 40,
            transcendentals=slot * width * 16,
        ),
    )(
        order, proj, proj, proj, proj, proj_shared, proj_shared, y, states, grad_heads, dq, dkv,
        lane_params, conv_shared, head_params, seg,
    )


class Places:
    def __init__(self):
        self.dp = lax.axis_size("dp")
        self.tp = lax.axis_size("tensor")
        d = lax.axis_index("dp")
        t = lax.axis_index("tensor")
        self.d, self.t = d, t
        self.c = d % 2
        self.k = d // 2
        self.zq = t % 2
        self.home = self.c == t // 2
        self.quarter = 2 * self.c + self.zq
        self.column = self.zq + 2 * self.c
        self.slot = 2 * self.k + t // 2
        self.blocks = self.dp // 2
        self.bits = self.blocks.bit_length() - 1

    def pairs(self, where_to):
        out = []
        for d in range(self.dp):
            for t in range(self.tp):
                target = where_to(d, t)
                if target is not None:
                    out.append((d * self.tp + t, target[0] * self.tp + target[1]))
        return out

    def send(self, values, where_to):
        return lax.ppermute(values, ("dp", "tensor"), self.pairs(where_to))

    def over_core(self, values):
        return self.send(values, lambda d, t: (d ^ 1, t))

    def over_z(self, values):
        return self.send(values, lambda d, t: (d, t ^ 1))

    def over_far(self, values):
        return self.send(values, lambda d, t: (d, t ^ 2))

    def over_bit(self, values, bit):
        return self.send(values, lambda d, t: (d ^ (2 << bit), t))

    def swap_away(self, values):
        def where_to(d, t):
            if d % 2 == t // 2:
                return None
            return (d ^ 1, t ^ 2)

        return self.send(values, where_to)

    def column_out(self, values):
        def where_to(d, t):
            if d % 2 == t // 2:
                return (d, t ^ 2)
            return (d ^ 1, t)

        return self.send(values, where_to)

    def column_back(self, values):
        def where_to(d, t):
            if d % 2 == t // 2:
                return (d ^ 1, t)
            return (d, t ^ 2)

        return self.send(values, where_to)


def relocate(values, at):
    return jnp.where(at.home, values, at.swap_away(values))


MESH = pl.DeviceIdType.MESH


class Lanes:
    def __init__(self, blocks):
        d = lax.axis_index("dp")
        t = lax.axis_index("tensor")
        self.c = lax.rem(d, 2)
        self.k = lax.div(d, 2)
        self.d, self.t = d, t
        self.home = self.c == lax.div(t, 2)
        self.away = self.c != lax.div(t, 2)
        self.other = d + 1 - 2 * self.c
        self.near = t + 1 - 2 * lax.rem(t, 2)
        self.far = lax.rem(t + 2, 4)
        self.blocks = blocks
        self.bits = blocks.bit_length() - 1

    def block(self, place):
        value = self.k
        for bit in range(self.bits):
            if (place >> bit) & 1:
                value = value + (1 << bit) * (1 - 2 * lax.rem(lax.div(self.k, 1 << bit), 2))
        return value

    def across(self, bit):
        return (2 * self.block(1 << bit) + self.c, self.t)

    def greet(self):
        partners = [
            (self.other, self.t),
            (self.d, self.near),
            (self.d, self.far),
            (self.other, self.far),
        ] + [self.across(bit) for bit in range(self.bits)]
        barrier = pltpu.get_barrier_semaphore()
        for partner in partners:
            pl.semaphore_signal(barrier, inc=1, device_id=partner, device_id_type=MESH)
        pl.semaphore_wait(barrier, len(partners))


def remote(src, dst, send_sem, recv_sem, device):
    return pltpu.make_async_remote_copy(
        src_ref=src,
        dst_ref=dst,
        send_sem=send_sem,
        recv_sem=recv_sem,
        device_id=device,
        device_id_type=MESH,
    )


def onward(place, half, bits):
    if half == 0:
        return [bit for bit in range(bits) if place < (1 << bit)]
    return [bit for bit in reversed(range(bits)) if place % (2 << bit) == 0]


class Spread:
    def __init__(self, lanes, full, rows, chunks, send_sems, recv_sems, cols=slice(None)):
        self.lanes, self.full, self.rows, self.chunks = lanes, full, rows, chunks
        self.cols = cols
        self.piece = rows // chunks
        self.send_sems, self.recv_sems = send_sems, recv_sems

    def view(self, place, half, chunk):
        start = self.lanes.block(place) * (2 * self.rows) + half * self.rows + chunk * self.piece
        return self.full.at[pl.ds(pl.multiple_of(start, self.piece), self.piece), self.cols]

    def copy(self, place, half, chunk, bit):
        view = self.view(place, half, chunk)
        to = place | (1 << bit)
        return remote(
            view,
            view,
            self.send_sems.at[half, to, chunk],
            self.recv_sems.at[half, to, chunk],
            self.lanes.across(bit),
        )

    def give(self, place, half, chunk):
        for bit in onward(place, half, self.lanes.bits):
            self.copy(place, half, chunk, bit).start()

    def take(self, place, half, chunk):
        view = self.view(place, half, chunk)
        remote(
            view,
            view,
            self.send_sems.at[half, place, chunk],
            self.recv_sems.at[half, place, chunk],
            self.lanes.across(0),
        ).wait_recv()

    def pass_on(self, chunk):
        for half in range(2):
            places = range(1, self.lanes.blocks)
            if half == 1:
                key = lambda place: [-bit for bit in reversed(range(8)) if (place >> bit) & 1]
                places = sorted(places, key=key)
            for place in places:
                if onward(place, half, self.lanes.bits):
                    self.take(place, half, chunk)
                    self.give(place, half, chunk)

    def finish(self, chunk):
        for half in range(2):
            for place in range(1, self.lanes.blocks):
                if not onward(place, half, self.lanes.bits):
                    self.take(place, half, chunk)
        for half in range(2):
            for place in range(self.lanes.blocks):
                for bit in onward(place, half, self.lanes.bits):
                    self.copy(place, half, chunk, bit).wait_send()


def front_body(
    blocks, chunks, in_ref, out_ref, shared_ref, x_ref, gain_ref,
    full_ref, pair_ref, act_ref, xr_ref, sh_ref,
    x_s, act_s, home_sems, z_send, z_recv, o_sems, o_recv, send_sems, recv_sems, x_sems, a_send,
    a_recv, line_send, line_recv, sh_send, sh_recv, swap_send, swap_recv,
):
    lanes = Lanes(blocks)
    rows = in_ref.shape[0]
    piece = rows // chunks
    here = x_ref.shape[0]
    c, t = lanes.c, lanes.t
    lanes.greet()
    spread = Spread(lanes, full_ref, rows, chunks, send_sems, recv_sems)
    few, wide = shared_ref.shape
    side = wide // 2
    mine = pl.ds(pl.multiple_of(c * side, side), side)
    theirs = pl.ds(pl.multiple_of((1 - c) * side, side), side)

    def line_view(half, at_t, cols):
        start = lanes.k * (2 * rows) + half * rows + at_t * few
        return sh_ref.at[pl.ds(pl.multiple_of(start, few), few), cols]

    def line_own():
        return pltpu.make_async_copy(
            shared_ref.at[:, mine], line_view(c, t, mine), line_send.at[0]
        )

    def line_swap():
        return remote(
            shared_ref.at[:, theirs],
            line_view(c, t, theirs),
            line_send.at[1],
            line_recv.at[0],
            (lanes.other, t),
        )

    def line_swapped():
        view = line_view(1 - c, t, mine)
        return remote(view, view, line_send.at[1], line_recv.at[0], (lanes.other, t))

    def line_near(half, came):
        view = line_view(half, lanes.near if came else t, mine)
        return remote(
            view, view, line_send.at[2 + half], line_recv.at[1 + half], (lanes.d, lanes.near)
        )

    def line_far(half, near, came):
        at_t = lanes.near if near else t
        if came:
            at_t = lax.rem(at_t + 2, 4)
        view = line_view(half, at_t, mine)
        place = 2 * near + half
        return remote(
            view, view, line_send.at[4 + place], line_recv.at[3 + place], (lanes.d, lanes.far)
        )

    shared_spread = Spread(lanes, sh_ref, rows, 1, sh_send, sh_recv, mine)

    def swap_copy(place, half, came):
        start = lanes.block(place) * (2 * rows) + half * rows
        view = sh_ref.at[pl.ds(pl.multiple_of(start, rows), rows), theirs if came else mine]
        return remote(
            view, view, swap_send.at[half, place], swap_recv.at[half, place], (lanes.other, t)
        )

    def slot(chunk):
        start = lanes.k * (2 * rows) + c * rows + chunk * piece
        return full_ref.at[pl.ds(pl.multiple_of(start, piece), piece), :]

    def first_copy(chunk, device):
        return remote(
            in_ref.at[pl.ds(chunk * piece, piece), :],
            slot(chunk),
            z_send.at[0, chunk],
            z_recv.at[c, chunk],
            device,
        )

    def second_copy(chunk):
        return remote(
            in_ref.at[pl.ds(chunk * piece, piece), :],
            slot(chunk),
            z_send.at[1, chunk],
            z_recv.at[c, chunk],
            (lanes.other, lanes.far),
        )

    def own_copy(chunk):
        return pltpu.make_async_copy(
            in_ref.at[pl.ds(chunk * piece, piece), :], slot(chunk), home_sems.at[chunk]
        )

    def out_slot():
        return pair_ref.at[pl.ds(pl.multiple_of(c * rows, rows), rows), :]

    def out_first(device):
        return remote(out_ref, out_slot(), o_sems.at[0], o_recv.at[c], device)

    def out_second():
        return remote(out_ref, out_slot(), o_sems.at[1], o_recv.at[c], (lanes.other, lanes.far))

    def x_away():
        return remote(x_ref, x_s, x_sems.at[0], x_sems.at[1], (lanes.other, lanes.far))

    def x_home():
        return pltpu.make_async_copy(x_ref, x_s, x_sems.at[2])

    def send_first(chunk):
        @pl.when(lanes.home)
        def _():
            own_copy(chunk).start()
            first_copy(chunk, (lanes.d, lanes.far)).start()

        @pl.when(lanes.away)
        def _():
            first_copy(chunk, (lanes.other, t)).start()
            second_copy(chunk).start()

    def z_view(half, chunk):
        start = lanes.k * (2 * rows) + half * rows + chunk * piece
        return full_ref.at[pl.ds(pl.multiple_of(start, piece), piece), :]

    def came(half, chunk):
        view = z_view(half, chunk)
        return remote(
            view, view, z_send.at[0, chunk], z_recv.at[half, chunk], (lanes.other, t)
        )

    def arrive_home(chunk):
        own_copy(chunk).wait()
        start = lanes.k * (2 * rows) + (1 - c) * rows + chunk * piece
        view = full_ref.at[pl.ds(pl.multiple_of(start, piece), piece), :]
        remote(
            view, view, z_send.at[0, chunk], z_recv.at[1 - c, chunk], (lanes.other, t)
        ).wait_recv()
        for half in range(2):
            spread.give(0, half, chunk)

    def arrive_away(chunk):
        for half in range(2):
            came(half, chunk).wait_recv()
        for half in range(2):
            spread.give(0, half, chunk)

    def arrive(chunk):
        @pl.when(lanes.home)
        def _():
            arrive_home(chunk)

        @pl.when(lanes.away)
        def _():
            arrive_away(chunk)

    def act_slot(index):
        return act_ref.at[pl.ds(index * here, here), :]

    def act_far():
        return remote(act_s, act_slot(2), a_send.at[0], a_recv.at[0], (lanes.d, lanes.near))

    def act_core():
        return remote(act_s, act_slot(1), a_send.at[1], a_recv.at[1], (lanes.other, t))

    def act_both():
        return remote(act_slot(2), act_slot(3), a_send.at[2], a_recv.at[2], (lanes.other, t))

    def norm():
        @pl.when(lanes.home)
        def _():
            x_home().wait()

        @pl.when(lanes.away)
        def _():
            x_away().wait_recv()

        @pl.loop(0, here // 32)
        def _(step):
            part = pl.ds(pl.multiple_of(step * 32, 32), 32)
            x = x_s[part, :].astype(jnp.float32)
            scale = lax.rsqrt(jnp.mean(x * x, axis=1, keepdims=True) + EPS)
            act_s[part, :] = (x * scale * gain_ref[...]).astype(jnp.bfloat16)

        act_far().start()
        act_core().start()
        pltpu.make_async_copy(act_s, act_slot(0), a_send.at[3]).start()
        pltpu.make_async_copy(x_s, xr_ref, x_sems.at[3]).start()

    early = list(range(max(chunks // 2, 1)))
    late = list(range(len(early), chunks))
    line_own().start()
    line_swap().start()
    for chunk in early:
        send_first(chunk)

    @pl.when(lanes.home)
    def _():
        x_home().start()

    @pl.when(lanes.away)
    def _():
        x_away().start()

    line_own().wait()
    line_swapped().wait_recv()
    for half in range(2):
        line_near(half, False).start()
    for chunk in early:
        arrive(chunk)
        if chunk:
            spread.pass_on(chunk - 1)
    for half in range(2):
        line_near(half, True).wait_recv()
    for near in range(2):
        for half in range(2):
            line_far(half, near, False).start()
    for chunk in late:
        send_first(chunk)
    spread.pass_on(early[-1])

    @pl.when(lanes.home)
    def _():
        for chunk in late:
            arrive_home(chunk)
            spread.pass_on(chunk)

    norm()

    @pl.when(lanes.home)
    def _():
        out_first((lanes.d, lanes.far)).start()
        pltpu.make_async_copy(out_ref, out_slot(), o_sems.at[2]).start()

    @pl.when(lanes.away)
    def _():
        out_first((lanes.other, t)).start()
        out_second().start()

    for near in range(2):
        for half in range(2):
            line_far(half, near, True).wait_recv()
    for half in range(2):
        shared_spread.give(0, half, 0)
        swap_copy(0, half, False).start()

    @pl.when(lanes.away)
    def _():
        for chunk in late:
            arrive_away(chunk)
            if chunk > late[0]:
                spread.pass_on(chunk - 1)

    shared_spread.pass_on(0)

    @pl.when(lanes.away)
    def _():
        for chunk in late[-1:]:
            spread.pass_on(chunk)

    shared_spread.finish(0)
    for half in range(2):
        for place in range(1, blocks):
            swap_copy(place, half, False).start()
    act_far().wait_recv()
    act_both().start()
    act_core().wait_recv()
    for chunk in range(chunks):
        spread.finish(chunk)
    for half in range(2):
        for place in range(blocks):
            swap_copy(place, half, True).wait_recv()
            swap_copy(place, half, False).wait_send()
    line_swap().wait_send()
    for half in range(2):
        line_near(half, False).wait_send()
        for near in range(2):
            line_far(half, near, False).wait_send()
    act_both().wait_recv()
    act_far().wait_send()
    act_core().wait_send()
    act_both().wait_send()
    pltpu.make_async_copy(act_s, act_slot(0), a_send.at[3]).wait()
    pltpu.make_async_copy(x_s, xr_ref, x_sems.at[3]).wait()

    @pl.when(lanes.home)
    def _():
        for chunk in range(chunks):
            first_copy(chunk, (lanes.d, lanes.far)).wait_send()
        out_first((lanes.d, lanes.far)).wait_send()
        pltpu.make_async_copy(out_ref, out_slot(), o_sems.at[2]).wait()
        start = (1 - c) * rows
        view = pair_ref.at[pl.ds(pl.multiple_of(start, rows), rows), :]
        remote(view, view, o_sems.at[0], o_recv.at[1 - c], (lanes.other, t)).wait_recv()

    @pl.when(lanes.away)
    def _():
        x_away().wait_send()
        for chunk in range(chunks):
            first_copy(chunk, (lanes.other, t)).wait_send()
            second_copy(chunk).wait_send()
        out_first((lanes.other, t)).wait_send()
        out_second().wait_send()
        for half in range(2):
            view = pair_ref.at[pl.ds(half * rows, rows), :]
            remote(view, view, o_sems.at[0], o_recv.at[half], (lanes.other, t)).wait_recv()


def front(in_pack, out_pack, shared, layer_in, gain, at):
    bf16 = jnp.bfloat16
    rows = in_pack.shape[0]
    blocks = at.blocks
    chunks = 4 if rows >= 256 else 1
    dma = pltpu.SemaphoreType.DMA
    anywhere = pl.BlockSpec(memory_space=pl.ANY)
    here, features = layer_in.shape
    total = 2 * blocks * rows
    return pl.pallas_call(
        functools.partial(front_body, blocks, chunks),
        in_specs=[anywhere] * 4 + [pl.BlockSpec(memory_space=pltpu.VMEM)],
        out_specs=[anywhere] * 5,
        out_shape=[
            jax.ShapeDtypeStruct((total, in_pack.shape[1]), bf16),
            jax.ShapeDtypeStruct((2 * rows, out_pack.shape[1]), bf16),
            jax.ShapeDtypeStruct((4 * here, features), bf16),
            jax.ShapeDtypeStruct((here, features), bf16),
            jax.ShapeDtypeStruct((total, shared.shape[1]), bf16),
        ],
        scratch_shapes=[
            pltpu.VMEM((here, features), bf16),
            pltpu.VMEM((here, features), bf16),
            dma((chunks,)),
            dma((2, chunks)),
            dma((2, chunks)),
            dma((3,)),
            dma((2,)),
            dma((2, blocks, chunks)),
            dma((2, blocks, chunks)),
            dma((4,)),
            dma((4,)),
            dma((3,)),
            dma((8,)),
            dma((7,)),
            dma((2, blocks, 1)),
            dma((2, blocks, 1)),
            dma((2, blocks)),
            dma((2, blocks)),
        ],
        compiler_params=pltpu.CompilerParams(
            collective_id=1, has_side_effects=True, vmem_limit_bytes=16 * 1024 * 1024
        ),
        cost_estimate=pl.CostEstimate(
            flops=here * features * 8, bytes_accessed=300_000_000, transcendentals=0
        ),
    )(in_pack, out_pack, shared, layer_in, gain.reshape(1, -1))


class Collect:
    def __init__(self, lanes, part, rows, cols, send_s, recv_s, load_s, total_s, sems):
        self.lanes, self.part, self.rows, self.cols = lanes, part, rows, cols
        self.send_s, self.recv_s, self.load_s, self.total_s = send_s, recv_s, load_s, total_s
        self.send_sems, self.recv_sems, self.load_sems = sems
        self.loads = [
            (half, place)
            for half in range(2)
            for place in range(lanes.blocks)
            if onward(place, half, lanes.bits)
        ]

    def source(self, place, half, chunk):
        start = self.lanes.block(place) * (2 * self.rows) + half * self.rows
        return self.part.at[pl.ds(pl.multiple_of(start, self.rows), self.rows), self.cols[chunk]]

    def bit_of(self, place, half):
        bits = [bit for bit in range(self.lanes.bits) if (place >> bit) & 1]
        return bits[-1] if half == 0 else bits[0]

    def load(self, half, place):
        index = self.loads.index((half, place))
        start = self.lanes.block(place) * (2 * self.rows) + half * self.rows
        view = self.part.at[pl.ds(pl.multiple_of(start, self.rows), self.rows), :]
        return pltpu.make_async_copy(view, self.load_s.at[index], self.load_sems.at[index])

    def copy(self, place, half, chunk):
        if (half, place) in self.loads:
            source = self.send_s.at[self.loads.index((half, place)), :, self.cols[chunk]]
        else:
            source = self.source(place, half, chunk)
        return remote(
            source,
            self.recv_s.at[half, place, :, self.cols[chunk]],
            self.send_sems.at[half, place, chunk],
            self.recv_sems.at[half, place, chunk],
            self.lanes.across(self.bit_of(place, half)),
        )

    def order(self, half):
        places = list(range(1, self.lanes.blocks))
        places.sort(key=lambda place: -len([b for b in range(8) if (place >> b) & 1]))
        return places

    def start(self):
        for half, place in self.loads:
            self.load(half, place).start()

    def direct(self, chunk):
        for half in range(2):
            for place in self.order(half):
                if (half, place) not in self.loads:
                    self.copy(place, half, chunk).start()

    def add(self, place, half, chunk):
        cols = self.cols[chunk]
        index = self.loads.index((half, place))
        total = self.load_s[index, :, cols].astype(jnp.float32)
        for bit in onward(place, half, self.lanes.bits):
            came = place | (1 << bit)
            self.copy(came, half, chunk).wait_recv()
            total = total + self.recv_s[half, came, :, cols].astype(jnp.float32)
        return total

    def middle(self, chunk):
        for half in range(2):
            for place in self.order(half):
                if (half, place) in self.loads:
                    index = self.loads.index((half, place))
                    if chunk == 0:
                        self.load(half, place).wait()
                    total = self.add(place, half, chunk)
                    self.send_s[index, :, self.cols[chunk]] = total.astype(jnp.bfloat16)
                    self.copy(place, half, chunk).start()

    def last(self, chunk):
        for half in range(2):
            if chunk == 0:
                self.load(half, 0).wait()
            self.total_s[half, :, self.cols[chunk]] = self.add(0, half, chunk)

    def finish(self):
        for chunk in range(len(self.cols)):
            for half in range(2):
                for place in range(1, self.lanes.blocks):
                    self.copy(place, half, chunk).wait_send()


def back_body(
    blocks, in_cols, small_row, part_ref, bc_ref, kv_ref, own_ref, far_ref, core_ref, both_ref,
    resid_ref, x_ref, gain_ref, small_ref,
    gin_ref, gsh_ref, gx_ref, sum_ref,
    in_send, in_recv, in_load, in_total, settle_s, settle_r, sh_came, sh_part, sh_send, sh_recv,
    sh_load, sh_total, line_s, line_r, near_s, near_r, swap_s, swap_r,
    buf_both, buf_core, buf_far, pass_s, gx_s, gx_r, small_s, small_r,
    in_ssem, in_rsem, in_lsem, sh_ssem, sh_rsem, sh_lsem, set_ssem, set_rsem, misc_s, misc_r,
    pass_ssem, pass_rsem, small_ssem, small_rsem,
):
    f32, bf16 = jnp.float32, jnp.bfloat16
    lanes = Lanes(blocks)
    c, t = lanes.c, lanes.t
    rows = gin_ref.shape[0]
    here = own_ref.shape[0]
    wide = bc_ref.shape[1]
    few = gsh_ref.shape[0]
    chunks = len(in_cols)
    step = min(here, 32)
    lanes.greet()
    core_at = (lanes.other, t)
    near_at = (lanes.d, lanes.near)
    far_at = (lanes.d, lanes.far)
    cross_at = (lanes.other, lanes.far)
    first = c == 0
    second = c == 1

    collect = Collect(
        lanes, part_ref, rows, in_cols, in_send, in_recv, in_load, in_total,
        (in_ssem, in_rsem, in_lsem),
    )
    shared = Collect(
        lanes, sh_part, rows, [slice(0, wide)], sh_send, sh_recv, sh_load, sh_total,
        (sh_ssem, sh_rsem, sh_lsem),
    )
    half_kv = kv_ref.shape[1] // 2

    def send_both():
        return remote(both_ref, buf_both, misc_s.at[0], misc_r.at[0], core_at)

    def send_core():
        return remote(core_ref, buf_core, misc_s.at[1], misc_r.at[1], core_at)

    def send_kv():
        return remote(
            kv_ref, sh_came.at[:, : 2 * half_kv], misc_s.at[2], misc_r.at[2], core_at
        )

    def send_bc():
        return remote(bc_ref, sh_came, misc_s.at[3], misc_r.at[3], core_at)

    send_both().start()
    collect.start()
    for chunk in range(chunks):
        collect.direct(chunk)
    send_core().start()

    @pl.when(first)
    def _():
        send_kv().start()

    @pl.when(second)
    def _():
        send_bc().start()

    parts = 2 if here >= 64 else 1
    share = here // parts

    def send_pass(part):
        view = pl.ds(part * share, share)
        return remote(
            pass_s.at[view, :], buf_far.at[view, :], pass_ssem.at[part], pass_rsem.at[part], near_at
        )

    send_both().wait_recv()
    for part in range(parts):

        @pl.loop(0, share // step)
        def _(i, part=part):
            view = pl.ds(pl.multiple_of(part * share + i * step, step), step)
            pass_s[view, :] = (far_ref[view, :] + buf_both[view, :].astype(f32)).astype(bf16)

        send_pass(part).start()

    @pl.when(first)
    def _():
        send_bc().wait_recv()

        @pl.loop(0, bc_ref.shape[0] // 64)
        def _(i):
            view = pl.ds(pl.multiple_of(i * 64, 64), 64)
            total = bc_ref[view, :].astype(f32) + sh_came[view, :].astype(f32)
            sh_part[view, :] = total.astype(bf16)

    @pl.when(second)
    def _():
        send_kv().wait_recv()

        @pl.loop(0, bc_ref.shape[0] // 64)
        def _(i):
            view = pl.ds(pl.multiple_of(i * 64, 64), 64)
            for piece in range(2):
                kept = pl.ds(piece * half_kv, half_kv)
                sh_part[view, pl.ds(2 * piece * half_kv, half_kv)] = sh_came[view, kept]
                sh_part[view, pl.ds((2 * piece + 1) * half_kv, half_kv)] = kv_ref[view, kept]

    shared.start()
    for chunk in range(chunks):
        collect.middle(chunk)
    shared.direct(0)

    def send_x():
        return remote(gx_s, gx_r, misc_s.at[4], misc_r.at[4], cross_at)

    send_core().wait_recv()
    for part in range(parts):
        send_pass(part).wait_recv()
    small_s[0] = small_ref[...]
    features = gain_ref.shape[1]

    def one_part(i, gains):
        view = pl.ds(pl.multiple_of(i * step, step), step)
        grad = own_ref[view, :] + buf_core[view, :].astype(f32) + buf_far[view, :].astype(f32)
        x = x_ref[view, :].astype(f32)
        scale = lax.rsqrt(jnp.mean(x * x, axis=1, keepdims=True) + EPS)
        gains = gains + jnp.sum(grad * (x * scale), axis=0, keepdims=True)
        grad = grad * gain_ref[...]
        mean = jnp.mean(grad * x, axis=1, keepdims=True)
        result = resid_ref[view, :] + scale * grad - x * (scale * scale * scale * mean)
        gx_ref[view, :] = result
        gx_s[view, :] = result.astype(bf16)
        return gains

    gains = lax.fori_loop(0, here // step, one_part, jnp.zeros((1, features), f32))
    for i in range(features // WIDE):
        small_s[0, small_row + i : small_row + i + 1, :] = gains[:, i * WIDE : (i + 1) * WIDE]

    @pl.when(lanes.away)
    def _():
        send_x().start()

    stops = [near_at, core_at, far_at] + [lanes.across(bit) for bit in range(lanes.bits)]

    def send_small(index):
        return remote(
            small_s.at[index], small_r.at[index], small_ssem.at[index], small_rsem.at[index],
            stops[index],
        )

    def step_small(index):
        send_small(index).wait_recv()
        small_s[index + 1] = small_s[index] + small_r[index]
        if index + 1 < len(stops):
            send_small(index + 1).start()

    send_small(0).start()

    def send_first(chunk, device):
        cols = in_cols[chunk]
        return remote(
            settle_s.at[0, :, cols], settle_r.at[0, :, cols],
            set_ssem.at[0, chunk], set_rsem.at[0, chunk], device,
        )

    def send_second(chunk):
        cols = in_cols[chunk]
        return remote(
            settle_s.at[1, :, cols], settle_r.at[1, :, cols],
            set_ssem.at[1, chunk], set_rsem.at[1, chunk], cross_at,
        )

    for chunk in range(chunks):
        collect.last(chunk)
        cols = in_cols[chunk]

        @pl.when(lanes.home)
        def _(chunk=chunk, cols=cols):
            settle_s[0, :, cols] = in_total[1 - c, :, cols].astype(bf16)
            send_first(chunk, core_at).start()

        @pl.when(lanes.away)
        def _(chunk=chunk, cols=cols):
            settle_s[0, :, cols] = in_total[c, :, cols].astype(bf16)
            send_first(chunk, far_at).start()
            settle_s[1, :, cols] = in_total[1 - c, :, cols].astype(bf16)
            send_second(chunk).start()

        if chunk == 0:
            step_small(0)
            shared.middle(0)
    step_small(1)
    shared.last(0)

    t_high, t_low = lax.div(t, 2), lax.rem(t, 2)
    line = 2 * few

    def send_line():
        return remote(line_s, line_r, misc_s.at[5], misc_r.at[5], far_at)

    def send_near():
        return remote(near_s, near_r, misc_s.at[6], misc_r.at[6], near_at)

    def send_swap():
        return remote(swap_s, swap_r, misc_s.at[7], misc_r.at[7], core_at)

    theirs = pl.ds(pl.multiple_of((1 - t_high) * line, line), line)
    mine = pl.ds(pl.multiple_of(t_high * line, line), line)
    for half in range(2):
        line_s[half] = sh_total[half, theirs, :].astype(bf16)
    send_line().start()
    step_small(2)
    send_line().wait_recv()
    for half in range(2):
        sh_total[half, mine, :] = sh_total[half, mine, :] + line_r[half].astype(f32)
    theirs = pl.ds(pl.multiple_of(t_high * line + (1 - t_low) * few, few), few)
    mine = pl.ds(pl.multiple_of(t_high * line + t_low * few, few), few)
    for half in range(2):
        near_s[half] = sh_total[half, theirs, :].astype(bf16)
    send_near().start()
    for index in range(3, len(stops)):
        step_small(index)
    send_near().wait_recv()
    for half in range(2):
        sh_total[half, mine, :] = sh_total[half, mine, :] + near_r[half].astype(f32)
    swap_s[...] = sh_total[1 - c, mine, :].astype(bf16)
    send_swap().start()
    sum_ref[...] = small_s[len(stops)]

    for chunk in range(chunks):
        cols = in_cols[chunk]
        send_first(chunk, core_at).wait_recv()

        @pl.when(lanes.home)
        def _(chunk=chunk, cols=cols):
            gin_ref[:, cols] = in_total[c, :, cols] + settle_r[0, :, cols].astype(f32)

        @pl.when(lanes.away)
        def _(chunk=chunk, cols=cols):
            send_second(chunk).wait_recv()
            gin_ref[:, cols] = settle_r[0, :, cols].astype(f32) + settle_r[1, :, cols].astype(f32)

    send_swap().wait_recv()

    @pl.when(first)
    def _():
        gsh_ref[:, :wide] = sh_total[0, mine, :]
        gsh_ref[:, wide:] = swap_r[...].astype(f32)

    @pl.when(second)
    def _():
        gsh_ref[:, :wide] = swap_r[...].astype(f32)
        gsh_ref[:, wide:] = sh_total[1, mine, :]

    @pl.when(lanes.away)
    def _():
        send_x().wait_recv()

        @pl.loop(0, here // step)
        def _(i):
            view = pl.ds(pl.multiple_of(i * step, step), step)
            gx_ref[view, :] = gx_r[view, :].astype(f32)

    collect.finish()
    shared.finish()
    send_both().wait_send()
    send_core().wait_send()

    @pl.when(first)
    def _():
        send_kv().wait_send()

    @pl.when(second)
    def _():
        send_bc().wait_send()

    for part in range(parts):
        send_pass(part).wait_send()
    for chunk in range(chunks):
        send_first(chunk, core_at).wait_send()

    @pl.when(lanes.away)
    def _():
        send_x().wait_send()
        for chunk in range(chunks):
            send_second(chunk).wait_send()

    for index in range(len(stops)):
        send_small(index).wait_send()
    send_line().wait_send()
    send_near().wait_send()
    send_swap().wait_send()


def back(part_in, bc, kv, act_parts, grad_resid, x, gain, small, small_row, few, at):
    f32, bf16 = jnp.float32, jnp.bfloat16
    own, core, far, both = act_parts
    blocks = at.blocks
    features, width = part_in.shape
    rows = features // (2 * blocks)
    here = own.shape[0]
    wide = bc.shape[1]
    chunks = 3
    piece = width // chunks
    in_cols = [slice(i * piece, (i + 1) * piece) for i in range(chunks)]
    loads = sum(bool(onward(p, h, at.bits)) for h in range(2) for p in range(blocks))
    steps = 3 + at.bits
    parts = 2 if here >= 64 else 1
    dma = pltpu.SemaphoreType.DMA
    vmem = pl.BlockSpec(memory_space=pltpu.VMEM)
    anywhere = pl.BlockSpec(memory_space=pl.ANY)
    line = 2 * few
    return pl.pallas_call(
        functools.partial(back_body, blocks, in_cols, small_row),
        in_specs=[anywhere, vmem, vmem, vmem, vmem, anywhere, anywhere, vmem, vmem, vmem, vmem],
        out_specs=[vmem] * 4,
        out_shape=[
            jax.ShapeDtypeStruct((rows, width), f32),
            jax.ShapeDtypeStruct((few, 2 * wide), f32),
            jax.ShapeDtypeStruct((here, features), f32),
            jax.ShapeDtypeStruct(small.shape, f32),
        ],
        scratch_shapes=[
            pltpu.VMEM((loads, rows, width), bf16),
            pltpu.VMEM((2, blocks, rows, width), bf16),
            pltpu.VMEM((loads, rows, width), bf16),
            pltpu.VMEM((2, rows, width), f32),
            pltpu.VMEM((2, rows, width), bf16),
            pltpu.VMEM((2, rows, width), bf16),
            pltpu.VMEM((features, wide), bf16),
            pltpu.VMEM((features, wide), bf16),
            pltpu.VMEM((loads, rows, wide), bf16),
            pltpu.VMEM((2, blocks, rows, wide), bf16),
            pltpu.VMEM((loads, rows, wide), bf16),
            pltpu.VMEM((2, rows, wide), f32),
            pltpu.VMEM((2, line, wide), bf16),
            pltpu.VMEM((2, line, wide), bf16),
            pltpu.VMEM((2, few, wide), bf16),
            pltpu.VMEM((2, few, wide), bf16),
            pltpu.VMEM((few, wide), bf16),
            pltpu.VMEM((few, wide), bf16),
            pltpu.VMEM((here, features), bf16),
            pltpu.VMEM((here, features), bf16),
            pltpu.VMEM((here, features), bf16),
            pltpu.VMEM((here, features), bf16),
            pltpu.VMEM((here, features), bf16),
            pltpu.VMEM((here, features), bf16),
            pltpu.VMEM((steps + 1,) + small.shape, f32),
            pltpu.VMEM((steps,) + small.shape, f32),
            dma((2, blocks, chunks)),
            dma((2, blocks, chunks)),
            dma((loads,)),
            dma((2, blocks, 1)),
            dma((2, blocks, 1)),
            dma((loads,)),
            dma((2, chunks)),
            dma((2, chunks)),
            dma((8,)),
            dma((8,)),
            dma((parts,)),
            dma((parts,)),
            dma((steps,)),
            dma((steps,)),
        ],
        compiler_params=pltpu.CompilerParams(
            collective_id=2, has_side_effects=True, vmem_limit_bytes=58 * 1024 * 1024
        ),
        cost_estimate=pl.CostEstimate(
            flops=here * features * 20, bytes_accessed=300_000_000, transcendentals=0
        ),
    )(
        part_in, bc, kv, own, far, core, both, grad_resid, x, gain.reshape(1, -1), small,
    )


def after(values, *others):
    return lax.optimization_barrier((values,) + others)[0]


def share_rows(values, at):
    far = at.over_z(values)
    core = at.over_core(values)
    both = at.over_core(far)
    return (values, core, far, both)


def sum_rows(pieces, at):
    own, core, far, both = pieces
    bf16 = jnp.bfloat16
    from_both = at.over_core(both.astype(bf16))
    passed = (far + from_both.astype(jnp.float32)).astype(bf16)
    from_far = at.over_z(passed)
    from_core = at.over_core(core.astype(bf16))
    return own + from_core.astype(jnp.float32) + from_far.astype(jnp.float32)


def groups(at):
    return [[d for d in range(at.dp) if d % 2 == c] for c in range(2)]


def gather_blocks(block, at):
    return lax.all_gather(block, "dp", axis=0, tiled=True, axis_index_groups=groups(at))


def sum_blocks(values, at):
    return lax.psum_scatter(
        values, "dp", scatter_dimension=0, tiled=True, axis_index_groups=groups(at)
    )


def pair_up(own, other, at):
    first = at.c == 0
    return jnp.concatenate([jnp.where(first, own, other), jnp.where(first, other, own)], axis=0)


def pair_weight(shard, at):
    first_in = at.column_out(shard)
    second_in = at.swap_away(shard)
    own = jnp.where(at.home, shard, first_in)
    other = jnp.where(at.home, first_in, second_in)
    return pair_up(own, other, at)


def gather_weight(shard, at):
    return gather_blocks(pair_weight(shard, at), at)


def settle_weight(mine, at):
    f32 = jnp.float32
    rows = mine.shape[0] // 2
    low, high = mine[:rows], mine[rows:]
    own = jnp.where(at.c == 0, low, high)
    other = jnp.where(at.c == 0, high, low)
    first_in = at.column_back(jnp.where(at.home, other, own)).astype(f32)
    second_in = at.swap_away(other).astype(f32)
    return first_in + jnp.where(at.home, own.astype(f32), second_in)


def gather_shared(shard, at):
    rows, width = shard.shape
    half = width // 2
    mine = jnp.where(at.c == 0, shard[:, :half], shard[:, half:])
    theirs = jnp.where(at.c == 0, shard[:, half:], shard[:, :half])
    came = at.over_core(theirs)
    both = jnp.stack([jnp.where(at.c == 0, mine, came), jnp.where(at.c == 0, came, mine)])
    near = at.over_z(both)
    lowest = at.t % 2 == 0
    two = jnp.stack([jnp.where(lowest, both, near), jnp.where(lowest, near, both)], axis=1)
    far = at.over_far(two)
    lower = at.t // 2 == 0
    four = jnp.stack([jnp.where(lower, two, far), jnp.where(lower, far, two)], axis=1)
    part = gather_blocks(four.reshape(2 * rows * at.tp, half), at)
    other = at.over_core(part)
    return jnp.where(at.c == 0, part, other), jnp.where(at.c == 0, other, part)


def scatter_shared(grad_bc, grad_kv, earlier, at):
    f32, bf16 = jnp.float32, jnp.bfloat16
    first = at.c == 0
    bc_width = grad_bc.shape[1]
    going = jnp.where(
        first, jnp.pad(grad_kv, ((0, 0), (0, bc_width - grad_kv.shape[1]))), grad_bc
    )
    came = at.over_core(going.astype(bf16)).astype(f32)
    kept = jnp.concatenate(
        [came[:, :HD], grad_kv[:, :HD], came[:, HD : 2 * HD], grad_kv[:, HD:]], axis=1
    )
    total = jnp.where(first, grad_bc + came, kept)
    mine = sum_blocks(after(total.astype(bf16), earlier), at)
    piece = mine.shape[0] // (2 * at.tp)
    line = mine.astype(f32).reshape(2, 2, 2, piece, total.shape[1])
    lower = at.t // 2 == 0
    went = at.over_far(jnp.where(lower, line[:, 1], line[:, 0]).astype(bf16)).astype(f32)
    line = jnp.where(lower, line[:, 0], line[:, 1]) + went
    lowest = at.t % 2 == 0
    went = at.over_z(jnp.where(lowest, line[:, 1], line[:, 0]).astype(bf16)).astype(f32)
    line = jnp.where(lowest, line[:, 0], line[:, 1]) + went
    mine = jnp.where(first, line[0], line[1])
    came = at.over_core(jnp.where(first, line[1], line[0]).astype(bf16)).astype(f32)
    return jnp.concatenate([jnp.where(first, mine, came), jnp.where(first, came, mine)], axis=1)


def sum_tensor(values, at):
    for bit in range(at.tp.bit_length() - 1):
        values = values + at.send(values, lambda d, t: (d, t ^ (1 << bit)))
    return values


def sum_data(values, at):
    for bit in range(at.dp.bit_length() - 1):
        values = values + at.send(values, lambda d, t: (d ^ (1 << bit), t))
    return values


def per_device(
    layer_in,
    teacher,
    lengths,
    input_gain,
    mixer_in_weight,
    step_weight,
    query_weight,
    shared_weight,
    conv_inner,
    conv_shared,
    step_bias,
    decay_log,
    skip_gain,
    inner_gain,
    mixer_out_weight,
    attn_out_weight,
    middle_gain,
    gate_up_weight,
    down_weight,
):
    f32 = jnp.float32
    bf16 = jnp.bfloat16
    contract_last = (((1,), (1,)), ((), ()))
    contract_first = (((0,), (0,)), ((), ()))
    at = Places()
    rows_here = layer_in.shape[0]
    slot_len = rows_here * at.tp
    local_heads = step_bias.shape[0]
    width = inner_gain.shape[0]
    head_dim = width // local_heads
    query_width = query_weight.shape[1]
    hidden_width = down_weight.shape[1]
    bc_width = conv_shared.shape[1]
    w_rows = step_weight.shape[0]

    column_params = jnp.concatenate(
        [conv_inner.reshape(-1), inner_gain, step_bias, decay_log, skip_gain]
    )
    column_params = relocate(column_params, at)
    lane_params = jnp.concatenate(
        [
            column_params[: (KC + 1) * width].reshape(KC + 1, width),
            jnp.repeat(column_params[(KC + 1) * width + 2 * local_heads :], head_dim)[None],
            jnp.zeros((2, width), f32),
        ],
        axis=0,
    )
    head_rows = column_params[(KC + 1) * width :][: 2 * local_heads].reshape(2, local_heads)
    head_rows = jnp.concatenate([head_rows[:1], -jnp.exp(head_rows[1:])], axis=0)
    head_params = jnp.pad(head_rows, ((0, 6), (0, WIDE - local_heads)))
    seg = (
        lax.broadcasted_iota(jnp.int32, (width, WIDE), 0) // head_dim
        == lax.broadcasted_iota(jnp.int32, (width, WIDE), 1)
    ).astype(bf16)
    half = HD // 2
    freqs = jnp.exp(-jnp.log(ROPE_BASE) * 2.0 * jnp.arange(half, dtype=f32) / HD)
    angles = jnp.arange(slot_len).astype(f32)[:, None] * freqs[None, :]
    cosine, sine = jnp.cos(angles), jnp.sin(angles)
    cosine = jnp.concatenate([cosine, cosine], axis=1)
    sine = jnp.concatenate([-sine, sine], axis=1)
    quarters = jnp.arange(at.tp, dtype=jnp.int32)
    order = (at.c ^ (quarters // 2)) + 2 * (at.zq ^ (quarters % 2))

    in_pack = jnp.concatenate(
        [
            mixer_in_weight.reshape(w_rows, 2 * width),
            query_weight,
            step_weight,
            jnp.zeros((w_rows, WIDE - local_heads), bf16),
        ],
        axis=1,
    )
    out_pack = jnp.concatenate([mixer_out_weight, attn_out_weight], axis=1)
    in_all, out_pair, act_all, inputs, shared_full = front(
        in_pack, out_pack, shared_weight, layer_in, input_gain, at
    )
    left, right = shared_full[:, :bc_width], shared_full[:, bc_width:]
    kv_index = at.column * (query_width // HD) // (QH // KVH)
    second = kv_index == 1
    shared_all = jnp.concatenate(
        [
            left,
            jnp.where(second, right[:, HD : 2 * HD], right[:, :HD]),
            jnp.where(second, right[:, 3 * HD :], right[:, 2 * HD : 3 * HD]),
        ],
        axis=1,
    )
    x_low = inputs
    inputs = inputs.astype(f32)

    def row_split(values):
        return [values[i * rows_here : (i + 1) * rows_here] for i in range(at.tp)]

    out_all = gather_blocks(out_pair, at)
    rest = jnp.concatenate(
        [gate_up_weight.reshape(w_rows, 2 * hidden_width), down_weight], axis=1
    )
    rest = pair_weight(after(rest, act_all), at)
    gate_up_all = gather_blocks(rest[:, : 2 * hidden_width], at)
    down_all = gather_blocks(rest[:, 2 * hidden_width :], at)
    proj_shared = jnp.dot(act_all, shared_all, preferred_element_type=f32)
    proj = jnp.dot(act_all, in_all, preferred_element_type=f32)
    target = relocate(after(teacher, proj), at).astype(f32)
    attn_low = attn_forward(order, proj, proj_shared, cosine, sine, query_width, width, bc_width)
    heads_all, y, states = mixer_forward(
        order, proj, proj_shared, attn_low, lane_params, conv_shared, head_params
    )
    mix_parts = [
        lax.dot_general(piece, out_all, contract_last, preferred_element_type=f32)
        for piece in row_split(heads_all)
    ]
    resid = inputs + sum_rows(mix_parts, at)
    normed_mid, norm_mid_back = jax.vjp(rms_norm, resid, middle_gain)
    mid_all = jnp.concatenate(share_rows(normed_mid.astype(bf16), at), axis=0)
    gate_up = jnp.dot(mid_all, gate_up_all, preferred_element_type=f32)
    gate_val = gate_up[:, :hidden_width]
    up_val = gate_up[:, hidden_width:]
    sigmoid_gate = jax.nn.sigmoid(gate_val)
    hidden = (gate_val * sigmoid_gate * up_val).astype(bf16)
    mlp_parts = [
        lax.dot_general(piece, down_all, contract_last, preferred_element_type=f32)
        for piece in row_split(hidden)
    ]
    outputs = resid + sum_rows(mlp_parts, at)
    seq_len = lax.dynamic_index_in_dim(lengths, at.slot, keepdims=False)
    positions = at.quarter * rows_here + jnp.arange(rows_here)
    live = (positions < seq_len).astype(f32)
    error = (outputs - target) * live[:, None]
    err_local = 0.5 * jnp.sum(error * error)

    grad_all = jnp.concatenate(share_rows(error.astype(bf16), at), axis=0)
    def weight_grad(left, right):
        return lax.dot_general(left, right, contract_first, preferred_element_type=f32).astype(bf16)

    part_down = weight_grad(grad_all, hidden)
    grad_hidden = jnp.dot(grad_all, down_all, preferred_element_type=f32)
    grad_gate = grad_hidden * up_val * sigmoid_gate * (1.0 + gate_val * (1.0 - sigmoid_gate))
    grad_up = grad_hidden * gate_val * sigmoid_gate
    grad_gu = jnp.concatenate([grad_gate.astype(bf16), grad_up.astype(bf16)], axis=1)
    grad_mid_parts = [
        lax.dot_general(piece, gate_up_all, contract_last, preferred_element_type=f32)
        for piece in row_split(grad_gu)
    ]
    part_gate_up = weight_grad(mid_all, grad_gu)
    grad_mid = sum_rows(grad_mid_parts, at)
    grad_mid, part_down, part_gate_up = lax.optimization_barrier((grad_mid, part_down, part_gate_up))
    raw_down = sum_blocks(part_down, at)
    raw_gate_up = sum_blocks(part_gate_up, at)
    grad_resid_norm, grad_middle_gain = norm_mid_back(grad_mid)
    grad_resid = error + grad_resid_norm
    mix_grad_all = jnp.concatenate(share_rows(grad_resid.astype(bf16), at), axis=0)
    grad_heads = jnp.dot(mix_grad_all, out_all, preferred_element_type=f32)
    part_out = weight_grad(mix_grad_all, heads_all)
    grad_heads, part_out = lax.optimization_barrier((grad_heads, part_out))
    layer_out = relocate(after(outputs.astype(bf16), grad_heads), at)
    raw_out = sum_blocks(after(part_out, raw_gate_up), at)
    dq, dkv = attn_backward(
        order, proj, proj_shared, cosine, sine, grad_heads, query_width, width, bc_width
    )
    low_pack, low_shared, dlane, dconv, dhead = mixer_backward(
        order, proj, proj_shared, y, states, grad_heads, dq, dkv, lane_params, conv_shared,
        head_params, seg, query_width,
    )
    column = at.column
    lanes_full = lax.dynamic_update_slice(
        jnp.zeros((KC + 1, DI), f32), dlane[: KC + 1], (0, column * width)
    )
    head_stack = jnp.concatenate(
        [dhead[:2, :local_heads], dlane[KC + 1].reshape(1, local_heads, head_dim).sum(2)], axis=0
    )
    heads_full = lax.dynamic_update_slice(
        jnp.zeros((3, H), f32), head_stack, (0, column * local_heads)
    )
    small = (
        jnp.zeros_like(input_gain),
        grad_middle_gain,
        lanes_full,
        dconv[:KC],
        heads_full,
        err_local,
    )
    flat = jnp.concatenate([part.reshape(-1) for part in small])
    padded = -(-flat.shape[0] // 1024) * 1024
    flat = jnp.pad(flat, (0, padded - flat.shape[0])).reshape(-1, WIDE)

    grad_act_parts = [
        lax.dot_general(a, in_all, contract_last, preferred_element_type=f32)
        + lax.dot_general(b, shared_all, contract_last, preferred_element_type=f32)
        for a, b in zip(row_split(low_pack), row_split(low_shared))
    ]
    grad_act_parts[1] = grad_act_parts[1].astype(bf16)
    grad_act_parts[3] = grad_act_parts[3].astype(bf16)
    part_bc = weight_grad(act_all, low_shared[:, :bc_width])
    part_kv = weight_grad(act_all, low_shared[:, bc_width:])
    part_in = weight_grad(act_all, low_pack)
    grad_rest = settle_weight(jnp.concatenate([raw_out, raw_gate_up, raw_down], axis=1), at)
    grad_in, grad_shared_weight, input_grad, flat = back(
        part_in, part_bc, part_kv, grad_act_parts, grad_resid, x_low, input_gain, flat, 0,
        shared_weight.shape[0], at,
    )
    out_width = width + query_width
    gate_up_to = out_width + 2 * hidden_width
    flat = flat.reshape(-1)
    sums = []
    start = 0
    for part in small:
        sums.append(flat[start : start + part.size].reshape(part.shape))
        start += part.size
    sum_input_gain, sum_middle_gain, sum_lanes, sum_convs, sum_heads, err_total = sums
    lanes_local = lax.dynamic_slice_in_dim(sum_lanes, at.t * width, width, 1)
    heads_local = lax.dynamic_slice_in_dim(sum_heads, at.t * local_heads, local_heads, 1)
    loss = err_total / jnp.sum(lengths).astype(f32)
    query_from = 2 * width
    step_from = query_from + query_width
    return (
        layer_out,
        loss,
        input_grad,
        sum_input_gain,
        grad_in[:, :query_from].reshape(w_rows, 2, width),
        grad_in[:, step_from : step_from + local_heads],
        grad_in[:, query_from:step_from],
        grad_shared_weight,
        lanes_local[:KC],
        sum_convs,
        heads_local[0],
        heads_local[1],
        heads_local[2],
        lanes_local[KC],
        grad_rest[:, :width],
        grad_rest[:, width:out_width],
        sum_middle_gain,
        grad_rest[:, out_width:gate_up_to].reshape(w_rows, 2, hidden_width),
        grad_rest[:, gate_up_to:],
    )


def solution(mesh):
    placed = (
        P(("dp", "tensor"), None),
        P(("dp", "tensor"), None),
        P(),
        P(),
        P("dp", None, "tensor"),
        P("dp", "tensor"),
        P("dp", "tensor"),
        P(("dp", "tensor"), None),
        P(None, "tensor"),
        P(),
        P("tensor"),
        P("tensor"),
        P("tensor"),
        P("tensor"),
        P("dp", "tensor"),
        P("dp", "tensor"),
        P(),
        P("dp", None, "tensor"),
        P("dp", "tensor"),
    )
    return jax.shard_map(
        per_device,
        mesh=mesh,
        in_specs=placed,
        out_specs=(
            P(("dp", "tensor"), None),
            P(),
            P(("dp", "tensor"), None),
            P(),
            P("dp", None, "tensor"),
            P("dp", "tensor"),
            P("dp", "tensor"),
            P(("dp", "tensor"), None),
            P(None, "tensor"),
            P(),
            P("tensor"),
            P("tensor"),
            P("tensor"),
            P("tensor"),
            P("dp", "tensor"),
            P("dp", "tensor"),
            P(),
            P("dp", None, "tensor"),
            P("dp", "tensor"),
        ),
        check_vma=False,
    )
```

```python
import functools

import jax
import jax.numpy as jnp
from jax import lax
from jax.experimental import pallas as pl
from jax.experimental.pallas import tpu as pltpu
from jax.sharding import PartitionSpec as P

H = 48
KC = 4
QH = 8
KVH = 2
HD = 128
DI = 3072

EPS = 1e-05
ROPE_BASE = 100000000000.0


def rms_norm(values, gain):
    return values * lax.rsqrt(jnp.mean(values * values, axis=-1, keepdims=True) + EPS) * gain


def low_dot(left, right, dims):
    return lax.dot_general(left, right, (dims, ((), ())), preferred_element_type=jnp.float32)


NN = ((1,), (0,))
NT = ((1,), (1,))
TN = ((0,), (0,))
CHUNK = 128
ROWS = 256
WIDE = 128
FAR = -1e30


def exact_dot(ones, values, parts=3):
    total = None
    for _ in range(parts):
        part = values.astype(jnp.bfloat16)
        values = values - part.astype(jnp.float32)
        term = low_dot(ones, part, NN)
        total = term if total is None else total + term
    return total


def split_dot(values, ones, parts=2):
    total = None
    for _ in range(parts):
        part = values.astype(jnp.bfloat16)
        values = values - part.astype(jnp.float32)
        term = low_dot(part, ones, NN)
        total = term if total is None else total + term
    return total


def sigmoid(v):
    return 1.0 / (1.0 + jnp.exp(-v))


def softplus(v):
    return jnp.maximum(v, 0.0) + jnp.log1p(jnp.exp(-jnp.abs(v)))


def iota(shape, axis):
    return lax.broadcasted_iota(jnp.int32, shape, axis)


def spin(values, cosine, sine):
    return values * cosine + pltpu.roll(values, HD // 2, 1) * sine


def unspin(values, cosine, sine):
    return values * cosine - pltpu.roll(values, HD // 2, 1) * sine


def attn_probs(query_low, key_low, first_row, scale):
    scores = low_dot(query_low, key_low, NT) * scale
    rows, keys = scores.shape
    allowed = iota((rows, keys), 1) <= iota((rows, keys), 0) + first_row
    scores = jnp.where(allowed, scores, FAR)
    top = jnp.max(scores, axis=1, keepdims=True)
    weights = jnp.exp(scores - top)
    return weights / jnp.sum(weights, axis=1, keepdims=True)


def attn_fwd_body(order, q_ref, kv_ref, cos_ref, sin_ref, out_ref, key_s, value_s):
    bf16 = jnp.bfloat16
    step = pl.program_id(0)
    cosine, sine = cos_ref[...], sin_ref[...]
    rows = pl.ds(pl.multiple_of(step * ROWS, ROWS), ROWS)
    key_s[rows, :] = spin(kv_ref[:, :HD], cosine, sine).astype(bf16)
    value_s[rows, :] = kv_ref[:, HD:].astype(bf16)
    heads = q_ref.shape[1] // HD
    blocks = key_s.shape[0] // ROWS
    for block in range(blocks):

        @pl.when(step == block)
        def _(block=block):
            keys = (block + 1) * ROWS
            for head in range(heads):
                lanes = slice(head * HD, (head + 1) * HD)
                query = spin(q_ref[:, lanes], cosine, sine).astype(bf16)
                probs = attn_probs(query, key_s[:keys, :], block * ROWS, HD**-0.5)
                out_ref[:, lanes] = low_dot(
                    probs.astype(bf16), value_s[:keys, :], NN
                ).astype(bf16)


def attn_bwd_body(
    order, q_ref, kv_ref, cos_ref, sin_ref, grad_ref, all_cos, all_sin, dq_ref, dkv_ref,
    key_s, value_s, dkey_s, dvalue_s,
):
    bf16, f32 = jnp.bfloat16, jnp.float32
    step = pl.program_id(0)

    @pl.when(step == 0)
    def _():
        dkey_s[...] = jnp.zeros_like(dkey_s)
        dvalue_s[...] = jnp.zeros_like(dvalue_s)

    cosine, sine = cos_ref[...], sin_ref[...]
    rows = pl.ds(pl.multiple_of(step * ROWS, ROWS), ROWS)
    key_s[rows, :] = spin(kv_ref[:, :HD], cosine, sine).astype(bf16)
    value_s[rows, :] = kv_ref[:, HD:].astype(bf16)
    heads = q_ref.shape[1] // HD
    blocks = key_s.shape[0] // ROWS
    scale = HD**-0.5
    for block in range(blocks):

        @pl.when(step == block)
        def _(block=block):
            keys = (block + 1) * ROWS
            for head in range(heads):
                lanes = slice(head * HD, (head + 1) * HD)
                query = spin(q_ref[:, lanes], cosine, sine).astype(bf16)
                probs = attn_probs(query, key_s[:keys, :], block * ROWS, scale)
                grad = grad_ref[:, lanes].astype(bf16)
                dprobs = low_dot(grad, value_s[:keys, :], NT)
                dvalue_s[:keys, :] += low_dot(probs.astype(bf16), grad, TN)
                inner = jnp.sum(dprobs * probs, axis=1, keepdims=True)
                dscores = (probs * (dprobs - inner) * scale).astype(bf16)
                dquery = low_dot(dscores, key_s[:keys, :], NN)
                dkey_s[:keys, :] += low_dot(dscores, query, TN)
                dq_ref[:, lanes] = unspin(dquery, cosine, sine).astype(bf16)

    @pl.when(step == blocks - 1)
    def _():
        dkv_ref[:, :HD] = unspin(dkey_s[...], all_cos[...], all_sin[...]).astype(bf16)
        dkv_ref[:, HD:] = dvalue_s[...].astype(bf16)


def conv_taps(ext, taps, first, width):
    rows = ext.shape[0] - 8
    total = None
    for tap in range(width):
        at = 8 - (width - 1) + tap
        term = ext[at : at + rows, :] * taps[first + tap : first + tap + 1, :]
        total = term if total is None else total + term
    return total


def decays(steps, head_params, tri):
    shifted = steps + head_params[0:1, :]
    dt = softplus(shifted)
    la = dt * head_params[1:2, :]
    cum = exact_dot(tri, la)
    return shifted, dt, la, cum


def spread_lanes(values, pair, first):
    rows = values.shape[0]
    a = jnp.broadcast_to(values[:, 2 * pair : 2 * pair + 1], (rows, WIDE))
    b = jnp.broadcast_to(values[:, 2 * pair + 1 : 2 * pair + 2], (rows, WIDE))
    return a, b, jnp.where(first, a, b)


def mixer_fwd_body(
    order, gate_ref, inner_ref, step_ref, bc_ref, attn_ref, lane_ref, conv_ref, head_ref,
    out_ref, y_ref, state_ref, ext_s, extbc_s, state_s, x_s,
):
    bf16, f32 = jnp.bfloat16, jnp.float32
    step = pl.program_id(0)
    width = inner_ref.shape[1]
    states = bc_ref.shape[1] // 2

    @pl.when(step == 0)
    def _():
        ext_s[0:8, :] = jnp.zeros((8, width), f32)
        extbc_s[0:8, :] = jnp.zeros((8, 2 * states), f32)
        state_s[...] = jnp.zeros_like(state_s)

    ext_s[8:, :] = inner_ref[...]
    extbc_s[8:, :] = bc_ref[...]
    pre = conv_taps(ext_s, lane_ref, 0, KC)
    x_s[...] = pre * sigmoid(pre)
    pre = conv_taps(extbc_s, conv_ref, 0, KC)
    bc = (pre * sigmoid(pre)).astype(bf16)
    ext_s[0:8, :] = ext_s[ROWS : ROWS + 8, :]
    extbc_s[0:8, :] = extbc_s[ROWS : ROWS + 8, :]
    row, col = iota((CHUNK, CHUNK), 0), iota((CHUNK, CHUNK), 1)
    causal = row >= col
    tri = jnp.where(causal, 1.0, 0.0).astype(bf16)
    first = iota((CHUNK, WIDE), 1) < WIDE // 2
    for sub in range(ROWS // CHUNK):
        lo = sub * CHUNK
        b_low = bc[lo : lo + CHUNK, :states]
        c_low = bc[lo : lo + CHUNK, states:]
        _, dt, _, cum = decays(step_ref[lo : lo + CHUNK, :], head_ref, tri)
        cum_t = cum.T
        cross = low_dot(c_low, b_low, NT)
        state_low = state_s[...].astype(bf16)
        state_ref[sub] = state_low
        b_t = b_low.T
        for pair in range(width // WIDE):
            lanes = slice(pair * WIDE, (pair + 1) * WIDE)
            cum_a, cum_b, cum_p = spread_lanes(cum, pair, first)
            _, _, dt_p = spread_lanes(dt, pair, first)
            weights = []
            for wide, head in ((cum_a, 2 * pair), (cum_b, 2 * pair + 1)):
                gap = jnp.where(causal, wide - cum_t[head : head + 1, :], FAR)
                weights.append((cross * jnp.exp(gap)).astype(bf16))
            x = x_s[lo : lo + CHUNK, lanes]
            scaled = x * dt_p
            zero = jnp.zeros_like(scaled)
            stacked = jnp.concatenate(
                [jnp.where(first, scaled, zero), jnp.where(first, zero, scaled)], axis=0
            ).astype(bf16)
            y = low_dot(jnp.concatenate(weights, axis=1), stacked, NN)
            y = y + jnp.exp(cum_p) * low_dot(c_low, state_low[:, lanes], NN)
            y_ref[lo : lo + CHUNK, lanes] = y + lane_ref[5:6, lanes] * x
            last = cum_p[CHUNK - 1 : CHUNK, :]
            ends = (scaled * jnp.exp(last - cum_p)).astype(bf16)
            state_s[:, lanes] = state_s[:, lanes] * jnp.exp(last) + low_dot(b_t, ends, NN)
    gate = gate_ref[...]
    gated = y_ref[...] * (gate * sigmoid(gate))
    scale = lax.rsqrt(jnp.mean(gated * gated, axis=1, keepdims=True) + EPS)
    out_ref[:, :width] = (gated * scale * lane_ref[4:5, :]).astype(bf16)
    out_ref[:, width:] = attn_ref[...]


def mixer_bwd_body(
    order, gate_ref, inner_ref, before_ref, step_ref, bc_ref, bcbefore_ref, y_ref, state_ref,
    grad_ref, dq_ref, dkv_ref, lane_ref, conv_ref, head_ref, seg_ref,
    low_ref, lowsh_ref, dlane_ref, dconv_ref, dhead_ref,
    ext_s, extbc_s, pre_s, prebc_s, x_s, bc_s, g_s, dx_s, dbc_s, dpre_s, dprebc_s, dstate_s,
    z_s, rows_s,
):
    bf16, f32 = jnp.bfloat16, jnp.float32
    step = pl.program_id(0)
    blocks = pl.num_programs(0)
    width = inner_ref.shape[1]
    states = bc_ref.shape[1] // 2
    query_width = dq_ref.shape[1]

    @pl.when(step == 0)
    def _():
        dlane_ref[...] = jnp.zeros_like(dlane_ref)
        dconv_ref[...] = jnp.zeros_like(dconv_ref)
        dhead_ref[...] = jnp.zeros_like(dhead_ref)
        dstate_s[...] = jnp.zeros_like(dstate_s)
        dpre_s[ROWS:, :] = jnp.zeros((8, width), f32)
        dprebc_s[ROWS:, :] = jnp.zeros((8, 2 * states), f32)
        z_s[...] = jnp.zeros_like(z_s)
        rows_s[...] = jnp.zeros_like(rows_s)

    keep = jnp.where(step == blocks - 1, 0.0, 1.0)
    ext_s[0:8, :] = before_ref[...] * keep
    extbc_s[0:8, :] = bcbefore_ref[...] * keep
    ext_s[8:, :] = inner_ref[...]
    extbc_s[8:, :] = bc_ref[...]
    pre = conv_taps(ext_s, lane_ref, 0, KC)
    pre_s[...] = pre
    x_s[...] = pre * sigmoid(pre)
    pre = conv_taps(extbc_s, conv_ref, 0, KC)
    prebc_s[...] = pre
    bc_s[...] = (pre * sigmoid(pre)).astype(bf16)

    gate = gate_ref[...]
    sig = sigmoid(gate)
    gate_act = gate * sig
    y = y_ref[...]
    gated = y * gate_act
    scale = lax.rsqrt(jnp.mean(gated * gated, axis=1, keepdims=True) + EPS)
    grad = grad_ref[...]
    dlane_ref[4:5, :] += jnp.sum(grad * gated * scale, axis=0, keepdims=True)
    grad = grad * lane_ref[4:5, :]
    mean = jnp.mean(grad * gated, axis=1, keepdims=True)
    dgated = scale * grad - gated * (scale * scale * scale * mean)
    g_s[...] = dgated * gate_act
    low_ref[:, :width] = (dgated * y * sig * (1.0 + gate * (1.0 - sig))).astype(bf16)

    row, col = iota((CHUNK, CHUNK), 0), iota((CHUNK, CHUNK), 1)
    tri = jnp.where(row >= col, 1.0, 0.0).astype(bf16)
    tri_up = jnp.where(row <= col, 1.0, 0.0).astype(bf16)
    later = row <= col
    first = iota((CHUNK, WIDE), 1) < WIDE // 2
    last_row = iota((CHUNK, WIDE), 0) == CHUNK - 1
    for sub in reversed(range(ROWS // CHUNK)):
        lo = sub * CHUNK
        b_low = bc_s[lo : lo + CHUNK, :states]
        c_low = bc_s[lo : lo + CHUNK, states:]
        shifted, dt, la, cum = decays(step_ref[lo : lo + CHUNK, :], head_ref, tri)
        cum_t = cum.T
        cross_t = low_dot(b_low, c_low, NT)
        c_t = c_low.T
        state_low = state_ref[sub]
        dstate_low = dstate_s[...].astype(bf16)
        dcross_t = jnp.zeros((CHUNK, CHUNK), f32)
        db = jnp.zeros((CHUNK, states), f32)
        dc = jnp.zeros((CHUNK, states), f32)
        for pair in range(width // WIDE):
            lanes = slice(pair * WIDE, (pair + 1) * WIDE)
            cum_a, cum_b, cum_p = spread_lanes(cum, pair, first)
            _, _, dt_p = spread_lanes(dt, pair, first)
            x = x_s[lo : lo + CHUNK, lanes]
            g = g_s[lo : lo + CHUNK, lanes]
            scaled = x * dt_p
            scaled_low = scaled.astype(bf16)
            zero = jnp.zeros_like(g)
            g_stack = jnp.concatenate(
                [jnp.where(first, g, zero), jnp.where(first, zero, g)], axis=0
            ).astype(bf16)
            dweights_t = low_dot(scaled_low, g_stack, NT)
            weights_t = []
            for place, wide, head in ((0, cum_a, 2 * pair), (1, cum_b, 2 * pair + 1)):
                gap = jnp.where(later, cum_t[head : head + 1, :] - wide, FAR)
                grow = jnp.exp(gap)
                weight = (cross_t * grow).astype(bf16)
                weights_t.append(weight)
                dweight = dweights_t[:, place * CHUNK : (place + 1) * CHUNK]
                dcross_t = dcross_t + dweight * grow
                rows_s[head : head + 1, :] = jnp.sum(
                    dweight * weight.astype(f32), axis=0, keepdims=True
                )
            dx_in = low_dot(jnp.concatenate(weights_t, axis=1), g_stack, NN)
            grown = jnp.exp(cum_p)
            last = cum_p[CHUNK - 1 : CHUNK, :]
            tail = jnp.exp(last - cum_p)
            last = jnp.exp(last)
            dx_tail = tail * low_dot(b_low, dstate_low[:, lanes], NN)
            dscaled = dx_in + dx_tail
            g_grown = g * grown
            g_low = g_grown.astype(bf16)
            ends = (scaled * tail).astype(bf16)
            carried = low_dot(c_low, state_low[:, lanes], NN)
            dc = dc + low_dot(g_low, state_low[:, lanes], NT)
            db = db + low_dot(ends, dstate_low[:, lanes], NT)
            dstate = dstate_s[:, lanes]
            kept = jnp.sum(dstate * state_low[:, lanes].astype(f32), axis=0, keepdims=True) * last
            dstate_s[:, lanes] = dstate * last + low_dot(c_t, g_low, NN)
            tails = scaled * dx_tail
            z_s[0:CHUNK, lanes] = g_grown * carried - tails - scaled_low.astype(f32) * dx_in
            z_s[CHUNK : 2 * CHUNK, lanes] = dscaled * x
            z_s[2 * CHUNK : 2 * CHUNK + 1, lanes] = (
                jnp.sum(tails, axis=0, keepdims=True) + kept
            )
            dx_s[lo : lo + CHUNK, lanes] = dscaled * dt_p + lane_ref[5:6, lanes] * g
            dlane_ref[5:6, lanes] += jnp.sum(g * x, axis=0, keepdims=True)
        sums = split_dot(z_s[...], seg_ref[...])
        dcum = sums[0:CHUNK, :] + rows_s[...].T
        dcum = dcum + jnp.where(last_row, sums[2 * CHUNK : 2 * CHUNK + 1, :], 0.0)
        dla = exact_dot(tri_up, dcum)
        ddt = sums[CHUNK : 2 * CHUNK, :] + dla * head_ref[1:2, :]
        dsteps = ddt * sigmoid(shifted)
        dhead_ref[0:1, :] += jnp.sum(dsteps, axis=0, keepdims=True)
        dhead_ref[1:2, :] += jnp.sum(dla * la, axis=0, keepdims=True)
        low_ref[lo : lo + CHUNK, 2 * width + query_width :] = dsteps.astype(bf16)
        dcross_low = dcross_t.astype(bf16)
        dbc_s[lo : lo + CHUNK, :states] = db + low_dot(dcross_low, c_low, NN)
        dbc_s[lo : lo + CHUNK, states:] = dc + low_dot(dcross_low, b_low, TN)

    def conv_back(pre_ref, dact, dpre_ref, ext, taps, dtaps_ref):
        pre = pre_ref[...]
        sig = sigmoid(pre)
        dpre = dact * (sig * (1.0 + pre * (1.0 - sig)))
        dpre_ref[0:ROWS, :] = dpre
        total = None
        for tap in range(KC):
            ahead = KC - 1 - tap
            term = dpre_ref[ahead : ahead + ROWS, :] * taps[tap : tap + 1, :]
            total = term if total is None else total + term
            at = 8 - (KC - 1) + tap
            dtaps_ref[tap : tap + 1, :] += jnp.sum(
                dpre * ext[at : at + ROWS, :], axis=0, keepdims=True
            )
        dpre_ref[ROWS:, :] = dpre_ref[0:8, :]
        return total

    dinner = conv_back(pre_s, dx_s[...], dpre_s, ext_s, lane_ref, dlane_ref)
    low_ref[:, width : 2 * width] = dinner.astype(bf16)
    dbc = conv_back(prebc_s, dbc_s[...], dprebc_s, extbc_s, conv_ref, dconv_ref)
    lowsh_ref[:, : 2 * states] = dbc.astype(bf16)
    lowsh_ref[:, 2 * states :] = dkv_ref[...]
    low_ref[:, 2 * width : 2 * width + query_width] = dq_ref[...]


def block_at(rows, cols, col):
    return pl.BlockSpec((rows, cols), lambda i, order: (order[i], col))


def whole_at(shape):
    return pl.BlockSpec(shape, lambda i, order: (0,) * len(shape))


def kernel_params():
    return pltpu.CompilerParams(
        dimension_semantics=("arbitrary",), vmem_limit_bytes=56 * 1024 * 1024
    )


def attn_forward(order, proj, proj_shared, cosine, sine, query_width, width, bc_width):
    slot = proj.shape[0]
    scratch = [pltpu.VMEM((slot, HD), jnp.bfloat16)] * 2
    return pl.pallas_call(
        attn_fwd_body,
        grid_spec=pltpu.PrefetchScalarGridSpec(
            num_scalar_prefetch=1,
            grid=(slot // ROWS,),
            in_specs=[
                block_at(ROWS, query_width, 2 * width // query_width),
                block_at(ROWS, 2 * HD, bc_width // (2 * HD)),
                pl.BlockSpec((ROWS, HD), lambda i, order: (i, 0)),
                pl.BlockSpec((ROWS, HD), lambda i, order: (i, 0)),
            ],
            out_specs=block_at(ROWS, query_width, 0),
            scratch_shapes=scratch,
        ),
        out_shape=jax.ShapeDtypeStruct((slot, query_width), jnp.bfloat16),
        compiler_params=kernel_params(),
        cost_estimate=pl.CostEstimate(
            flops=slot * slot * query_width * 3,
            bytes_accessed=slot * 4 * (query_width + 4 * HD),
            transcendentals=slot * slot * query_width // HD,
        ),
    )(order, proj, proj_shared, cosine, sine)


def attn_backward(order, proj, proj_shared, cosine, sine, grad_heads, query_width, width, bc_width):
    slot = proj.shape[0]
    return pl.pallas_call(
        attn_bwd_body,
        grid_spec=pltpu.PrefetchScalarGridSpec(
            num_scalar_prefetch=1,
            grid=(slot // ROWS,),
            in_specs=[
                block_at(ROWS, query_width, 2 * width // query_width),
                block_at(ROWS, 2 * HD, bc_width // (2 * HD)),
                pl.BlockSpec((ROWS, HD), lambda i, order: (i, 0)),
                pl.BlockSpec((ROWS, HD), lambda i, order: (i, 0)),
                block_at(ROWS, query_width, width // query_width),
                whole_at((slot, HD)),
                whole_at((slot, HD)),
            ],
            out_specs=[block_at(ROWS, query_width, 0), whole_at((slot, 2 * HD))],
            scratch_shapes=[pltpu.VMEM((slot, HD), jnp.bfloat16)] * 2
            + [pltpu.VMEM((slot, HD), jnp.float32)] * 2,
        ),
        out_shape=[
            jax.ShapeDtypeStruct((slot, query_width), jnp.bfloat16),
            jax.ShapeDtypeStruct((slot, 2 * HD), jnp.bfloat16),
        ],
        compiler_params=kernel_params(),
        cost_estimate=pl.CostEstimate(
            flops=slot * slot * query_width * 8,
            bytes_accessed=slot * 4 * (2 * query_width + 6 * HD),
            transcendentals=slot * slot * query_width // HD,
        ),
    )(order, proj, proj_shared, cosine, sine, grad_heads, cosine, sine)


def mixer_forward(order, proj, proj_shared, attn_low, lane_params, conv_shared, head_params):
    slot = proj.shape[0]
    f32, bf16 = jnp.float32, jnp.bfloat16
    width = lane_params.shape[1]
    bc_width = conv_shared.shape[1]
    query_width = attn_low.shape[1]
    chunks = ROWS // CHUNK
    return pl.pallas_call(
        mixer_fwd_body,
        grid_spec=pltpu.PrefetchScalarGridSpec(
            num_scalar_prefetch=1,
            grid=(slot // ROWS,),
            in_specs=[
                block_at(ROWS, width, 0),
                block_at(ROWS, width, 1),
                block_at(ROWS, WIDE, (2 * width + query_width) // WIDE),
                block_at(ROWS, bc_width, 0),
                block_at(ROWS, query_width, 0),
                whole_at(lane_params.shape),
                whole_at(conv_shared.shape),
                whole_at(head_params.shape),
            ],
            out_specs=[
                block_at(ROWS, width + query_width, 0),
                pl.BlockSpec((ROWS, width), lambda i, order: (i, 0)),
                pl.BlockSpec((chunks, bc_width // 2, width), lambda i, order: (i, 0, 0)),
            ],
            scratch_shapes=[
                pltpu.VMEM((ROWS + 8, width), f32),
                pltpu.VMEM((ROWS + 8, bc_width), f32),
                pltpu.VMEM((bc_width // 2, width), f32),
                pltpu.VMEM((ROWS, width), f32),
            ],
        ),
        out_shape=[
            jax.ShapeDtypeStruct((slot, width + query_width), bf16),
            jax.ShapeDtypeStruct((slot, width), f32),
            jax.ShapeDtypeStruct((slot // CHUNK, bc_width // 2, width), bf16),
        ],
        compiler_params=kernel_params(),
        cost_estimate=pl.CostEstimate(
            flops=slot * width * bc_width * 8,
            bytes_accessed=slot * width * 20,
            transcendentals=slot * width * 8,
        ),
    )(order, proj, proj, proj, proj_shared, attn_low, lane_params, conv_shared, head_params)


def mixer_backward(
    order, proj, proj_shared, y, states, grad_heads, dq, dkv, lane_params, conv_shared,
    head_params, seg, query_width,
):
    slot = proj.shape[0]
    f32, bf16 = jnp.float32, jnp.bfloat16
    width = lane_params.shape[1]
    bc_width = conv_shared.shape[1]
    blocks = slot // ROWS
    chunks = ROWS // CHUNK

    def back(rows, cols, col):
        return pl.BlockSpec((rows, cols), lambda i, order: (order[blocks - 1 - i], col))

    def straight(shape):
        return pl.BlockSpec(
            shape, lambda i, order: (blocks - 1 - i,) + (0,) * (len(shape) - 1)
        )

    def before(cols, col):
        return pl.BlockSpec(
            (8, cols),
            lambda i, order: (
                order[jnp.maximum(blocks - 2 - i, 0)] * (ROWS // 8) + ROWS // 8 - 1,
                col,
            ),
        )

    return pl.pallas_call(
        mixer_bwd_body,
        grid_spec=pltpu.PrefetchScalarGridSpec(
            num_scalar_prefetch=1,
            grid=(blocks,),
            in_specs=[
                back(ROWS, width, 0),
                back(ROWS, width, 1),
                before(width, 1),
                back(ROWS, WIDE, (2 * width + query_width) // WIDE),
                back(ROWS, bc_width, 0),
                before(bc_width, 0),
                straight((ROWS, width)),
                straight((chunks, bc_width // 2, width)),
                back(ROWS, width, 0),
                back(ROWS, query_width, 0),
                straight((ROWS, 2 * HD)),
                whole_at(lane_params.shape),
                whole_at(conv_shared.shape),
                whole_at(head_params.shape),
                whole_at(seg.shape),
            ],
            out_specs=[
                back(ROWS, 2 * width + query_width + WIDE, 0),
                back(ROWS, bc_width + 2 * HD, 0),
                whole_at((8, width)),
                whole_at((8, bc_width)),
                whole_at((8, WIDE)),
            ],
            scratch_shapes=[
                pltpu.VMEM((ROWS + 8, width), f32),
                pltpu.VMEM((ROWS + 8, bc_width), f32),
                pltpu.VMEM((ROWS, width), f32),
                pltpu.VMEM((ROWS, bc_width), f32),
                pltpu.VMEM((ROWS, width), f32),
                pltpu.VMEM((ROWS, bc_width), bf16),
                pltpu.VMEM((ROWS, width), f32),
                pltpu.VMEM((ROWS, width), f32),
                pltpu.VMEM((ROWS, bc_width), f32),
                pltpu.VMEM((ROWS + 8, width), f32),
                pltpu.VMEM((ROWS + 8, bc_width), f32),
                pltpu.VMEM((bc_width // 2, width), f32),
                pltpu.VMEM((2 * CHUNK + 8, width), f32),
                pltpu.VMEM((WIDE, CHUNK), f32),
            ],
        ),
        out_shape=[
            jax.ShapeDtypeStruct((slot, 2 * width + query_width + WIDE), bf16),
            jax.ShapeDtypeStruct((slot, bc_width + 2 * HD), bf16),
            jax.ShapeDtypeStruct((8, width), f32),
            jax.ShapeDtypeStruct((8, bc_width), f32),
            jax.ShapeDtypeStruct((8, WIDE), f32),
        ],
        compiler_params=kernel_params(),
        cost_estimate=pl.CostEstimate(
            flops=slot * width * bc_width * 20,
            bytes_accessed=slot * width * 40,
            transcendentals=slot * width * 16,
        ),
    )(
        order, proj, proj, proj, proj, proj_shared, proj_shared, y, states, grad_heads, dq, dkv,
        lane_params, conv_shared, head_params, seg,
    )


class Places:
    def __init__(self):
        self.dp = lax.axis_size("dp")
        self.tp = lax.axis_size("tensor")
        d = lax.axis_index("dp")
        t = lax.axis_index("tensor")
        self.d, self.t = d, t
        self.c = d % 2
        self.k = d // 2
        self.zq = t % 2
        self.home = self.c == t // 2
        self.quarter = 2 * self.c + self.zq
        self.column = self.zq + 2 * self.c
        self.slot = 2 * self.k + t // 2
        self.blocks = self.dp // 2
        self.bits = self.blocks.bit_length() - 1

    def pairs(self, where_to):
        out = []
        for d in range(self.dp):
            for t in range(self.tp):
                target = where_to(d, t)
                if target is not None:
                    out.append((d * self.tp + t, target[0] * self.tp + target[1]))
        return out

    def send(self, values, where_to):
        return lax.ppermute(values, ("dp", "tensor"), self.pairs(where_to))

    def over_core(self, values):
        return self.send(values, lambda d, t: (d ^ 1, t))

    def over_z(self, values):
        return self.send(values, lambda d, t: (d, t ^ 1))

    def over_far(self, values):
        return self.send(values, lambda d, t: (d, t ^ 2))

    def over_bit(self, values, bit):
        return self.send(values, lambda d, t: (d ^ (2 << bit), t))

    def swap_away(self, values):
        def where_to(d, t):
            if d % 2 == t // 2:
                return None
            return (d ^ 1, t ^ 2)

        return self.send(values, where_to)

    def column_out(self, values):
        def where_to(d, t):
            if d % 2 == t // 2:
                return (d, t ^ 2)
            return (d ^ 1, t)

        return self.send(values, where_to)

    def column_back(self, values):
        def where_to(d, t):
            if d % 2 == t // 2:
                return (d ^ 1, t)
            return (d, t ^ 2)

        return self.send(values, where_to)


def relocate(values, at):
    return jnp.where(at.home, values, at.swap_away(values))


MESH = pl.DeviceIdType.MESH


class Lanes:
    def __init__(self, blocks):
        d = lax.axis_index("dp")
        t = lax.axis_index("tensor")
        self.c = lax.rem(d, 2)
        self.k = lax.div(d, 2)
        self.d, self.t = d, t
        self.home = self.c == lax.div(t, 2)
        self.away = self.c != lax.div(t, 2)
        self.other = d + 1 - 2 * self.c
        self.near = t + 1 - 2 * lax.rem(t, 2)
        self.far = lax.rem(t + 2, 4)
        self.blocks = blocks
        self.bits = blocks.bit_length() - 1

    def block(self, place):
        value = self.k
        for bit in range(self.bits):
            if (place >> bit) & 1:
                value = value + (1 << bit) * (1 - 2 * lax.rem(lax.div(self.k, 1 << bit), 2))
        return value

    def across(self, bit):
        return (2 * self.block(1 << bit) + self.c, self.t)

    def greet(self):
        partners = [
            (self.other, self.t),
            (self.d, self.near),
            (self.d, self.far),
            (self.other, self.far),
        ] + [self.across(bit) for bit in range(self.bits)]
        barrier = pltpu.get_barrier_semaphore()
        for partner in partners:
            pl.semaphore_signal(barrier, inc=1, device_id=partner, device_id_type=MESH)
        pl.semaphore_wait(barrier, len(partners))


def remote(src, dst, send_sem, recv_sem, device):
    return pltpu.make_async_remote_copy(
        src_ref=src,
        dst_ref=dst,
        send_sem=send_sem,
        recv_sem=recv_sem,
        device_id=device,
        device_id_type=MESH,
    )


def onward(place, half, bits):
    if half == 0:
        return [bit for bit in range(bits) if place < (1 << bit)]
    return [bit for bit in reversed(range(bits)) if place % (2 << bit) == 0]


class Spread:
    def __init__(self, lanes, full, rows, chunks, send_sems, recv_sems, cols=slice(None)):
        self.lanes, self.full, self.rows, self.chunks = lanes, full, rows, chunks
        self.cols = cols
        self.piece = rows // chunks
        self.send_sems, self.recv_sems = send_sems, recv_sems

    def view(self, place, half, chunk):
        start = self.lanes.block(place) * (2 * self.rows) + half * self.rows + chunk * self.piece
        return self.full.at[pl.ds(pl.multiple_of(start, self.piece), self.piece), self.cols]

    def copy(self, place, half, chunk, bit):
        view = self.view(place, half, chunk)
        to = place | (1 << bit)
        return remote(
            view,
            view,
            self.send_sems.at[half, to, chunk],
            self.recv_sems.at[half, to, chunk],
            self.lanes.across(bit),
        )

    def give(self, place, half, chunk):
        for bit in onward(place, half, self.lanes.bits):
            self.copy(place, half, chunk, bit).start()

    def take(self, place, half, chunk):
        view = self.view(place, half, chunk)
        remote(
            view,
            view,
            self.send_sems.at[half, place, chunk],
            self.recv_sems.at[half, place, chunk],
            self.lanes.across(0),
        ).wait_recv()

    def pass_on(self, chunk):
        for half in range(2):
            places = range(1, self.lanes.blocks)
            if half == 1:
                key = lambda place: [-bit for bit in reversed(range(8)) if (place >> bit) & 1]
                places = sorted(places, key=key)
            for place in places:
                if onward(place, half, self.lanes.bits):
                    self.take(place, half, chunk)
                    self.give(place, half, chunk)

    def finish(self, chunk):
        for half in range(2):
            for place in range(1, self.lanes.blocks):
                if not onward(place, half, self.lanes.bits):
                    self.take(place, half, chunk)
        for half in range(2):
            for place in range(self.lanes.blocks):
                for bit in onward(place, half, self.lanes.bits):
                    self.copy(place, half, chunk, bit).wait_send()


def front_body(
    blocks, chunks, in_ref, out_ref, shared_ref, x_ref, gain_ref,
    full_ref, pair_ref, act_ref, xr_ref, sh_ref,
    x_s, act_s, home_sems, z_send, z_recv, o_sems, o_recv, send_sems, recv_sems, x_sems, a_send,
    a_recv, line_send, line_recv, sh_send, sh_recv, swap_send, swap_recv,
):
    lanes = Lanes(blocks)
    rows = in_ref.shape[0]
    piece = rows // chunks
    here = x_ref.shape[0]
    c, t = lanes.c, lanes.t
    lanes.greet()
    spread = Spread(lanes, full_ref, rows, chunks, send_sems, recv_sems)
    few, wide = shared_ref.shape
    side = wide // 2
    mine = pl.ds(pl.multiple_of(c * side, side), side)
    theirs = pl.ds(pl.multiple_of((1 - c) * side, side), side)

    def line_view(half, at_t, cols):
        start = lanes.k * (2 * rows) + half * rows + at_t * few
        return sh_ref.at[pl.ds(pl.multiple_of(start, few), few), cols]

    def line_own():
        return pltpu.make_async_copy(
            shared_ref.at[:, mine], line_view(c, t, mine), line_send.at[0]
        )

    def line_swap():
        return remote(
            shared_ref.at[:, theirs],
            line_view(c, t, theirs),
            line_send.at[1],
            line_recv.at[0],
            (lanes.other, t),
        )

    def line_swapped():
        view = line_view(1 - c, t, mine)
        return remote(view, view, line_send.at[1], line_recv.at[0], (lanes.other, t))

    def line_near(half, came):
        view = line_view(half, lanes.near if came else t, mine)
        return remote(
            view, view, line_send.at[2 + half], line_recv.at[1 + half], (lanes.d, lanes.near)
        )

    def line_far(half, near, came):
        at_t = lanes.near if near else t
        if came:
            at_t = lax.rem(at_t + 2, 4)
        view = line_view(half, at_t, mine)
        place = 2 * near + half
        return remote(
            view, view, line_send.at[4 + place], line_recv.at[3 + place], (lanes.d, lanes.far)
        )

    shared_spread = Spread(lanes, sh_ref, rows, 1, sh_send, sh_recv, mine)

    def swap_copy(place, half, came):
        start = lanes.block(place) * (2 * rows) + half * rows
        view = sh_ref.at[pl.ds(pl.multiple_of(start, rows), rows), theirs if came else mine]
        return remote(
            view, view, swap_send.at[half, place], swap_recv.at[half, place], (lanes.other, t)
        )

    def slot(chunk):
        start = lanes.k * (2 * rows) + c * rows + chunk * piece
        return full_ref.at[pl.ds(pl.multiple_of(start, piece), piece), :]

    def first_copy(chunk, device):
        return remote(
            in_ref.at[pl.ds(chunk * piece, piece), :],
            slot(chunk),
            z_send.at[0, chunk],
            z_recv.at[c, chunk],
            device,
        )

    def second_copy(chunk):
        return remote(
            in_ref.at[pl.ds(chunk * piece, piece), :],
            slot(chunk),
            z_send.at[1, chunk],
            z_recv.at[c, chunk],
            (lanes.other, lanes.far),
        )

    def own_copy(chunk):
        return pltpu.make_async_copy(
            in_ref.at[pl.ds(chunk * piece, piece), :], slot(chunk), home_sems.at[chunk]
        )

    def out_slot():
        return pair_ref.at[pl.ds(pl.multiple_of(c * rows, rows), rows), :]

    def out_first(device):
        return remote(out_ref, out_slot(), o_sems.at[0], o_recv.at[c], device)

    def out_second():
        return remote(out_ref, out_slot(), o_sems.at[1], o_recv.at[c], (lanes.other, lanes.far))

    def x_away():
        return remote(x_ref, x_s, x_sems.at[0], x_sems.at[1], (lanes.other, lanes.far))

    def x_home():
        return pltpu.make_async_copy(x_ref, x_s, x_sems.at[2])

    def send_first(chunk):
        @pl.when(lanes.home)
        def _():
            own_copy(chunk).start()
            first_copy(chunk, (lanes.d, lanes.far)).start()

        @pl.when(lanes.away)
        def _():
            first_copy(chunk, (lanes.other, t)).start()
            second_copy(chunk).start()

    def z_view(half, chunk):
        start = lanes.k * (2 * rows) + half * rows + chunk * piece
        return full_ref.at[pl.ds(pl.multiple_of(start, piece), piece), :]

    def came(half, chunk):
        view = z_view(half, chunk)
        return remote(
            view, view, z_send.at[0, chunk], z_recv.at[half, chunk], (lanes.other, t)
        )

    def arrive_home(chunk):
        own_copy(chunk).wait()
        start = lanes.k * (2 * rows) + (1 - c) * rows + chunk * piece
        view = full_ref.at[pl.ds(pl.multiple_of(start, piece), piece), :]
        remote(
            view, view, z_send.at[0, chunk], z_recv.at[1 - c, chunk], (lanes.other, t)
        ).wait_recv()
        for half in range(2):
            spread.give(0, half, chunk)

    def arrive_away(chunk):
        for half in range(2):
            came(half, chunk).wait_recv()
        for half in range(2):
            spread.give(0, half, chunk)

    def arrive(chunk):
        @pl.when(lanes.home)
        def _():
            arrive_home(chunk)

        @pl.when(lanes.away)
        def _():
            arrive_away(chunk)

    def act_slot(index):
        return act_ref.at[pl.ds(index * here, here), :]

    def act_far():
        return remote(act_s, act_slot(2), a_send.at[0], a_recv.at[0], (lanes.d, lanes.near))

    def act_core():
        return remote(act_s, act_slot(1), a_send.at[1], a_recv.at[1], (lanes.other, t))

    def act_both():
        return remote(act_slot(2), act_slot(3), a_send.at[2], a_recv.at[2], (lanes.other, t))

    def norm():
        @pl.when(lanes.home)
        def _():
            x_home().wait()

        @pl.when(lanes.away)
        def _():
            x_away().wait_recv()

        @pl.loop(0, here // 32)
        def _(step):
            part = pl.ds(pl.multiple_of(step * 32, 32), 32)
            x = x_s[part, :].astype(jnp.float32)
            scale = lax.rsqrt(jnp.mean(x * x, axis=1, keepdims=True) + EPS)
            act_s[part, :] = (x * scale * gain_ref[...]).astype(jnp.bfloat16)

        act_far().start()
        act_core().start()
        pltpu.make_async_copy(act_s, act_slot(0), a_send.at[3]).start()
        pltpu.make_async_copy(x_s, xr_ref, x_sems.at[3]).start()

    early = list(range(max(chunks // 2, 1)))
    late = list(range(len(early), chunks))
    line_own().start()
    line_swap().start()
    for chunk in early:
        send_first(chunk)

    @pl.when(lanes.home)
    def _():
        x_home().start()

    @pl.when(lanes.away)
    def _():
        x_away().start()

    line_own().wait()
    line_swapped().wait_recv()
    for half in range(2):
        line_near(half, False).start()
    for chunk in early:
        arrive(chunk)
        if chunk:
            spread.pass_on(chunk - 1)
    for half in range(2):
        line_near(half, True).wait_recv()
    for near in range(2):
        for half in range(2):
            line_far(half, near, False).start()
    for chunk in late:
        send_first(chunk)
    spread.pass_on(early[-1])

    @pl.when(lanes.home)
    def _():
        for chunk in late:
            arrive_home(chunk)
            spread.pass_on(chunk)

    norm()

    @pl.when(lanes.home)
    def _():
        out_first((lanes.d, lanes.far)).start()
        pltpu.make_async_copy(out_ref, out_slot(), o_sems.at[2]).start()

    @pl.when(lanes.away)
    def _():
        out_first((lanes.other, t)).start()
        out_second().start()

    for near in range(2):
        for half in range(2):
            line_far(half, near, True).wait_recv()
    for half in range(2):
        shared_spread.give(0, half, 0)
        swap_copy(0, half, False).start()

    @pl.when(lanes.away)
    def _():
        for chunk in late:
            arrive_away(chunk)
            if chunk > late[0]:
                spread.pass_on(chunk - 1)

    shared_spread.pass_on(0)

    @pl.when(lanes.away)
    def _():
        for chunk in late[-1:]:
            spread.pass_on(chunk)

    shared_spread.finish(0)
    for half in range(2):
        for place in range(1, blocks):
            swap_copy(place, half, False).start()
    act_far().wait_recv()
    act_both().start()
    act_core().wait_recv()
    for chunk in range(chunks):
        spread.finish(chunk)
    for half in range(2):
        for place in range(blocks):
            swap_copy(place, half, True).wait_recv()
            swap_copy(place, half, False).wait_send()
    line_swap().wait_send()
    for half in range(2):
        line_near(half, False).wait_send()
        for near in range(2):
            line_far(half, near, False).wait_send()
    act_both().wait_recv()
    act_far().wait_send()
    act_core().wait_send()
    act_both().wait_send()
    pltpu.make_async_copy(act_s, act_slot(0), a_send.at[3]).wait()
    pltpu.make_async_copy(x_s, xr_ref, x_sems.at[3]).wait()

    @pl.when(lanes.home)
    def _():
        for chunk in range(chunks):
            first_copy(chunk, (lanes.d, lanes.far)).wait_send()
        out_first((lanes.d, lanes.far)).wait_send()
        pltpu.make_async_copy(out_ref, out_slot(), o_sems.at[2]).wait()
        start = (1 - c) * rows
        view = pair_ref.at[pl.ds(pl.multiple_of(start, rows), rows), :]
        remote(view, view, o_sems.at[0], o_recv.at[1 - c], (lanes.other, t)).wait_recv()

    @pl.when(lanes.away)
    def _():
        x_away().wait_send()
        for chunk in range(chunks):
            first_copy(chunk, (lanes.other, t)).wait_send()
            second_copy(chunk).wait_send()
        out_first((lanes.other, t)).wait_send()
        out_second().wait_send()
        for half in range(2):
            view = pair_ref.at[pl.ds(half * rows, rows), :]
            remote(view, view, o_sems.at[0], o_recv.at[half], (lanes.other, t)).wait_recv()


def front(in_pack, out_pack, shared, layer_in, gain, at):
    bf16 = jnp.bfloat16
    rows = in_pack.shape[0]
    blocks = at.blocks
    chunks = 4 if rows >= 256 else 1
    dma = pltpu.SemaphoreType.DMA
    anywhere = pl.BlockSpec(memory_space=pl.ANY)
    here, features = layer_in.shape
    total = 2 * blocks * rows
    return pl.pallas_call(
        functools.partial(front_body, blocks, chunks),
        in_specs=[anywhere] * 4 + [pl.BlockSpec(memory_space=pltpu.VMEM)],
        out_specs=[anywhere] * 5,
        out_shape=[
            jax.ShapeDtypeStruct((total, in_pack.shape[1]), bf16),
            jax.ShapeDtypeStruct((2 * rows, out_pack.shape[1]), bf16),
            jax.ShapeDtypeStruct((4 * here, features), bf16),
            jax.ShapeDtypeStruct((here, features), bf16),
            jax.ShapeDtypeStruct((total, shared.shape[1]), bf16),
        ],
        scratch_shapes=[
            pltpu.VMEM((here, features), bf16),
            pltpu.VMEM((here, features), bf16),
            dma((chunks,)),
            dma((2, chunks)),
            dma((2, chunks)),
            dma((3,)),
            dma((2,)),
            dma((2, blocks, chunks)),
            dma((2, blocks, chunks)),
            dma((4,)),
            dma((4,)),
            dma((3,)),
            dma((8,)),
            dma((7,)),
            dma((2, blocks, 1)),
            dma((2, blocks, 1)),
            dma((2, blocks)),
            dma((2, blocks)),
        ],
        compiler_params=pltpu.CompilerParams(
            collective_id=1, has_side_effects=True, vmem_limit_bytes=16 * 1024 * 1024
        ),
        cost_estimate=pl.CostEstimate(
            flops=here * features * 8, bytes_accessed=300_000_000, transcendentals=0
        ),
    )(in_pack, out_pack, shared, layer_in, gain.reshape(1, -1))


class Stage:
    def __init__(self, lanes, src, full, rows, cols, chunks, sems):
        self.lanes, self.src, self.full, self.rows, self.cols = lanes, src, full, rows, cols
        self.chunks = chunks
        self.piece = rows // chunks
        self.send_sems, self.recv_sems, self.home_sems, ssem, rsem = sems
        self.spread = Spread(lanes, full, rows, chunks, ssem, rsem, cols)

    def view(self, half, chunk):
        start = self.lanes.k * (2 * self.rows) + half * self.rows + chunk * self.piece
        return self.full.at[pl.ds(pl.multiple_of(start, self.piece), self.piece), self.cols]

    def part(self, chunk):
        return self.src.at[pl.ds(chunk * self.piece, self.piece), self.cols]

    def own(self, chunk):
        return pltpu.make_async_copy(
            self.part(chunk), self.view(self.lanes.c, chunk), self.home_sems.at[chunk]
        )

    def first(self, chunk, device):
        c = self.lanes.c
        return remote(
            self.part(chunk),
            self.view(c, chunk),
            self.send_sems.at[0, chunk],
            self.recv_sems.at[c, chunk],
            device,
        )

    def second(self, chunk):
        c = self.lanes.c
        return remote(
            self.part(chunk),
            self.view(c, chunk),
            self.send_sems.at[1, chunk],
            self.recv_sems.at[c, chunk],
            (self.lanes.other, self.lanes.far),
        )

    def start(self):
        lanes = self.lanes

        @pl.when(lanes.home)
        def _():
            for chunk in range(self.chunks):
                self.own(chunk).start()
                self.first(chunk, (lanes.d, lanes.far)).start()

        @pl.when(lanes.away)
        def _():
            for chunk in range(self.chunks):
                self.first(chunk, (lanes.other, lanes.t)).start()
                self.second(chunk).start()

    def came(self, half, chunk):
        view = self.view(half, chunk)
        remote(
            view,
            view,
            self.send_sems.at[0, chunk],
            self.recv_sems.at[half, chunk],
            (self.lanes.other, self.lanes.t),
        ).wait_recv()

    def give(self, chunk):
        for half in range(2):
            self.spread.give(0, half, chunk)

    def arrive_home(self, chunk):
        self.own(chunk).wait()
        self.came(1 - self.lanes.c, chunk)
        self.give(chunk)

    def arrive_away(self, chunk):
        for half in range(2):
            self.came(half, chunk)
        self.give(chunk)

    def settle(self, place):
        for half in range(2):
            if not onward(place, half, self.lanes.bits):
                for chunk in range(self.chunks):
                    self.spread.take(place, half, chunk)

    def finish(self):
        lanes = self.lanes
        for chunk in range(self.chunks):
            for half in range(2):
                for place in range(lanes.blocks):
                    for bit in onward(place, half, lanes.bits):
                        self.spread.copy(place, half, chunk, bit).wait_send()

        @pl.when(lanes.home)
        def _():
            for chunk in range(self.chunks):
                self.first(chunk, (lanes.d, lanes.far)).wait_send()

        @pl.when(lanes.away)
        def _():
            for chunk in range(self.chunks):
                self.first(chunk, (lanes.other, lanes.t)).wait_send()
                self.second(chunk).wait_send()


class Exchange:
    def __init__(self, lanes, work, own, sends, recvs, ssem, rsem):
        self.lanes, self.work, self.own = lanes, work, own
        self.both_s, self.core_s, self.pass_s = sends
        self.both_r, self.core_r, self.far_r = recvs
        self.ssem, self.rsem = ssem, rsem
        self.blocks, self.here, self.block = own.shape
        self.step = min(self.here, 64)

    def copies(self, index, place):
        core, near = (self.lanes.other, self.lanes.t), (self.lanes.d, self.lanes.near)
        table = (
            (self.both_s, self.both_r, core),
            (self.core_s, self.core_r, core),
            (self.pass_s, self.far_r, near),
        )

        def copy(kind):
            src, dst, device = table[kind]
            return remote(
                src.at[index], dst.at[index], self.ssem.at[kind, place], self.rsem.at[kind, place],
                device,
            )

        return copy

    def columns(self, place):
        return slice(place * self.block, (place + 1) * self.block)

    def rows(self, piece, i):
        start = piece * self.here + i * self.step
        return pl.ds(pl.multiple_of(start, self.step), self.step)

    def give(self, index, place, left, weight):
        bf16 = jnp.bfloat16
        cols = self.columns(place)

        @pl.loop(0, 4)
        def _(piece):
            rows = pl.ds(pl.multiple_of(piece * self.here, self.here), self.here)
            self.work[rows, cols] = low_dot(left[rows, :], weight(), NT)

        @pl.loop(0, self.here // self.step)
        def _(i):
            part = self.rows(0, i)
            self.both_s[index, part, :] = self.work[self.rows(3, i), cols].astype(bf16)
            self.core_s[index, part, :] = self.work[self.rows(1, i), cols].astype(bf16)
            self.own[index, part, :] = self.work[part, cols]

        copy = self.copies(index, place)
        copy(0).start()
        copy(1).start()

    def pass_on(self, index, place):
        copy = self.copies(index, place)
        copy(0).wait_recv()
        cols = self.columns(place)

        @pl.loop(0, self.here // self.step)
        def _(i):
            part = self.rows(0, i)
            total = self.work[self.rows(2, i), cols] + self.both_r[index, part, :].astype(
                jnp.float32
            )
            self.pass_s[index, part, :] = total.astype(jnp.bfloat16)

        copy(2).start()

    def take(self, index, place):
        copy = self.copies(index, place)
        copy(1).wait_recv()
        copy(2).wait_recv()

    def total(self, index, rows):
        f32 = jnp.float32
        return (
            self.own[index, rows, :]
            + self.core_r[index, rows, :].astype(f32)
            + self.far_r[index, rows, :].astype(f32)
        )

    def finish(self, index, place):
        copy = self.copies(index, place)
        for kind in range(3):
            copy(kind).wait_send()


def middle_body(
    blocks, gu_chunks, down_chunks,
    ff_ref, heads_ref, out_ref, x_ref, gain_ref, target_ref, live_ref,
    full_ref, mid_ref, gate_ref, up_ref, hidden_ref, grads_ref, resid_ref, error_ref, low_ref,
    loss_ref,
    wbuf, mid_s, acc_s, hid_s, gate_s, up_s, own_s, both_s, core_s, pass_s,
    both_r, core_r, far_r, both_q, core_q, far_q, err_s,
    w_sems, one_s, one_r, two_s, two_r, mid_ssem, mid_rsem, err_ssem, err_rsem, keep_sems,
    gz_s, gz_r, g_home, g_s, g_r, dz_s, dz_r, d_home, d_s, d_r,
):
    f32, bf16 = jnp.float32, jnp.bfloat16
    lanes = Lanes(blocks)
    rows = ff_ref.shape[0]
    here = x_ref.shape[0]
    block = 2 * rows
    inner = heads_ref.shape[1]
    hidden_width = hid_s.shape[1]
    core_at = (lanes.other, lanes.t)
    near_at = (lanes.d, lanes.near)
    lanes.greet()
    gate_up = Stage(
        lanes, ff_ref, full_ref, rows, slice(0, 2 * hidden_width), gu_chunks,
        (gz_s, gz_r, g_home, g_s, g_r),
    )
    down = Stage(
        lanes, ff_ref, full_ref, rows, slice(2 * hidden_width, 3 * hidden_width), down_chunks,
        (dz_s, dz_r, d_home, d_s, d_r),
    )
    sends = (both_s, core_s, pass_s)
    one = Exchange(lanes, acc_s, own_s, sends, (both_r, core_r, far_r), one_s, one_r)
    two = Exchange(lanes, acc_s, own_s, sends, (both_q, core_q, far_q), two_s, two_r)

    def load(src, slot, width, cols):
        return pltpu.make_async_copy(src, wbuf.at[slot, :, cols], w_sems.at[slot])

    def out_load(index):
        return load(
            out_ref.at[pl.ds(index * block, block), :], index % 2, inner, pl.ds(0, inner)
        )

    gate_up.start()
    out_load(0).start()
    down.start()

    for index in range(blocks):
        if index + 1 < blocks:
            out_load(index + 1).start()
        out_load(index).wait()
        one.give(index, index, heads_ref, lambda: wbuf[index % 2, :, :inner])
        if index == 0:

            @pl.when(lanes.home)
            def _():
                for chunk in range(gu_chunks):
                    gate_up.arrive_home(chunk)

    for index in range(blocks):
        one.pass_on(index, index)

    @pl.when(lanes.away)
    def _():
        for chunk in range(gu_chunks):
            gate_up.arrive_away(chunk)
            if chunk:
                gate_up.spread.pass_on(chunk - 1)

    @pl.when(lanes.home)
    def _():
        for chunk in range(gu_chunks - 1):
            gate_up.spread.pass_on(chunk)

    for index in range(blocks):
        one.take(index, index)

    step = min(here, 32)

    def columns(index):
        return slice(index * block, (index + 1) * block)

    @pl.loop(0, here // step)
    def _(i):
        part = pl.ds(pl.multiple_of(i * step, step), step)
        total = jnp.zeros((step, 1), f32)
        for index in range(blocks):
            resid = x_ref[part, columns(index)].astype(f32) + one.total(index, part)
            resid_ref[part, columns(index)] = resid
            total = total + jnp.sum(resid * resid, axis=1, keepdims=True)
        scale = lax.rsqrt(total / (blocks * block) + EPS)
        for index in range(blocks):
            mid = resid_ref[part, columns(index)] * scale * gain_ref[:, columns(index)]
            mid_s[index, part, :] = mid.astype(bf16)

    def mid_view(slot):
        return mid_s.at[:, pl.ds(slot * here, here), :]

    def mid_near():
        return remote(mid_view(0), mid_view(2), mid_ssem.at[0], mid_rsem.at[0], near_at)

    def mid_core():
        return remote(mid_view(0), mid_view(1), mid_ssem.at[1], mid_rsem.at[1], core_at)

    def mid_both():
        return remote(mid_view(2), mid_view(3), mid_ssem.at[2], mid_rsem.at[2], core_at)

    mid_near().start()
    mid_core().start()
    gate_up.spread.pass_on(gu_chunks - 1)

    @pl.when(lanes.home)
    def _():
        for chunk in range(down_chunks):
            down.arrive_home(chunk)

    @pl.when(lanes.away)
    def _():
        for chunk in range(down_chunks):
            down.arrive_away(chunk)

    def gu_load(place, slot):
        start = lanes.block(place) * block
        view = full_ref.at[pl.ds(pl.multiple_of(start, block), block), pl.ds(0, 2 * hidden_width)]
        return load(view, slot, 2 * hidden_width, pl.ds(0, 2 * hidden_width))

    def down_load(place, slot):
        start = lanes.block(place) * block
        view = full_ref.at[
            pl.ds(pl.multiple_of(start, block), block), pl.ds(2 * hidden_width, hidden_width)
        ]
        return load(view, slot, hidden_width, pl.ds(0, hidden_width))

    gu_load(0, 0).start()
    mid_near().wait_recv()
    mid_both().start()
    mid_core().wait_recv()

    wide = 2 * hidden_width
    tile = min(wide, 512)

    def accumulate(place, first, last):
        slot = place % 2
        index = lanes.block(place)

        @pl.loop(first, last)
        def _(piece):
            part = pl.ds(pl.multiple_of(piece * here, here), here)
            left = mid_s[index, part, :]
            for col in range(0, wide, tile):
                cols = slice(col, col + tile)
                product = low_dot(left, wbuf[slot, :, cols], NN)
                if place:
                    product = product + acc_s[part, cols]
                acc_s[part, cols] = product

    for place in range(blocks):
        if place + 1 < blocks:
            gate_up.settle(place + 1)
            gu_load(place + 1, (place + 1) % 2).start()
        gu_load(place, place % 2).wait()
        accumulate(place, 0, 3)
        if place == 0:
            mid_both().wait_recv()
        accumulate(place, 3, 4)
        if place < down_chunks:
            down.spread.pass_on(place)

    for chunk in range(blocks, down_chunks):
        down.spread.pass_on(chunk)

    down_load(0, 0).start()

    @pl.loop(0, 4 * here // step)
    def _(i):
        part = pl.ds(pl.multiple_of(i * step, step), step)
        gate = acc_s[part, :hidden_width]
        up = acc_s[part, hidden_width : 2 * hidden_width]
        gate_s[part, :] = gate.astype(bf16)
        up_s[part, :] = up.astype(bf16)
        hid_s[part, :] = (gate * sigmoid(gate) * up).astype(bf16)

    kept = [
        pltpu.make_async_copy(hid_s, hidden_ref, keep_sems.at[0]),
        pltpu.make_async_copy(gate_s, gate_ref, keep_sems.at[1]),
        pltpu.make_async_copy(up_s, up_ref, keep_sems.at[2]),
    ] + [
        pltpu.make_async_copy(
            mid_s.at[index], mid_ref.at[:, pl.ds(index * block, block)], keep_sems.at[3 + index]
        )
        for index in range(blocks)
    ]
    for copy in kept:
        copy.start()
    for index in range(blocks):
        one.finish(index, index)

    for place in range(blocks):
        index = lanes.block(place)
        if place + 1 < blocks:
            down.settle(place + 1)
            down_load(place + 1, (place + 1) % 2).start()
        down_load(place, place % 2).wait()
        two.give(index, place, hid_s, lambda: wbuf[place % 2, :, :hidden_width])
        if place:
            two.pass_on(lanes.block(place - 1), place - 1)
    two.pass_on(lanes.block(blocks - 1), blocks - 1)
    for place in range(blocks):
        two.take(lanes.block(place), place)

    def output_part(i, loss):
        part = pl.ds(pl.multiple_of(i * step, step), step)
        live = live_ref[part, :]
        for index in range(blocks):
            cols = columns(index)
            outputs = resid_ref[part, cols] + two.total(index, part)
            low_ref[part, cols] = outputs.astype(bf16)
            error = (outputs - target_ref[part, cols].astype(f32)) * live
            error_ref[part, cols] = error
            err_s[part, cols] = error.astype(bf16)
            loss = loss + jnp.sum(error * error)
        return loss

    loss = lax.fori_loop(0, here // step, output_part, jnp.zeros((), f32))
    loss_ref[...] = jnp.zeros((8, WIDE), f32) + 0.5 * loss

    def grads_view(slot):
        return grads_ref.at[pl.ds(slot * here, here), :]

    def err_near():
        return remote(err_s, grads_view(2), err_ssem.at[0], err_rsem.at[0], near_at)

    def err_core():
        return remote(err_s, grads_view(1), err_ssem.at[1], err_rsem.at[1], core_at)

    def err_both():
        return remote(grads_view(2), grads_view(3), err_ssem.at[2], err_rsem.at[2], core_at)

    own_err = pltpu.make_async_copy(err_s, grads_view(0), err_ssem.at[3])
    err_near().start()
    err_core().start()
    own_err.start()
    for copy in kept:
        copy.wait()
    gate_up.finish()
    down.finish()
    for place in range(blocks):
        two.finish(lanes.block(place), place)
    for copy in (mid_near(), mid_core(), mid_both()):
        copy.wait_send()
    err_near().wait_recv()
    err_both().start()
    err_core().wait_recv()
    err_both().wait_recv()
    own_err.wait()
    for copy in (err_near(), err_core(), err_both()):
        copy.wait_send()


def middle(ff_pack, heads_all, out_all, x, gain, target, live, at):
    f32, bf16 = jnp.float32, jnp.bfloat16
    rows = ff_pack.shape[0]
    hidden_width = ff_pack.shape[1] // 3
    slot, inner = heads_all.shape
    here, features = x.shape
    blocks = at.blocks
    block = 2 * rows
    gu_chunks = 4 if rows >= 256 else 1
    down_chunks = 2 if rows >= 256 else 1
    dma = pltpu.SemaphoreType.DMA
    vmem = pl.BlockSpec(memory_space=pltpu.VMEM)
    anywhere = pl.BlockSpec(memory_space=pl.ANY)

    def stage_sems(chunks):
        return [
            dma((2, chunks)),
            dma((2, chunks)),
            dma((chunks,)),
            dma((2, blocks, chunks)),
            dma((2, blocks, chunks)),
        ]

    shape = jax.ShapeDtypeStruct
    buffers = [pltpu.VMEM((blocks, here, block), bf16)]
    return pl.pallas_call(
        functools.partial(middle_body, blocks, gu_chunks, down_chunks),
        in_specs=[anywhere, vmem, anywhere, vmem, vmem, vmem, vmem],
        out_specs=[anywhere] * 6 + [vmem] * 4,
        out_shape=[
            shape((features, 3 * hidden_width), bf16),
            shape((slot, features), bf16),
            shape((slot, hidden_width), bf16),
            shape((slot, hidden_width), bf16),
            shape((slot, hidden_width), bf16),
            shape((slot, features), bf16),
            shape((here, features), f32),
            shape((here, features), f32),
            shape((here, features), bf16),
            shape((8, WIDE), f32),
        ],
        scratch_shapes=[
            pltpu.VMEM((2, block, 2 * hidden_width), bf16),
            pltpu.VMEM((blocks, slot, block), bf16),
            pltpu.VMEM((slot, max(2 * hidden_width, features)), f32),
            pltpu.VMEM((slot, hidden_width), bf16),
            pltpu.VMEM((slot, hidden_width), bf16),
            pltpu.VMEM((slot, hidden_width), bf16),
            pltpu.VMEM((blocks, here, block), f32),
        ]
        + buffers * 9
        + [
            pltpu.VMEM((here, features), bf16),
            dma((2,)),
            dma((3, blocks)),
            dma((3, blocks)),
            dma((3, blocks)),
            dma((3, blocks)),
            dma((3,)),
            dma((3,)),
            dma((4,)),
            dma((3,)),
            dma((3 + blocks,)),
        ]
        + stage_sems(gu_chunks)
        + stage_sems(down_chunks),
        compiler_params=pltpu.CompilerParams(
            collective_id=3, has_side_effects=True, vmem_limit_bytes=58 * 1024 * 1024
        ),
        cost_estimate=pl.CostEstimate(
            flops=slot * features * hidden_width * 8, bytes_accessed=400_000_000, transcendentals=0
        ),
    )(ff_pack, heads_all, out_all, x, gain.reshape(1, -1), target, live)


class Collect:
    def __init__(self, lanes, part, rows, cols, send_s, recv_s, load_s, total_s, sems):
        self.lanes, self.part, self.rows, self.cols = lanes, part, rows, cols
        self.send_s, self.recv_s, self.load_s, self.total_s = send_s, recv_s, load_s, total_s
        self.send_sems, self.recv_sems, self.load_sems = sems
        self.loads = [
            (half, place)
            for half in range(2)
            for place in range(lanes.blocks)
            if onward(place, half, lanes.bits)
        ]

    def source(self, place, half, chunk):
        start = self.lanes.block(place) * (2 * self.rows) + half * self.rows
        return self.part.at[pl.ds(pl.multiple_of(start, self.rows), self.rows), self.cols[chunk]]

    def bit_of(self, place, half):
        bits = [bit for bit in range(self.lanes.bits) if (place >> bit) & 1]
        return bits[-1] if half == 0 else bits[0]

    def load(self, half, place):
        index = self.loads.index((half, place))
        start = self.lanes.block(place) * (2 * self.rows) + half * self.rows
        view = self.part.at[pl.ds(pl.multiple_of(start, self.rows), self.rows), :]
        return pltpu.make_async_copy(view, self.load_s.at[index], self.load_sems.at[index])

    def copy(self, place, half, chunk):
        if (half, place) in self.loads:
            source = self.send_s.at[self.loads.index((half, place)), :, self.cols[chunk]]
        else:
            source = self.source(place, half, chunk)
        return remote(
            source,
            self.recv_s.at[half, place - 1, :, self.cols[chunk]],
            self.send_sems.at[half, place, chunk],
            self.recv_sems.at[half, place, chunk],
            self.lanes.across(self.bit_of(place, half)),
        )

    def order(self, half):
        places = list(range(1, self.lanes.blocks))
        places.sort(key=lambda place: -len([b for b in range(8) if (place >> b) & 1]))
        return places

    def start(self):
        for half, place in self.loads:
            self.load(half, place).start()

    def direct(self, chunk):
        for half in range(2):
            for place in self.order(half):
                if (half, place) not in self.loads:
                    self.copy(place, half, chunk).start()

    def add(self, place, half, chunk):
        cols = self.cols[chunk]
        index = self.loads.index((half, place))
        total = self.load_s[index, :, cols].astype(jnp.float32)
        for bit in onward(place, half, self.lanes.bits):
            came = place | (1 << bit)
            self.copy(came, half, chunk).wait_recv()
            total = total + self.recv_s[half, came - 1, :, cols].astype(jnp.float32)
        return total

    def middle(self, chunk):
        for half in range(2):
            for place in self.order(half):
                if (half, place) in self.loads:
                    index = self.loads.index((half, place))
                    if chunk == 0:
                        self.load(half, place).wait()
                    total = self.add(place, half, chunk)
                    self.send_s[index, :, self.cols[chunk]] = total.astype(jnp.bfloat16)
                    self.copy(place, half, chunk).start()

    def last(self, chunk):
        for half in range(2):
            if chunk == 0:
                self.load(half, 0).wait()
            self.total_s[half, :, self.cols[chunk]] = self.add(0, half, chunk)

    def finish(self):
        for chunk in range(len(self.cols)):
            for half in range(2):
                for place in range(1, self.lanes.blocks):
                    self.copy(place, half, chunk).wait_send()


def back_body(
    blocks, in_cols, small_row, part_ref, bc_ref, kv_ref, own_ref, far_ref, core_ref, both_ref,
    resid_ref, x_ref, gain_ref, small_ref, out_ref,
    gin_ref, gsh_ref, gx_ref, sum_ref, gout_ref,
    in_send, in_recv, in_load, in_total, settle_s, settle_r, sh_came, sh_part, sh_send, sh_recv,
    sh_load, sh_total, line_s, line_r, near_s, near_r, swap_s, swap_r,
    buf_both, buf_core, buf_far, pass_s, gx_s, gx_r, small_s, small_r,
    in_ssem, in_rsem, in_lsem, sh_ssem, sh_rsem, sh_lsem, set_ssem, set_rsem, misc_s, misc_r,
    pass_ssem, pass_rsem, small_ssem, small_rsem, out_r, out_ssem, out_rsem,
):
    f32, bf16 = jnp.float32, jnp.bfloat16
    lanes = Lanes(blocks)
    c, t = lanes.c, lanes.t
    rows = gin_ref.shape[0]
    here = own_ref.shape[0]
    wide = bc_ref.shape[1]
    few = gsh_ref.shape[0]
    chunks = len(in_cols)
    step = min(here, 32)
    lanes.greet()
    core_at = (lanes.other, t)
    near_at = (lanes.d, lanes.near)
    far_at = (lanes.d, lanes.far)
    cross_at = (lanes.other, lanes.far)
    first = c == 0
    second = c == 1

    collect = Collect(
        lanes, part_ref, rows, in_cols, in_send, in_recv, in_load, in_total,
        (in_ssem, in_rsem, in_lsem),
    )
    shared = Collect(
        lanes, sh_part, rows, [slice(0, wide)], sh_send, sh_recv, sh_load, sh_total,
        (sh_ssem, sh_rsem, sh_lsem),
    )
    half_kv = kv_ref.shape[1] // 2

    def send_both():
        return remote(both_ref, buf_both, misc_s.at[0], misc_r.at[0], core_at)

    def send_core():
        return remote(core_ref, buf_core, misc_s.at[1], misc_r.at[1], core_at)

    def send_kv():
        return remote(
            kv_ref, sh_came.at[:, : 2 * half_kv], misc_s.at[2], misc_r.at[2], core_at
        )

    def send_bc():
        return remote(bc_ref, sh_came, misc_s.at[3], misc_r.at[3], core_at)

    def out_block(half):
        return out_ref.at[pl.ds(pl.multiple_of(half * rows, rows), rows), :]

    def out_first(half, device):
        return remote(out_block(half), out_r.at[0], out_ssem.at[0], out_rsem.at[0], device)

    def out_second():
        return remote(out_block(1 - c), out_r.at[1], out_ssem.at[1], out_rsem.at[1], cross_at)

    send_both().start()

    @pl.when(lanes.home)
    def _():
        out_first(1 - c, core_at).start()

    @pl.when(lanes.away)
    def _():
        out_first(c, far_at).start()
        out_second().start()

    collect.start()
    for chunk in range(chunks):
        collect.direct(chunk)
    send_core().start()

    @pl.when(first)
    def _():
        send_kv().start()

    @pl.when(second)
    def _():
        send_bc().start()

    parts = 2 if here >= 64 else 1
    share = here // parts

    def send_pass(part):
        view = pl.ds(part * share, share)
        return remote(
            pass_s.at[view, :], buf_far.at[view, :], pass_ssem.at[part], pass_rsem.at[part], near_at
        )

    send_both().wait_recv()
    for part in range(parts):

        @pl.loop(0, share // step)
        def _(i, part=part):
            view = pl.ds(pl.multiple_of(part * share + i * step, step), step)
            pass_s[view, :] = (far_ref[view, :] + buf_both[view, :].astype(f32)).astype(bf16)

        send_pass(part).start()

    @pl.when(first)
    def _():
        send_bc().wait_recv()

        @pl.loop(0, bc_ref.shape[0] // 64)
        def _(i):
            view = pl.ds(pl.multiple_of(i * 64, 64), 64)
            total = bc_ref[view, :].astype(f32) + sh_came[view, :].astype(f32)
            sh_part[view, :] = total.astype(bf16)

    @pl.when(second)
    def _():
        send_kv().wait_recv()

        @pl.loop(0, bc_ref.shape[0] // 64)
        def _(i):
            view = pl.ds(pl.multiple_of(i * 64, 64), 64)
            for piece in range(2):
                kept = pl.ds(piece * half_kv, half_kv)
                sh_part[view, pl.ds(2 * piece * half_kv, half_kv)] = sh_came[view, kept]
                sh_part[view, pl.ds((2 * piece + 1) * half_kv, half_kv)] = kv_ref[view, kept]

    shared.start()
    for chunk in range(chunks):
        collect.middle(chunk)
    shared.direct(0)

    def send_x():
        return remote(gx_s, gx_r, misc_s.at[4], misc_r.at[4], cross_at)

    send_core().wait_recv()
    for part in range(parts):
        send_pass(part).wait_recv()
    small_s[0] = small_ref[...]
    features = gain_ref.shape[1]

    def one_part(i, gains):
        view = pl.ds(pl.multiple_of(i * step, step), step)
        grad = own_ref[view, :] + buf_core[view, :].astype(f32) + buf_far[view, :].astype(f32)
        x = x_ref[view, :].astype(f32)
        scale = lax.rsqrt(jnp.mean(x * x, axis=1, keepdims=True) + EPS)
        gains = gains + jnp.sum(grad * (x * scale), axis=0, keepdims=True)
        grad = grad * gain_ref[...]
        mean = jnp.mean(grad * x, axis=1, keepdims=True)
        result = resid_ref[view, :] + scale * grad - x * (scale * scale * scale * mean)
        gx_ref[view, :] = result
        gx_s[view, :] = result.astype(bf16)
        return gains

    gains = lax.fori_loop(0, here // step, one_part, jnp.zeros((1, features), f32))
    for i in range(features // WIDE):
        small_s[0, small_row + i : small_row + i + 1, :] = gains[:, i * WIDE : (i + 1) * WIDE]

    @pl.when(lanes.away)
    def _():
        send_x().start()

    stops = [near_at, core_at, far_at] + [lanes.across(bit) for bit in range(lanes.bits)]

    def send_small(index):
        return remote(
            small_s.at[index], small_r.at[index], small_ssem.at[index], small_rsem.at[index],
            stops[index],
        )

    def step_small(index):
        send_small(index).wait_recv()
        small_s[index + 1] = small_s[index] + small_r[index]
        if index + 1 < len(stops):
            send_small(index + 1).start()

    send_small(0).start()

    def send_first(chunk, device):
        cols = in_cols[chunk]
        return remote(
            settle_s.at[0, :, cols], settle_r.at[0, :, cols],
            set_ssem.at[0, chunk], set_rsem.at[0, chunk], device,
        )

    def send_second(chunk):
        cols = in_cols[chunk]
        return remote(
            settle_s.at[1, :, cols], settle_r.at[1, :, cols],
            set_ssem.at[1, chunk], set_rsem.at[1, chunk], cross_at,
        )

    for chunk in range(chunks):
        collect.last(chunk)
        cols = in_cols[chunk]

        @pl.when(lanes.home)
        def _(chunk=chunk, cols=cols):
            settle_s[0, :, cols] = in_total[1 - c, :, cols].astype(bf16)
            send_first(chunk, core_at).start()

        @pl.when(lanes.away)
        def _(chunk=chunk, cols=cols):
            settle_s[0, :, cols] = in_total[c, :, cols].astype(bf16)
            send_first(chunk, far_at).start()
            settle_s[1, :, cols] = in_total[1 - c, :, cols].astype(bf16)
            send_second(chunk).start()

        if chunk == 0:
            step_small(0)
            shared.middle(0)
    step_small(1)
    shared.last(0)

    t_high, t_low = lax.div(t, 2), lax.rem(t, 2)
    line = 2 * few

    def send_line():
        return remote(line_s, line_r, misc_s.at[5], misc_r.at[5], far_at)

    def send_near():
        return remote(near_s, near_r, misc_s.at[6], misc_r.at[6], near_at)

    def send_swap():
        return remote(swap_s, swap_r, misc_s.at[7], misc_r.at[7], core_at)

    theirs = pl.ds(pl.multiple_of((1 - t_high) * line, line), line)
    mine = pl.ds(pl.multiple_of(t_high * line, line), line)
    for half in range(2):
        line_s[half] = sh_total[half, theirs, :].astype(bf16)
    send_line().start()
    step_small(2)
    send_line().wait_recv()
    for half in range(2):
        sh_total[half, mine, :] = sh_total[half, mine, :] + line_r[half].astype(f32)
    theirs = pl.ds(pl.multiple_of(t_high * line + (1 - t_low) * few, few), few)
    mine = pl.ds(pl.multiple_of(t_high * line + t_low * few, few), few)
    for half in range(2):
        near_s[half] = sh_total[half, theirs, :].astype(bf16)
    send_near().start()
    for index in range(3, len(stops)):
        step_small(index)
    send_near().wait_recv()
    for half in range(2):
        sh_total[half, mine, :] = sh_total[half, mine, :] + near_r[half].astype(f32)
    swap_s[...] = sh_total[1 - c, mine, :].astype(bf16)
    send_swap().start()
    sum_ref[...] = small_s[len(stops)]

    for chunk in range(chunks):
        cols = in_cols[chunk]
        send_first(chunk, core_at).wait_recv()

        @pl.when(lanes.home)
        def _(chunk=chunk, cols=cols):
            gin_ref[:, cols] = in_total[c, :, cols] + settle_r[0, :, cols].astype(f32)

        @pl.when(lanes.away)
        def _(chunk=chunk, cols=cols):
            send_second(chunk).wait_recv()
            gin_ref[:, cols] = settle_r[0, :, cols].astype(f32) + settle_r[1, :, cols].astype(f32)

    out_first(0, core_at).wait_recv()

    @pl.when(lanes.home)
    def _():
        own_rows = pl.ds(pl.multiple_of(c * rows, rows), rows)
        gout_ref[...] = out_ref[own_rows, :].astype(f32) + out_r[0].astype(f32)
        out_first(1 - c, core_at).wait_send()

    @pl.when(lanes.away)
    def _():
        out_second().wait_recv()
        gout_ref[...] = out_r[0].astype(f32) + out_r[1].astype(f32)
        out_first(c, far_at).wait_send()
        out_second().wait_send()

    send_swap().wait_recv()

    @pl.when(first)
    def _():
        gsh_ref[:, :wide] = sh_total[0, mine, :]
        gsh_ref[:, wide:] = swap_r[...].astype(f32)

    @pl.when(second)
    def _():
        gsh_ref[:, :wide] = swap_r[...].astype(f32)
        gsh_ref[:, wide:] = sh_total[1, mine, :]

    @pl.when(lanes.away)
    def _():
        send_x().wait_recv()

        @pl.loop(0, here // step)
        def _(i):
            view = pl.ds(pl.multiple_of(i * step, step), step)
            gx_ref[view, :] = gx_r[view, :].astype(f32)

    collect.finish()
    shared.finish()
    send_both().wait_send()
    send_core().wait_send()

    @pl.when(first)
    def _():
        send_kv().wait_send()

    @pl.when(second)
    def _():
        send_bc().wait_send()

    for part in range(parts):
        send_pass(part).wait_send()
    for chunk in range(chunks):
        send_first(chunk, core_at).wait_send()

    @pl.when(lanes.away)
    def _():
        send_x().wait_send()
        for chunk in range(chunks):
            send_second(chunk).wait_send()

    for index in range(len(stops)):
        send_small(index).wait_send()
    send_line().wait_send()
    send_near().wait_send()
    send_swap().wait_send()


def back(part_in, bc, kv, act_parts, grad_resid, x, gain, small, small_row, raw_out, few, at):
    f32, bf16 = jnp.float32, jnp.bfloat16
    own, core, far, both = act_parts
    blocks = at.blocks
    features, width = part_in.shape
    rows = features // (2 * blocks)
    here = own.shape[0]
    wide = bc.shape[1]
    chunks = 3
    piece = width // chunks
    in_cols = [slice(i * piece, (i + 1) * piece) for i in range(chunks)]
    loads = sum(bool(onward(p, h, at.bits)) for h in range(2) for p in range(blocks))
    steps = 3 + at.bits
    parts = 2 if here >= 64 else 1
    dma = pltpu.SemaphoreType.DMA
    vmem = pl.BlockSpec(memory_space=pltpu.VMEM)
    anywhere = pl.BlockSpec(memory_space=pl.ANY)
    line = 2 * few
    return pl.pallas_call(
        functools.partial(back_body, blocks, in_cols, small_row),
        in_specs=[anywhere, vmem, vmem, vmem, vmem, anywhere, anywhere]
        + [vmem] * 5,
        out_specs=[vmem] * 5,
        out_shape=[
            jax.ShapeDtypeStruct((rows, width), f32),
            jax.ShapeDtypeStruct((few, 2 * wide), f32),
            jax.ShapeDtypeStruct((here, features), f32),
            jax.ShapeDtypeStruct(small.shape, f32),
            jax.ShapeDtypeStruct((rows, raw_out.shape[1]), f32),
        ],
        scratch_shapes=[
            pltpu.VMEM((loads, rows, width), bf16),
            pltpu.VMEM((2, blocks - 1, rows, width), bf16),
            pltpu.VMEM((loads, rows, width), bf16),
            pltpu.VMEM((2, rows, width), f32),
            pltpu.VMEM((2, rows, width), bf16),
            pltpu.VMEM((2, rows, width), bf16),
            pltpu.VMEM((features, wide), bf16),
            pltpu.VMEM((features, wide), bf16),
            pltpu.VMEM((loads, rows, wide), bf16),
            pltpu.VMEM((2, blocks - 1, rows, wide), bf16),
            pltpu.VMEM((loads, rows, wide), bf16),
            pltpu.VMEM((2, rows, wide), f32),
            pltpu.VMEM((2, line, wide), bf16),
            pltpu.VMEM((2, line, wide), bf16),
            pltpu.VMEM((2, few, wide), bf16),
            pltpu.VMEM((2, few, wide), bf16),
            pltpu.VMEM((few, wide), bf16),
            pltpu.VMEM((few, wide), bf16),
            pltpu.VMEM((here, features), bf16),
            pltpu.VMEM((here, features), bf16),
            pltpu.VMEM((here, features), bf16),
            pltpu.VMEM((here, features), bf16),
            pltpu.VMEM((here, features), bf16),
            pltpu.VMEM((here, features), bf16),
            pltpu.VMEM((steps + 1,) + small.shape, f32),
            pltpu.VMEM((steps,) + small.shape, f32),
            dma((2, blocks, chunks)),
            dma((2, blocks, chunks)),
            dma((loads,)),
            dma((2, blocks, 1)),
            dma((2, blocks, 1)),
            dma((loads,)),
            dma((2, chunks)),
            dma((2, chunks)),
            dma((8,)),
            dma((8,)),
            dma((parts,)),
            dma((parts,)),
            dma((steps,)),
            dma((steps,)),
            pltpu.VMEM((2, rows, raw_out.shape[1]), bf16),
            dma((2,)),
            dma((2,)),
        ],
        compiler_params=pltpu.CompilerParams(
            collective_id=2, has_side_effects=True, vmem_limit_bytes=58 * 1024 * 1024
        ),
        cost_estimate=pl.CostEstimate(
            flops=here * features * 20, bytes_accessed=300_000_000, transcendentals=0
        ),
    )(
        part_in, bc, kv, own, far, core, both, grad_resid, x, gain.reshape(1, -1), small,
        raw_out,
    )


def after(values, *others):
    return lax.optimization_barrier((values,) + others)[0]


def share_rows(values, at):
    far = at.over_z(values)
    core = at.over_core(values)
    both = at.over_core(far)
    return (values, core, far, both)


def sum_rows(pieces, at):
    own, core, far, both = pieces
    bf16 = jnp.bfloat16
    from_both = at.over_core(both.astype(bf16))
    passed = (far + from_both.astype(jnp.float32)).astype(bf16)
    from_far = at.over_z(passed)
    from_core = at.over_core(core.astype(bf16))
    return own + from_core.astype(jnp.float32) + from_far.astype(jnp.float32)


def groups(at):
    return [[d for d in range(at.dp) if d % 2 == c] for c in range(2)]


def gather_blocks(block, at):
    return lax.all_gather(block, "dp", axis=0, tiled=True, axis_index_groups=groups(at))


def sum_blocks(values, at):
    return lax.psum_scatter(
        values, "dp", scatter_dimension=0, tiled=True, axis_index_groups=groups(at)
    )


def pair_up(own, other, at):
    first = at.c == 0
    return jnp.concatenate([jnp.where(first, own, other), jnp.where(first, other, own)], axis=0)


def pair_weight(shard, at):
    first_in = at.column_out(shard)
    second_in = at.swap_away(shard)
    own = jnp.where(at.home, shard, first_in)
    other = jnp.where(at.home, first_in, second_in)
    return pair_up(own, other, at)


def gather_weight(shard, at):
    return gather_blocks(pair_weight(shard, at), at)


def settle_weight(mine, later, at):
    f32 = jnp.float32
    rows = mine.shape[0] // 2
    low, high = mine[:rows], mine[rows:]
    own = jnp.where(at.c == 0, low, high)
    other = jnp.where(at.c == 0, high, low)
    first_in = at.column_back(jnp.where(at.home, other, own))
    second_in = at.swap_away(other)
    first_in, second_in, own, _ = lax.optimization_barrier((first_in, second_in, own, later))
    first_in, second_in = first_in.astype(f32), second_in.astype(f32)
    return first_in + jnp.where(at.home, own.astype(f32), second_in)


def gather_shared(shard, at):
    rows, width = shard.shape
    half = width // 2
    mine = jnp.where(at.c == 0, shard[:, :half], shard[:, half:])
    theirs = jnp.where(at.c == 0, shard[:, half:], shard[:, :half])
    came = at.over_core(theirs)
    both = jnp.stack([jnp.where(at.c == 0, mine, came), jnp.where(at.c == 0, came, mine)])
    near = at.over_z(both)
    lowest = at.t % 2 == 0
    two = jnp.stack([jnp.where(lowest, both, near), jnp.where(lowest, near, both)], axis=1)
    far = at.over_far(two)
    lower = at.t // 2 == 0
    four = jnp.stack([jnp.where(lower, two, far), jnp.where(lower, far, two)], axis=1)
    part = gather_blocks(four.reshape(2 * rows * at.tp, half), at)
    other = at.over_core(part)
    return jnp.where(at.c == 0, part, other), jnp.where(at.c == 0, other, part)


def scatter_shared(grad_bc, grad_kv, earlier, at):
    f32, bf16 = jnp.float32, jnp.bfloat16
    first = at.c == 0
    bc_width = grad_bc.shape[1]
    going = jnp.where(
        first, jnp.pad(grad_kv, ((0, 0), (0, bc_width - grad_kv.shape[1]))), grad_bc
    )
    came = at.over_core(going.astype(bf16)).astype(f32)
    kept = jnp.concatenate(
        [came[:, :HD], grad_kv[:, :HD], came[:, HD : 2 * HD], grad_kv[:, HD:]], axis=1
    )
    total = jnp.where(first, grad_bc + came, kept)
    mine = sum_blocks(after(total.astype(bf16), earlier), at)
    piece = mine.shape[0] // (2 * at.tp)
    line = mine.astype(f32).reshape(2, 2, 2, piece, total.shape[1])
    lower = at.t // 2 == 0
    went = at.over_far(jnp.where(lower, line[:, 1], line[:, 0]).astype(bf16)).astype(f32)
    line = jnp.where(lower, line[:, 0], line[:, 1]) + went
    lowest = at.t % 2 == 0
    went = at.over_z(jnp.where(lowest, line[:, 1], line[:, 0]).astype(bf16)).astype(f32)
    line = jnp.where(lowest, line[:, 0], line[:, 1]) + went
    mine = jnp.where(first, line[0], line[1])
    came = at.over_core(jnp.where(first, line[1], line[0]).astype(bf16)).astype(f32)
    return jnp.concatenate([jnp.where(first, mine, came), jnp.where(first, came, mine)], axis=1)


def sum_tensor(values, at):
    for bit in range(at.tp.bit_length() - 1):
        values = values + at.send(values, lambda d, t: (d, t ^ (1 << bit)))
    return values


def sum_data(values, at):
    for bit in range(at.dp.bit_length() - 1):
        values = values + at.send(values, lambda d, t: (d ^ (1 << bit), t))
    return values


def per_device(
    layer_in,
    teacher,
    lengths,
    input_gain,
    mixer_in_weight,
    step_weight,
    query_weight,
    shared_weight,
    conv_inner,
    conv_shared,
    step_bias,
    decay_log,
    skip_gain,
    inner_gain,
    mixer_out_weight,
    attn_out_weight,
    middle_gain,
    gate_up_weight,
    down_weight,
):
    f32 = jnp.float32
    bf16 = jnp.bfloat16
    contract_last = (((1,), (1,)), ((), ()))
    contract_first = (((0,), (0,)), ((), ()))
    at = Places()
    rows_here = layer_in.shape[0]
    slot_len = rows_here * at.tp
    local_heads = step_bias.shape[0]
    width = inner_gain.shape[0]
    head_dim = width // local_heads
    query_width = query_weight.shape[1]
    hidden_width = down_weight.shape[1]
    bc_width = conv_shared.shape[1]
    w_rows = step_weight.shape[0]

    column_params = jnp.concatenate(
        [conv_inner.reshape(-1), inner_gain, step_bias, decay_log, skip_gain]
    )
    column_params = relocate(column_params, at)
    lane_params = jnp.concatenate(
        [
            column_params[: (KC + 1) * width].reshape(KC + 1, width),
            jnp.repeat(column_params[(KC + 1) * width + 2 * local_heads :], head_dim)[None],
            jnp.zeros((2, width), f32),
        ],
        axis=0,
    )
    head_rows = column_params[(KC + 1) * width :][: 2 * local_heads].reshape(2, local_heads)
    head_rows = jnp.concatenate([head_rows[:1], -jnp.exp(head_rows[1:])], axis=0)
    head_params = jnp.pad(head_rows, ((0, 6), (0, WIDE - local_heads)))
    seg = (
        lax.broadcasted_iota(jnp.int32, (width, WIDE), 0) // head_dim
        == lax.broadcasted_iota(jnp.int32, (width, WIDE), 1)
    ).astype(bf16)
    half = HD // 2
    freqs = jnp.exp(-jnp.log(ROPE_BASE) * 2.0 * jnp.arange(half, dtype=f32) / HD)
    angles = jnp.arange(slot_len).astype(f32)[:, None] * freqs[None, :]
    cosine, sine = jnp.cos(angles), jnp.sin(angles)
    cosine = jnp.concatenate([cosine, cosine], axis=1)
    sine = jnp.concatenate([-sine, sine], axis=1)
    quarters = jnp.arange(at.tp, dtype=jnp.int32)
    order = (at.c ^ (quarters // 2)) + 2 * (at.zq ^ (quarters % 2))

    in_pack = jnp.concatenate(
        [
            mixer_in_weight.reshape(w_rows, 2 * width),
            query_weight,
            step_weight,
            jnp.zeros((w_rows, WIDE - local_heads), bf16),
        ],
        axis=1,
    )
    out_pack = jnp.concatenate([mixer_out_weight, attn_out_weight], axis=1)
    in_all, out_pair, act_all, x_low, shared_full = front(
        in_pack, out_pack, shared_weight, layer_in, input_gain, at
    )
    left, right = shared_full[:, :bc_width], shared_full[:, bc_width:]
    kv_index = at.column * (query_width // HD) // (QH // KVH)
    second = kv_index == 1
    shared_all = jnp.concatenate(
        [
            left,
            jnp.where(second, right[:, HD : 2 * HD], right[:, :HD]),
            jnp.where(second, right[:, 3 * HD :], right[:, 2 * HD : 3 * HD]),
        ],
        axis=1,
    )

    def row_split(values):
        return [values[i * rows_here : (i + 1) * rows_here] for i in range(at.tp)]

    out_all = gather_blocks(out_pair, at)
    proj_shared = jnp.dot(act_all, shared_all, preferred_element_type=f32)
    proj = jnp.dot(act_all, in_all, preferred_element_type=f32)
    target = relocate(after(teacher, proj), at)
    attn_low = attn_forward(order, proj, proj_shared, cosine, sine, query_width, width, bc_width)
    heads_all, y, states = mixer_forward(
        order, proj, proj_shared, attn_low, lane_params, conv_shared, head_params
    )
    ff_pack = jnp.concatenate(
        [gate_up_weight.reshape(w_rows, 2 * hidden_width), down_weight], axis=1
    )
    seq_len = lax.dynamic_index_in_dim(lengths, at.slot, keepdims=False)
    positions = at.quarter * rows_here + jnp.arange(rows_here)
    live = (positions < seq_len).astype(f32)[:, None]
    ff_all, mid_all, gate_low, up_low, hidden, grad_all, resid, error, outputs, loss_part = middle(
        ff_pack, heads_all, out_all, x_low, middle_gain, target, live, at
    )
    err_local = loss_part[0, 0]
    _, norm_mid_back = jax.vjp(rms_norm, resid, middle_gain)
    gate_up_all = ff_all[:, : 2 * hidden_width]
    down_all = ff_all[:, 2 * hidden_width :]
    gate_val, up_val = gate_low.astype(f32), up_low.astype(f32)
    sigmoid_gate = jax.nn.sigmoid(gate_val)

    def weight_grad(left, right):
        return lax.dot_general(left, right, contract_first, preferred_element_type=f32).astype(bf16)

    part_down = weight_grad(grad_all, hidden)
    grad_all, part_down = lax.optimization_barrier((grad_all, part_down))
    raw_down = sum_blocks(part_down, at)
    grad_hidden = jnp.dot(grad_all, down_all, preferred_element_type=f32)
    grad_gate = grad_hidden * up_val * sigmoid_gate * (1.0 + gate_val * (1.0 - sigmoid_gate))
    grad_up = grad_hidden * gate_val * sigmoid_gate
    grad_gu = jnp.concatenate([grad_gate.astype(bf16), grad_up.astype(bf16)], axis=1)
    grad_mid_parts = [
        lax.dot_general(piece, gate_up_all, contract_last, preferred_element_type=f32)
        for piece in row_split(grad_gu)
    ]
    part_gate_up = weight_grad(mid_all, grad_gu)
    grad_mid = sum_rows(grad_mid_parts, at)
    grad_mid, part_gate_up = lax.optimization_barrier((grad_mid, part_gate_up))
    raw_gate_up = sum_blocks(part_gate_up, at)
    grad_resid_norm, grad_middle_gain = norm_mid_back(grad_mid)
    grad_resid = error + grad_resid_norm
    mix_grad_all = jnp.concatenate(share_rows(grad_resid.astype(bf16), at), axis=0)
    grad_heads = jnp.dot(mix_grad_all, out_all, preferred_element_type=f32)
    part_out = weight_grad(mix_grad_all, heads_all)
    grad_heads, part_out, raw_down = lax.optimization_barrier((grad_heads, part_out, raw_down))
    layer_out = relocate(after(outputs, grad_heads), at)
    dq, dkv = attn_backward(
        order, proj, proj_shared, cosine, sine, grad_heads, query_width, width, bc_width
    )
    low_pack, low_shared, dlane, dconv, dhead = mixer_backward(
        order, proj, proj_shared, y, states, grad_heads, dq, dkv, lane_params, conv_shared,
        head_params, seg, query_width,
    )
    low_pack, low_shared, raw_gate_up, part_out = lax.optimization_barrier(
        (low_pack, low_shared, raw_gate_up, part_out)
    )
    raw_out = sum_blocks(part_out, at)
    column = at.column
    lanes_full = lax.dynamic_update_slice(
        jnp.zeros((KC + 1, DI), f32), dlane[: KC + 1], (0, column * width)
    )
    head_stack = jnp.concatenate(
        [dhead[:2, :local_heads], dlane[KC + 1].reshape(1, local_heads, head_dim).sum(2)], axis=0
    )
    heads_full = lax.dynamic_update_slice(
        jnp.zeros((3, H), f32), head_stack, (0, column * local_heads)
    )
    small = (
        jnp.zeros_like(input_gain),
        grad_middle_gain,
        lanes_full,
        dconv[:KC],
        heads_full,
        err_local,
    )
    flat = jnp.concatenate([part.reshape(-1) for part in small])
    padded = -(-flat.shape[0] // 1024) * 1024
    flat = jnp.pad(flat, (0, padded - flat.shape[0])).reshape(-1, WIDE)

    grad_act_parts = [
        lax.dot_general(a, in_all, contract_last, preferred_element_type=f32)
        + lax.dot_general(b, shared_all, contract_last, preferred_element_type=f32)
        for a, b in zip(row_split(low_pack), row_split(low_shared))
    ]
    grad_act_parts[1] = grad_act_parts[1].astype(bf16)
    grad_act_parts[3] = grad_act_parts[3].astype(bf16)
    part_bc = weight_grad(act_all, low_shared[:, :bc_width])
    part_kv = weight_grad(act_all, low_shared[:, bc_width:])
    part_in = weight_grad(act_all, low_pack)
    grad_in, grad_shared_weight, input_grad, flat, grad_out = back(
        part_in, part_bc, part_kv, grad_act_parts, grad_resid, x_low, input_gain, flat, 0,
        raw_out, shared_weight.shape[0], at,
    )
    grad_ff = settle_weight(jnp.concatenate([raw_gate_up, raw_down], axis=1), grad_in, at)
    flat = flat.reshape(-1)
    sums = []
    start = 0
    for part in small:
        sums.append(flat[start : start + part.size].reshape(part.shape))
        start += part.size
    sum_input_gain, sum_middle_gain, sum_lanes, sum_convs, sum_heads, err_total = sums
    lanes_local = lax.dynamic_slice_in_dim(sum_lanes, at.t * width, width, 1)
    heads_local = lax.dynamic_slice_in_dim(sum_heads, at.t * local_heads, local_heads, 1)
    loss = err_total / jnp.sum(lengths).astype(f32)
    query_from = 2 * width
    step_from = query_from + query_width
    return (
        layer_out,
        loss,
        input_grad,
        sum_input_gain,
        grad_in[:, :query_from].reshape(w_rows, 2, width),
        grad_in[:, step_from : step_from + local_heads],
        grad_in[:, query_from:step_from],
        grad_shared_weight,
        lanes_local[:KC],
        sum_convs,
        heads_local[0],
        heads_local[1],
        heads_local[2],
        lanes_local[KC],
        grad_out[:, :width],
        grad_out[:, width:],
        sum_middle_gain,
        grad_ff[:, : 2 * hidden_width].reshape(w_rows, 2, hidden_width),
        grad_ff[:, 2 * hidden_width :],
    )


def solution(mesh):
    placed = (
        P(("dp", "tensor"), None),
        P(("dp", "tensor"), None),
        P(),
        P(),
        P("dp", None, "tensor"),
        P("dp", "tensor"),
        P("dp", "tensor"),
        P(("dp", "tensor"), None),
        P(None, "tensor"),
        P(),
        P("tensor"),
        P("tensor"),
        P("tensor"),
        P("tensor"),
        P("dp", "tensor"),
        P("dp", "tensor"),
        P(),
        P("dp", None, "tensor"),
        P("dp", "tensor"),
    )
    return jax.shard_map(
        per_device,
        mesh=mesh,
        in_specs=placed,
        out_specs=(
            P(("dp", "tensor"), None),
            P(),
            P(("dp", "tensor"), None),
            P(),
            P("dp", None, "tensor"),
            P("dp", "tensor"),
            P("dp", "tensor"),
            P(("dp", "tensor"), None),
            P(None, "tensor"),
            P(),
            P("tensor"),
            P("tensor"),
            P("tensor"),
            P("tensor"),
            P("dp", "tensor"),
            P("dp", "tensor"),
            P(),
            P("dp", None, "tensor"),
            P("dp", "tensor"),
        ),
        check_vma=False,
    )
```

```python
import functools

import jax
import jax.numpy as jnp
from jax import lax
from jax.experimental import pallas as pl
from jax.experimental.pallas import tpu as pltpu
from jax.sharding import PartitionSpec as P

H = 48
KC = 4
QH = 8
KVH = 2
HD = 128
DI = 3072

EPS = 1e-05
ROPE_BASE = 100000000000.0


def rms_norm(values, gain):
    return values * lax.rsqrt(jnp.mean(values * values, axis=-1, keepdims=True) + EPS) * gain


def low_dot(left, right, dims):
    return lax.dot_general(left, right, (dims, ((), ())), preferred_element_type=jnp.float32)


NN = ((1,), (0,))
NT = ((1,), (1,))
TN = ((0,), (0,))
CHUNK = 128
ROWS = 256
WIDE = 128
FAR = -1e30


def exact_dot(ones, values, parts=3):
    total = None
    for _ in range(parts):
        part = values.astype(jnp.bfloat16)
        values = values - part.astype(jnp.float32)
        term = low_dot(ones, part, NN)
        total = term if total is None else total + term
    return total


def split_dot(values, ones, parts=2):
    total = None
    for _ in range(parts):
        part = values.astype(jnp.bfloat16)
        values = values - part.astype(jnp.float32)
        term = low_dot(part, ones, NN)
        total = term if total is None else total + term
    return total


def sigmoid(v):
    return 1.0 / (1.0 + jnp.exp(-v))


def softplus(v):
    return jnp.maximum(v, 0.0) + jnp.log1p(jnp.exp(-jnp.abs(v)))


def iota(shape, axis):
    return lax.broadcasted_iota(jnp.int32, shape, axis)


def spin(values, cosine, sine):
    return values * cosine + pltpu.roll(values, HD // 2, 1) * sine


def unspin(values, cosine, sine):
    return values * cosine - pltpu.roll(values, HD // 2, 1) * sine


def attn_probs(query_low, key_low, first_row, scale):
    scores = low_dot(query_low, key_low, NT) * scale
    rows, keys = scores.shape
    allowed = iota((rows, keys), 1) <= iota((rows, keys), 0) + first_row
    scores = jnp.where(allowed, scores, FAR)
    top = jnp.max(scores, axis=1, keepdims=True)
    weights = jnp.exp(scores - top)
    return weights / jnp.sum(weights, axis=1, keepdims=True)


def attn_fwd_body(order, q_ref, kv_ref, cos_ref, sin_ref, out_ref, key_s, value_s):
    bf16 = jnp.bfloat16
    step = pl.program_id(0)
    cosine, sine = cos_ref[...], sin_ref[...]
    rows = pl.ds(pl.multiple_of(step * ROWS, ROWS), ROWS)
    key_s[rows, :] = spin(kv_ref[:, :HD], cosine, sine).astype(bf16)
    value_s[rows, :] = kv_ref[:, HD:].astype(bf16)
    heads = q_ref.shape[1] // HD
    blocks = key_s.shape[0] // ROWS
    for block in range(blocks):

        @pl.when(step == block)
        def _(block=block):
            keys = (block + 1) * ROWS
            for head in range(heads):
                lanes = slice(head * HD, (head + 1) * HD)
                query = spin(q_ref[:, lanes], cosine, sine).astype(bf16)
                probs = attn_probs(query, key_s[:keys, :], block * ROWS, HD**-0.5)
                out_ref[:, lanes] = low_dot(
                    probs.astype(bf16), value_s[:keys, :], NN
                ).astype(bf16)


def attn_bwd_body(
    order, q_ref, kv_ref, cos_ref, sin_ref, grad_ref, all_cos, all_sin, dq_ref, dkv_ref,
    key_s, value_s, dkey_s, dvalue_s,
):
    bf16, f32 = jnp.bfloat16, jnp.float32
    step = pl.program_id(0)

    @pl.when(step == 0)
    def _():
        dkey_s[...] = jnp.zeros_like(dkey_s)
        dvalue_s[...] = jnp.zeros_like(dvalue_s)

    cosine, sine = cos_ref[...], sin_ref[...]
    rows = pl.ds(pl.multiple_of(step * ROWS, ROWS), ROWS)
    key_s[rows, :] = spin(kv_ref[:, :HD], cosine, sine).astype(bf16)
    value_s[rows, :] = kv_ref[:, HD:].astype(bf16)
    heads = q_ref.shape[1] // HD
    blocks = key_s.shape[0] // ROWS
    scale = HD**-0.5
    for block in range(blocks):

        @pl.when(step == block)
        def _(block=block):
            keys = (block + 1) * ROWS
            for head in range(heads):
                lanes = slice(head * HD, (head + 1) * HD)
                query = spin(q_ref[:, lanes], cosine, sine).astype(bf16)
                probs = attn_probs(query, key_s[:keys, :], block * ROWS, scale)
                grad = grad_ref[:, lanes].astype(bf16)
                dprobs = low_dot(grad, value_s[:keys, :], NT)
                dvalue_s[:keys, :] += low_dot(probs.astype(bf16), grad, TN)
                inner = jnp.sum(dprobs * probs, axis=1, keepdims=True)
                dscores = (probs * (dprobs - inner) * scale).astype(bf16)
                dquery = low_dot(dscores, key_s[:keys, :], NN)
                dkey_s[:keys, :] += low_dot(dscores, query, TN)
                dq_ref[:, lanes] = unspin(dquery, cosine, sine).astype(bf16)

    @pl.when(step == blocks - 1)
    def _():
        dkv_ref[:, :HD] = unspin(dkey_s[...], all_cos[...], all_sin[...]).astype(bf16)
        dkv_ref[:, HD:] = dvalue_s[...].astype(bf16)


def conv_taps(ext, taps, first, width):
    rows = ext.shape[0] - 8
    total = None
    for tap in range(width):
        at = 8 - (width - 1) + tap
        term = ext[at : at + rows, :] * taps[first + tap : first + tap + 1, :]
        total = term if total is None else total + term
    return total


def decays(steps, head_params, tri):
    shifted = steps + head_params[0:1, :]
    dt = softplus(shifted)
    la = dt * head_params[1:2, :]
    cum = exact_dot(tri, la)
    return shifted, dt, la, cum


def spread_lanes(values, pair, first):
    rows = values.shape[0]
    a = jnp.broadcast_to(values[:, 2 * pair : 2 * pair + 1], (rows, WIDE))
    b = jnp.broadcast_to(values[:, 2 * pair + 1 : 2 * pair + 2], (rows, WIDE))
    return a, b, jnp.where(first, a, b)


def mixer_fwd_body(
    order, gate_ref, inner_ref, step_ref, bc_ref, attn_ref, lane_ref, conv_ref, head_ref,
    out_ref, y_ref, state_ref, ext_s, extbc_s, state_s, x_s,
):
    bf16, f32 = jnp.bfloat16, jnp.float32
    step = pl.program_id(0)
    width = inner_ref.shape[1]
    states = bc_ref.shape[1] // 2

    @pl.when(step == 0)
    def _():
        ext_s[0:8, :] = jnp.zeros((8, width), f32)
        extbc_s[0:8, :] = jnp.zeros((8, 2 * states), f32)
        state_s[...] = jnp.zeros_like(state_s)

    ext_s[8:, :] = inner_ref[...]
    extbc_s[8:, :] = bc_ref[...]
    pre = conv_taps(ext_s, lane_ref, 0, KC)
    x_s[...] = pre * sigmoid(pre)
    pre = conv_taps(extbc_s, conv_ref, 0, KC)
    bc = (pre * sigmoid(pre)).astype(bf16)
    ext_s[0:8, :] = ext_s[ROWS : ROWS + 8, :]
    extbc_s[0:8, :] = extbc_s[ROWS : ROWS + 8, :]
    row, col = iota((CHUNK, CHUNK), 0), iota((CHUNK, CHUNK), 1)
    causal = row >= col
    tri = jnp.where(causal, 1.0, 0.0).astype(bf16)
    first = iota((CHUNK, WIDE), 1) < WIDE // 2
    for sub in range(ROWS // CHUNK):
        lo = sub * CHUNK
        b_low = bc[lo : lo + CHUNK, :states]
        c_low = bc[lo : lo + CHUNK, states:]
        _, dt, _, cum = decays(step_ref[lo : lo + CHUNK, :], head_ref, tri)
        cum_t = cum.T
        cross = low_dot(c_low, b_low, NT)
        state_low = state_s[...].astype(bf16)
        state_ref[sub] = state_low
        b_t = b_low.T
        for pair in range(width // WIDE):
            lanes = slice(pair * WIDE, (pair + 1) * WIDE)
            cum_a, cum_b, cum_p = spread_lanes(cum, pair, first)
            _, _, dt_p = spread_lanes(dt, pair, first)
            weights = []
            for wide, head in ((cum_a, 2 * pair), (cum_b, 2 * pair + 1)):
                gap = jnp.where(causal, wide - cum_t[head : head + 1, :], FAR)
                weights.append((cross * jnp.exp(gap)).astype(bf16))
            x = x_s[lo : lo + CHUNK, lanes]
            scaled = x * dt_p
            zero = jnp.zeros_like(scaled)
            stacked = jnp.concatenate(
                [jnp.where(first, scaled, zero), jnp.where(first, zero, scaled)], axis=0
            ).astype(bf16)
            y = low_dot(jnp.concatenate(weights, axis=1), stacked, NN)
            y = y + jnp.exp(cum_p) * low_dot(c_low, state_low[:, lanes], NN)
            y_ref[lo : lo + CHUNK, lanes] = y + lane_ref[5:6, lanes] * x
            last = cum_p[CHUNK - 1 : CHUNK, :]
            ends = (scaled * jnp.exp(last - cum_p)).astype(bf16)
            state_s[:, lanes] = state_s[:, lanes] * jnp.exp(last) + low_dot(b_t, ends, NN)
    gate = gate_ref[...]
    gated = y_ref[...] * (gate * sigmoid(gate))
    scale = lax.rsqrt(jnp.mean(gated * gated, axis=1, keepdims=True) + EPS)
    out_ref[:, :width] = (gated * scale * lane_ref[4:5, :]).astype(bf16)
    out_ref[:, width:] = attn_ref[...]


def mixer_bwd_body(
    order, gate_ref, inner_ref, before_ref, step_ref, bc_ref, bcbefore_ref, y_ref, state_ref,
    grad_ref, dq_ref, dkv_ref, lane_ref, conv_ref, head_ref, seg_ref,
    low_ref, lowsh_ref, dlane_ref, dconv_ref, dhead_ref,
    ext_s, extbc_s, pre_s, prebc_s, x_s, bc_s, g_s, dx_s, dbc_s, dpre_s, dprebc_s, dstate_s,
    z_s, rows_s,
):
    bf16, f32 = jnp.bfloat16, jnp.float32
    step = pl.program_id(0)
    blocks = pl.num_programs(0)
    width = inner_ref.shape[1]
    states = bc_ref.shape[1] // 2
    query_width = dq_ref.shape[1]

    @pl.when(step == 0)
    def _():
        dlane_ref[...] = jnp.zeros_like(dlane_ref)
        dconv_ref[...] = jnp.zeros_like(dconv_ref)
        dhead_ref[...] = jnp.zeros_like(dhead_ref)
        dstate_s[...] = jnp.zeros_like(dstate_s)
        dpre_s[ROWS:, :] = jnp.zeros((8, width), f32)
        dprebc_s[ROWS:, :] = jnp.zeros((8, 2 * states), f32)
        z_s[...] = jnp.zeros_like(z_s)
        rows_s[...] = jnp.zeros_like(rows_s)

    keep = jnp.where(step == blocks - 1, 0.0, 1.0)
    ext_s[0:8, :] = before_ref[...] * keep
    extbc_s[0:8, :] = bcbefore_ref[...] * keep
    ext_s[8:, :] = inner_ref[...]
    extbc_s[8:, :] = bc_ref[...]
    pre = conv_taps(ext_s, lane_ref, 0, KC)
    pre_s[...] = pre
    x_s[...] = pre * sigmoid(pre)
    pre = conv_taps(extbc_s, conv_ref, 0, KC)
    prebc_s[...] = pre
    bc_s[...] = (pre * sigmoid(pre)).astype(bf16)

    gate = gate_ref[...]
    sig = sigmoid(gate)
    gate_act = gate * sig
    y = y_ref[...]
    gated = y * gate_act
    scale = lax.rsqrt(jnp.mean(gated * gated, axis=1, keepdims=True) + EPS)
    grad = grad_ref[...]
    dlane_ref[4:5, :] += jnp.sum(grad * gated * scale, axis=0, keepdims=True)
    grad = grad * lane_ref[4:5, :]
    mean = jnp.mean(grad * gated, axis=1, keepdims=True)
    dgated = scale * grad - gated * (scale * scale * scale * mean)
    g_s[...] = dgated * gate_act
    low_ref[:, :width] = (dgated * y * sig * (1.0 + gate * (1.0 - sig))).astype(bf16)

    row, col = iota((CHUNK, CHUNK), 0), iota((CHUNK, CHUNK), 1)
    tri = jnp.where(row >= col, 1.0, 0.0).astype(bf16)
    tri_up = jnp.where(row <= col, 1.0, 0.0).astype(bf16)
    later = row <= col
    first = iota((CHUNK, WIDE), 1) < WIDE // 2
    last_row = iota((CHUNK, WIDE), 0) == CHUNK - 1
    for sub in reversed(range(ROWS // CHUNK)):
        lo = sub * CHUNK
        b_low = bc_s[lo : lo + CHUNK, :states]
        c_low = bc_s[lo : lo + CHUNK, states:]
        shifted, dt, la, cum = decays(step_ref[lo : lo + CHUNK, :], head_ref, tri)
        cum_t = cum.T
        cross_t = low_dot(b_low, c_low, NT)
        c_t = c_low.T
        state_low = state_ref[sub]
        dstate_low = dstate_s[...].astype(bf16)
        dcross_t = jnp.zeros((CHUNK, CHUNK), f32)
        db = jnp.zeros((CHUNK, states), f32)
        dc = jnp.zeros((CHUNK, states), f32)
        for pair in range(width // WIDE):
            lanes = slice(pair * WIDE, (pair + 1) * WIDE)
            cum_a, cum_b, cum_p = spread_lanes(cum, pair, first)
            _, _, dt_p = spread_lanes(dt, pair, first)
            x = x_s[lo : lo + CHUNK, lanes]
            g = g_s[lo : lo + CHUNK, lanes]
            scaled = x * dt_p
            scaled_low = scaled.astype(bf16)
            zero = jnp.zeros_like(g)
            g_stack = jnp.concatenate(
                [jnp.where(first, g, zero), jnp.where(first, zero, g)], axis=0
            ).astype(bf16)
            dweights_t = low_dot(scaled_low, g_stack, NT)
            weights_t = []
            for place, wide, head in ((0, cum_a, 2 * pair), (1, cum_b, 2 * pair + 1)):
                gap = jnp.where(later, cum_t[head : head + 1, :] - wide, FAR)
                grow = jnp.exp(gap)
                weight = (cross_t * grow).astype(bf16)
                weights_t.append(weight)
                dweight = dweights_t[:, place * CHUNK : (place + 1) * CHUNK]
                dcross_t = dcross_t + dweight * grow
                rows_s[head : head + 1, :] = jnp.sum(
                    dweight * weight.astype(f32), axis=0, keepdims=True
                )
            dx_in = low_dot(jnp.concatenate(weights_t, axis=1), g_stack, NN)
            grown = jnp.exp(cum_p)
            last = cum_p[CHUNK - 1 : CHUNK, :]
            tail = jnp.exp(last - cum_p)
            last = jnp.exp(last)
            dx_tail = tail * low_dot(b_low, dstate_low[:, lanes], NN)
            dscaled = dx_in + dx_tail
            g_grown = g * grown
            g_low = g_grown.astype(bf16)
            ends = (scaled * tail).astype(bf16)
            carried = low_dot(c_low, state_low[:, lanes], NN)
            dc = dc + low_dot(g_low, state_low[:, lanes], NT)
            db = db + low_dot(ends, dstate_low[:, lanes], NT)
            dstate = dstate_s[:, lanes]
            kept = jnp.sum(dstate * state_low[:, lanes].astype(f32), axis=0, keepdims=True) * last
            dstate_s[:, lanes] = dstate * last + low_dot(c_t, g_low, NN)
            tails = scaled * dx_tail
            z_s[0:CHUNK, lanes] = g_grown * carried - tails - scaled_low.astype(f32) * dx_in
            z_s[CHUNK : 2 * CHUNK, lanes] = dscaled * x
            z_s[2 * CHUNK : 2 * CHUNK + 1, lanes] = (
                jnp.sum(tails, axis=0, keepdims=True) + kept
            )
            dx_s[lo : lo + CHUNK, lanes] = dscaled * dt_p + lane_ref[5:6, lanes] * g
            dlane_ref[5:6, lanes] += jnp.sum(g * x, axis=0, keepdims=True)
        sums = split_dot(z_s[...], seg_ref[...])
        dcum = sums[0:CHUNK, :] + rows_s[...].T
        dcum = dcum + jnp.where(last_row, sums[2 * CHUNK : 2 * CHUNK + 1, :], 0.0)
        dla = exact_dot(tri_up, dcum)
        ddt = sums[CHUNK : 2 * CHUNK, :] + dla * head_ref[1:2, :]
        dsteps = ddt * sigmoid(shifted)
        dhead_ref[0:1, :] += jnp.sum(dsteps, axis=0, keepdims=True)
        dhead_ref[1:2, :] += jnp.sum(dla * la, axis=0, keepdims=True)
        low_ref[lo : lo + CHUNK, 2 * width + query_width :] = dsteps.astype(bf16)
        dcross_low = dcross_t.astype(bf16)
        dbc_s[lo : lo + CHUNK, :states] = db + low_dot(dcross_low, c_low, NN)
        dbc_s[lo : lo + CHUNK, states:] = dc + low_dot(dcross_low, b_low, TN)

    def conv_back(pre_ref, dact, dpre_ref, ext, taps, dtaps_ref):
        pre = pre_ref[...]
        sig = sigmoid(pre)
        dpre = dact * (sig * (1.0 + pre * (1.0 - sig)))
        dpre_ref[0:ROWS, :] = dpre
        total = None
        for tap in range(KC):
            ahead = KC - 1 - tap
            term = dpre_ref[ahead : ahead + ROWS, :] * taps[tap : tap + 1, :]
            total = term if total is None else total + term
            at = 8 - (KC - 1) + tap
            dtaps_ref[tap : tap + 1, :] += jnp.sum(
                dpre * ext[at : at + ROWS, :], axis=0, keepdims=True
            )
        dpre_ref[ROWS:, :] = dpre_ref[0:8, :]
        return total

    dinner = conv_back(pre_s, dx_s[...], dpre_s, ext_s, lane_ref, dlane_ref)
    low_ref[:, width : 2 * width] = dinner.astype(bf16)
    dbc = conv_back(prebc_s, dbc_s[...], dprebc_s, extbc_s, conv_ref, dconv_ref)
    lowsh_ref[:, : 2 * states] = dbc.astype(bf16)
    lowsh_ref[:, 2 * states :] = dkv_ref[...]
    low_ref[:, 2 * width : 2 * width + query_width] = dq_ref[...]


def block_at(rows, cols, col):
    return pl.BlockSpec((rows, cols), lambda i, order: (order[i], col))


def whole_at(shape):
    return pl.BlockSpec(shape, lambda i, order: (0,) * len(shape))


def kernel_params():
    return pltpu.CompilerParams(
        dimension_semantics=("arbitrary",), vmem_limit_bytes=56 * 1024 * 1024
    )


def attn_forward(order, proj, proj_shared, cosine, sine, query_width, width, bc_width):
    slot = proj.shape[0]
    scratch = [pltpu.VMEM((slot, HD), jnp.bfloat16)] * 2
    return pl.pallas_call(
        attn_fwd_body,
        grid_spec=pltpu.PrefetchScalarGridSpec(
            num_scalar_prefetch=1,
            grid=(slot // ROWS,),
            in_specs=[
                block_at(ROWS, query_width, 2 * width // query_width),
                block_at(ROWS, 2 * HD, bc_width // (2 * HD)),
                pl.BlockSpec((ROWS, HD), lambda i, order: (i, 0)),
                pl.BlockSpec((ROWS, HD), lambda i, order: (i, 0)),
            ],
            out_specs=block_at(ROWS, query_width, 0),
            scratch_shapes=scratch,
        ),
        out_shape=jax.ShapeDtypeStruct((slot, query_width), jnp.bfloat16),
        compiler_params=kernel_params(),
        cost_estimate=pl.CostEstimate(
            flops=slot * slot * query_width * 3,
            bytes_accessed=slot * 4 * (query_width + 4 * HD),
            transcendentals=slot * slot * query_width // HD,
        ),
    )(order, proj, proj_shared, cosine, sine)


def attn_backward(order, proj, proj_shared, cosine, sine, grad_heads, query_width, width, bc_width):
    slot = proj.shape[0]
    return pl.pallas_call(
        attn_bwd_body,
        grid_spec=pltpu.PrefetchScalarGridSpec(
            num_scalar_prefetch=1,
            grid=(slot // ROWS,),
            in_specs=[
                block_at(ROWS, query_width, 2 * width // query_width),
                block_at(ROWS, 2 * HD, bc_width // (2 * HD)),
                pl.BlockSpec((ROWS, HD), lambda i, order: (i, 0)),
                pl.BlockSpec((ROWS, HD), lambda i, order: (i, 0)),
                block_at(ROWS, query_width, width // query_width),
                whole_at((slot, HD)),
                whole_at((slot, HD)),
            ],
            out_specs=[block_at(ROWS, query_width, 0), whole_at((slot, 2 * HD))],
            scratch_shapes=[pltpu.VMEM((slot, HD), jnp.bfloat16)] * 2
            + [pltpu.VMEM((slot, HD), jnp.float32)] * 2,
        ),
        out_shape=[
            jax.ShapeDtypeStruct((slot, query_width), jnp.bfloat16),
            jax.ShapeDtypeStruct((slot, 2 * HD), jnp.bfloat16),
        ],
        compiler_params=kernel_params(),
        cost_estimate=pl.CostEstimate(
            flops=slot * slot * query_width * 8,
            bytes_accessed=slot * 4 * (2 * query_width + 6 * HD),
            transcendentals=slot * slot * query_width // HD,
        ),
    )(order, proj, proj_shared, cosine, sine, grad_heads, cosine, sine)


def mixer_forward(order, proj, proj_shared, attn_low, lane_params, conv_shared, head_params):
    slot = proj.shape[0]
    f32, bf16 = jnp.float32, jnp.bfloat16
    width = lane_params.shape[1]
    bc_width = conv_shared.shape[1]
    query_width = attn_low.shape[1]
    chunks = ROWS // CHUNK
    return pl.pallas_call(
        mixer_fwd_body,
        grid_spec=pltpu.PrefetchScalarGridSpec(
            num_scalar_prefetch=1,
            grid=(slot // ROWS,),
            in_specs=[
                block_at(ROWS, width, 0),
                block_at(ROWS, width, 1),
                block_at(ROWS, WIDE, (2 * width + query_width) // WIDE),
                block_at(ROWS, bc_width, 0),
                block_at(ROWS, query_width, 0),
                whole_at(lane_params.shape),
                whole_at(conv_shared.shape),
                whole_at(head_params.shape),
            ],
            out_specs=[
                block_at(ROWS, width + query_width, 0),
                pl.BlockSpec((ROWS, width), lambda i, order: (i, 0)),
                pl.BlockSpec((chunks, bc_width // 2, width), lambda i, order: (i, 0, 0)),
            ],
            scratch_shapes=[
                pltpu.VMEM((ROWS + 8, width), f32),
                pltpu.VMEM((ROWS + 8, bc_width), f32),
                pltpu.VMEM((bc_width // 2, width), f32),
                pltpu.VMEM((ROWS, width), f32),
            ],
        ),
        out_shape=[
            jax.ShapeDtypeStruct((slot, width + query_width), bf16),
            jax.ShapeDtypeStruct((slot, width), f32),
            jax.ShapeDtypeStruct((slot // CHUNK, bc_width // 2, width), bf16),
        ],
        compiler_params=kernel_params(),
        cost_estimate=pl.CostEstimate(
            flops=slot * width * bc_width * 8,
            bytes_accessed=slot * width * 20,
            transcendentals=slot * width * 8,
        ),
    )(order, proj, proj, proj, proj_shared, attn_low, lane_params, conv_shared, head_params)


def mixer_backward(
    order, proj, proj_shared, y, states, grad_heads, dq, dkv, lane_params, conv_shared,
    head_params, seg, query_width,
):
    slot = proj.shape[0]
    f32, bf16 = jnp.float32, jnp.bfloat16
    width = lane_params.shape[1]
    bc_width = conv_shared.shape[1]
    blocks = slot // ROWS
    chunks = ROWS // CHUNK

    def back(rows, cols, col):
        return pl.BlockSpec((rows, cols), lambda i, order: (order[blocks - 1 - i], col))

    def straight(shape):
        return pl.BlockSpec(
            shape, lambda i, order: (blocks - 1 - i,) + (0,) * (len(shape) - 1)
        )

    def before(cols, col):
        return pl.BlockSpec(
            (8, cols),
            lambda i, order: (
                order[jnp.maximum(blocks - 2 - i, 0)] * (ROWS // 8) + ROWS // 8 - 1,
                col,
            ),
        )

    return pl.pallas_call(
        mixer_bwd_body,
        grid_spec=pltpu.PrefetchScalarGridSpec(
            num_scalar_prefetch=1,
            grid=(blocks,),
            in_specs=[
                back(ROWS, width, 0),
                back(ROWS, width, 1),
                before(width, 1),
                back(ROWS, WIDE, (2 * width + query_width) // WIDE),
                back(ROWS, bc_width, 0),
                before(bc_width, 0),
                straight((ROWS, width)),
                straight((chunks, bc_width // 2, width)),
                back(ROWS, width, 0),
                back(ROWS, query_width, 0),
                straight((ROWS, 2 * HD)),
                whole_at(lane_params.shape),
                whole_at(conv_shared.shape),
                whole_at(head_params.shape),
                whole_at(seg.shape),
            ],
            out_specs=[
                back(ROWS, 2 * width + query_width + WIDE, 0),
                back(ROWS, bc_width + 2 * HD, 0),
                whole_at((8, width)),
                whole_at((8, bc_width)),
                whole_at((8, WIDE)),
            ],
            scratch_shapes=[
                pltpu.VMEM((ROWS + 8, width), f32),
                pltpu.VMEM((ROWS + 8, bc_width), f32),
                pltpu.VMEM((ROWS, width), f32),
                pltpu.VMEM((ROWS, bc_width), f32),
                pltpu.VMEM((ROWS, width), f32),
                pltpu.VMEM((ROWS, bc_width), bf16),
                pltpu.VMEM((ROWS, width), f32),
                pltpu.VMEM((ROWS, width), f32),
                pltpu.VMEM((ROWS, bc_width), f32),
                pltpu.VMEM((ROWS + 8, width), f32),
                pltpu.VMEM((ROWS + 8, bc_width), f32),
                pltpu.VMEM((bc_width // 2, width), f32),
                pltpu.VMEM((2 * CHUNK + 8, width), f32),
                pltpu.VMEM((WIDE, CHUNK), f32),
            ],
        ),
        out_shape=[
            jax.ShapeDtypeStruct((slot, 2 * width + query_width + WIDE), bf16),
            jax.ShapeDtypeStruct((slot, bc_width + 2 * HD), bf16),
            jax.ShapeDtypeStruct((8, width), f32),
            jax.ShapeDtypeStruct((8, bc_width), f32),
            jax.ShapeDtypeStruct((8, WIDE), f32),
        ],
        compiler_params=kernel_params(),
        cost_estimate=pl.CostEstimate(
            flops=slot * width * bc_width * 20,
            bytes_accessed=slot * width * 40,
            transcendentals=slot * width * 16,
        ),
    )(
        order, proj, proj, proj, proj, proj_shared, proj_shared, y, states, grad_heads, dq, dkv,
        lane_params, conv_shared, head_params, seg,
    )


class Places:
    def __init__(self):
        self.dp = lax.axis_size("dp")
        self.tp = lax.axis_size("tensor")
        d = lax.axis_index("dp")
        t = lax.axis_index("tensor")
        self.d, self.t = d, t
        self.c = d % 2
        self.k = d // 2
        self.zq = t % 2
        self.home = self.c == t // 2
        self.quarter = 2 * self.c + self.zq
        self.column = self.zq + 2 * self.c
        self.slot = 2 * self.k + t // 2
        self.blocks = self.dp // 2
        self.bits = self.blocks.bit_length() - 1

    def pairs(self, where_to):
        out = []
        for d in range(self.dp):
            for t in range(self.tp):
                target = where_to(d, t)
                if target is not None:
                    out.append((d * self.tp + t, target[0] * self.tp + target[1]))
        return out

    def send(self, values, where_to):
        return lax.ppermute(values, ("dp", "tensor"), self.pairs(where_to))

    def over_core(self, values):
        return self.send(values, lambda d, t: (d ^ 1, t))

    def over_z(self, values):
        return self.send(values, lambda d, t: (d, t ^ 1))

    def over_far(self, values):
        return self.send(values, lambda d, t: (d, t ^ 2))

    def over_bit(self, values, bit):
        return self.send(values, lambda d, t: (d ^ (2 << bit), t))

    def swap_away(self, values):
        def where_to(d, t):
            if d % 2 == t // 2:
                return None
            return (d ^ 1, t ^ 2)

        return self.send(values, where_to)

    def column_out(self, values):
        def where_to(d, t):
            if d % 2 == t // 2:
                return (d, t ^ 2)
            return (d ^ 1, t)

        return self.send(values, where_to)

    def column_back(self, values):
        def where_to(d, t):
            if d % 2 == t // 2:
                return (d ^ 1, t)
            return (d, t ^ 2)

        return self.send(values, where_to)


def relocate(values, at):
    return jnp.where(at.home, values, at.swap_away(values))


MESH = pl.DeviceIdType.MESH


class Lanes:
    def __init__(self, blocks):
        d = lax.axis_index("dp")
        t = lax.axis_index("tensor")
        self.c = lax.rem(d, 2)
        self.k = lax.div(d, 2)
        self.d, self.t = d, t
        self.home = self.c == lax.div(t, 2)
        self.away = self.c != lax.div(t, 2)
        self.other = d + 1 - 2 * self.c
        self.near = t + 1 - 2 * lax.rem(t, 2)
        self.far = lax.rem(t + 2, 4)
        self.blocks = blocks
        self.bits = blocks.bit_length() - 1

    def block(self, place):
        value = self.k
        for bit in range(self.bits):
            if (place >> bit) & 1:
                value = value + (1 << bit) * (1 - 2 * lax.rem(lax.div(self.k, 1 << bit), 2))
        return value

    def across(self, bit):
        return (2 * self.block(1 << bit) + self.c, self.t)

    def greet(self):
        partners = [
            (self.other, self.t),
            (self.d, self.near),
            (self.d, self.far),
            (self.other, self.far),
        ] + [self.across(bit) for bit in range(self.bits)]
        barrier = pltpu.get_barrier_semaphore()
        for partner in partners:
            pl.semaphore_signal(barrier, inc=1, device_id=partner, device_id_type=MESH)
        pl.semaphore_wait(barrier, len(partners))


def remote(src, dst, send_sem, recv_sem, device):
    return pltpu.make_async_remote_copy(
        src_ref=src,
        dst_ref=dst,
        send_sem=send_sem,
        recv_sem=recv_sem,
        device_id=device,
        device_id_type=MESH,
    )


def onward(place, half, bits):
    if half == 0:
        return [bit for bit in range(bits) if place < (1 << bit)]
    return [bit for bit in reversed(range(bits)) if place % (2 << bit) == 0]


class Spread:
    def __init__(self, lanes, full, rows, chunks, send_sems, recv_sems, cols=slice(None), first=None):
        self.lanes, self.full, self.rows, self.chunks = lanes, full, rows, chunks
        self.cols, self.first = cols, first
        self.piece = rows // chunks
        self.send_sems, self.recv_sems = send_sems, recv_sems

    def view(self, place, half, chunk):
        start = self.lanes.block(place) * (2 * self.rows) + half * self.rows + chunk * self.piece
        return self.full.at[pl.ds(pl.multiple_of(start, self.piece), self.piece), self.cols]

    def copy(self, place, half, chunk, bit):
        view = self.view(place, half, chunk)
        to = place | (1 << bit)
        source = view
        if place == 0 and self.first is not None:
            start = half * self.rows + chunk * self.piece
            source = self.first.at[pl.ds(start, self.piece), self.cols]
        return remote(
            source,
            view,
            self.send_sems.at[half, to, chunk],
            self.recv_sems.at[half, to, chunk],
            self.lanes.across(bit),
        )

    def give(self, place, half, chunk):
        for bit in onward(place, half, self.lanes.bits):
            self.copy(place, half, chunk, bit).start()

    def take(self, place, half, chunk):
        view = self.view(place, half, chunk)
        remote(
            view,
            view,
            self.send_sems.at[half, place, chunk],
            self.recv_sems.at[half, place, chunk],
            self.lanes.across(0),
        ).wait_recv()

    def pass_on(self, chunk):
        for half in range(2):
            places = range(1, self.lanes.blocks)
            if half == 1:
                key = lambda place: [-bit for bit in reversed(range(8)) if (place >> bit) & 1]
                places = sorted(places, key=key)
            for place in places:
                if onward(place, half, self.lanes.bits):
                    self.take(place, half, chunk)
                    self.give(place, half, chunk)

    def finish(self, chunk):
        for half in range(2):
            for place in range(1, self.lanes.blocks):
                if not onward(place, half, self.lanes.bits):
                    self.take(place, half, chunk)
        for half in range(2):
            for place in range(self.lanes.blocks):
                for bit in onward(place, half, self.lanes.bits):
                    self.copy(place, half, chunk, bit).wait_send()


def front_body(
    blocks, chunks, in_ref, out_ref, shared_ref, x_ref, gain_ref, par_ref,
    full_ref, pair_ref, act_ref, xr_ref, sh_ref, parr_ref,
    x_s, act_s, home_sems, z_send, z_recv, o_sems, o_recv, send_sems, recv_sems, x_sems, a_send,
    a_recv, line_send, line_recv, sh_send, sh_recv, swap_send, swap_recv, par_sems,
):
    lanes = Lanes(blocks)
    rows = in_ref.shape[0]
    piece = rows // chunks
    here = x_ref.shape[0]
    c, t = lanes.c, lanes.t
    lanes.greet()
    spread = Spread(lanes, full_ref, rows, chunks, send_sems, recv_sems)
    few, wide = shared_ref.shape
    side = wide // 2
    mine = pl.ds(pl.multiple_of(c * side, side), side)
    theirs = pl.ds(pl.multiple_of((1 - c) * side, side), side)

    def line_view(half, at_t, cols):
        start = lanes.k * (2 * rows) + half * rows + at_t * few
        return sh_ref.at[pl.ds(pl.multiple_of(start, few), few), cols]

    def line_own():
        return pltpu.make_async_copy(
            shared_ref.at[:, mine], line_view(c, t, mine), line_send.at[0]
        )

    def line_swap():
        return remote(
            shared_ref.at[:, theirs],
            line_view(c, t, theirs),
            line_send.at[1],
            line_recv.at[0],
            (lanes.other, t),
        )

    def line_swapped():
        view = line_view(1 - c, t, mine)
        return remote(view, view, line_send.at[1], line_recv.at[0], (lanes.other, t))

    def line_near(half, came):
        view = line_view(half, lanes.near if came else t, mine)
        return remote(
            view, view, line_send.at[2 + half], line_recv.at[1 + half], (lanes.d, lanes.near)
        )

    def line_far(half, near, came):
        at_t = lanes.near if near else t
        if came:
            at_t = lax.rem(at_t + 2, 4)
        view = line_view(half, at_t, mine)
        place = 2 * near + half
        return remote(
            view, view, line_send.at[4 + place], line_recv.at[3 + place], (lanes.d, lanes.far)
        )

    shared_spread = Spread(lanes, sh_ref, rows, 1, sh_send, sh_recv, mine)

    def swap_copy(place, half, came):
        start = lanes.block(place) * (2 * rows) + half * rows
        view = sh_ref.at[pl.ds(pl.multiple_of(start, rows), rows), theirs if came else mine]
        return remote(
            view, view, swap_send.at[half, place], swap_recv.at[half, place], (lanes.other, t)
        )

    def slot(chunk):
        start = lanes.k * (2 * rows) + c * rows + chunk * piece
        return full_ref.at[pl.ds(pl.multiple_of(start, piece), piece), :]

    def first_copy(chunk, device):
        return remote(
            in_ref.at[pl.ds(chunk * piece, piece), :],
            slot(chunk),
            z_send.at[0, chunk],
            z_recv.at[c, chunk],
            device,
        )

    def second_copy(chunk):
        return remote(
            in_ref.at[pl.ds(chunk * piece, piece), :],
            slot(chunk),
            z_send.at[1, chunk],
            z_recv.at[c, chunk],
            (lanes.other, lanes.far),
        )

    def own_copy(chunk):
        return pltpu.make_async_copy(
            in_ref.at[pl.ds(chunk * piece, piece), :], slot(chunk), home_sems.at[chunk]
        )

    def out_slot():
        return pair_ref.at[pl.ds(pl.multiple_of(c * rows, rows), rows), :]

    def out_first(device):
        return remote(out_ref, out_slot(), o_sems.at[0], o_recv.at[c], device)

    def out_second():
        return remote(out_ref, out_slot(), o_sems.at[1], o_recv.at[c], (lanes.other, lanes.far))

    def x_away():
        return remote(x_ref, x_s, x_sems.at[0], x_sems.at[1], (lanes.other, lanes.far))

    def x_home():
        return pltpu.make_async_copy(x_ref, x_s, x_sems.at[2])

    def send_first(chunk):
        @pl.when(lanes.home)
        def _():
            own_copy(chunk).start()
            first_copy(chunk, (lanes.d, lanes.far)).start()

        @pl.when(lanes.away)
        def _():
            first_copy(chunk, (lanes.other, t)).start()
            second_copy(chunk).start()

    def z_view(half, chunk):
        start = lanes.k * (2 * rows) + half * rows + chunk * piece
        return full_ref.at[pl.ds(pl.multiple_of(start, piece), piece), :]

    def came(half, chunk):
        view = z_view(half, chunk)
        return remote(
            view, view, z_send.at[0, chunk], z_recv.at[half, chunk], (lanes.other, t)
        )

    def arrive_home(chunk):
        own_copy(chunk).wait()
        start = lanes.k * (2 * rows) + (1 - c) * rows + chunk * piece
        view = full_ref.at[pl.ds(pl.multiple_of(start, piece), piece), :]
        remote(
            view, view, z_send.at[0, chunk], z_recv.at[1 - c, chunk], (lanes.other, t)
        ).wait_recv()
        for half in range(2):
            spread.give(0, half, chunk)

    def arrive_away(chunk):
        for half in range(2):
            came(half, chunk).wait_recv()
        for half in range(2):
            spread.give(0, half, chunk)

    def arrive(chunk):
        @pl.when(lanes.home)
        def _():
            arrive_home(chunk)

        @pl.when(lanes.away)
        def _():
            arrive_away(chunk)

    def act_slot(index):
        return act_ref.at[pl.ds(index * here, here), :]

    def act_far():
        return remote(act_s, act_slot(2), a_send.at[0], a_recv.at[0], (lanes.d, lanes.near))

    def act_core():
        return remote(act_s, act_slot(1), a_send.at[1], a_recv.at[1], (lanes.other, t))

    def act_both():
        return remote(act_slot(2), act_slot(3), a_send.at[2], a_recv.at[2], (lanes.other, t))

    def norm():
        @pl.when(lanes.home)
        def _():
            x_home().wait()

        @pl.when(lanes.away)
        def _():
            x_away().wait_recv()

        @pl.loop(0, here // 32)
        def _(step):
            part = pl.ds(pl.multiple_of(step * 32, 32), 32)
            x = x_s[part, :].astype(jnp.float32)
            scale = lax.rsqrt(jnp.mean(x * x, axis=1, keepdims=True) + EPS)
            act_s[part, :] = (x * scale * gain_ref[...]).astype(jnp.bfloat16)

        act_far().start()
        act_core().start()
        pltpu.make_async_copy(act_s, act_slot(0), a_send.at[3]).start()
        pltpu.make_async_copy(x_s, xr_ref, x_sems.at[3]).start()

    def par_away():
        return remote(
            par_ref, parr_ref, par_sems.at[0], par_sems.at[1], (lanes.other, lanes.far)
        )

    @pl.when(lanes.home)
    def _():
        parr_ref[...] = par_ref[...]

    @pl.when(lanes.away)
    def _():
        par_away().start()

    early = list(range(max(chunks // 2, 1)))
    late = list(range(len(early), chunks))
    line_own().start()
    line_swap().start()
    for chunk in early:
        send_first(chunk)

    @pl.when(lanes.home)
    def _():
        x_home().start()

    @pl.when(lanes.away)
    def _():
        x_away().start()

    line_own().wait()
    line_swapped().wait_recv()
    for half in range(2):
        line_near(half, False).start()
    for chunk in early:
        arrive(chunk)
        if chunk:
            spread.pass_on(chunk - 1)
    for half in range(2):
        line_near(half, True).wait_recv()
    for near in range(2):
        for half in range(2):
            line_far(half, near, False).start()
    for chunk in late:
        send_first(chunk)
    spread.pass_on(early[-1])

    @pl.when(lanes.home)
    def _():
        for chunk in late:
            arrive_home(chunk)
            spread.pass_on(chunk)

    norm()

    @pl.when(lanes.home)
    def _():
        out_first((lanes.d, lanes.far)).start()
        pltpu.make_async_copy(out_ref, out_slot(), o_sems.at[2]).start()

    @pl.when(lanes.away)
    def _():
        out_first((lanes.other, t)).start()
        out_second().start()

    for near in range(2):
        for half in range(2):
            line_far(half, near, True).wait_recv()
    for half in range(2):
        shared_spread.give(0, half, 0)
        swap_copy(0, half, False).start()

    @pl.when(lanes.away)
    def _():
        for chunk in late:
            arrive_away(chunk)
            if chunk > late[0]:
                spread.pass_on(chunk - 1)

    shared_spread.pass_on(0)

    @pl.when(lanes.away)
    def _():
        for chunk in late[-1:]:
            spread.pass_on(chunk)

    shared_spread.finish(0)
    for half in range(2):
        for place in range(1, blocks):
            swap_copy(place, half, False).start()
    act_far().wait_recv()
    act_both().start()
    act_core().wait_recv()
    for chunk in range(chunks):
        spread.finish(chunk)
    for half in range(2):
        for place in range(blocks):
            swap_copy(place, half, True).wait_recv()
            swap_copy(place, half, False).wait_send()
    line_swap().wait_send()
    for half in range(2):
        line_near(half, False).wait_send()
        for near in range(2):
            line_far(half, near, False).wait_send()
    act_both().wait_recv()
    act_far().wait_send()
    act_core().wait_send()
    act_both().wait_send()
    pltpu.make_async_copy(act_s, act_slot(0), a_send.at[3]).wait()
    pltpu.make_async_copy(x_s, xr_ref, x_sems.at[3]).wait()

    @pl.when(lanes.home)
    def _():
        for chunk in range(chunks):
            first_copy(chunk, (lanes.d, lanes.far)).wait_send()
        out_first((lanes.d, lanes.far)).wait_send()
        pltpu.make_async_copy(out_ref, out_slot(), o_sems.at[2]).wait()
        start = (1 - c) * rows
        view = pair_ref.at[pl.ds(pl.multiple_of(start, rows), rows), :]
        remote(view, view, o_sems.at[0], o_recv.at[1 - c], (lanes.other, t)).wait_recv()

    @pl.when(lanes.away)
    def _():
        par_away().wait_recv()
        par_away().wait_send()
        x_away().wait_send()
        for chunk in range(chunks):
            first_copy(chunk, (lanes.other, t)).wait_send()
            second_copy(chunk).wait_send()
        out_first((lanes.other, t)).wait_send()
        out_second().wait_send()
        for half in range(2):
            view = pair_ref.at[pl.ds(half * rows, rows), :]
            remote(view, view, o_sems.at[0], o_recv.at[half], (lanes.other, t)).wait_recv()


def front(in_pack, out_pack, shared, layer_in, gain, params, at):
    bf16 = jnp.bfloat16
    rows = in_pack.shape[0]
    blocks = at.blocks
    chunks = 4 if rows >= 256 else 1
    dma = pltpu.SemaphoreType.DMA
    anywhere = pl.BlockSpec(memory_space=pl.ANY)
    here, features = layer_in.shape
    total = 2 * blocks * rows
    return pl.pallas_call(
        functools.partial(front_body, blocks, chunks),
        in_specs=[pl.BlockSpec(memory_space=pltpu.VMEM)] * 6,
        out_specs=[anywhere] * 5 + [pl.BlockSpec(memory_space=pltpu.VMEM)],
        out_shape=[
            jax.ShapeDtypeStruct((total, in_pack.shape[1]), bf16),
            jax.ShapeDtypeStruct((2 * rows, out_pack.shape[1]), bf16),
            jax.ShapeDtypeStruct((4 * here, features), bf16),
            jax.ShapeDtypeStruct((here, features), bf16),
            jax.ShapeDtypeStruct((total, shared.shape[1]), bf16),
            jax.ShapeDtypeStruct(params.shape, jnp.float32),
        ],
        scratch_shapes=[
            pltpu.VMEM((here, features), bf16),
            pltpu.VMEM((here, features), bf16),
            dma((chunks,)),
            dma((2, chunks)),
            dma((2, chunks)),
            dma((3,)),
            dma((2,)),
            dma((2, blocks, chunks)),
            dma((2, blocks, chunks)),
            dma((4,)),
            dma((4,)),
            dma((3,)),
            dma((8,)),
            dma((7,)),
            dma((2, blocks, 1)),
            dma((2, blocks, 1)),
            dma((2, blocks)),
            dma((2, blocks)),
            dma((2,)),
        ],
        compiler_params=pltpu.CompilerParams(
            collective_id=1, has_side_effects=True, vmem_limit_bytes=16 * 1024 * 1024
        ),
        cost_estimate=pl.CostEstimate(
            flops=here * features * 8, bytes_accessed=300_000_000, transcendentals=0
        ),
    )(in_pack, out_pack, shared, layer_in, gain.reshape(1, -1), params)


class Stage:
    def __init__(self, lanes, pair, full, rows, cols, chunks, sems):
        self.lanes, self.pair, self.full, self.rows, self.cols = lanes, pair, full, rows, cols
        self.chunks = chunks
        self.own_sem, ssem, rsem = sems
        self.spread = Spread(lanes, full, rows, chunks, ssem, rsem, cols, pair)

    def own(self):
        start = self.lanes.k * (2 * self.rows)
        view = self.full.at[pl.ds(pl.multiple_of(start, 2 * self.rows), 2 * self.rows), self.cols]
        return pltpu.make_async_copy(self.pair.at[:, self.cols], view, self.own_sem.at[0])

    def give(self):
        for chunk in range(self.chunks):
            for half in range(2):
                self.spread.give(0, half, chunk)

    def settle(self, place):
        for half in range(2):
            if not onward(place, half, self.lanes.bits):
                for chunk in range(self.chunks):
                    self.spread.take(place, half, chunk)

    def finish(self):
        for chunk in range(self.chunks):
            for half in range(2):
                for place in range(self.lanes.blocks):
                    for bit in onward(place, half, self.lanes.bits):
                        self.spread.copy(place, half, chunk, bit).wait_send()


class Exchange:
    def __init__(self, lanes, work, own, sends, recvs, ssem, rsem):
        self.lanes, self.work, self.own = lanes, work, own
        self.both_s, self.core_s, self.pass_s = sends
        self.both_r, self.core_r, self.far_r = recvs
        self.ssem, self.rsem = ssem, rsem
        self.blocks, self.here, self.block = own.shape
        self.step = min(self.here, 64)

    def copies(self, index, place):
        core, near = (self.lanes.other, self.lanes.t), (self.lanes.d, self.lanes.near)
        table = (
            (self.both_s, self.both_r, core),
            (self.core_s, self.core_r, core),
            (self.pass_s, self.far_r, near),
        )

        def copy(kind):
            src, dst, device = table[kind]
            return remote(
                src.at[index], dst.at[index], self.ssem.at[kind, place], self.rsem.at[kind, place],
                device,
            )

        return copy

    def columns(self, place):
        return slice(place * self.block, (place + 1) * self.block)

    def rows(self, piece, i):
        start = piece * self.here + i * self.step
        return pl.ds(pl.multiple_of(start, self.step), self.step)

    def give(self, index, place, product):
        bf16 = jnp.bfloat16
        cols = self.columns(place)

        @pl.loop(0, 4)
        def _(piece):
            rows = pl.ds(pl.multiple_of(piece * self.here, self.here), self.here)
            self.work[rows, cols] = product(rows)

        @pl.loop(0, self.here // self.step)
        def _(i):
            part = self.rows(0, i)
            self.both_s[index, part, :] = self.work[self.rows(3, i), cols].astype(bf16)
            self.core_s[index, part, :] = self.work[self.rows(1, i), cols].astype(bf16)
            self.own[index, part, :] = self.work[part, cols]

        copy = self.copies(index, place)
        copy(0).start()
        copy(1).start()

    def pass_on(self, index, place):
        copy = self.copies(index, place)
        copy(0).wait_recv()
        cols = self.columns(place)

        @pl.loop(0, self.here // self.step)
        def _(i):
            part = self.rows(0, i)
            total = self.work[self.rows(2, i), cols] + self.both_r[index, part, :].astype(
                jnp.float32
            )
            self.pass_s[index, part, :] = total.astype(jnp.bfloat16)

        copy(2).start()

    def take(self, index, place):
        copy = self.copies(index, place)
        copy(1).wait_recv()
        copy(2).wait_recv()

    def total(self, index, rows):
        f32 = jnp.float32
        return (
            self.own[index, rows, :]
            + self.core_r[index, rows, :].astype(f32)
            + self.far_r[index, rows, :].astype(f32)
        )

    def finish(self, index, place):
        copy = self.copies(index, place)
        for kind in range(3):
            copy(kind).wait_send()


def middle_body(
    blocks, gu_chunks, down_chunks,
    pair_ref, heads_ref, out_ref, teacher_ref, x_ref, gain_ref, live_ref,
    full_ref, mid_ref, gate_ref, up_ref, hidden_ref, grads_ref, resid_ref, error_ref, low_ref,
    loss_ref,
    wbuf, mid_s, acc_s, hid_s, gate_s, up_s, own_s, both_s, core_s, pass_s,
    both_r, core_r, far_r, both_q, core_q, far_q, err_s,
    w_sems, one_s, one_r, two_s, two_r, mid_ssem, mid_rsem, err_ssem, err_rsem, keep_sems,
    g_home, g_s, g_r, d_home, d_s, d_r, target_ref, t_sems, out_s,
):
    f32, bf16 = jnp.float32, jnp.bfloat16
    lanes = Lanes(blocks)
    rows = pair_ref.shape[0] // 2
    here = x_ref.shape[0]
    block = 2 * rows
    inner = heads_ref.shape[1]
    hidden_width = hid_s.shape[1]
    core_at = (lanes.other, lanes.t)
    near_at = (lanes.d, lanes.near)
    lanes.greet()
    gate_up = Stage(
        lanes, pair_ref, full_ref, rows, slice(0, 2 * hidden_width), gu_chunks,
        (g_home, g_s, g_r),
    )
    down = Stage(
        lanes, pair_ref, full_ref, rows, slice(2 * hidden_width, 3 * hidden_width), down_chunks,
        (d_home, d_s, d_r),
    )

    def target_away():
        return remote(
            teacher_ref, target_ref, t_sems.at[0], t_sems.at[1], (lanes.other, lanes.far)
        )

    def target_home():
        return pltpu.make_async_copy(teacher_ref, target_ref, t_sems.at[2])

    sends = (both_s, core_s, pass_s)
    one = Exchange(lanes, acc_s, own_s, sends, (both_r, core_r, far_r), one_s, one_r)
    two = Exchange(lanes, acc_s, own_s, sends, (both_q, core_q, far_q), two_s, two_r)

    def load(src, slot, width, cols):
        return pltpu.make_async_copy(src, wbuf.at[slot, :, cols], w_sems.at[slot])

    def out_load(index):
        return load(
            out_ref.at[pl.ds(index * block, block), :], index % 2, inner, pl.ds(0, inner)
        )

    out_load(0).start()
    gate_up.give()
    gate_up.own().start()
    down.own().start()

    for index in range(blocks):
        if index + 1 < blocks:
            out_load(index + 1).start()
        out_load(index).wait()
        one.give(
            index,
            index,
            lambda rows: low_dot(heads_ref[rows, :], wbuf[index % 2, :, :inner], NT),
        )
    for index in range(blocks):
        one.pass_on(index, index)

    for chunk in range(gu_chunks):
        gate_up.spread.pass_on(chunk)
    down.give()

    for index in range(blocks):
        one.take(index, index)

    step = min(here, 32)

    def columns(index):
        return slice(index * block, (index + 1) * block)

    @pl.loop(0, here // step)
    def _(i):
        part = pl.ds(pl.multiple_of(i * step, step), step)
        total = jnp.zeros((step, 1), f32)
        for index in range(blocks):
            resid = x_ref[part, columns(index)].astype(f32) + one.total(index, part)
            resid_ref[part, columns(index)] = resid
            total = total + jnp.sum(resid * resid, axis=1, keepdims=True)
        scale = lax.rsqrt(total / (blocks * block) + EPS)
        for index in range(blocks):
            mid = resid_ref[part, columns(index)] * scale * gain_ref[:, columns(index)]
            mid_s[index, part, :] = mid.astype(bf16)

    def mid_view(slot):
        return mid_s.at[:, pl.ds(slot * here, here), :]

    def mid_near():
        return remote(mid_view(0), mid_view(2), mid_ssem.at[0], mid_rsem.at[0], near_at)

    def mid_core():
        return remote(mid_view(0), mid_view(1), mid_ssem.at[1], mid_rsem.at[1], core_at)

    def mid_both():
        return remote(mid_view(2), mid_view(3), mid_ssem.at[2], mid_rsem.at[2], core_at)

    mid_near().start()
    mid_core().start()

    @pl.when(lanes.home)
    def _():
        target_home().start()

    @pl.when(lanes.away)
    def _():
        target_away().start()

    def gu_load(place, slot):
        start = lanes.block(place) * block
        view = full_ref.at[pl.ds(pl.multiple_of(start, block), block), pl.ds(0, 2 * hidden_width)]
        return load(view, slot, 2 * hidden_width, pl.ds(0, 2 * hidden_width))

    def down_load(place, slot):
        start = lanes.block(place) * block
        view = full_ref.at[
            pl.ds(pl.multiple_of(start, block), block), pl.ds(2 * hidden_width, hidden_width)
        ]
        return load(view, slot, hidden_width, pl.ds(0, hidden_width))

    gate_up.own().wait()
    gu_load(0, 0).start()
    mid_near().wait_recv()
    mid_both().start()
    mid_core().wait_recv()

    wide = 2 * hidden_width
    tile = min(wide, 512)

    def accumulate(place, first, last):
        slot = place % 2
        index = lanes.block(place)

        @pl.loop(first, last)
        def _(piece):
            part = pl.ds(pl.multiple_of(piece * here, here), here)
            left = mid_s[index, part, :]
            for col in range(0, wide, tile):
                cols = slice(col, col + tile)
                product = low_dot(left, wbuf[slot, :, cols], NN)
                if place:
                    product = product + acc_s[part, cols]
                acc_s[part, cols] = product

    for place in range(blocks):
        if place + 1 < blocks:
            gate_up.settle(place + 1)
            gu_load(place + 1, (place + 1) % 2).start()
        gu_load(place, place % 2).wait()
        accumulate(place, 0, 3)
        if place == 0:
            mid_both().wait_recv()
        accumulate(place, 3, 4)
        if place < down_chunks:
            down.spread.pass_on(place)

    for chunk in range(blocks, down_chunks):
        down.spread.pass_on(chunk)

    down.own().wait()
    down_load(0, 0).start()

    @pl.loop(0, 4 * here // step)
    def _(i):
        part = pl.ds(pl.multiple_of(i * step, step), step)
        gate = acc_s[part, :hidden_width]
        up = acc_s[part, hidden_width : 2 * hidden_width]
        gate_s[part, :] = gate.astype(bf16)
        up_s[part, :] = up.astype(bf16)
        hid_s[part, :] = (gate * sigmoid(gate) * up).astype(bf16)

    kept = [
        pltpu.make_async_copy(hid_s, hidden_ref, keep_sems.at[0]),
        pltpu.make_async_copy(gate_s, gate_ref, keep_sems.at[1]),
        pltpu.make_async_copy(up_s, up_ref, keep_sems.at[2]),
    ] + [
        pltpu.make_async_copy(
            mid_s.at[index], mid_ref.at[:, pl.ds(index * block, block)], keep_sems.at[3 + index]
        )
        for index in range(blocks)
    ]
    for copy in kept:
        copy.start()
    for index in range(blocks):
        one.finish(index, index)

    for place in range(blocks):
        index = lanes.block(place)
        if place + 1 < blocks:
            down.settle(place + 1)
            down_load(place + 1, (place + 1) % 2).start()
        down_load(place, place % 2).wait()
        two.give(
            index,
            place,
            lambda rows: low_dot(hid_s[rows, :], wbuf[place % 2, :, :hidden_width], NT),
        )
        if place:
            two.pass_on(lanes.block(place - 1), place - 1)
    two.pass_on(lanes.block(blocks - 1), blocks - 1)
    for place in range(blocks):
        two.take(lanes.block(place), place)

    @pl.when(lanes.home)
    def _():
        target_home().wait()

    @pl.when(lanes.away)
    def _():
        target_away().wait_recv()
        target_away().wait_send()

    def output_part(i, loss):
        part = pl.ds(pl.multiple_of(i * step, step), step)
        live = live_ref[part, :]
        for index in range(blocks):
            cols = columns(index)
            outputs = resid_ref[part, cols] + two.total(index, part)
            out_s[part, cols] = outputs.astype(bf16)
            error = (outputs - target_ref[part, cols].astype(f32)) * live
            error_ref[part, cols] = error
            err_s[part, cols] = error.astype(bf16)
            loss = loss + jnp.sum(error * error)
        return loss

    loss = lax.fori_loop(0, here // step, output_part, jnp.zeros((), f32))
    loss_ref[...] = jnp.zeros((8, WIDE), f32) + 0.5 * loss

    def grads_view(slot):
        return grads_ref.at[pl.ds(slot * here, here), :]

    def err_near():
        return remote(err_s, grads_view(2), err_ssem.at[0], err_rsem.at[0], near_at)

    def err_core():
        return remote(err_s, grads_view(1), err_ssem.at[1], err_rsem.at[1], core_at)

    def err_both():
        return remote(grads_view(2), grads_view(3), err_ssem.at[2], err_rsem.at[2], core_at)

    own_err = pltpu.make_async_copy(err_s, grads_view(0), err_ssem.at[3])
    err_near().start()
    err_core().start()
    own_err.start()

    def out_home():
        return pltpu.make_async_copy(out_s, low_ref, t_sems.at[5])

    def out_away():
        return remote(out_s, low_ref, t_sems.at[3], t_sems.at[4], (lanes.other, lanes.far))

    @pl.when(lanes.home)
    def _():
        out_home().start()

    @pl.when(lanes.away)
    def _():
        out_away().start()

    for copy in kept:
        copy.wait()
    gate_up.finish()
    down.finish()
    for place in range(blocks):
        two.finish(lanes.block(place), place)
    for copy in (mid_near(), mid_core(), mid_both()):
        copy.wait_send()
    err_near().wait_recv()
    err_both().start()
    err_core().wait_recv()
    err_both().wait_recv()
    own_err.wait()

    @pl.when(lanes.home)
    def _():
        out_home().wait()

    @pl.when(lanes.away)
    def _():
        out_away().wait()

    for copy in (err_near(), err_core(), err_both()):
        copy.wait_send()


def middle(pair, heads_all, out_all, x, gain, teacher, live, at):
    f32, bf16 = jnp.float32, jnp.bfloat16
    rows = pair.shape[0] // 2
    hidden_width = pair.shape[1] // 3
    slot, inner = heads_all.shape
    here, features = x.shape
    blocks = at.blocks
    block = 2 * rows
    gu_chunks = 4 if rows >= 256 else 1
    down_chunks = 2 if rows >= 256 else 1
    dma = pltpu.SemaphoreType.DMA
    vmem = pl.BlockSpec(memory_space=pltpu.VMEM)
    anywhere = pl.BlockSpec(memory_space=pl.ANY)

    def stage_sems(chunks):
        return [dma((1,)), dma((2, blocks, chunks)), dma((2, blocks, chunks))]

    shape = jax.ShapeDtypeStruct
    buffers = [pltpu.VMEM((blocks, here, block), bf16)]
    return pl.pallas_call(
        functools.partial(middle_body, blocks, gu_chunks, down_chunks),
        in_specs=[vmem, vmem, anywhere, anywhere, vmem, vmem, vmem],
        out_specs=[anywhere] * 6 + [vmem] * 4,
        out_shape=[
            shape((features, 3 * hidden_width), bf16),
            shape((slot, features), bf16),
            shape((slot, hidden_width), bf16),
            shape((slot, hidden_width), bf16),
            shape((slot, hidden_width), bf16),
            shape((slot, features), bf16),
            shape((here, features), f32),
            shape((here, features), f32),
            shape((here, features), bf16),
            shape((8, WIDE), f32),
        ],
        scratch_shapes=[
            pltpu.VMEM((2, block, 2 * hidden_width), bf16),
            pltpu.VMEM((blocks, slot, block), bf16),
            pltpu.VMEM((slot, max(2 * hidden_width, features)), f32),
            pltpu.VMEM((slot, hidden_width), bf16),
            pltpu.VMEM((slot, hidden_width), bf16),
            pltpu.VMEM((slot, hidden_width), bf16),
            pltpu.VMEM((blocks, here, block), f32),
        ]
        + buffers * 9
        + [
            pltpu.VMEM((here, features), bf16),
            dma((2,)),
            dma((3, blocks)),
            dma((3, blocks)),
            dma((3, blocks)),
            dma((3, blocks)),
            dma((3,)),
            dma((3,)),
            dma((4,)),
            dma((3,)),
            dma((3 + blocks,)),
        ]
        + stage_sems(gu_chunks)
        + stage_sems(down_chunks)
        + [pltpu.VMEM((here, features), bf16), dma((6,)), pltpu.VMEM((here, features), bf16)],
        compiler_params=pltpu.CompilerParams(
            collective_id=3, has_side_effects=True, vmem_limit_bytes=58 * 1024 * 1024
        ),
        cost_estimate=pl.CostEstimate(
            flops=slot * features * hidden_width * 8, bytes_accessed=400_000_000, transcendentals=0
        ),
    )(
        pair, heads_all, out_all, teacher, x, gain.reshape(1, -1), live,
    )


def turn_body(
    blocks, low_ref, lowsh_ref, act_ref, in_ref, sh_ref, rawgu_ref, rawdown_ref,
    part_ref, bc_ref, kv_ref, sum_ref, gu_ref, down_ref,
    win_s, wsh_s, work_s, own_s, both_s, core_s, pass_s, both_r, core_r, far_r, stage_s,
    gu_r, down_r, w_sems, x_ssem, x_rsem, stage_sems, ff_ssem, ff_rsem,
):
    f32, bf16 = jnp.float32, jnp.bfloat16
    lanes = Lanes(blocks)
    c, t = lanes.c, lanes.t
    here = sum_ref.shape[0]
    rows = rawgu_ref.shape[0] // 2
    block = 2 * rows
    width = low_ref.shape[1]
    bc_width = bc_ref.shape[1]
    features = act_ref.shape[1]
    core_at, far_at, cross_at = (
        (lanes.other, t), (lanes.d, lanes.far), (lanes.other, lanes.far),
    )
    lanes.greet()

    def ff_copies(kind, half, device):
        view = pl.ds(pl.multiple_of(half * rows, rows), rows)
        return [
            remote(
                src.at[view, :], dst.at[kind], ff_ssem.at[kind, i], ff_rsem.at[kind, i], device
            )
            for i, (src, dst) in enumerate(((rawgu_ref, gu_r), (rawdown_ref, down_r)))
        ]

    def first_home():
        return ff_copies(0, 1 - c, core_at)

    def first_away():
        return ff_copies(0, c, far_at)

    def second_away():
        return ff_copies(1, 1 - c, cross_at)

    def load(index):
        slot = index % 2
        view = pl.ds(index * block, block)
        return (
            pltpu.make_async_copy(in_ref.at[view, :], win_s.at[slot], w_sems.at[slot, 0]),
            pltpu.make_async_copy(sh_ref.at[view, :], wsh_s.at[slot], w_sems.at[slot, 1]),
        )

    for copy in load(0):
        copy.start()

    @pl.when(lanes.home)
    def _():
        for copy in first_home():
            copy.start()

    @pl.when(lanes.away)
    def _():
        for one, two in zip(first_away(), second_away()):
            one.start()
            two.start()

    exchange = Exchange(
        lanes, work_s, own_s, (both_s, core_s, pass_s), (both_r, core_r, far_r), x_ssem, x_rsem
    )
    for index in range(blocks):
        slot = index % 2
        if index + 1 < blocks:
            for copy in load(index + 1):
                copy.start()
        for copy in load(index):
            copy.wait()
        exchange.give(
            index,
            index,
            lambda part: low_dot(low_ref[part, :], win_s[slot], NT)
            + low_dot(lowsh_ref[part, :], wsh_s[slot], NT),
        )
        if index:
            exchange.pass_on(index - 1, index - 1)
    exchange.pass_on(blocks - 1, blocks - 1)

    tall = 256
    steps = features // tall

    def out_copies(i, slot):
        view = pl.ds(pl.multiple_of(i * tall, tall), tall)
        kv_from = width + bc_width
        return (
            pltpu.make_async_copy(
                stage_s.at[slot, :, :width], part_ref.at[view, :], stage_sems.at[slot, 0]
            ),
            pltpu.make_async_copy(
                stage_s.at[slot, :, width:kv_from], bc_ref.at[view, :], stage_sems.at[slot, 1]
            ),
            pltpu.make_async_copy(
                stage_s.at[slot, :, kv_from:], kv_ref.at[view, :], stage_sems.at[slot, 2]
            ),
        )

    @pl.loop(0, steps)
    def _(i):
        slot = lax.rem(i, 2)

        @pl.when(i >= 2)
        def _():
            for copy in out_copies(i - 2, slot):
                copy.wait()

        left = act_ref[:, pl.ds(pl.multiple_of(i * tall, tall), tall)]
        for src, base in ((low_ref, 0), (lowsh_ref, width)):
            total = src.shape[1]
            tile = total // 3
            for col in range(0, total, tile):
                product = low_dot(left, src[:, col : col + tile], TN)
                stage_s[slot, :, base + col : base + col + tile] = product.astype(bf16)
        for copy in out_copies(i, slot):
            copy.start()

    for index in range(blocks):
        exchange.take(index, index)
    step = min(here, 32)

    @pl.loop(0, here // step)
    def _(i):
        part = pl.ds(pl.multiple_of(i * step, step), step)
        for index in range(blocks):
            sum_ref[part, index * block : (index + 1) * block] = exchange.total(index, part)

    for i in (steps - 2, steps - 1):
        for copy in out_copies(i, i % 2):
            copy.wait()
    for index in range(blocks):
        exchange.finish(index, index)
    for copy in first_home():
        copy.wait_recv()
    span = min(rows, 32)

    @pl.when(lanes.home)
    def _():
        for copy in first_home():
            copy.wait_send()

        @pl.loop(0, rows // span)
        def _(i):
            part = pl.ds(pl.multiple_of(i * span, span), span)
            mine = pl.ds(pl.multiple_of(c * rows + i * span, span), span)
            gu_ref[part, :] = rawgu_ref[mine, :].astype(f32) + gu_r[0, part, :].astype(f32)
            down_ref[part, :] = rawdown_ref[mine, :].astype(f32) + down_r[0, part, :].astype(f32)

    @pl.when(lanes.away)
    def _():
        for copy in second_away():
            copy.wait_recv()
        for copy in first_away() + second_away():
            copy.wait_send()

        @pl.loop(0, rows // span)
        def _(i):
            part = pl.ds(pl.multiple_of(i * span, span), span)
            gu_ref[part, :] = gu_r[0, part, :].astype(f32) + gu_r[1, part, :].astype(f32)
            down_ref[part, :] = down_r[0, part, :].astype(f32) + down_r[1, part, :].astype(f32)


def turn(low_pack, low_shared, act_all, in_all, shared_all, raw_gate_up, raw_down, bc_width, at):
    f32, bf16 = jnp.float32, jnp.bfloat16
    slot, width = low_pack.shape
    shared_width = low_shared.shape[1]
    features = act_all.shape[1]
    here = slot // 4
    blocks = at.blocks
    rows = raw_gate_up.shape[0] // 2
    block = 2 * rows
    gu_width, down_width = raw_gate_up.shape[1], raw_down.shape[1]
    dma = pltpu.SemaphoreType.DMA
    vmem = pl.BlockSpec(memory_space=pltpu.VMEM)
    anywhere = pl.BlockSpec(memory_space=pl.ANY)
    shape = jax.ShapeDtypeStruct
    return pl.pallas_call(
        functools.partial(turn_body, blocks),
        in_specs=[vmem] * 3 + [anywhere] * 2 + [vmem] * 2,
        out_specs=[anywhere] * 3 + [vmem] * 3,
        out_shape=[
            shape((features, width), bf16),
            shape((features, bc_width), bf16),
            shape((features, shared_width - bc_width), bf16),
            shape((here, features), f32),
            shape((rows, gu_width), f32),
            shape((rows, down_width), f32),
        ],
        scratch_shapes=[
            pltpu.VMEM((2, block, width), bf16),
            pltpu.VMEM((2, block, shared_width), bf16),
            pltpu.VMEM((slot, features), f32),
            pltpu.VMEM((blocks, here, block), f32),
        ]
        + [pltpu.VMEM((blocks, here, block), bf16)] * 6
        + [
            pltpu.VMEM((2, 256, width + shared_width), bf16),
            pltpu.VMEM((2, rows, gu_width), bf16),
            pltpu.VMEM((2, rows, down_width), bf16),
            dma((2, 2)),
            dma((3, blocks)),
            dma((3, blocks)),
            dma((2, 3)),
            dma((2, 2)),
            dma((2, 2)),
        ],
        compiler_params=pltpu.CompilerParams(
            collective_id=4, has_side_effects=True, vmem_limit_bytes=58 * 1024 * 1024
        ),
        cost_estimate=pl.CostEstimate(
            flops=slot * features * width * 5, bytes_accessed=60_000_000, transcendentals=0
        ),
    )(low_pack, low_shared, act_all, in_all, shared_all, raw_gate_up, raw_down)


class Collect:
    def __init__(self, lanes, part, rows, cols, send_s, recv_s, load_s, total_s, sems):
        self.lanes, self.part, self.rows, self.cols = lanes, part, rows, cols
        self.send_s, self.recv_s, self.load_s, self.total_s = send_s, recv_s, load_s, total_s
        self.send_sems, self.recv_sems, self.load_sems = sems
        self.loads = [
            (half, place)
            for half in range(2)
            for place in range(lanes.blocks)
            if onward(place, half, lanes.bits)
        ]

    def source(self, place, half, chunk):
        start = self.lanes.block(place) * (2 * self.rows) + half * self.rows
        return self.part.at[pl.ds(pl.multiple_of(start, self.rows), self.rows), self.cols[chunk]]

    def bit_of(self, place, half):
        bits = [bit for bit in range(self.lanes.bits) if (place >> bit) & 1]
        return bits[-1] if half == 0 else bits[0]

    def load(self, half, place):
        index = self.loads.index((half, place))
        start = self.lanes.block(place) * (2 * self.rows) + half * self.rows
        view = self.part.at[pl.ds(pl.multiple_of(start, self.rows), self.rows), :]
        return pltpu.make_async_copy(view, self.load_s.at[index], self.load_sems.at[index])

    def copy(self, place, half, chunk):
        if (half, place) in self.loads:
            source = self.send_s.at[self.loads.index((half, place)), :, self.cols[chunk]]
        else:
            source = self.source(place, half, chunk)
        return remote(
            source,
            self.recv_s.at[half, place - 1, :, self.cols[chunk]],
            self.send_sems.at[half, place, chunk],
            self.recv_sems.at[half, place, chunk],
            self.lanes.across(self.bit_of(place, half)),
        )

    def order(self, half):
        places = list(range(1, self.lanes.blocks))
        places.sort(key=lambda place: -len([b for b in range(8) if (place >> b) & 1]))
        return places

    def start(self):
        for half, place in self.loads:
            self.load(half, place).start()

    def direct(self, chunk):
        for half in range(2):
            for place in self.order(half):
                if (half, place) not in self.loads:
                    self.copy(place, half, chunk).start()

    def add(self, place, half, chunk):
        cols = self.cols[chunk]
        index = self.loads.index((half, place))
        total = self.load_s[index, :, cols].astype(jnp.float32)
        for bit in onward(place, half, self.lanes.bits):
            came = place | (1 << bit)
            self.copy(came, half, chunk).wait_recv()
            total = total + self.recv_s[half, came - 1, :, cols].astype(jnp.float32)
        return total

    def middle(self, chunk):
        for half in range(2):
            for place in self.order(half):
                if (half, place) in self.loads:
                    index = self.loads.index((half, place))
                    if chunk == 0:
                        self.load(half, place).wait()
                    total = self.add(place, half, chunk)
                    self.send_s[index, :, self.cols[chunk]] = total.astype(jnp.bfloat16)
                    self.copy(place, half, chunk).start()

    def last(self, chunk):
        for half in range(2):
            if chunk == 0:
                self.load(half, 0).wait()
            self.total_s[half, :, self.cols[chunk]] = self.add(0, half, chunk)

    def finish(self):
        for chunk in range(len(self.cols)):
            for half in range(2):
                for place in range(1, self.lanes.blocks):
                    self.copy(place, half, chunk).wait_send()


def back_body(
    blocks, in_cols, small_row, part_ref, bc_ref, kv_ref, act_ref,
    resid_ref, x_ref, gain_ref, small_ref, out_ref,
    gin_ref, gsh_ref, gx_ref, sum_ref, gout_ref,
    in_send, in_recv, in_load, in_total, settle_s, settle_r, sh_came, sh_part, sh_send, sh_recv,
    sh_load, sh_total, line_s, line_r, near_s, near_r, swap_s, swap_r,
    gx_s, gx_r, small_s, small_r,
    in_ssem, in_rsem, in_lsem, sh_ssem, sh_rsem, sh_lsem, set_ssem, set_rsem, misc_s, misc_r,
    small_ssem, small_rsem, out_r, out_ssem, out_rsem,
):
    f32, bf16 = jnp.float32, jnp.bfloat16
    lanes = Lanes(blocks)
    c, t = lanes.c, lanes.t
    rows = gin_ref.shape[0]
    here = act_ref.shape[0]
    wide = bc_ref.shape[1]
    few = gsh_ref.shape[0]
    chunks = len(in_cols)
    step = min(here, 32)
    lanes.greet()
    core_at = (lanes.other, t)
    near_at = (lanes.d, lanes.near)
    far_at = (lanes.d, lanes.far)
    cross_at = (lanes.other, lanes.far)
    first = c == 0
    second = c == 1

    collect = Collect(
        lanes, part_ref, rows, in_cols, in_send, in_recv, in_load, in_total,
        (in_ssem, in_rsem, in_lsem),
    )
    shared = Collect(
        lanes, sh_part, rows, [slice(0, wide)], sh_send, sh_recv, sh_load, sh_total,
        (sh_ssem, sh_rsem, sh_lsem),
    )
    half_kv = kv_ref.shape[1] // 2

    def send_kv():
        return remote(
            kv_ref, sh_came.at[:, : 2 * half_kv], misc_s.at[2], misc_r.at[2], core_at
        )

    def send_bc():
        return remote(bc_ref, sh_came, misc_s.at[3], misc_r.at[3], core_at)

    def out_block(half):
        return out_ref.at[pl.ds(pl.multiple_of(half * rows, rows), rows), :]

    def out_first(half, device):
        return remote(out_block(half), out_r.at[0], out_ssem.at[0], out_rsem.at[0], device)

    def out_second():
        return remote(out_block(1 - c), out_r.at[1], out_ssem.at[1], out_rsem.at[1], cross_at)

    collect.start()
    for chunk in range(chunks):
        collect.direct(chunk)
    @pl.when(first)
    def _():
        send_kv().start()

    @pl.when(second)
    def _():
        send_bc().start()

    def send_x():
        return remote(gx_s, gx_r, misc_s.at[4], misc_r.at[4], cross_at)

    small_s[0] = small_ref[...]
    features = gain_ref.shape[1]

    def one_part(i, gains):
        view = pl.ds(pl.multiple_of(i * step, step), step)
        grad = act_ref[view, :]
        x = x_ref[view, :].astype(f32)
        scale = lax.rsqrt(jnp.mean(x * x, axis=1, keepdims=True) + EPS)
        gains = gains + jnp.sum(grad * (x * scale), axis=0, keepdims=True)
        grad = grad * gain_ref[...]
        mean = jnp.mean(grad * x, axis=1, keepdims=True)
        result = resid_ref[view, :] + scale * grad - x * (scale * scale * scale * mean)
        gx_ref[view, :] = result
        gx_s[view, :] = result.astype(bf16)
        return gains

    gains = lax.fori_loop(0, here // step, one_part, jnp.zeros((1, features), f32))
    for i in range(features // WIDE):
        small_s[0, small_row + i : small_row + i + 1, :] = gains[:, i * WIDE : (i + 1) * WIDE]

    stops = [far_at, near_at, core_at] + [lanes.across(bit) for bit in range(lanes.bits)]

    def send_small(index):
        return remote(
            small_s.at[index], small_r.at[index], small_ssem.at[index], small_rsem.at[index],
            stops[index],
        )

    def step_small(index):
        send_small(index).wait_recv()
        small_s[index + 1] = small_s[index] + small_r[index]
        if index + 1 < len(stops):
            send_small(index + 1).start()

    send_small(0).start()

    @pl.when(lanes.away)
    def _():
        send_x().start()

    @pl.when(lanes.home)
    def _():
        out_first(1 - c, core_at).start()

    @pl.when(lanes.away)
    def _():
        out_first(c, far_at).start()
        out_second().start()

    @pl.when(first)
    def _():
        send_bc().wait_recv()

        @pl.loop(0, bc_ref.shape[0] // 64)
        def _(i):
            view = pl.ds(pl.multiple_of(i * 64, 64), 64)
            total = bc_ref[view, :].astype(f32) + sh_came[view, :].astype(f32)
            sh_part[view, :] = total.astype(bf16)

    @pl.when(second)
    def _():
        send_kv().wait_recv()

        @pl.loop(0, bc_ref.shape[0] // 64)
        def _(i):
            view = pl.ds(pl.multiple_of(i * 64, 64), 64)
            for piece in range(2):
                kept = pl.ds(piece * half_kv, half_kv)
                sh_part[view, pl.ds(2 * piece * half_kv, half_kv)] = sh_came[view, kept]
                sh_part[view, pl.ds((2 * piece + 1) * half_kv, half_kv)] = kv_ref[view, kept]

    shared.start()
    for chunk in range(chunks):
        collect.middle(chunk)
    shared.direct(0)

    def send_first(chunk, device):
        cols = in_cols[chunk]
        return remote(
            settle_s.at[0, :, cols], settle_r.at[0, :, cols],
            set_ssem.at[0, chunk], set_rsem.at[0, chunk], device,
        )

    def send_second(chunk):
        cols = in_cols[chunk]
        return remote(
            settle_s.at[1, :, cols], settle_r.at[1, :, cols],
            set_ssem.at[1, chunk], set_rsem.at[1, chunk], cross_at,
        )

    for chunk in range(chunks):
        collect.last(chunk)
        cols = in_cols[chunk]

        @pl.when(lanes.home)
        def _(chunk=chunk, cols=cols):
            settle_s[0, :, cols] = in_total[1 - c, :, cols].astype(bf16)
            send_first(chunk, core_at).start()

        @pl.when(lanes.away)
        def _(chunk=chunk, cols=cols):
            settle_s[0, :, cols] = in_total[c, :, cols].astype(bf16)
            send_first(chunk, far_at).start()
            settle_s[1, :, cols] = in_total[1 - c, :, cols].astype(bf16)
            send_second(chunk).start()

        if chunk == 0:
            step_small(0)
            shared.middle(0)
        if chunk == 1:
            step_small(1)
    step_small(2)
    shared.last(0)

    t_high, t_low = lax.div(t, 2), lax.rem(t, 2)
    line = 2 * few

    def send_line():
        return remote(line_s, line_r, misc_s.at[5], misc_r.at[5], far_at)

    def send_near():
        return remote(near_s, near_r, misc_s.at[6], misc_r.at[6], near_at)

    def send_swap():
        return remote(swap_s, swap_r, misc_s.at[7], misc_r.at[7], core_at)

    theirs = pl.ds(pl.multiple_of((1 - t_high) * line, line), line)
    mine = pl.ds(pl.multiple_of(t_high * line, line), line)
    for half in range(2):
        line_s[half] = sh_total[half, theirs, :].astype(bf16)
    send_line().start()
    step_small(3)
    send_line().wait_recv()
    for half in range(2):
        sh_total[half, mine, :] = sh_total[half, mine, :] + line_r[half].astype(f32)
    theirs = pl.ds(pl.multiple_of(t_high * line + (1 - t_low) * few, few), few)
    mine = pl.ds(pl.multiple_of(t_high * line + t_low * few, few), few)
    for half in range(2):
        near_s[half] = sh_total[half, theirs, :].astype(bf16)
    send_near().start()
    for index in range(4, len(stops)):
        step_small(index)
    send_near().wait_recv()
    for half in range(2):
        sh_total[half, mine, :] = sh_total[half, mine, :] + near_r[half].astype(f32)
    swap_s[...] = sh_total[1 - c, mine, :].astype(bf16)
    send_swap().start()
    sum_ref[...] = small_s[len(stops)]

    for chunk in range(chunks):
        cols = in_cols[chunk]
        send_first(chunk, core_at).wait_recv()

        @pl.when(lanes.home)
        def _(chunk=chunk, cols=cols):
            gin_ref[:, cols] = in_total[c, :, cols] + settle_r[0, :, cols].astype(f32)

        @pl.when(lanes.away)
        def _(chunk=chunk, cols=cols):
            send_second(chunk).wait_recv()
            gin_ref[:, cols] = settle_r[0, :, cols].astype(f32) + settle_r[1, :, cols].astype(f32)

    out_first(0, core_at).wait_recv()

    @pl.when(lanes.home)
    def _():
        own_rows = pl.ds(pl.multiple_of(c * rows, rows), rows)
        gout_ref[...] = out_ref[own_rows, :].astype(f32) + out_r[0].astype(f32)
        out_first(1 - c, core_at).wait_send()

    @pl.when(lanes.away)
    def _():
        out_second().wait_recv()
        gout_ref[...] = out_r[0].astype(f32) + out_r[1].astype(f32)
        out_first(c, far_at).wait_send()
        out_second().wait_send()

    send_swap().wait_recv()

    @pl.when(first)
    def _():
        gsh_ref[:, :wide] = sh_total[0, mine, :]
        gsh_ref[:, wide:] = swap_r[...].astype(f32)

    @pl.when(second)
    def _():
        gsh_ref[:, :wide] = swap_r[...].astype(f32)
        gsh_ref[:, wide:] = sh_total[1, mine, :]

    @pl.when(lanes.away)
    def _():
        send_x().wait_recv()

        @pl.loop(0, here // step)
        def _(i):
            view = pl.ds(pl.multiple_of(i * step, step), step)
            gx_ref[view, :] = gx_r[view, :].astype(f32)

    collect.finish()
    shared.finish()

    @pl.when(first)
    def _():
        send_kv().wait_send()

    @pl.when(second)
    def _():
        send_bc().wait_send()

    for chunk in range(chunks):
        send_first(chunk, core_at).wait_send()

    @pl.when(lanes.away)
    def _():
        send_x().wait_send()
        for chunk in range(chunks):
            send_second(chunk).wait_send()

    for index in range(len(stops)):
        send_small(index).wait_send()
    send_line().wait_send()
    send_near().wait_send()
    send_swap().wait_send()


def back(part_in, bc, kv, grad_act, grad_resid, x, gain, small, small_row, raw_out, few, at):
    f32, bf16 = jnp.float32, jnp.bfloat16
    blocks = at.blocks
    features, width = part_in.shape
    rows = features // (2 * blocks)
    here = grad_act.shape[0]
    wide = bc.shape[1]
    chunks = 3
    piece = width // chunks
    in_cols = [slice(i * piece, (i + 1) * piece) for i in range(chunks)]
    loads = sum(bool(onward(p, h, at.bits)) for h in range(2) for p in range(blocks))
    steps = 3 + at.bits
    dma = pltpu.SemaphoreType.DMA
    vmem = pl.BlockSpec(memory_space=pltpu.VMEM)
    anywhere = pl.BlockSpec(memory_space=pl.ANY)
    line = 2 * few
    return pl.pallas_call(
        functools.partial(back_body, blocks, in_cols, small_row),
        in_specs=[anywhere] + [vmem] * 8,
        out_specs=[vmem] * 5,
        out_shape=[
            jax.ShapeDtypeStruct((rows, width), f32),
            jax.ShapeDtypeStruct((few, 2 * wide), f32),
            jax.ShapeDtypeStruct((here, features), f32),
            jax.ShapeDtypeStruct(small.shape, f32),
            jax.ShapeDtypeStruct((rows, raw_out.shape[1]), f32),
        ],
        scratch_shapes=[
            pltpu.VMEM((loads, rows, width), bf16),
            pltpu.VMEM((2, blocks - 1, rows, width), bf16),
            pltpu.VMEM((loads, rows, width), bf16),
            pltpu.VMEM((2, rows, width), f32),
            pltpu.VMEM((2, rows, width), bf16),
            pltpu.VMEM((2, rows, width), bf16),
            pltpu.VMEM((features, wide), bf16),
            pltpu.VMEM((features, wide), bf16),
            pltpu.VMEM((loads, rows, wide), bf16),
            pltpu.VMEM((2, blocks - 1, rows, wide), bf16),
            pltpu.VMEM((loads, rows, wide), bf16),
            pltpu.VMEM((2, rows, wide), f32),
            pltpu.VMEM((2, line, wide), bf16),
            pltpu.VMEM((2, line, wide), bf16),
            pltpu.VMEM((2, few, wide), bf16),
            pltpu.VMEM((2, few, wide), bf16),
            pltpu.VMEM((few, wide), bf16),
            pltpu.VMEM((few, wide), bf16),
            pltpu.VMEM((here, features), bf16),
            pltpu.VMEM((here, features), bf16),
            pltpu.VMEM((steps + 1,) + small.shape, f32),
            pltpu.VMEM((steps,) + small.shape, f32),
            dma((2, blocks, chunks)),
            dma((2, blocks, chunks)),
            dma((loads,)),
            dma((2, blocks, 1)),
            dma((2, blocks, 1)),
            dma((loads,)),
            dma((2, chunks)),
            dma((2, chunks)),
            dma((8,)),
            dma((8,)),
            dma((steps,)),
            dma((steps,)),
            pltpu.VMEM((2, rows, raw_out.shape[1]), bf16),
            dma((2,)),
            dma((2,)),
        ],
        compiler_params=pltpu.CompilerParams(
            collective_id=2, has_side_effects=True, vmem_limit_bytes=58 * 1024 * 1024
        ),
        cost_estimate=pl.CostEstimate(
            flops=here, bytes_accessed=here, transcendentals=0
        ),
    )(
        part_in, bc, kv, grad_act, grad_resid, x, gain.reshape(1, -1), small,
        raw_out,
    )


def after(values, *others):
    return lax.optimization_barrier((values,) + others)[0]


def share_rows(values, at):
    far = at.over_z(values)
    core = at.over_core(values)
    both = at.over_core(far)
    return (values, core, far, both)


def sum_rows(pieces, at):
    own, core, far, both = pieces
    bf16 = jnp.bfloat16
    from_both = at.over_core(both.astype(bf16))
    passed = (far + from_both.astype(jnp.float32)).astype(bf16)
    from_far = at.over_z(passed)
    from_core = at.over_core(core.astype(bf16))
    return own + from_core.astype(jnp.float32) + from_far.astype(jnp.float32)


def groups(at):
    return [[d for d in range(at.dp) if d % 2 == c] for c in range(2)]


def gather_blocks(block, at):
    return lax.all_gather(block, "dp", axis=0, tiled=True, axis_index_groups=groups(at))


def sum_blocks(values, at):
    return lax.psum_scatter(
        values, "dp", scatter_dimension=0, tiled=True, axis_index_groups=groups(at)
    )


def pair_up(own, other, at):
    first = at.c == 0
    return jnp.concatenate([jnp.where(first, own, other), jnp.where(first, other, own)], axis=0)


def pair_weight(shard, at):
    first_in = at.column_out(shard)
    second_in = at.swap_away(shard)
    own = jnp.where(at.home, shard, first_in)
    other = jnp.where(at.home, first_in, second_in)
    return pair_up(own, other, at)


def gather_weight(shard, at):
    return gather_blocks(pair_weight(shard, at), at)


def send_settle(mine, at):
    rows = mine.shape[0] // 2
    low, high = mine[:rows], mine[rows:]
    own = jnp.where(at.c == 0, low, high)
    other = jnp.where(at.c == 0, high, low)
    return at.column_back(jnp.where(at.home, other, own)), at.swap_away(other), own


def end_settle(moves, at):
    first_in, second_in, own = moves
    f32 = jnp.float32
    return first_in.astype(f32) + jnp.where(at.home, own, second_in).astype(f32)


def gather_shared(shard, at):
    rows, width = shard.shape
    half = width // 2
    mine = jnp.where(at.c == 0, shard[:, :half], shard[:, half:])
    theirs = jnp.where(at.c == 0, shard[:, half:], shard[:, :half])
    came = at.over_core(theirs)
    both = jnp.stack([jnp.where(at.c == 0, mine, came), jnp.where(at.c == 0, came, mine)])
    near = at.over_z(both)
    lowest = at.t % 2 == 0
    two = jnp.stack([jnp.where(lowest, both, near), jnp.where(lowest, near, both)], axis=1)
    far = at.over_far(two)
    lower = at.t // 2 == 0
    four = jnp.stack([jnp.where(lower, two, far), jnp.where(lower, far, two)], axis=1)
    part = gather_blocks(four.reshape(2 * rows * at.tp, half), at)
    other = at.over_core(part)
    return jnp.where(at.c == 0, part, other), jnp.where(at.c == 0, other, part)


def scatter_shared(grad_bc, grad_kv, earlier, at):
    f32, bf16 = jnp.float32, jnp.bfloat16
    first = at.c == 0
    bc_width = grad_bc.shape[1]
    going = jnp.where(
        first, jnp.pad(grad_kv, ((0, 0), (0, bc_width - grad_kv.shape[1]))), grad_bc
    )
    came = at.over_core(going.astype(bf16)).astype(f32)
    kept = jnp.concatenate(
        [came[:, :HD], grad_kv[:, :HD], came[:, HD : 2 * HD], grad_kv[:, HD:]], axis=1
    )
    total = jnp.where(first, grad_bc + came, kept)
    mine = sum_blocks(after(total.astype(bf16), earlier), at)
    piece = mine.shape[0] // (2 * at.tp)
    line = mine.astype(f32).reshape(2, 2, 2, piece, total.shape[1])
    lower = at.t // 2 == 0
    went = at.over_far(jnp.where(lower, line[:, 1], line[:, 0]).astype(bf16)).astype(f32)
    line = jnp.where(lower, line[:, 0], line[:, 1]) + went
    lowest = at.t % 2 == 0
    went = at.over_z(jnp.where(lowest, line[:, 1], line[:, 0]).astype(bf16)).astype(f32)
    line = jnp.where(lowest, line[:, 0], line[:, 1]) + went
    mine = jnp.where(first, line[0], line[1])
    came = at.over_core(jnp.where(first, line[1], line[0]).astype(bf16)).astype(f32)
    return jnp.concatenate([jnp.where(first, mine, came), jnp.where(first, came, mine)], axis=1)


def sum_tensor(values, at):
    for bit in range(at.tp.bit_length() - 1):
        values = values + at.send(values, lambda d, t: (d, t ^ (1 << bit)))
    return values


def sum_data(values, at):
    for bit in range(at.dp.bit_length() - 1):
        values = values + at.send(values, lambda d, t: (d ^ (1 << bit), t))
    return values


def per_device(
    layer_in,
    teacher,
    lengths,
    input_gain,
    mixer_in_weight,
    step_weight,
    query_weight,
    shared_weight,
    conv_inner,
    conv_shared,
    step_bias,
    decay_log,
    skip_gain,
    inner_gain,
    mixer_out_weight,
    attn_out_weight,
    middle_gain,
    gate_up_weight,
    down_weight,
):
    f32 = jnp.float32
    bf16 = jnp.bfloat16
    contract_last = (((1,), (1,)), ((), ()))
    contract_first = (((0,), (0,)), ((), ()))
    at = Places()
    rows_here = layer_in.shape[0]
    slot_len = rows_here * at.tp
    local_heads = step_bias.shape[0]
    width = inner_gain.shape[0]
    head_dim = width // local_heads
    query_width = query_weight.shape[1]
    hidden_width = down_weight.shape[1]
    bc_width = conv_shared.shape[1]
    w_rows = step_weight.shape[0]

    seg = (
        lax.broadcasted_iota(jnp.int32, (width, WIDE), 0) // head_dim
        == lax.broadcasted_iota(jnp.int32, (width, WIDE), 1)
    ).astype(bf16)
    half = HD // 2
    freqs = jnp.exp(-jnp.log(ROPE_BASE) * 2.0 * jnp.arange(half, dtype=f32) / HD)
    angles = jnp.arange(slot_len).astype(f32)[:, None] * freqs[None, :]
    cosine, sine = jnp.cos(angles), jnp.sin(angles)
    cosine = jnp.concatenate([cosine, cosine], axis=1)
    sine = jnp.concatenate([-sine, sine], axis=1)
    quarters = jnp.arange(at.tp, dtype=jnp.int32)
    order = (at.c ^ (quarters // 2)) + 2 * (at.zq ^ (quarters % 2))

    in_pack = jnp.concatenate(
        [
            mixer_in_weight.reshape(w_rows, 2 * width),
            query_weight,
            step_weight,
            jnp.zeros((w_rows, WIDE - local_heads), bf16),
        ],
        axis=1,
    )
    out_pack = jnp.concatenate([mixer_out_weight, attn_out_weight], axis=1)
    column_params = jnp.concatenate(
        [conv_inner.reshape(-1), inner_gain, step_bias, decay_log, skip_gain]
    )
    params = jnp.pad(column_params, (0, -column_params.shape[0] % 1024)).reshape(-1, WIDE)
    in_all, out_pair, act_all, x_low, shared_full, params = front(
        in_pack, out_pack, shared_weight, layer_in, input_gain, params, at
    )
    column_params = params.reshape(-1)[: column_params.shape[0]]
    lane_params = jnp.concatenate(
        [
            column_params[: (KC + 1) * width].reshape(KC + 1, width),
            jnp.repeat(column_params[(KC + 1) * width + 2 * local_heads :], head_dim)[None],
            jnp.zeros((2, width), f32),
        ],
        axis=0,
    )
    head_rows = column_params[(KC + 1) * width :][: 2 * local_heads].reshape(2, local_heads)
    head_rows = jnp.concatenate([head_rows[:1], -jnp.exp(head_rows[1:])], axis=0)
    head_params = jnp.pad(head_rows, ((0, 6), (0, WIDE - local_heads)))
    left, right = shared_full[:, :bc_width], shared_full[:, bc_width:]
    kv_index = at.column * (query_width // HD) // (QH // KVH)
    second = kv_index == 1
    shared_all = jnp.concatenate(
        [
            left,
            jnp.where(second, right[:, HD : 2 * HD], right[:, :HD]),
            jnp.where(second, right[:, 3 * HD :], right[:, 2 * HD : 3 * HD]),
        ],
        axis=1,
    )

    def row_split(values):
        return [values[i * rows_here : (i + 1) * rows_here] for i in range(at.tp)]

    out_all = gather_blocks(out_pair, at)
    proj_shared = jnp.dot(act_all, shared_all, preferred_element_type=f32)
    proj = jnp.dot(act_all, in_all, preferred_element_type=f32)
    attn_low = attn_forward(order, proj, proj_shared, cosine, sine, query_width, width, bc_width)
    heads_all, y, states = mixer_forward(
        order, proj, proj_shared, attn_low, lane_params, conv_shared, head_params
    )
    ff_pack = jnp.concatenate(
        [gate_up_weight.reshape(w_rows, 2 * hidden_width), down_weight], axis=1
    )
    seq_len = lax.dynamic_index_in_dim(lengths, at.slot, keepdims=False)
    positions = at.quarter * rows_here + jnp.arange(rows_here)
    live = (positions < seq_len).astype(f32)[:, None]
    ff_pair = pair_weight(ff_pack, at)
    ff_all, mid_all, gate_low, up_low, hidden, grad_all, resid, error, layer_out, loss_part = middle(
        ff_pair, heads_all, out_all, x_low, middle_gain, teacher, live, at
    )
    err_local = loss_part[0, 0]
    _, norm_mid_back = jax.vjp(rms_norm, resid, middle_gain)
    gate_up_all = ff_all[:, : 2 * hidden_width]
    down_all = ff_all[:, 2 * hidden_width :]
    gate_val, up_val = gate_low.astype(f32), up_low.astype(f32)
    sigmoid_gate = jax.nn.sigmoid(gate_val)

    def weight_grad(left, right):
        return lax.dot_general(left, right, contract_first, preferred_element_type=f32).astype(bf16)

    part_down = weight_grad(grad_all, hidden)
    grad_all, part_down = lax.optimization_barrier((grad_all, part_down))
    raw_down = sum_blocks(part_down, at)
    grad_hidden = jnp.dot(grad_all, down_all, preferred_element_type=f32)
    grad_gate = grad_hidden * up_val * sigmoid_gate * (1.0 + gate_val * (1.0 - sigmoid_gate))
    grad_up = grad_hidden * gate_val * sigmoid_gate
    grad_gu = jnp.concatenate([grad_gate.astype(bf16), grad_up.astype(bf16)], axis=1)
    grad_mid_parts = [
        lax.dot_general(piece, gate_up_all, contract_last, preferred_element_type=f32)
        for piece in row_split(grad_gu)
    ]
    part_gate_up = weight_grad(mid_all, grad_gu)
    grad_mid = sum_rows(grad_mid_parts, at)
    grad_mid, part_gate_up = lax.optimization_barrier((grad_mid, part_gate_up))
    raw_gate_up = sum_blocks(part_gate_up, at)
    grad_resid_norm, grad_middle_gain = norm_mid_back(grad_mid)
    grad_resid = error + grad_resid_norm
    mix_grad_all = jnp.concatenate(share_rows(grad_resid.astype(bf16), at), axis=0)
    grad_heads = jnp.dot(mix_grad_all, out_all, preferred_element_type=f32)
    part_out = weight_grad(mix_grad_all, heads_all)
    grad_heads, part_out, raw_down = lax.optimization_barrier((grad_heads, part_out, raw_down))
    dq, dkv = attn_backward(
        order, proj, proj_shared, cosine, sine, grad_heads, query_width, width, bc_width
    )
    low_pack, low_shared, dlane, dconv, dhead = mixer_backward(
        order, proj, proj_shared, y, states, grad_heads, dq, dkv, lane_params, conv_shared,
        head_params, seg, query_width,
    )
    low_pack, low_shared, raw_gate_up, part_out = lax.optimization_barrier(
        (low_pack, low_shared, raw_gate_up, part_out)
    )
    raw_out = sum_blocks(part_out, at)
    column = at.column
    lanes_full = lax.dynamic_update_slice(
        jnp.zeros((KC + 1, DI), f32), dlane[: KC + 1], (0, column * width)
    )
    head_stack = jnp.concatenate(
        [dhead[:2, :local_heads], dlane[KC + 1].reshape(1, local_heads, head_dim).sum(2)], axis=0
    )
    heads_full = lax.dynamic_update_slice(
        jnp.zeros((3, H), f32), head_stack, (0, column * local_heads)
    )
    small = (
        jnp.zeros_like(input_gain),
        grad_middle_gain,
        lanes_full,
        dconv[:KC],
        heads_full,
        err_local,
    )
    flat = jnp.concatenate([part.reshape(-1) for part in small])
    padded = -(-flat.shape[0] // 1024) * 1024
    flat = jnp.pad(flat, (0, padded - flat.shape[0])).reshape(-1, WIDE)

    part_in, part_bc, part_kv, grad_act, grad_gate_up, grad_down = turn(
        low_pack, low_shared, act_all, in_all, shared_all, raw_gate_up, raw_down, bc_width, at
    )
    grad_in, grad_shared_weight, input_grad, flat, grad_out = back(
        part_in, part_bc, part_kv, grad_act, grad_resid, x_low, input_gain, flat, 0,
        raw_out, shared_weight.shape[0], at,
    )
    flat = flat.reshape(-1)
    sums = []
    start = 0
    for part in small:
        sums.append(flat[start : start + part.size].reshape(part.shape))
        start += part.size
    sum_input_gain, sum_middle_gain, sum_lanes, sum_convs, sum_heads, err_total = sums
    lanes_local = lax.dynamic_slice_in_dim(sum_lanes, at.t * width, width, 1)
    heads_local = lax.dynamic_slice_in_dim(sum_heads, at.t * local_heads, local_heads, 1)
    loss = err_total / jnp.sum(lengths).astype(f32)
    query_from = 2 * width
    step_from = query_from + query_width
    return (
        layer_out,
        loss,
        input_grad,
        sum_input_gain,
        grad_in[:, :query_from].reshape(w_rows, 2, width),
        grad_in[:, step_from : step_from + local_heads],
        grad_in[:, query_from:step_from],
        grad_shared_weight,
        lanes_local[:KC],
        sum_convs,
        heads_local[0],
        heads_local[1],
        heads_local[2],
        lanes_local[KC],
        grad_out[:, :width],
        grad_out[:, width:],
        sum_middle_gain,
        grad_gate_up.reshape(w_rows, 2, hidden_width),
        grad_down,
    )


def solution(mesh):
    placed = (
        P(("dp", "tensor"), None),
        P(("dp", "tensor"), None),
        P(),
        P(),
        P("dp", None, "tensor"),
        P("dp", "tensor"),
        P("dp", "tensor"),
        P(("dp", "tensor"), None),
        P(None, "tensor"),
        P(),
        P("tensor"),
        P("tensor"),
        P("tensor"),
        P("tensor"),
        P("dp", "tensor"),
        P("dp", "tensor"),
        P(),
        P("dp", None, "tensor"),
        P("dp", "tensor"),
    )
    return jax.shard_map(
        per_device,
        mesh=mesh,
        in_specs=placed,
        out_specs=(
            P(("dp", "tensor"), None),
            P(),
            P(("dp", "tensor"), None),
            P(),
            P("dp", None, "tensor"),
            P("dp", "tensor"),
            P("dp", "tensor"),
            P(("dp", "tensor"), None),
            P(None, "tensor"),
            P(),
            P("tensor"),
            P("tensor"),
            P("tensor"),
            P("tensor"),
            P("dp", "tensor"),
            P("dp", "tensor"),
            P(),
            P("dp", None, "tensor"),
            P("dp", "tensor"),
        ),
        check_vma=False,
    )
```

```python
import functools

import jax
import jax.numpy as jnp
from jax import lax
from jax.experimental import pallas as pl
from jax.experimental.pallas import tpu as pltpu
from jax.sharding import PartitionSpec as P

H = 48
KC = 4
QH = 8
KVH = 2
HD = 128
DI = 3072

EPS = 1e-05
ROPE_BASE = 100000000000.0


def rms_norm(values, gain):
    return values * lax.rsqrt(jnp.mean(values * values, axis=-1, keepdims=True) + EPS) * gain


def low_dot(left, right, dims):
    return lax.dot_general(left, right, (dims, ((), ())), preferred_element_type=jnp.float32)


NN = ((1,), (0,))
NT = ((1,), (1,))
TN = ((0,), (0,))
CHUNK = 128
ROWS = 256
WIDE = 128
FAR = -1e30


def exact_dot(ones, values, parts=3):
    total = None
    for _ in range(parts):
        part = values.astype(jnp.bfloat16)
        values = values - part.astype(jnp.float32)
        term = low_dot(ones, part, NN)
        total = term if total is None else total + term
    return total


def split_dot(values, ones, parts=2):
    total = None
    for _ in range(parts):
        part = values.astype(jnp.bfloat16)
        values = values - part.astype(jnp.float32)
        term = low_dot(part, ones, NN)
        total = term if total is None else total + term
    return total


def sigmoid(v):
    return 1.0 / (1.0 + jnp.exp(-v))


def softplus(v):
    return jnp.maximum(v, 0.0) + jnp.log1p(jnp.exp(-jnp.abs(v)))


def iota(shape, axis):
    return lax.broadcasted_iota(jnp.int32, shape, axis)


def spin(values, cosine, sine):
    return values * cosine + pltpu.roll(values, HD // 2, 1) * sine


def unspin(values, cosine, sine):
    return values * cosine - pltpu.roll(values, HD // 2, 1) * sine


def attn_probs(query_low, key_low, first_row, scale):
    scores = low_dot(query_low, key_low, NT) * scale
    rows, keys = scores.shape
    allowed = iota((rows, keys), 1) <= iota((rows, keys), 0) + first_row
    scores = jnp.where(allowed, scores, FAR)
    top = jnp.max(scores, axis=1, keepdims=True)
    weights = jnp.exp(scores - top)
    return weights / jnp.sum(weights, axis=1, keepdims=True)


def attn_fwd_body(order, q_ref, kv_ref, cos_ref, sin_ref, out_ref, key_s, value_s):
    bf16 = jnp.bfloat16
    step = pl.program_id(0)
    cosine, sine = cos_ref[...], sin_ref[...]
    rows = pl.ds(pl.multiple_of(step * ROWS, ROWS), ROWS)
    key_s[rows, :] = spin(kv_ref[:, :HD], cosine, sine).astype(bf16)
    value_s[rows, :] = kv_ref[:, HD:].astype(bf16)
    heads = q_ref.shape[1] // HD
    blocks = key_s.shape[0] // ROWS
    for block in range(blocks):

        @pl.when(step == block)
        def _(block=block):
            keys = (block + 1) * ROWS
            for head in range(heads):
                lanes = slice(head * HD, (head + 1) * HD)
                query = spin(q_ref[:, lanes], cosine, sine).astype(bf16)
                probs = attn_probs(query, key_s[:keys, :], block * ROWS, HD**-0.5)
                out_ref[:, lanes] = low_dot(
                    probs.astype(bf16), value_s[:keys, :], NN
                ).astype(bf16)


def attn_bwd_body(
    order, q_ref, kv_ref, cos_ref, sin_ref, grad_ref, all_cos, all_sin, dq_ref, dkv_ref,
    key_s, value_s, dkey_s, dvalue_s,
):
    bf16, f32 = jnp.bfloat16, jnp.float32
    step = pl.program_id(0)

    @pl.when(step == 0)
    def _():
        dkey_s[...] = jnp.zeros_like(dkey_s)
        dvalue_s[...] = jnp.zeros_like(dvalue_s)

    cosine, sine = cos_ref[...], sin_ref[...]
    rows = pl.ds(pl.multiple_of(step * ROWS, ROWS), ROWS)
    key_s[rows, :] = spin(kv_ref[:, :HD], cosine, sine).astype(bf16)
    value_s[rows, :] = kv_ref[:, HD:].astype(bf16)
    heads = q_ref.shape[1] // HD
    blocks = key_s.shape[0] // ROWS
    scale = HD**-0.5
    for block in range(blocks):

        @pl.when(step == block)
        def _(block=block):
            keys = (block + 1) * ROWS
            for head in range(heads):
                lanes = slice(head * HD, (head + 1) * HD)
                query = spin(q_ref[:, lanes], cosine, sine).astype(bf16)
                probs = attn_probs(query, key_s[:keys, :], block * ROWS, scale)
                grad = grad_ref[:, lanes].astype(bf16)
                dprobs = low_dot(grad, value_s[:keys, :], NT)
                dvalue_s[:keys, :] += low_dot(probs.astype(bf16), grad, TN)
                inner = jnp.sum(dprobs * probs, axis=1, keepdims=True)
                dscores = (probs * (dprobs - inner) * scale).astype(bf16)
                dquery = low_dot(dscores, key_s[:keys, :], NN)
                dkey_s[:keys, :] += low_dot(dscores, query, TN)
                dq_ref[:, lanes] = unspin(dquery, cosine, sine).astype(bf16)

    @pl.when(step == blocks - 1)
    def _():
        dkv_ref[:, :HD] = unspin(dkey_s[...], all_cos[...], all_sin[...]).astype(bf16)
        dkv_ref[:, HD:] = dvalue_s[...].astype(bf16)


def conv_taps(ext, taps, first, width):
    rows = ext.shape[0] - 8
    total = None
    for tap in range(width):
        at = 8 - (width - 1) + tap
        term = ext[at : at + rows, :] * taps[first + tap : first + tap + 1, :]
        total = term if total is None else total + term
    return total


def decays(steps, head_params, tri):
    shifted = steps + head_params[0:1, :]
    dt = softplus(shifted)
    la = dt * head_params[1:2, :]
    cum = exact_dot(tri, la)
    return shifted, dt, la, cum


def spread_lanes(values, pair, first):
    rows = values.shape[0]
    a = jnp.broadcast_to(values[:, 2 * pair : 2 * pair + 1], (rows, WIDE))
    b = jnp.broadcast_to(values[:, 2 * pair + 1 : 2 * pair + 2], (rows, WIDE))
    return a, b, jnp.where(first, a, b)


def mixer_fwd_body(
    order, gate_ref, inner_ref, step_ref, bc_ref, attn_ref, lane_ref, conv_ref, head_ref,
    out_ref, y_ref, state_ref, ext_s, extbc_s, state_s, x_s,
):
    bf16, f32 = jnp.bfloat16, jnp.float32
    step = pl.program_id(0)
    width = inner_ref.shape[1]
    states = bc_ref.shape[1] // 2

    @pl.when(step == 0)
    def _():
        ext_s[0:8, :] = jnp.zeros((8, width), f32)
        extbc_s[0:8, :] = jnp.zeros((8, 2 * states), f32)
        state_s[...] = jnp.zeros_like(state_s)

    ext_s[8:, :] = inner_ref[...]
    extbc_s[8:, :] = bc_ref[...]
    pre = conv_taps(ext_s, lane_ref, 0, KC)
    x_s[...] = pre * sigmoid(pre)
    pre = conv_taps(extbc_s, conv_ref, 0, KC)
    bc = (pre * sigmoid(pre)).astype(bf16)
    ext_s[0:8, :] = ext_s[ROWS : ROWS + 8, :]
    extbc_s[0:8, :] = extbc_s[ROWS : ROWS + 8, :]
    row, col = iota((CHUNK, CHUNK), 0), iota((CHUNK, CHUNK), 1)
    causal = row >= col
    tri = jnp.where(causal, 1.0, 0.0).astype(bf16)
    first = iota((CHUNK, WIDE), 1) < WIDE // 2
    for sub in range(ROWS // CHUNK):
        lo = sub * CHUNK
        b_low = bc[lo : lo + CHUNK, :states]
        c_low = bc[lo : lo + CHUNK, states:]
        _, dt, _, cum = decays(step_ref[lo : lo + CHUNK, :], head_ref, tri)
        cum_t = cum.T
        cross = low_dot(c_low, b_low, NT)
        state_low = state_s[...].astype(bf16)
        state_ref[sub] = state_low
        b_t = b_low.T
        for pair in range(width // WIDE):
            lanes = slice(pair * WIDE, (pair + 1) * WIDE)
            cum_a, cum_b, cum_p = spread_lanes(cum, pair, first)
            _, _, dt_p = spread_lanes(dt, pair, first)
            weights = []
            for wide, head in ((cum_a, 2 * pair), (cum_b, 2 * pair + 1)):
                gap = jnp.where(causal, wide - cum_t[head : head + 1, :], FAR)
                weights.append((cross * jnp.exp(gap)).astype(bf16))
            x = x_s[lo : lo + CHUNK, lanes]
            scaled = x * dt_p
            zero = jnp.zeros_like(scaled)
            stacked = jnp.concatenate(
                [jnp.where(first, scaled, zero), jnp.where(first, zero, scaled)], axis=0
            ).astype(bf16)
            y = low_dot(jnp.concatenate(weights, axis=1), stacked, NN)
            y = y + jnp.exp(cum_p) * low_dot(c_low, state_low[:, lanes], NN)
            y_ref[lo : lo + CHUNK, lanes] = y + lane_ref[5:6, lanes] * x
            last = cum_p[CHUNK - 1 : CHUNK, :]
            ends = (scaled * jnp.exp(last - cum_p)).astype(bf16)
            state_s[:, lanes] = state_s[:, lanes] * jnp.exp(last) + low_dot(b_t, ends, NN)
    gate = gate_ref[...]
    gated = y_ref[...] * (gate * sigmoid(gate))
    scale = lax.rsqrt(jnp.mean(gated * gated, axis=1, keepdims=True) + EPS)
    out_ref[:, :width] = (gated * scale * lane_ref[4:5, :]).astype(bf16)
    out_ref[:, width:] = attn_ref[...]


def mixer_bwd_body(
    order, gate_ref, inner_ref, before_ref, step_ref, bc_ref, bcbefore_ref, y_ref, state_ref,
    grad_ref, dq_ref, dkv_ref, lane_ref, conv_ref, head_ref, seg_ref, first_ref, second_ref,
    low_ref, lowsh_ref, dlane_ref, dconv_ref, dhead_ref,
    ext_s, extbc_s, pre_s, prebc_s, x_s, bc_s, g_s, dx_s, dbc_s, dpre_s, dprebc_s, dstate_s,
    z_s, rows_s,
):
    bf16, f32 = jnp.bfloat16, jnp.float32
    step = pl.program_id(0)
    blocks = pl.num_programs(0)
    width = inner_ref.shape[1]
    states = bc_ref.shape[1] // 2
    query_width = dq_ref.shape[1]

    @pl.when(step == 0)
    def _():
        dlane_ref[...] = jnp.zeros_like(dlane_ref)
        dconv_ref[...] = jnp.zeros_like(dconv_ref)
        dhead_ref[...] = jnp.zeros_like(dhead_ref)
        dstate_s[...] = jnp.zeros_like(dstate_s)
        dpre_s[ROWS:, :] = jnp.zeros((8, width), f32)
        dprebc_s[ROWS:, :] = jnp.zeros((8, 2 * states), f32)
        z_s[...] = jnp.zeros_like(z_s)
        rows_s[...] = jnp.zeros_like(rows_s)

    keep = jnp.where(step == blocks - 1, 0.0, 1.0)
    ext_s[0:8, :] = before_ref[...] * keep
    extbc_s[0:8, :] = bcbefore_ref[...] * keep
    ext_s[8:, :] = inner_ref[...]
    extbc_s[8:, :] = bc_ref[...]
    pre = conv_taps(ext_s, lane_ref, 0, KC)
    pre_s[...] = pre
    x_s[...] = pre * sigmoid(pre)
    pre = conv_taps(extbc_s, conv_ref, 0, KC)
    prebc_s[...] = pre
    bc_s[...] = (pre * sigmoid(pre)).astype(bf16)

    gate = gate_ref[...]
    sig = sigmoid(gate)
    gate_act = gate * sig
    y = y_ref[...]
    gated = y * gate_act
    scale = lax.rsqrt(jnp.mean(gated * gated, axis=1, keepdims=True) + EPS)
    grad = grad_ref[...]
    dlane_ref[4:5, :] += jnp.sum(grad * gated * scale, axis=0, keepdims=True)
    grad = grad * lane_ref[4:5, :]
    mean = jnp.mean(grad * gated, axis=1, keepdims=True)
    dgated = scale * grad - gated * (scale * scale * scale * mean)
    g_s[...] = dgated * gate_act
    low_ref[:, :width] = (dgated * y * sig * (1.0 + gate * (1.0 - sig))).astype(bf16)

    row, col = iota((CHUNK, CHUNK), 0), iota((CHUNK, CHUNK), 1)
    tri = jnp.where(row >= col, 1.0, 0.0).astype(bf16)
    tri_up = jnp.where(row <= col, 1.0, 0.0).astype(bf16)
    later = row <= col
    first = iota((CHUNK, WIDE), 1) < WIDE // 2
    last_row = iota((CHUNK, WIDE), 0) == CHUNK - 1
    for sub in reversed(range(ROWS // CHUNK)):
        lo = sub * CHUNK
        b_low = bc_s[lo : lo + CHUNK, :states]
        c_low = bc_s[lo : lo + CHUNK, states:]
        shifted, dt, la, cum = decays(step_ref[lo : lo + CHUNK, :], head_ref, tri)
        cum_t = cum.T
        cross_t = low_dot(b_low, c_low, NT)
        c_t = c_low.T
        state_low = state_ref[sub]
        dstate_low = dstate_s[...].astype(bf16)
        dcross_t = jnp.zeros((CHUNK, CHUNK), f32)
        db = jnp.zeros((CHUNK, states), f32)
        dc = jnp.zeros((CHUNK, states), f32)
        for pair in range(width // WIDE):
            lanes = slice(pair * WIDE, (pair + 1) * WIDE)
            cum_a, cum_b, cum_p = spread_lanes(cum, pair, first)
            _, _, dt_p = spread_lanes(dt, pair, first)
            x = x_s[lo : lo + CHUNK, lanes]
            g = g_s[lo : lo + CHUNK, lanes]
            scaled = x * dt_p
            scaled_low = scaled.astype(bf16)
            zero = jnp.zeros_like(g)
            g_stack = jnp.concatenate(
                [jnp.where(first, g, zero), jnp.where(first, zero, g)], axis=0
            ).astype(bf16)
            dweights_t = low_dot(scaled_low, g_stack, NT)
            weights_t = []
            for place, wide, head in ((0, cum_a, 2 * pair), (1, cum_b, 2 * pair + 1)):
                gap = jnp.where(later, cum_t[head : head + 1, :] - wide, FAR)
                grow = jnp.exp(gap)
                weight = (cross_t * grow).astype(bf16)
                weights_t.append(weight)
                dweight = dweights_t[:, place * CHUNK : (place + 1) * CHUNK]
                dcross_t = dcross_t + dweight * grow
                rows_s[head : head + 1, :] = jnp.sum(
                    dweight * weight.astype(f32), axis=0, keepdims=True
                )
            dx_in = low_dot(jnp.concatenate(weights_t, axis=1), g_stack, NN)
            grown = jnp.exp(cum_p)
            last = cum_p[CHUNK - 1 : CHUNK, :]
            tail = jnp.exp(last - cum_p)
            last = jnp.exp(last)
            dx_tail = tail * low_dot(b_low, dstate_low[:, lanes], NN)
            dscaled = dx_in + dx_tail
            g_grown = g * grown
            g_low = g_grown.astype(bf16)
            ends = (scaled * tail).astype(bf16)
            carried = low_dot(c_low, state_low[:, lanes], NN)
            dc = dc + low_dot(g_low, state_low[:, lanes], NT)
            db = db + low_dot(ends, dstate_low[:, lanes], NT)
            dstate = dstate_s[:, lanes]
            kept = jnp.sum(dstate * state_low[:, lanes].astype(f32), axis=0, keepdims=True) * last
            dstate_s[:, lanes] = dstate * last + low_dot(c_t, g_low, NN)
            tails = scaled * dx_tail
            z_s[0:CHUNK, lanes] = g_grown * carried - tails - scaled_low.astype(f32) * dx_in
            z_s[CHUNK : 2 * CHUNK, lanes] = dscaled * x
            z_s[2 * CHUNK : 2 * CHUNK + 1, lanes] = (
                jnp.sum(tails, axis=0, keepdims=True) + kept
            )
            dx_s[lo : lo + CHUNK, lanes] = dscaled * dt_p + lane_ref[5:6, lanes] * g
            dlane_ref[5:6, lanes] += jnp.sum(g * x, axis=0, keepdims=True)
        sums = split_dot(z_s[...], seg_ref[...])
        dcum = sums[0:CHUNK, :] + rows_s[...].T
        dcum = dcum + jnp.where(last_row, sums[2 * CHUNK : 2 * CHUNK + 1, :], 0.0)
        dla = exact_dot(tri_up, dcum)
        ddt = sums[CHUNK : 2 * CHUNK, :] + dla * head_ref[1:2, :]
        dsteps = ddt * sigmoid(shifted)
        dhead_ref[0:1, :] += jnp.sum(dsteps, axis=0, keepdims=True)
        dhead_ref[1:2, :] += jnp.sum(dla * la, axis=0, keepdims=True)
        low_ref[lo : lo + CHUNK, 2 * width + query_width :] = dsteps.astype(bf16)
        dcross_low = dcross_t.astype(bf16)
        dbc_s[lo : lo + CHUNK, :states] = db + low_dot(dcross_low, c_low, NN)
        dbc_s[lo : lo + CHUNK, states:] = dc + low_dot(dcross_low, b_low, TN)

    def conv_back(pre_ref, dact, dpre_ref, ext, taps, dtaps_ref):
        pre = pre_ref[...]
        sig = sigmoid(pre)
        dpre = dact * (sig * (1.0 + pre * (1.0 - sig)))
        dpre_ref[0:ROWS, :] = dpre
        total = None
        for tap in range(KC):
            ahead = KC - 1 - tap
            term = dpre_ref[ahead : ahead + ROWS, :] * taps[tap : tap + 1, :]
            total = term if total is None else total + term
            at = 8 - (KC - 1) + tap
            dtaps_ref[tap : tap + 1, :] += jnp.sum(
                dpre * ext[at : at + ROWS, :], axis=0, keepdims=True
            )
        dpre_ref[ROWS:, :] = dpre_ref[0:8, :]
        return total

    dinner = conv_back(pre_s, dx_s[...], dpre_s, ext_s, lane_ref, dlane_ref)
    low_ref[:, width : 2 * width] = dinner.astype(bf16)
    dbc = conv_back(prebc_s, dbc_s[...], dprebc_s, extbc_s, conv_ref, dconv_ref)
    lowsh_ref[:, : 2 * states] = dbc.astype(bf16)
    lowsh_ref[:, 2 * states :] = dkv_ref[...]
    low_ref[:, 2 * width : 2 * width + query_width] = dq_ref[...]


def block_at(rows, cols, col):
    return pl.BlockSpec((rows, cols), lambda i, order: (order[i], col))


def whole_at(shape):
    return pl.BlockSpec(shape, lambda i, order: (0,) * len(shape))


def kernel_params():
    return pltpu.CompilerParams(
        dimension_semantics=("arbitrary",), vmem_limit_bytes=56 * 1024 * 1024
    )


def attn_forward(order, proj, proj_shared, cosine, sine, query_width, width, bc_width):
    slot = proj.shape[0]
    scratch = [pltpu.VMEM((slot, HD), jnp.bfloat16)] * 2
    return pl.pallas_call(
        attn_fwd_body,
        grid_spec=pltpu.PrefetchScalarGridSpec(
            num_scalar_prefetch=1,
            grid=(slot // ROWS,),
            in_specs=[
                block_at(ROWS, query_width, 2 * width // query_width),
                block_at(ROWS, 2 * HD, bc_width // (2 * HD)),
                pl.BlockSpec((ROWS, HD), lambda i, order: (i, 0)),
                pl.BlockSpec((ROWS, HD), lambda i, order: (i, 0)),
            ],
            out_specs=block_at(ROWS, query_width, 0),
            scratch_shapes=scratch,
        ),
        out_shape=jax.ShapeDtypeStruct((slot, query_width), jnp.bfloat16),
        compiler_params=kernel_params(),
        cost_estimate=pl.CostEstimate(
            flops=slot * slot * query_width * 3,
            bytes_accessed=slot * 4 * (query_width + 4 * HD),
            transcendentals=slot * slot * query_width // HD,
        ),
    )(order, proj, proj_shared, cosine, sine)


def attn_backward(order, proj, proj_shared, cosine, sine, grad_heads, query_width, width, bc_width):
    slot = proj.shape[0]
    return pl.pallas_call(
        attn_bwd_body,
        grid_spec=pltpu.PrefetchScalarGridSpec(
            num_scalar_prefetch=1,
            grid=(slot // ROWS,),
            in_specs=[
                block_at(ROWS, query_width, 2 * width // query_width),
                block_at(ROWS, 2 * HD, bc_width // (2 * HD)),
                pl.BlockSpec((ROWS, HD), lambda i, order: (i, 0)),
                pl.BlockSpec((ROWS, HD), lambda i, order: (i, 0)),
                block_at(ROWS, query_width, width // query_width),
                whole_at((slot, HD)),
                whole_at((slot, HD)),
            ],
            out_specs=[block_at(ROWS, query_width, 0), whole_at((slot, 2 * HD))],
            scratch_shapes=[pltpu.VMEM((slot, HD), jnp.bfloat16)] * 2
            + [pltpu.VMEM((slot, HD), jnp.float32)] * 2,
        ),
        out_shape=[
            jax.ShapeDtypeStruct((slot, query_width), jnp.bfloat16),
            jax.ShapeDtypeStruct((slot, 2 * HD), jnp.bfloat16),
        ],
        compiler_params=kernel_params(),
        cost_estimate=pl.CostEstimate(
            flops=slot * slot * query_width * 8,
            bytes_accessed=slot * 4 * (2 * query_width + 6 * HD),
            transcendentals=slot * slot * query_width // HD,
        ),
    )(order, proj, proj_shared, cosine, sine, grad_heads, cosine, sine)


def mixer_forward(order, proj, proj_shared, attn_low, lane_params, conv_shared, head_params):
    slot = proj.shape[0]
    f32, bf16 = jnp.float32, jnp.bfloat16
    width = lane_params.shape[1]
    bc_width = conv_shared.shape[1]
    query_width = attn_low.shape[1]
    chunks = ROWS // CHUNK
    return pl.pallas_call(
        mixer_fwd_body,
        grid_spec=pltpu.PrefetchScalarGridSpec(
            num_scalar_prefetch=1,
            grid=(slot // ROWS,),
            in_specs=[
                block_at(ROWS, width, 0),
                block_at(ROWS, width, 1),
                block_at(ROWS, WIDE, (2 * width + query_width) // WIDE),
                block_at(ROWS, bc_width, 0),
                block_at(ROWS, query_width, 0),
                whole_at(lane_params.shape),
                whole_at(conv_shared.shape),
                whole_at(head_params.shape),
            ],
            out_specs=[
                block_at(ROWS, width + query_width, 0),
                pl.BlockSpec((ROWS, width), lambda i, order: (i, 0)),
                pl.BlockSpec((chunks, bc_width // 2, width), lambda i, order: (i, 0, 0)),
            ],
            scratch_shapes=[
                pltpu.VMEM((ROWS + 8, width), f32),
                pltpu.VMEM((ROWS + 8, bc_width), f32),
                pltpu.VMEM((bc_width // 2, width), f32),
                pltpu.VMEM((ROWS, width), f32),
            ],
        ),
        out_shape=[
            jax.ShapeDtypeStruct((slot, width + query_width), bf16),
            jax.ShapeDtypeStruct((slot, width), f32),
            jax.ShapeDtypeStruct((slot // CHUNK, bc_width // 2, width), bf16),
        ],
        compiler_params=kernel_params(),
        cost_estimate=pl.CostEstimate(
            flops=slot * width * bc_width * 8,
            bytes_accessed=slot * width * 20,
            transcendentals=slot * width * 8,
        ),
    )(order, proj, proj, proj, proj_shared, attn_low, lane_params, conv_shared, head_params)


def mixer_backward(
    order, proj, proj_shared, y, states, grad_heads, dq, dkv, lane_params, conv_shared,
    head_params, seg, query_width, moved,
):
    slot = proj.shape[0]
    f32, bf16 = jnp.float32, jnp.bfloat16
    width = lane_params.shape[1]
    bc_width = conv_shared.shape[1]
    blocks = slot // ROWS
    chunks = ROWS // CHUNK

    def back(rows, cols, col):
        return pl.BlockSpec((rows, cols), lambda i, order: (order[blocks - 1 - i], col))

    def straight(shape):
        return pl.BlockSpec(
            shape, lambda i, order: (blocks - 1 - i,) + (0,) * (len(shape) - 1)
        )

    def before(cols, col):
        return pl.BlockSpec(
            (8, cols),
            lambda i, order: (
                order[jnp.maximum(blocks - 2 - i, 0)] * (ROWS // 8) + ROWS // 8 - 1,
                col,
            ),
        )

    return pl.pallas_call(
        mixer_bwd_body,
        grid_spec=pltpu.PrefetchScalarGridSpec(
            num_scalar_prefetch=1,
            grid=(blocks,),
            in_specs=[
                back(ROWS, width, 0),
                back(ROWS, width, 1),
                before(width, 1),
                back(ROWS, WIDE, (2 * width + query_width) // WIDE),
                back(ROWS, bc_width, 0),
                before(bc_width, 0),
                straight((ROWS, width)),
                straight((chunks, bc_width // 2, width)),
                back(ROWS, width, 0),
                back(ROWS, query_width, 0),
                straight((ROWS, 2 * HD)),
                whole_at(lane_params.shape),
                whole_at(conv_shared.shape),
                whole_at(head_params.shape),
                whole_at(seg.shape),
                pl.BlockSpec(memory_space=pl.ANY),
                pl.BlockSpec(memory_space=pl.ANY),
            ],
            out_specs=[
                back(ROWS, 2 * width + query_width + WIDE, 0),
                back(ROWS, bc_width + 2 * HD, 0),
                whole_at((8, width)),
                whole_at((8, bc_width)),
                whole_at((8, WIDE)),
            ],
            scratch_shapes=[
                pltpu.VMEM((ROWS + 8, width), f32),
                pltpu.VMEM((ROWS + 8, bc_width), f32),
                pltpu.VMEM((ROWS, width), f32),
                pltpu.VMEM((ROWS, bc_width), f32),
                pltpu.VMEM((ROWS, width), f32),
                pltpu.VMEM((ROWS, bc_width), bf16),
                pltpu.VMEM((ROWS, width), f32),
                pltpu.VMEM((ROWS, width), f32),
                pltpu.VMEM((ROWS, bc_width), f32),
                pltpu.VMEM((ROWS + 8, width), f32),
                pltpu.VMEM((ROWS + 8, bc_width), f32),
                pltpu.VMEM((bc_width // 2, width), f32),
                pltpu.VMEM((2 * CHUNK + 8, width), f32),
                pltpu.VMEM((WIDE, CHUNK), f32),
            ],
        ),
        out_shape=[
            jax.ShapeDtypeStruct((slot, 2 * width + query_width + WIDE), bf16),
            jax.ShapeDtypeStruct((slot, bc_width + 2 * HD), bf16),
            jax.ShapeDtypeStruct((8, width), f32),
            jax.ShapeDtypeStruct((8, bc_width), f32),
            jax.ShapeDtypeStruct((8, WIDE), f32),
        ],
        compiler_params=kernel_params(),
        cost_estimate=pl.CostEstimate(
            flops=slot * width * bc_width * 20,
            bytes_accessed=slot * width * 40,
            transcendentals=slot * width * 16,
        ),
    )(
        order, proj, proj, proj, proj, proj_shared, proj_shared, y, states, grad_heads, dq, dkv,
        lane_params, conv_shared, head_params, seg, *moved,
    )


class Places:
    def __init__(self):
        self.dp = lax.axis_size("dp")
        self.tp = lax.axis_size("tensor")
        d = lax.axis_index("dp")
        t = lax.axis_index("tensor")
        self.d, self.t = d, t
        self.c = d % 2
        self.k = d // 2
        self.zq = t % 2
        self.home = self.c == t // 2
        self.quarter = 2 * self.c + self.zq
        self.column = self.zq + 2 * self.c
        self.slot = 2 * self.k + t // 2
        self.blocks = self.dp // 2
        self.bits = self.blocks.bit_length() - 1

    def pairs(self, where_to):
        out = []
        for d in range(self.dp):
            for t in range(self.tp):
                target = where_to(d, t)
                if target is not None:
                    out.append((d * self.tp + t, target[0] * self.tp + target[1]))
        return out

    def send(self, values, where_to):
        return lax.ppermute(values, ("dp", "tensor"), self.pairs(where_to))

    def over_core(self, values):
        return self.send(values, lambda d, t: (d ^ 1, t))

    def over_z(self, values):
        return self.send(values, lambda d, t: (d, t ^ 1))

    def over_far(self, values):
        return self.send(values, lambda d, t: (d, t ^ 2))

    def over_bit(self, values, bit):
        return self.send(values, lambda d, t: (d ^ (2 << bit), t))

    def swap_away(self, values):
        def where_to(d, t):
            if d % 2 == t // 2:
                return None
            return (d ^ 1, t ^ 2)

        return self.send(values, where_to)

    def column_out(self, values):
        def where_to(d, t):
            if d % 2 == t // 2:
                return (d, t ^ 2)
            return (d ^ 1, t)

        return self.send(values, where_to)

    def column_back(self, values):
        def where_to(d, t):
            if d % 2 == t // 2:
                return (d ^ 1, t)
            return (d, t ^ 2)

        return self.send(values, where_to)


def relocate(values, at):
    return jnp.where(at.home, values, at.swap_away(values))


MESH = pl.DeviceIdType.MESH


class Lanes:
    def __init__(self, blocks):
        d = lax.axis_index("dp")
        t = lax.axis_index("tensor")
        self.c = lax.rem(d, 2)
        self.k = lax.div(d, 2)
        self.d, self.t = d, t
        self.home = self.c == lax.div(t, 2)
        self.away = self.c != lax.div(t, 2)
        self.other = d + 1 - 2 * self.c
        self.near = t + 1 - 2 * lax.rem(t, 2)
        self.far = lax.rem(t + 2, 4)
        self.blocks = blocks
        self.bits = blocks.bit_length() - 1

    def block(self, place):
        value = self.k
        for bit in range(self.bits):
            if (place >> bit) & 1:
                value = value + (1 << bit) * (1 - 2 * lax.rem(lax.div(self.k, 1 << bit), 2))
        return value

    def across(self, bit):
        return (2 * self.block(1 << bit) + self.c, self.t)

    def greet(self):
        partners = [
            (self.other, self.t),
            (self.d, self.near),
            (self.d, self.far),
            (self.other, self.far),
        ] + [self.across(bit) for bit in range(self.bits)]
        barrier = pltpu.get_barrier_semaphore()
        for partner in partners:
            pl.semaphore_signal(barrier, inc=1, device_id=partner, device_id_type=MESH)
        pl.semaphore_wait(barrier, len(partners))


def remote(src, dst, send_sem, recv_sem, device):
    return pltpu.make_async_remote_copy(
        src_ref=src,
        dst_ref=dst,
        send_sem=send_sem,
        recv_sem=recv_sem,
        device_id=device,
        device_id_type=MESH,
    )


def onward(place, half, bits):
    if half == 0:
        return [bit for bit in range(bits) if place < (1 << bit)]
    return [bit for bit in reversed(range(bits)) if place % (2 << bit) == 0]


class Spread:
    def __init__(self, lanes, full, rows, chunks, send_sems, recv_sems, cols=slice(None), first=None, first_cols=None):
        self.lanes, self.full, self.rows, self.chunks = lanes, full, rows, chunks
        self.cols, self.first, self.first_cols = cols, first, first_cols
        self.piece = rows // chunks
        self.send_sems, self.recv_sems = send_sems, recv_sems

    def view(self, place, half, chunk):
        start = self.lanes.block(place) * (2 * self.rows) + half * self.rows + chunk * self.piece
        return self.full.at[pl.ds(pl.multiple_of(start, self.piece), self.piece), self.cols]

    def copy(self, place, half, chunk, bit):
        view = self.view(place, half, chunk)
        to = place | (1 << bit)
        source = view
        if place == 0 and self.first is not None:
            start = half * self.rows + chunk * self.piece
            source = self.first.at[pl.ds(start, self.piece), self.first_cols]
        return remote(
            source,
            view,
            self.send_sems.at[half, to, chunk],
            self.recv_sems.at[half, to, chunk],
            self.lanes.across(bit),
        )

    def give(self, place, half, chunk):
        for bit in onward(place, half, self.lanes.bits):
            self.copy(place, half, chunk, bit).start()

    def take(self, place, half, chunk):
        view = self.view(place, half, chunk)
        remote(
            view,
            view,
            self.send_sems.at[half, place, chunk],
            self.recv_sems.at[half, place, chunk],
            self.lanes.across(0),
        ).wait_recv()

    def pass_on(self, chunk):
        for half in range(2):
            places = range(1, self.lanes.blocks)
            if half == 1:
                key = lambda place: [-bit for bit in reversed(range(8)) if (place >> bit) & 1]
                places = sorted(places, key=key)
            for place in places:
                if onward(place, half, self.lanes.bits):
                    self.take(place, half, chunk)
                    self.give(place, half, chunk)

    def settle(self, place):
        for half in range(2):
            if not onward(place, half, self.lanes.bits):
                for chunk in range(self.chunks):
                    self.take(place, half, chunk)

    def sent(self, chunk):
        for half in range(2):
            for place in range(self.lanes.blocks):
                for bit in onward(place, half, self.lanes.bits):
                    self.copy(place, half, chunk, bit).wait_send()


def front_body(
    blocks, chunks, in_ref, out_ref, down_ref, shared_ref, x_ref, gain_ref, par_ref,
    full_ref, pair_ref, dpair_ref, act_ref, xr_ref, sh_ref, parr_ref, proj_ref, projsh_ref, shall_ref,
    x_s, act_s, home_sems, z_send, z_recv, o_sems, o_recv, send_sems, recv_sems, x_sems, a_send,
    a_recv, line_send, line_recv, sh_send, sh_recv, swap_send, swap_recv, par_sems,
    win_s, wsh_s, acc_s, w_sems, keep_sems, out_sems,
):
    lanes = Lanes(blocks)
    rows = in_ref.shape[0]
    piece = rows // chunks
    here = x_ref.shape[0]
    c, t = lanes.c, lanes.t
    lanes.greet()
    spread = Spread(lanes, full_ref, rows, chunks, send_sems, recv_sems)
    few, wide = shared_ref.shape
    side = wide // 2
    mine = pl.ds(pl.multiple_of(c * side, side), side)
    theirs = pl.ds(pl.multiple_of((1 - c) * side, side), side)

    def line_view(half, at_t, cols):
        start = lanes.k * (2 * rows) + half * rows + at_t * few
        return sh_ref.at[pl.ds(pl.multiple_of(start, few), few), cols]

    def line_own():
        return pltpu.make_async_copy(
            shared_ref.at[:, mine], line_view(c, t, mine), line_send.at[0]
        )

    def line_swap():
        return remote(
            shared_ref.at[:, theirs],
            line_view(c, t, theirs),
            line_send.at[1],
            line_recv.at[0],
            (lanes.other, t),
        )

    def line_swapped():
        view = line_view(1 - c, t, mine)
        return remote(view, view, line_send.at[1], line_recv.at[0], (lanes.other, t))

    def line_near(half, came):
        view = line_view(half, lanes.near if came else t, mine)
        return remote(
            view, view, line_send.at[2 + half], line_recv.at[1 + half], (lanes.d, lanes.near)
        )

    def line_far(half, near, came):
        at_t = lanes.near if near else t
        if came:
            at_t = lax.rem(at_t + 2, 4)
        view = line_view(half, at_t, mine)
        place = 2 * near + half
        return remote(
            view, view, line_send.at[4 + place], line_recv.at[3 + place], (lanes.d, lanes.far)
        )

    shared_spread = Spread(lanes, sh_ref, rows, 1, sh_send, sh_recv, mine)

    def swap_copy(place, half, came):
        start = lanes.block(place) * (2 * rows) + half * rows
        view = sh_ref.at[pl.ds(pl.multiple_of(start, rows), rows), theirs if came else mine]
        return remote(
            view, view, swap_send.at[half, place], swap_recv.at[half, place], (lanes.other, t)
        )

    def slot(chunk):
        start = lanes.k * (2 * rows) + c * rows + chunk * piece
        return full_ref.at[pl.ds(pl.multiple_of(start, piece), piece), :]

    def first_copy(chunk, device):
        return remote(
            in_ref.at[pl.ds(chunk * piece, piece), :],
            slot(chunk),
            z_send.at[0, chunk],
            z_recv.at[c, chunk],
            device,
        )

    def second_copy(chunk):
        return remote(
            in_ref.at[pl.ds(chunk * piece, piece), :],
            slot(chunk),
            z_send.at[1, chunk],
            z_recv.at[c, chunk],
            (lanes.other, lanes.far),
        )

    def own_copy(chunk):
        return pltpu.make_async_copy(
            in_ref.at[pl.ds(chunk * piece, piece), :], slot(chunk), home_sems.at[chunk]
        )

    riders = ((out_ref, pair_ref), (down_ref, dpair_ref))

    def out_slot(i):
        return riders[i][1].at[pl.ds(pl.multiple_of(c * rows, rows), rows), :]

    def out_first(i, device):
        return remote(riders[i][0], out_slot(i), o_sems.at[i, 0], o_recv.at[i, c], device)

    def out_second(i):
        return remote(
            riders[i][0], out_slot(i), o_sems.at[i, 1], o_recv.at[i, c], (lanes.other, lanes.far)
        )

    def out_own(i):
        return pltpu.make_async_copy(riders[i][0], out_slot(i), o_sems.at[i, 2])

    def out_came(i, half):
        view = riders[i][1].at[pl.ds(pl.multiple_of(half * rows, rows), rows), :]
        remote(view, view, o_sems.at[i, 0], o_recv.at[i, half], (lanes.other, t)).wait_recv()

    def x_away():
        return remote(x_ref, x_s, x_sems.at[0], x_sems.at[1], (lanes.other, lanes.far))

    def x_home():
        return pltpu.make_async_copy(x_ref, x_s, x_sems.at[2])

    def send_first(chunk):
        @pl.when(lanes.home)
        def _():
            own_copy(chunk).start()
            first_copy(chunk, (lanes.d, lanes.far)).start()

        @pl.when(lanes.away)
        def _():
            first_copy(chunk, (lanes.other, t)).start()
            second_copy(chunk).start()

    def z_view(half, chunk):
        start = lanes.k * (2 * rows) + half * rows + chunk * piece
        return full_ref.at[pl.ds(pl.multiple_of(start, piece), piece), :]

    def came(half, chunk):
        view = z_view(half, chunk)
        return remote(
            view, view, z_send.at[0, chunk], z_recv.at[half, chunk], (lanes.other, t)
        )

    def arrive_home(chunk):
        own_copy(chunk).wait()
        start = lanes.k * (2 * rows) + (1 - c) * rows + chunk * piece
        view = full_ref.at[pl.ds(pl.multiple_of(start, piece), piece), :]
        remote(
            view, view, z_send.at[0, chunk], z_recv.at[1 - c, chunk], (lanes.other, t)
        ).wait_recv()
        for half in range(2):
            spread.give(0, half, chunk)

    def arrive_away(chunk):
        for half in range(2):
            came(half, chunk).wait_recv()
        for half in range(2):
            spread.give(0, half, chunk)

    def arrive(chunk):
        @pl.when(lanes.home)
        def _():
            arrive_home(chunk)

        @pl.when(lanes.away)
        def _():
            arrive_away(chunk)

    block = 2 * rows

    def act_slot(index):
        return act_s.at[:, pl.ds(index * here, here), :]

    def act_far():
        return remote(
            act_slot(0), act_slot(2), a_send.at[0], a_recv.at[0], (lanes.d, lanes.near)
        )

    def act_core():
        return remote(act_slot(0), act_slot(1), a_send.at[1], a_recv.at[1], (lanes.other, t))

    def act_both():
        return remote(act_slot(2), act_slot(3), a_send.at[2], a_recv.at[2], (lanes.other, t))

    def norm():
        @pl.when(lanes.home)
        def _():
            x_home().wait()

        @pl.when(lanes.away)
        def _():
            x_away().wait_recv()

        @pl.loop(0, here // 32)
        def _(step):
            part = pl.ds(pl.multiple_of(step * 32, 32), 32)
            x = x_s[part, :].astype(jnp.float32)
            scale = lax.rsqrt(jnp.mean(x * x, axis=1, keepdims=True) + EPS)
            act = (x * scale * gain_ref[...]).astype(jnp.bfloat16)
            for index in range(blocks):
                act_s[index, part, :] = act[:, index * block : (index + 1) * block]

        act_far().start()
        act_core().start()
        pltpu.make_async_copy(x_s, xr_ref, x_sems.at[3]).start()

    def par_away():
        return remote(
            par_ref, parr_ref, par_sems.at[0], par_sems.at[1], (lanes.other, lanes.far)
        )

    @pl.when(lanes.home)
    def _():
        parr_ref[...] = par_ref[...]

    @pl.when(lanes.away)
    def _():
        par_away().start()

    early = list(range(max(chunks // 2, 1)))
    late = list(range(len(early), chunks))
    line_own().start()
    line_swap().start()
    for chunk in early:
        send_first(chunk)

    @pl.when(lanes.home)
    def _():
        x_home().start()

    @pl.when(lanes.away)
    def _():
        x_away().start()

    line_own().wait()
    line_swapped().wait_recv()
    for half in range(2):
        line_near(half, False).start()
    for chunk in early:
        arrive(chunk)
        if chunk:
            spread.pass_on(chunk - 1)
    for half in range(2):
        line_near(half, True).wait_recv()
    for near in range(2):
        for half in range(2):
            line_far(half, near, False).start()
    for chunk in late:
        send_first(chunk)
    spread.pass_on(early[-1])

    @pl.when(lanes.home)
    def _():
        for chunk in late:
            arrive_home(chunk)
            spread.pass_on(chunk)

    norm()

    for i in range(2):

        @pl.when(lanes.home)
        def _(i=i):
            out_first(i, (lanes.d, lanes.far)).start()
            out_own(i).start()

        @pl.when(lanes.away)
        def _(i=i):
            out_first(i, (lanes.other, t)).start()
            out_second(i).start()

    for near in range(2):
        for half in range(2):
            line_far(half, near, True).wait_recv()
    for half in range(2):
        shared_spread.give(0, half, 0)
        swap_copy(0, half, False).start()

    @pl.when(lanes.away)
    def _():
        for chunk in late:
            arrive_away(chunk)
            if chunk > late[0]:
                spread.pass_on(chunk - 1)

    shared_spread.pass_on(0)

    @pl.when(lanes.away)
    def _():
        for chunk in late[-1:]:
            spread.pass_on(chunk)

    for place in range(1, blocks):
        shared_spread.settle(place)
    for half in range(2):
        for place in range(1, blocks):
            swap_copy(place, half, False).start()

    width = full_ref.shape[1]
    narrow = wsh_s.shape[2]
    kv = (narrow - side) // 2

    def weight_copies(place, slot):
        start = lanes.block(place) * block
        view = pl.ds(pl.multiple_of(start, block), block)
        key = pl.ds(pl.multiple_of(side + c * kv, kv), kv)
        value = pl.ds(pl.multiple_of(side + 2 * kv + c * kv, kv), kv)
        return [
            pltpu.make_async_copy(src, dst, w_sems.at[slot, i])
            for i, (src, dst) in enumerate(
                (
                    (full_ref.at[view, :], win_s.at[slot]),
                    (sh_ref.at[view, pl.ds(0, side)], wsh_s.at[slot, :, pl.ds(0, side)]),
                    (sh_ref.at[view, key], wsh_s.at[slot, :, pl.ds(side, kv)]),
                    (sh_ref.at[view, value], wsh_s.at[slot, :, pl.ds(side + kv, kv)]),
                )
            )
        ]

    def shared_copy(place, slot):
        start = lanes.block(place) * block
        view = pl.ds(pl.multiple_of(start, block), block)
        return pltpu.make_async_copy(wsh_s.at[slot], shall_ref.at[view, :], keep_sems.at[slot])

    def fetch(place):
        if place:
            spread.settle(place)
        for half in range(2):
            swap_copy(place, half, True).wait_recv()
        if place >= 2:
            shared_copy(place - 2, place % 2).wait()
        for copy in weight_copies(place, place % 2):
            copy.start()

    def accumulate(place, first, last):
        slot = place % 2
        index = lanes.block(place)

        @pl.loop(first, last)
        def _(part):
            at_rows = pl.ds(pl.multiple_of(part * here, here), here)
            left = act_s[index, at_rows, :]
            for src, base in ((win_s, 0), (wsh_s, width)):
                total = src.shape[2]
                tile = total // 3
                for col in range(0, total, tile):
                    cols = slice(base + col, base + col + tile)
                    product = low_dot(left, src[slot, :, col : col + tile], NN)
                    if place:
                        product = product + acc_s[at_rows, cols]
                    acc_s[at_rows, cols] = product

    def out_copies(part):
        at_rows = pl.ds(part * here, here)
        return [
            pltpu.make_async_copy(
                acc_s.at[at_rows, pl.ds(0, width)], proj_ref.at[at_rows, :], out_sems.at[0, part]
            ),
            pltpu.make_async_copy(
                acc_s.at[at_rows, pl.ds(width, narrow)],
                projsh_ref.at[at_rows, :],
                out_sems.at[1, part],
            ),
        ]

    act_far().wait_recv()
    act_both().start()
    fetch(0)
    act_core().wait_recv()
    act_both().wait_recv()
    act_copies = [
        pltpu.make_async_copy(
            act_s.at[index],
            act_ref.at[:, pl.ds(index * block, block)],
            keep_sems.at[2 + index],
        )
        for index in range(blocks)
    ]
    for copy in act_copies:
        copy.start()
    for place in range(blocks):
        if place + 1 < blocks:
            fetch(place + 1)
        for copy in weight_copies(place, place % 2):
            copy.wait()
        shared_copy(place, place % 2).start()
        if place + 1 < blocks:
            accumulate(place, 0, 4)
        else:
            for part in range(4):
                accumulate(place, part, part + 1)
                for copy in out_copies(part):
                    copy.start()
    for place in range(max(blocks - 2, 0), blocks):
        shared_copy(place, place % 2).wait()
    for copy in act_copies:
        copy.wait()
    for chunk in range(chunks):
        spread.sent(chunk)
    shared_spread.sent(0)
    for half in range(2):
        for place in range(blocks):
            swap_copy(place, half, False).wait_send()
    line_swap().wait_send()
    for half in range(2):
        line_near(half, False).wait_send()
        for near in range(2):
            line_far(half, near, False).wait_send()
    act_far().wait_send()
    act_core().wait_send()
    act_both().wait_send()
    for part in range(4):
        for copy in out_copies(part):
            copy.wait()
    pltpu.make_async_copy(x_s, xr_ref, x_sems.at[3]).wait()

    @pl.when(lanes.home)
    def _():
        for chunk in range(chunks):
            first_copy(chunk, (lanes.d, lanes.far)).wait_send()
        for i in range(2):
            out_first(i, (lanes.d, lanes.far)).wait_send()
            out_own(i).wait()
            out_came(i, 1 - c)

    @pl.when(lanes.away)
    def _():
        par_away().wait_recv()
        par_away().wait_send()
        x_away().wait_send()
        for chunk in range(chunks):
            first_copy(chunk, (lanes.other, t)).wait_send()
            second_copy(chunk).wait_send()
        for i in range(2):
            out_first(i, (lanes.other, t)).wait_send()
            out_second(i).wait_send()
            for half in range(2):
                out_came(i, half)


def front(in_pack, out_pack, down, shared, layer_in, gain, params, kv_width, at):
    bf16 = jnp.bfloat16
    rows = in_pack.shape[0]
    blocks = at.blocks
    chunks = 4 if rows >= 256 else 1
    dma = pltpu.SemaphoreType.DMA
    anywhere = pl.BlockSpec(memory_space=pl.ANY)
    here, features = layer_in.shape
    total = 2 * blocks * rows
    narrow = shared.shape[1] // 2 + 2 * kv_width
    return pl.pallas_call(
        functools.partial(front_body, blocks, chunks),
        in_specs=[pl.BlockSpec(memory_space=pltpu.VMEM)] * 7,
        out_specs=[anywhere] * 6 + [pl.BlockSpec(memory_space=pltpu.VMEM)] + [anywhere] * 3,
        out_shape=[
            jax.ShapeDtypeStruct((total, in_pack.shape[1]), bf16),
            jax.ShapeDtypeStruct((2 * rows, out_pack.shape[1]), bf16),
            jax.ShapeDtypeStruct((2 * rows, down.shape[1]), bf16),
            jax.ShapeDtypeStruct((4 * here, features), bf16),
            jax.ShapeDtypeStruct((here, features), bf16),
            jax.ShapeDtypeStruct((total, shared.shape[1]), bf16),
            jax.ShapeDtypeStruct(params.shape, jnp.float32),
            jax.ShapeDtypeStruct((4 * here, in_pack.shape[1]), jnp.float32),
            jax.ShapeDtypeStruct((4 * here, narrow), jnp.float32),
            jax.ShapeDtypeStruct((total, narrow), bf16),
        ],
        scratch_shapes=[
            pltpu.VMEM((here, features), bf16),
            pltpu.VMEM((blocks, 4 * here, 2 * rows), bf16),
            dma((chunks,)),
            dma((2, chunks)),
            dma((2, chunks)),
            dma((2, 3)),
            dma((2, 2)),
            dma((2, blocks, chunks)),
            dma((2, blocks, chunks)),
            dma((4,)),
            dma((4,)),
            dma((3,)),
            dma((8,)),
            dma((7,)),
            dma((2, blocks, 1)),
            dma((2, blocks, 1)),
            dma((2, blocks)),
            dma((2, blocks)),
            dma((2,)),
            pltpu.VMEM((2, 2 * rows, in_pack.shape[1]), bf16),
            pltpu.VMEM((2, 2 * rows, narrow), bf16),
            pltpu.VMEM((4 * here, in_pack.shape[1] + narrow), jnp.float32),
            dma((2, 4)),
            dma((2 + blocks,)),
            dma((2, 4)),
        ],
        compiler_params=pltpu.CompilerParams(
            collective_id=1, has_side_effects=True, vmem_limit_bytes=52 * 1024 * 1024
        ),
        cost_estimate=pl.CostEstimate(
            flops=here * features * 8, bytes_accessed=300_000_000, transcendentals=0
        ),
    )(in_pack, out_pack, down, shared, layer_in, gain.reshape(1, -1), params)


class Stage:
    def __init__(self, lanes, pair, full, rows, cols, chunks, sems):
        pair_cols = slice(0, pair.shape[1])
        self.lanes, self.pair, self.full, self.rows, self.cols = lanes, pair, full, rows, cols
        self.chunks = chunks
        self.own_sem, ssem, rsem = sems
        self.spread = Spread(lanes, full, rows, chunks, ssem, rsem, cols, pair, pair_cols)

    def own(self):
        start = self.lanes.k * (2 * self.rows)
        view = self.full.at[pl.ds(pl.multiple_of(start, 2 * self.rows), 2 * self.rows), self.cols]
        return pltpu.make_async_copy(self.pair, view, self.own_sem.at[0])

    def give(self):
        for chunk in range(self.chunks):
            for half in range(2):
                self.spread.give(0, half, chunk)

    def settle(self, place):
        for half in range(2):
            if not onward(place, half, self.lanes.bits):
                for chunk in range(self.chunks):
                    self.spread.take(place, half, chunk)

    def finish(self):
        for chunk in range(self.chunks):
            for half in range(2):
                for place in range(self.lanes.blocks):
                    for bit in onward(place, half, self.lanes.bits):
                        self.spread.copy(place, half, chunk, bit).wait_send()


class Exchange:
    def __init__(self, lanes, work, own, sends, recvs, ssem, rsem):
        self.lanes, self.work, self.own = lanes, work, own
        self.both_s, self.core_s, self.pass_s = sends
        self.both_r, self.core_r, self.far_r = recvs
        self.ssem, self.rsem = ssem, rsem
        self.blocks, self.here, self.block = own.shape
        self.step = min(self.here, 64)

    def copies(self, index, place):
        core, near = (self.lanes.other, self.lanes.t), (self.lanes.d, self.lanes.near)
        table = (
            (self.both_s, self.both_r, core),
            (self.core_s, self.core_r, core),
            (self.pass_s, self.far_r, near),
        )

        def copy(kind):
            src, dst, device = table[kind]
            return remote(
                src.at[index], dst.at[index], self.ssem.at[kind, place], self.rsem.at[kind, place],
                device,
            )

        return copy

    def columns(self, place):
        return slice(place * self.block, (place + 1) * self.block)

    def rows(self, piece, i):
        start = piece * self.here + i * self.step
        return pl.ds(pl.multiple_of(start, self.step), self.step)

    def give(self, index, place, product):
        bf16 = jnp.bfloat16
        cols = self.columns(place)

        @pl.loop(0, 4)
        def _(piece):
            rows = pl.ds(pl.multiple_of(piece * self.here, self.here), self.here)
            self.work[rows, cols] = product(rows)

        @pl.loop(0, self.here // self.step)
        def _(i):
            part = self.rows(0, i)
            self.both_s[index, part, :] = self.work[self.rows(3, i), cols].astype(bf16)
            self.core_s[index, part, :] = self.work[self.rows(1, i), cols].astype(bf16)
            self.own[index, part, :] = self.work[part, cols]

        copy = self.copies(index, place)
        copy(0).start()
        copy(1).start()

    def pass_on(self, index, place):
        copy = self.copies(index, place)
        copy(0).wait_recv()
        cols = self.columns(place)

        @pl.loop(0, self.here // self.step)
        def _(i):
            part = self.rows(0, i)
            total = self.work[self.rows(2, i), cols] + self.both_r[index, part, :].astype(
                jnp.float32
            )
            self.pass_s[index, part, :] = total.astype(jnp.bfloat16)

        copy(2).start()

    def take(self, index, place):
        copy = self.copies(index, place)
        copy(1).wait_recv()
        copy(2).wait_recv()

    def total(self, index, rows):
        f32 = jnp.float32
        return (
            self.own[index, rows, :]
            + self.core_r[index, rows, :].astype(f32)
            + self.far_r[index, rows, :].astype(f32)
        )

    def finish(self, index, place):
        copy = self.copies(index, place)
        for kind in range(3):
            copy(kind).wait_send()


def middle_body(
    blocks, gu_chunks, down_chunks,
    pair_ref, dpair_ref, heads_ref, out_ref, teacher_ref, x_ref, gain_ref, live_ref,
    full_ref, mid_ref, gate_ref, up_ref, hidden_ref, grads_ref, resid_ref, error_ref, low_ref,
    loss_ref,
    wbuf, mid_s, acc_s, hid_s, gate_s, up_s, own_s, both_s, core_s, pass_s,
    both_r, core_r, far_r, both_q, core_q, far_q, err_s,
    w_sems, one_s, one_r, two_s, two_r, mid_ssem, mid_rsem, err_ssem, err_rsem, keep_sems,
    g_home, g_s, g_r, d_home, d_s, d_r, target_ref, t_sems, out_s,
):
    f32, bf16 = jnp.float32, jnp.bfloat16
    lanes = Lanes(blocks)
    rows = pair_ref.shape[0] // 2
    here = x_ref.shape[0]
    block = 2 * rows
    inner = heads_ref.shape[1]
    hidden_width = hid_s.shape[1]
    core_at = (lanes.other, lanes.t)
    near_at = (lanes.d, lanes.near)
    lanes.greet()
    gate_up = Stage(
        lanes, pair_ref, full_ref, rows, slice(0, 2 * hidden_width), gu_chunks,
        (g_home, g_s, g_r),
    )
    down = Stage(
        lanes, dpair_ref, full_ref, rows, slice(2 * hidden_width, 3 * hidden_width), down_chunks,
        (d_home, d_s, d_r),
    )

    def target_away():
        return remote(
            teacher_ref, target_ref, t_sems.at[0], t_sems.at[1], (lanes.other, lanes.far)
        )

    def target_home():
        return pltpu.make_async_copy(teacher_ref, target_ref, t_sems.at[2])

    sends = (both_s, core_s, pass_s)
    one = Exchange(lanes, acc_s, own_s, sends, (both_r, core_r, far_r), one_s, one_r)
    two = Exchange(lanes, acc_s, own_s, sends, (both_q, core_q, far_q), two_s, two_r)

    def load(src, slot, width, cols):
        return pltpu.make_async_copy(src, wbuf.at[slot, :, cols], w_sems.at[slot])

    def out_load(index):
        return load(
            out_ref.at[pl.ds(index * block, block), :], index % 2, inner, pl.ds(0, inner)
        )

    out_load(0).start()
    gate_up.give()
    gate_up.own().start()
    down.own().start()

    for index in range(blocks):
        if index + 1 < blocks:
            out_load(index + 1).start()
        out_load(index).wait()
        one.give(
            index,
            index,
            lambda rows: low_dot(heads_ref[rows, :], wbuf[index % 2, :, :inner], NT),
        )
    for index in range(blocks):
        one.pass_on(index, index)

    for chunk in range(gu_chunks):
        gate_up.spread.pass_on(chunk)
    down.give()

    for index in range(blocks):
        one.take(index, index)

    step = min(here, 32)

    def columns(index):
        return slice(index * block, (index + 1) * block)

    @pl.loop(0, here // step)
    def _(i):
        part = pl.ds(pl.multiple_of(i * step, step), step)
        total = jnp.zeros((step, 1), f32)
        for index in range(blocks):
            resid = x_ref[part, columns(index)].astype(f32) + one.total(index, part)
            resid_ref[part, columns(index)] = resid
            total = total + jnp.sum(resid * resid, axis=1, keepdims=True)
        scale = lax.rsqrt(total / (blocks * block) + EPS)
        for index in range(blocks):
            mid = resid_ref[part, columns(index)] * scale * gain_ref[:, columns(index)]
            mid_s[index, part, :] = mid.astype(bf16)

    def mid_view(slot):
        return mid_s.at[:, pl.ds(slot * here, here), :]

    def mid_near():
        return remote(mid_view(0), mid_view(2), mid_ssem.at[0], mid_rsem.at[0], near_at)

    def mid_core():
        return remote(mid_view(0), mid_view(1), mid_ssem.at[1], mid_rsem.at[1], core_at)

    def mid_both():
        return remote(mid_view(2), mid_view(3), mid_ssem.at[2], mid_rsem.at[2], core_at)

    mid_near().start()
    mid_core().start()

    @pl.when(lanes.home)
    def _():
        target_home().start()

    @pl.when(lanes.away)
    def _():
        target_away().start()

    def gu_load(place, slot):
        start = lanes.block(place) * block
        view = full_ref.at[pl.ds(pl.multiple_of(start, block), block), pl.ds(0, 2 * hidden_width)]
        return load(view, slot, 2 * hidden_width, pl.ds(0, 2 * hidden_width))

    def down_load(place, slot):
        start = lanes.block(place) * block
        view = full_ref.at[
            pl.ds(pl.multiple_of(start, block), block), pl.ds(2 * hidden_width, hidden_width)
        ]
        return load(view, slot, hidden_width, pl.ds(0, hidden_width))

    gate_up.own().wait()
    gu_load(0, 0).start()
    mid_near().wait_recv()
    mid_both().start()
    mid_core().wait_recv()

    wide = 2 * hidden_width
    tile = min(wide, 512)

    def accumulate(place, first, last):
        slot = place % 2
        index = lanes.block(place)

        @pl.loop(first, last)
        def _(piece):
            part = pl.ds(pl.multiple_of(piece * here, here), here)
            left = mid_s[index, part, :]
            for col in range(0, wide, tile):
                cols = slice(col, col + tile)
                product = low_dot(left, wbuf[slot, :, cols], NN)
                if place:
                    product = product + acc_s[part, cols]
                acc_s[part, cols] = product

    for place in range(blocks):
        if place + 1 < blocks:
            gate_up.settle(place + 1)
            gu_load(place + 1, (place + 1) % 2).start()
        gu_load(place, place % 2).wait()
        accumulate(place, 0, 3)
        if place == 0:
            mid_both().wait_recv()
        accumulate(place, 3, 4)
        if place < down_chunks:
            down.spread.pass_on(place)

    for chunk in range(blocks, down_chunks):
        down.spread.pass_on(chunk)

    down.own().wait()
    down_load(0, 0).start()

    @pl.loop(0, 4 * here // step)
    def _(i):
        part = pl.ds(pl.multiple_of(i * step, step), step)
        gate = acc_s[part, :hidden_width]
        up = acc_s[part, hidden_width : 2 * hidden_width]
        gate_s[part, :] = gate.astype(bf16)
        up_s[part, :] = up.astype(bf16)
        hid_s[part, :] = (gate * sigmoid(gate) * up).astype(bf16)

    kept = [
        pltpu.make_async_copy(hid_s, hidden_ref, keep_sems.at[0]),
        pltpu.make_async_copy(gate_s, gate_ref, keep_sems.at[1]),
        pltpu.make_async_copy(up_s, up_ref, keep_sems.at[2]),
    ] + [
        pltpu.make_async_copy(
            mid_s.at[index], mid_ref.at[:, pl.ds(index * block, block)], keep_sems.at[3 + index]
        )
        for index in range(blocks)
    ]
    for copy in kept:
        copy.start()
    for index in range(blocks):
        one.finish(index, index)

    for place in range(blocks):
        index = lanes.block(place)
        if place + 1 < blocks:
            down.settle(place + 1)
            down_load(place + 1, (place + 1) % 2).start()
        down_load(place, place % 2).wait()
        two.give(
            index,
            place,
            lambda rows: low_dot(hid_s[rows, :], wbuf[place % 2, :, :hidden_width], NT),
        )
        if place:
            two.pass_on(lanes.block(place - 1), place - 1)
    two.pass_on(lanes.block(blocks - 1), blocks - 1)
    for place in range(blocks):
        two.take(lanes.block(place), place)

    @pl.when(lanes.home)
    def _():
        target_home().wait()

    @pl.when(lanes.away)
    def _():
        target_away().wait_recv()
        target_away().wait_send()

    def output_part(i, loss):
        part = pl.ds(pl.multiple_of(i * step, step), step)
        live = live_ref[part, :]
        for index in range(blocks):
            cols = columns(index)
            outputs = resid_ref[part, cols] + two.total(index, part)
            out_s[part, cols] = outputs.astype(bf16)
            error = (outputs - target_ref[part, cols].astype(f32)) * live
            error_ref[part, cols] = error
            err_s[part, cols] = error.astype(bf16)
            loss = loss + jnp.sum(error * error)
        return loss

    loss = lax.fori_loop(0, here // step, output_part, jnp.zeros((), f32))
    loss_ref[...] = jnp.zeros((8, WIDE), f32) + 0.5 * loss

    def grads_view(slot):
        return grads_ref.at[pl.ds(slot * here, here), :]

    def err_near():
        return remote(err_s, grads_view(2), err_ssem.at[0], err_rsem.at[0], near_at)

    def err_core():
        return remote(err_s, grads_view(1), err_ssem.at[1], err_rsem.at[1], core_at)

    def err_both():
        return remote(grads_view(2), grads_view(3), err_ssem.at[2], err_rsem.at[2], core_at)

    own_err = pltpu.make_async_copy(err_s, grads_view(0), err_ssem.at[3])
    err_near().start()
    err_core().start()
    own_err.start()

    def out_home():
        return pltpu.make_async_copy(out_s, low_ref, t_sems.at[5])

    def out_away():
        return remote(out_s, low_ref, t_sems.at[3], t_sems.at[4], (lanes.other, lanes.far))

    @pl.when(lanes.home)
    def _():
        out_home().start()

    @pl.when(lanes.away)
    def _():
        out_away().start()

    for copy in kept:
        copy.wait()
    gate_up.finish()
    down.finish()
    for place in range(blocks):
        two.finish(lanes.block(place), place)
    for copy in (mid_near(), mid_core(), mid_both()):
        copy.wait_send()
    err_near().wait_recv()
    err_both().start()
    err_core().wait_recv()
    err_both().wait_recv()
    own_err.wait()

    @pl.when(lanes.home)
    def _():
        out_home().wait()

    @pl.when(lanes.away)
    def _():
        out_away().wait()

    for copy in (err_near(), err_core(), err_both()):
        copy.wait_send()


def middle(pair, down_pair, heads_all, out_all, x, gain, teacher, live, at):
    f32, bf16 = jnp.float32, jnp.bfloat16
    rows = pair.shape[0] // 2
    hidden_width = down_pair.shape[1]
    slot, inner = heads_all.shape
    here, features = x.shape
    blocks = at.blocks
    block = 2 * rows
    gu_chunks = 4 if rows >= 256 else 1
    down_chunks = 2 if rows >= 256 else 1
    dma = pltpu.SemaphoreType.DMA
    vmem = pl.BlockSpec(memory_space=pltpu.VMEM)
    anywhere = pl.BlockSpec(memory_space=pl.ANY)

    def stage_sems(chunks):
        return [dma((1,)), dma((2, blocks, chunks)), dma((2, blocks, chunks))]

    shape = jax.ShapeDtypeStruct
    buffers = [pltpu.VMEM((blocks, here, block), bf16)]
    return pl.pallas_call(
        functools.partial(middle_body, blocks, gu_chunks, down_chunks),
        in_specs=[vmem] * 3 + [anywhere, anywhere, vmem, vmem, vmem],
        out_specs=[anywhere] * 6 + [vmem] * 4,
        out_shape=[
            shape((features, 3 * hidden_width), bf16),
            shape((slot, features), bf16),
            shape((slot, hidden_width), bf16),
            shape((slot, hidden_width), bf16),
            shape((slot, hidden_width), bf16),
            shape((slot, features), bf16),
            shape((here, features), f32),
            shape((here, features), f32),
            shape((here, features), bf16),
            shape((8, WIDE), f32),
        ],
        scratch_shapes=[
            pltpu.VMEM((2, block, 2 * hidden_width), bf16),
            pltpu.VMEM((blocks, slot, block), bf16),
            pltpu.VMEM((slot, max(2 * hidden_width, features)), f32),
            pltpu.VMEM((slot, hidden_width), bf16),
            pltpu.VMEM((slot, hidden_width), bf16),
            pltpu.VMEM((slot, hidden_width), bf16),
            pltpu.VMEM((blocks, here, block), f32),
        ]
        + buffers * 9
        + [
            pltpu.VMEM((here, features), bf16),
            dma((2,)),
            dma((3, blocks)),
            dma((3, blocks)),
            dma((3, blocks)),
            dma((3, blocks)),
            dma((3,)),
            dma((3,)),
            dma((4,)),
            dma((3,)),
            dma((3 + blocks,)),
        ]
        + stage_sems(gu_chunks)
        + stage_sems(down_chunks)
        + [pltpu.VMEM((here, features), bf16), dma((6,)), pltpu.VMEM((here, features), bf16)],
        compiler_params=pltpu.CompilerParams(
            collective_id=3, has_side_effects=True, vmem_limit_bytes=58 * 1024 * 1024
        ),
        cost_estimate=pl.CostEstimate(
            flops=slot * features * hidden_width * 8, bytes_accessed=400_000_000, transcendentals=0
        ),
    )(
        pair, down_pair, heads_all, out_all, teacher, x, gain.reshape(1, -1), live,
    )


def turn_body(
    blocks, low_ref, lowsh_ref, act_ref, in_ref, sh_ref, rawgu_ref,
    part_ref, bc_ref, kv_ref, sum_ref, gu_ref,
    win_s, wsh_s, work_s, own_s, both_s, core_s, pass_s, both_r, core_r, far_r, stage_s,
    gu_r, w_sems, x_ssem, x_rsem, stage_sems, ff_ssem, ff_rsem,
):
    f32, bf16 = jnp.float32, jnp.bfloat16
    lanes = Lanes(blocks)
    c, t = lanes.c, lanes.t
    here = sum_ref.shape[0]
    rows = rawgu_ref.shape[0] // 2
    block = 2 * rows
    width = low_ref.shape[1]
    bc_width = bc_ref.shape[1]
    features = act_ref.shape[1]
    core_at, far_at, cross_at = (
        (lanes.other, t), (lanes.d, lanes.far), (lanes.other, lanes.far),
    )
    lanes.greet()

    def ff_copies(kind, half, device):
        view = pl.ds(pl.multiple_of(half * rows, rows), rows)
        return [
            remote(
                src.at[view, :], dst.at[kind], ff_ssem.at[kind, i], ff_rsem.at[kind, i], device
            )
            for i, (src, dst) in enumerate(((rawgu_ref, gu_r),))
        ]

    def first_home():
        return ff_copies(0, 1 - c, core_at)

    def first_away():
        return ff_copies(0, c, far_at)

    def second_away():
        return ff_copies(1, 1 - c, cross_at)

    def load(index):
        slot = index % 2
        view = pl.ds(index * block, block)
        return (
            pltpu.make_async_copy(in_ref.at[view, :], win_s.at[slot], w_sems.at[slot, 0]),
            pltpu.make_async_copy(sh_ref.at[view, :], wsh_s.at[slot], w_sems.at[slot, 1]),
        )

    for copy in load(0):
        copy.start()

    @pl.when(lanes.home)
    def _():
        for copy in first_home():
            copy.start()

    @pl.when(lanes.away)
    def _():
        for one, two in zip(first_away(), second_away()):
            one.start()
            two.start()

    exchange = Exchange(
        lanes, work_s, own_s, (both_s, core_s, pass_s), (both_r, core_r, far_r), x_ssem, x_rsem
    )
    for index in range(blocks):
        slot = index % 2
        if index + 1 < blocks:
            for copy in load(index + 1):
                copy.start()
        for copy in load(index):
            copy.wait()
        exchange.give(
            index,
            index,
            lambda part: low_dot(low_ref[part, :], win_s[slot], NT)
            + low_dot(lowsh_ref[part, :], wsh_s[slot], NT),
        )
        if index:
            exchange.pass_on(index - 1, index - 1)
    exchange.pass_on(blocks - 1, blocks - 1)

    tall = 256
    steps = features // tall

    def out_copies(i, slot):
        view = pl.ds(pl.multiple_of(i * tall, tall), tall)
        kv_from = width + bc_width
        return (
            pltpu.make_async_copy(
                stage_s.at[slot, :, :width], part_ref.at[view, :], stage_sems.at[slot, 0]
            ),
            pltpu.make_async_copy(
                stage_s.at[slot, :, width:kv_from], bc_ref.at[view, :], stage_sems.at[slot, 1]
            ),
            pltpu.make_async_copy(
                stage_s.at[slot, :, kv_from:], kv_ref.at[view, :], stage_sems.at[slot, 2]
            ),
        )

    @pl.loop(0, steps)
    def _(i):
        slot = lax.rem(i, 2)

        @pl.when(i >= 2)
        def _():
            for copy in out_copies(i - 2, slot):
                copy.wait()

        left = act_ref[:, pl.ds(pl.multiple_of(i * tall, tall), tall)]
        for src, base in ((low_ref, 0), (lowsh_ref, width)):
            total = src.shape[1]
            tile = total // 3
            for col in range(0, total, tile):
                product = low_dot(left, src[:, col : col + tile], TN)
                stage_s[slot, :, base + col : base + col + tile] = product.astype(bf16)
        for copy in out_copies(i, slot):
            copy.start()

    for index in range(blocks):
        exchange.take(index, index)
    step = min(here, 32)

    @pl.loop(0, here // step)
    def _(i):
        part = pl.ds(pl.multiple_of(i * step, step), step)
        for index in range(blocks):
            sum_ref[part, index * block : (index + 1) * block] = exchange.total(index, part)

    for i in (steps - 2, steps - 1):
        for copy in out_copies(i, i % 2):
            copy.wait()
    for index in range(blocks):
        exchange.finish(index, index)
    for copy in first_home():
        copy.wait_recv()
    span = min(rows, 32)
    side_width = gu_ref.shape[2]

    @pl.when(lanes.home)
    def _():
        for copy in first_home():
            copy.wait_send()

        @pl.loop(0, rows // span)
        def _(i):
            part = pl.ds(pl.multiple_of(i * span, span), span)
            mine = pl.ds(pl.multiple_of(c * rows + i * span, span), span)
            for side in range(2):
                cols = slice(side * side_width, (side + 1) * side_width)
                total = rawgu_ref[mine, cols].astype(f32) + gu_r[0, part, cols].astype(f32)
                gu_ref[part, side, :] = total

    @pl.when(lanes.away)
    def _():
        for copy in second_away():
            copy.wait_recv()
        for copy in first_away() + second_away():
            copy.wait_send()

        @pl.loop(0, rows // span)
        def _(i):
            part = pl.ds(pl.multiple_of(i * span, span), span)
            for side in range(2):
                cols = slice(side * side_width, (side + 1) * side_width)
                total = gu_r[0, part, cols].astype(f32) + gu_r[1, part, cols].astype(f32)
                gu_ref[part, side, :] = total


def turn(low_pack, low_shared, act_all, in_all, shared_all, raw_gate_up, bc_width, at):
    f32, bf16 = jnp.float32, jnp.bfloat16
    slot, width = low_pack.shape
    shared_width = low_shared.shape[1]
    features = act_all.shape[1]
    here = slot // 4
    blocks = at.blocks
    rows = raw_gate_up.shape[0] // 2
    block = 2 * rows
    gu_width = raw_gate_up.shape[1]
    dma = pltpu.SemaphoreType.DMA
    vmem = pl.BlockSpec(memory_space=pltpu.VMEM)
    anywhere = pl.BlockSpec(memory_space=pl.ANY)
    shape = jax.ShapeDtypeStruct
    return pl.pallas_call(
        functools.partial(turn_body, blocks),
        in_specs=[vmem] * 3 + [anywhere] * 2 + [vmem],
        out_specs=[anywhere] * 3 + [vmem] * 2,
        out_shape=[
            shape((features, width), bf16),
            shape((features, bc_width), bf16),
            shape((features, shared_width - bc_width), bf16),
            shape((here, features), f32),
            shape((rows, 2, gu_width // 2), f32),
        ],
        scratch_shapes=[
            pltpu.VMEM((2, block, width), bf16),
            pltpu.VMEM((2, block, shared_width), bf16),
            pltpu.VMEM((slot, features), f32),
            pltpu.VMEM((blocks, here, block), f32),
        ]
        + [pltpu.VMEM((blocks, here, block), bf16)] * 6
        + [
            pltpu.VMEM((2, 256, width + shared_width), bf16),
            pltpu.VMEM((2, rows, gu_width), bf16),
            dma((2, 2)),
            dma((3, blocks)),
            dma((3, blocks)),
            dma((2, 3)),
            dma((2, 1)),
            dma((2, 1)),
        ],
        compiler_params=pltpu.CompilerParams(
            collective_id=4, has_side_effects=True, vmem_limit_bytes=58 * 1024 * 1024
        ),
        cost_estimate=pl.CostEstimate(
            flops=slot * features * width * 5, bytes_accessed=60_000_000, transcendentals=0
        ),
    )(low_pack, low_shared, act_all, in_all, shared_all, raw_gate_up)


class Collect:
    def __init__(self, lanes, part, rows, cols, send_s, recv_s, load_s, total_s, sems):
        self.lanes, self.part, self.rows, self.cols = lanes, part, rows, cols
        self.send_s, self.recv_s, self.load_s, self.total_s = send_s, recv_s, load_s, total_s
        self.send_sems, self.recv_sems, self.load_sems = sems
        self.loads = [
            (half, place)
            for half in range(2)
            for place in range(lanes.blocks)
            if onward(place, half, lanes.bits)
        ]

    def source(self, place, half, chunk):
        start = self.lanes.block(place) * (2 * self.rows) + half * self.rows
        return self.part.at[pl.ds(pl.multiple_of(start, self.rows), self.rows), self.cols[chunk]]

    def bit_of(self, place, half):
        bits = [bit for bit in range(self.lanes.bits) if (place >> bit) & 1]
        return bits[-1] if half == 0 else bits[0]

    def load(self, half, place):
        index = self.loads.index((half, place))
        start = self.lanes.block(place) * (2 * self.rows) + half * self.rows
        view = self.part.at[pl.ds(pl.multiple_of(start, self.rows), self.rows), :]
        return pltpu.make_async_copy(view, self.load_s.at[index], self.load_sems.at[index])

    def copy(self, place, half, chunk):
        if (half, place) in self.loads:
            source = self.send_s.at[self.loads.index((half, place)), :, self.cols[chunk]]
        else:
            source = self.source(place, half, chunk)
        return remote(
            source,
            self.recv_s.at[half, place - 1, :, self.cols[chunk]],
            self.send_sems.at[half, place, chunk],
            self.recv_sems.at[half, place, chunk],
            self.lanes.across(self.bit_of(place, half)),
        )

    def order(self, half):
        places = list(range(1, self.lanes.blocks))
        places.sort(key=lambda place: -len([b for b in range(8) if (place >> b) & 1]))
        return places

    def start(self):
        for half, place in self.loads:
            self.load(half, place).start()

    def direct(self, chunk):
        for half in range(2):
            for place in self.order(half):
                if (half, place) not in self.loads:
                    self.copy(place, half, chunk).start()

    def add(self, place, half, chunk):
        cols = self.cols[chunk]
        index = self.loads.index((half, place))
        total = self.load_s[index, :, cols].astype(jnp.float32)
        for bit in onward(place, half, self.lanes.bits):
            came = place | (1 << bit)
            self.copy(came, half, chunk).wait_recv()
            total = total + self.recv_s[half, came - 1, :, cols].astype(jnp.float32)
        return total

    def middle(self, chunk):
        for half in range(2):
            for place in self.order(half):
                if (half, place) in self.loads:
                    index = self.loads.index((half, place))
                    if chunk == 0:
                        self.load(half, place).wait()
                    total = self.add(place, half, chunk)
                    self.send_s[index, :, self.cols[chunk]] = total.astype(jnp.bfloat16)
                    self.copy(place, half, chunk).start()

    def last(self, chunk):
        for half in range(2):
            if chunk == 0:
                self.load(half, 0).wait()
            self.total_s[half, :, self.cols[chunk]] = self.add(0, half, chunk)

    def finish(self):
        for chunk in range(len(self.cols)):
            for half in range(2):
                for place in range(1, self.lanes.blocks):
                    self.copy(place, half, chunk).wait_send()


def back_body(
    blocks, in_cols, small_row, part_ref, bc_ref, kv_ref, act_ref,
    resid_ref, x_ref, gain_ref, small_ref, out_ref,
    gmix_ref, gquery_ref, gstep_ref, gsh_ref, gx_ref, sum_ref, gout_ref, gattn_ref,
    in_send, in_recv, in_load, in_total, settle_s, settle_r, sh_came, sh_part, sh_send, sh_recv,
    sh_load, sh_total, line_s, line_r, near_s, near_r, swap_s, swap_r,
    gx_s, gx_r, small_s, small_r,
    in_ssem, in_rsem, in_lsem, sh_ssem, sh_rsem, sh_lsem, set_ssem, set_rsem, misc_s, misc_r,
    small_ssem, small_rsem, out_r, out_ssem, out_rsem,
):
    f32, bf16 = jnp.float32, jnp.bfloat16
    lanes = Lanes(blocks)
    c, t = lanes.c, lanes.t
    rows = gquery_ref.shape[0]
    width = gmix_ref.shape[2]
    query_width = gquery_ref.shape[1]
    here = act_ref.shape[0]
    wide = bc_ref.shape[1]
    few = gsh_ref.shape[0]
    chunks = len(in_cols)
    step = min(here, 32)
    lanes.greet()
    core_at = (lanes.other, t)
    near_at = (lanes.d, lanes.near)
    far_at = (lanes.d, lanes.far)
    cross_at = (lanes.other, lanes.far)
    first = c == 0
    second = c == 1

    collect = Collect(
        lanes, part_ref, rows, in_cols, in_send, in_recv, in_load, in_total,
        (in_ssem, in_rsem, in_lsem),
    )
    shared = Collect(
        lanes, sh_part, rows, [slice(0, wide)], sh_send, sh_recv, sh_load, sh_total,
        (sh_ssem, sh_rsem, sh_lsem),
    )
    half_kv = kv_ref.shape[1] // 2

    def send_kv():
        return remote(
            kv_ref, sh_came.at[:, : 2 * half_kv], misc_s.at[2], misc_r.at[2], core_at
        )

    def send_bc():
        return remote(bc_ref, sh_came, misc_s.at[3], misc_r.at[3], core_at)

    def out_block(half):
        return out_ref.at[pl.ds(pl.multiple_of(half * rows, rows), rows), :]

    def out_first(half, device):
        return remote(out_block(half), out_r.at[0], out_ssem.at[0], out_rsem.at[0], device)

    def out_second():
        return remote(out_block(1 - c), out_r.at[1], out_ssem.at[1], out_rsem.at[1], cross_at)

    collect.start()
    for chunk in range(chunks):
        collect.direct(chunk)
    @pl.when(first)
    def _():
        send_kv().start()

    @pl.when(second)
    def _():
        send_bc().start()

    def send_x():
        return remote(gx_s, gx_r, misc_s.at[4], misc_r.at[4], cross_at)

    small_s[0] = small_ref[...]
    features = gain_ref.shape[1]

    def one_part(i, gains):
        view = pl.ds(pl.multiple_of(i * step, step), step)
        grad = act_ref[view, :]
        x = x_ref[view, :].astype(f32)
        scale = lax.rsqrt(jnp.mean(x * x, axis=1, keepdims=True) + EPS)
        gains = gains + jnp.sum(grad * (x * scale), axis=0, keepdims=True)
        grad = grad * gain_ref[...]
        mean = jnp.mean(grad * x, axis=1, keepdims=True)
        result = resid_ref[view, :] + scale * grad - x * (scale * scale * scale * mean)
        gx_ref[view, :] = result
        gx_s[view, :] = result.astype(bf16)
        return gains

    gains = lax.fori_loop(0, here // step, one_part, jnp.zeros((1, features), f32))
    for i in range(features // WIDE):
        small_s[0, small_row + i : small_row + i + 1, :] = gains[:, i * WIDE : (i + 1) * WIDE]

    stops = [far_at, near_at, core_at] + [lanes.across(bit) for bit in range(lanes.bits)]

    def send_small(index):
        return remote(
            small_s.at[index], small_r.at[index], small_ssem.at[index], small_rsem.at[index],
            stops[index],
        )

    def step_small(index):
        send_small(index).wait_recv()
        small_s[index + 1] = small_s[index] + small_r[index]
        if index + 1 < len(stops):
            send_small(index + 1).start()

    send_small(0).start()

    @pl.when(lanes.away)
    def _():
        send_x().start()

    @pl.when(lanes.home)
    def _():
        out_first(1 - c, core_at).start()

    @pl.when(lanes.away)
    def _():
        out_first(c, far_at).start()
        out_second().start()

    @pl.when(first)
    def _():
        send_bc().wait_recv()

        @pl.loop(0, bc_ref.shape[0] // 64)
        def _(i):
            view = pl.ds(pl.multiple_of(i * 64, 64), 64)
            total = bc_ref[view, :].astype(f32) + sh_came[view, :].astype(f32)
            sh_part[view, :] = total.astype(bf16)

    @pl.when(second)
    def _():
        send_kv().wait_recv()

        @pl.loop(0, bc_ref.shape[0] // 64)
        def _(i):
            view = pl.ds(pl.multiple_of(i * 64, 64), 64)
            for piece in range(2):
                kept = pl.ds(piece * half_kv, half_kv)
                sh_part[view, pl.ds(2 * piece * half_kv, half_kv)] = sh_came[view, kept]
                sh_part[view, pl.ds((2 * piece + 1) * half_kv, half_kv)] = kv_ref[view, kept]

    shared.start()
    for chunk in range(chunks):
        collect.middle(chunk)
    shared.direct(0)

    def send_first(chunk, device):
        cols = in_cols[chunk]
        return remote(
            settle_s.at[0, :, cols], settle_r.at[0, :, cols],
            set_ssem.at[0, chunk], set_rsem.at[0, chunk], device,
        )

    def send_second(chunk):
        cols = in_cols[chunk]
        return remote(
            settle_s.at[1, :, cols], settle_r.at[1, :, cols],
            set_ssem.at[1, chunk], set_rsem.at[1, chunk], cross_at,
        )

    for chunk in range(chunks):
        collect.last(chunk)
        cols = in_cols[chunk]

        @pl.when(lanes.home)
        def _(chunk=chunk, cols=cols):
            settle_s[0, :, cols] = in_total[1 - c, :, cols].astype(bf16)
            send_first(chunk, core_at).start()

        @pl.when(lanes.away)
        def _(chunk=chunk, cols=cols):
            settle_s[0, :, cols] = in_total[c, :, cols].astype(bf16)
            send_first(chunk, far_at).start()
            settle_s[1, :, cols] = in_total[1 - c, :, cols].astype(bf16)
            send_second(chunk).start()

        if chunk == 0:
            step_small(0)
            shared.middle(0)
        if chunk == 1:
            step_small(1)
    step_small(2)
    shared.last(0)

    t_high, t_low = lax.div(t, 2), lax.rem(t, 2)
    line = 2 * few

    def send_line():
        return remote(line_s, line_r, misc_s.at[5], misc_r.at[5], far_at)

    def send_near():
        return remote(near_s, near_r, misc_s.at[6], misc_r.at[6], near_at)

    def send_swap():
        return remote(swap_s, swap_r, misc_s.at[7], misc_r.at[7], core_at)

    theirs = pl.ds(pl.multiple_of((1 - t_high) * line, line), line)
    mine = pl.ds(pl.multiple_of(t_high * line, line), line)
    for half in range(2):
        line_s[half] = sh_total[half, theirs, :].astype(bf16)
    send_line().start()
    step_small(3)
    send_line().wait_recv()
    for half in range(2):
        sh_total[half, mine, :] = sh_total[half, mine, :] + line_r[half].astype(f32)
    theirs = pl.ds(pl.multiple_of(t_high * line + (1 - t_low) * few, few), few)
    mine = pl.ds(pl.multiple_of(t_high * line + t_low * few, few), few)
    for half in range(2):
        near_s[half] = sh_total[half, theirs, :].astype(bf16)
    send_near().start()
    for index in range(4, len(stops)):
        step_small(index)
    send_near().wait_recv()
    for half in range(2):
        sh_total[half, mine, :] = sh_total[half, mine, :] + near_r[half].astype(f32)
    swap_s[...] = sh_total[1 - c, mine, :].astype(bf16)
    send_swap().start()
    sum_ref[...] = small_s[len(stops)]

    bounds = [
        (0, gmix_ref.at[:, 0, :], width),
        (width, gmix_ref.at[:, 1, :], width),
        (2 * width, gquery_ref, query_width),
        (2 * width + query_width, gstep_ref, gstep_ref.shape[1]),
    ]

    def put_in(cols, other, kind):
        for start, dst, size in bounds:
            low, high = max(cols.start, start), min(cols.stop, start + size)
            if low < high:
                part = slice(low, high)
                total = settle_r[kind, :, part].astype(f32) + other(part)
                dst[:, low - start : high - start] = total

    for chunk in range(chunks):
        cols = in_cols[chunk]
        send_first(chunk, core_at).wait_recv()

        @pl.when(lanes.home)
        def _(chunk=chunk, cols=cols):
            put_in(cols, lambda part: in_total[c, :, part], 0)

        @pl.when(lanes.away)
        def _(chunk=chunk, cols=cols):
            send_second(chunk).wait_recv()
            put_in(cols, lambda part: settle_r[1, :, part].astype(f32), 0)

    out_first(0, core_at).wait_recv()

    @pl.when(lanes.home)
    def _():
        own_rows = pl.ds(pl.multiple_of(c * rows, rows), rows)
        gout_ref[...] = out_ref[own_rows, :width].astype(f32) + out_r[0, :, :width].astype(f32)
        gattn_ref[...] = out_ref[own_rows, width:].astype(f32) + out_r[0, :, width:].astype(f32)
        out_first(1 - c, core_at).wait_send()

    @pl.when(lanes.away)
    def _():
        out_second().wait_recv()
        gout_ref[...] = out_r[0, :, :width].astype(f32) + out_r[1, :, :width].astype(f32)
        gattn_ref[...] = out_r[0, :, width:].astype(f32) + out_r[1, :, width:].astype(f32)
        out_first(c, far_at).wait_send()
        out_second().wait_send()

    send_swap().wait_recv()

    @pl.when(first)
    def _():
        gsh_ref[:, :wide] = sh_total[0, mine, :]
        gsh_ref[:, wide:] = swap_r[...].astype(f32)

    @pl.when(second)
    def _():
        gsh_ref[:, :wide] = swap_r[...].astype(f32)
        gsh_ref[:, wide:] = sh_total[1, mine, :]

    @pl.when(lanes.away)
    def _():
        send_x().wait_recv()

        @pl.loop(0, here // step)
        def _(i):
            view = pl.ds(pl.multiple_of(i * step, step), step)
            gx_ref[view, :] = gx_r[view, :].astype(f32)

    collect.finish()
    shared.finish()

    @pl.when(first)
    def _():
        send_kv().wait_send()

    @pl.when(second)
    def _():
        send_bc().wait_send()

    for chunk in range(chunks):
        send_first(chunk, core_at).wait_send()

    @pl.when(lanes.away)
    def _():
        send_x().wait_send()
        for chunk in range(chunks):
            send_second(chunk).wait_send()

    for index in range(len(stops)):
        send_small(index).wait_send()
    send_line().wait_send()
    send_near().wait_send()
    send_swap().wait_send()


def back(part_in, bc, kv, grad_act, grad_resid, x, gain, small, small_row, raw_out, few, mixer_width, at):
    f32, bf16 = jnp.float32, jnp.bfloat16
    blocks = at.blocks
    features, width = part_in.shape
    query_width = width - 2 * mixer_width - WIDE
    rows = features // (2 * blocks)
    here = grad_act.shape[0]
    wide = bc.shape[1]
    chunks = 3
    piece = width // chunks
    in_cols = [slice(i * piece, (i + 1) * piece) for i in range(chunks)]
    loads = sum(bool(onward(p, h, at.bits)) for h in range(2) for p in range(blocks))
    steps = 3 + at.bits
    dma = pltpu.SemaphoreType.DMA
    vmem = pl.BlockSpec(memory_space=pltpu.VMEM)
    anywhere = pl.BlockSpec(memory_space=pl.ANY)
    line = 2 * few
    return pl.pallas_call(
        functools.partial(back_body, blocks, in_cols, small_row),
        in_specs=[anywhere] + [vmem] * 8,
        out_specs=[vmem] * 8,
        out_shape=[
            jax.ShapeDtypeStruct((rows, 2, mixer_width), f32),
            jax.ShapeDtypeStruct((rows, query_width), f32),
            jax.ShapeDtypeStruct((rows, WIDE), f32),
            jax.ShapeDtypeStruct((few, 2 * wide), f32),
            jax.ShapeDtypeStruct((here, features), f32),
            jax.ShapeDtypeStruct(small.shape, f32),
            jax.ShapeDtypeStruct((rows, mixer_width), f32),
            jax.ShapeDtypeStruct((rows, raw_out.shape[1] - mixer_width), f32),
        ],
        scratch_shapes=[
            pltpu.VMEM((loads, rows, width), bf16),
            pltpu.VMEM((2, blocks - 1, rows, width), bf16),
            pltpu.VMEM((loads, rows, width), bf16),
            pltpu.VMEM((2, rows, width), f32),
            pltpu.VMEM((2, rows, width), bf16),
            pltpu.VMEM((2, rows, width), bf16),
            pltpu.VMEM((features, wide), bf16),
            pltpu.VMEM((features, wide), bf16),
            pltpu.VMEM((loads, rows, wide), bf16),
            pltpu.VMEM((2, blocks - 1, rows, wide), bf16),
            pltpu.VMEM((loads, rows, wide), bf16),
            pltpu.VMEM((2, rows, wide), f32),
            pltpu.VMEM((2, line, wide), bf16),
            pltpu.VMEM((2, line, wide), bf16),
            pltpu.VMEM((2, few, wide), bf16),
            pltpu.VMEM((2, few, wide), bf16),
            pltpu.VMEM((few, wide), bf16),
            pltpu.VMEM((few, wide), bf16),
            pltpu.VMEM((here, features), bf16),
            pltpu.VMEM((here, features), bf16),
            pltpu.VMEM((steps + 1,) + small.shape, f32),
            pltpu.VMEM((steps,) + small.shape, f32),
            dma((2, blocks, chunks)),
            dma((2, blocks, chunks)),
            dma((loads,)),
            dma((2, blocks, 1)),
            dma((2, blocks, 1)),
            dma((loads,)),
            dma((2, chunks)),
            dma((2, chunks)),
            dma((8,)),
            dma((8,)),
            dma((steps,)),
            dma((steps,)),
            pltpu.VMEM((2, rows, raw_out.shape[1]), bf16),
            dma((2,)),
            dma((2,)),
        ],
        compiler_params=pltpu.CompilerParams(
            collective_id=2, has_side_effects=True, vmem_limit_bytes=58 * 1024 * 1024
        ),
        cost_estimate=pl.CostEstimate(
            flops=here, bytes_accessed=here, transcendentals=0
        ),
    )(
        part_in, bc, kv, grad_act, grad_resid, x, gain.reshape(1, -1), small,
        raw_out,
    )


def after(values, *others):
    return lax.optimization_barrier((values,) + others)[0]


def share_rows(values, at):
    far = at.over_z(values)
    core = at.over_core(values)
    both = at.over_core(far)
    return (values, core, far, both)


def sum_rows(pieces, at):
    own, core, far, both = pieces
    bf16 = jnp.bfloat16
    from_both = at.over_core(both.astype(bf16))
    passed = (far + from_both.astype(jnp.float32)).astype(bf16)
    from_far = at.over_z(passed)
    from_core = at.over_core(core.astype(bf16))
    return own + from_core.astype(jnp.float32) + from_far.astype(jnp.float32)


def groups(at):
    return [[d for d in range(at.dp) if d % 2 == c] for c in range(2)]


def gather_blocks(block, at):
    return lax.all_gather(block, "dp", axis=0, tiled=True, axis_index_groups=groups(at))


def sum_blocks(values, at):
    return lax.psum_scatter(
        values, "dp", scatter_dimension=0, tiled=True, axis_index_groups=groups(at)
    )


def pair_up(own, other, at):
    first = at.c == 0
    return jnp.concatenate([jnp.where(first, own, other), jnp.where(first, other, own)], axis=0)


def pair_weight(shard, at):
    first_in = at.column_out(shard)
    second_in = at.swap_away(shard)
    own = jnp.where(at.home, shard, first_in)
    other = jnp.where(at.home, first_in, second_in)
    return pair_up(own, other, at)


def gather_weight(shard, at):
    return gather_blocks(pair_weight(shard, at), at)


def send_settle(mine, at):
    rows = mine.shape[0] // 2
    low, high = mine[:rows], mine[rows:]
    own = jnp.where(at.c == 0, low, high)
    other = jnp.where(at.c == 0, high, low)
    return at.column_back(jnp.where(at.home, other, own)), at.swap_away(other), own


def end_settle(moves, at):
    first_in, second_in, own = moves
    f32 = jnp.float32
    return first_in.astype(f32) + jnp.where(at.home, own, second_in).astype(f32)


def gather_shared(shard, at):
    rows, width = shard.shape
    half = width // 2
    mine = jnp.where(at.c == 0, shard[:, :half], shard[:, half:])
    theirs = jnp.where(at.c == 0, shard[:, half:], shard[:, :half])
    came = at.over_core(theirs)
    both = jnp.stack([jnp.where(at.c == 0, mine, came), jnp.where(at.c == 0, came, mine)])
    near = at.over_z(both)
    lowest = at.t % 2 == 0
    two = jnp.stack([jnp.where(lowest, both, near), jnp.where(lowest, near, both)], axis=1)
    far = at.over_far(two)
    lower = at.t // 2 == 0
    four = jnp.stack([jnp.where(lower, two, far), jnp.where(lower, far, two)], axis=1)
    part = gather_blocks(four.reshape(2 * rows * at.tp, half), at)
    other = at.over_core(part)
    return jnp.where(at.c == 0, part, other), jnp.where(at.c == 0, other, part)


def scatter_shared(grad_bc, grad_kv, earlier, at):
    f32, bf16 = jnp.float32, jnp.bfloat16
    first = at.c == 0
    bc_width = grad_bc.shape[1]
    going = jnp.where(
        first, jnp.pad(grad_kv, ((0, 0), (0, bc_width - grad_kv.shape[1]))), grad_bc
    )
    came = at.over_core(going.astype(bf16)).astype(f32)
    kept = jnp.concatenate(
        [came[:, :HD], grad_kv[:, :HD], came[:, HD : 2 * HD], grad_kv[:, HD:]], axis=1
    )
    total = jnp.where(first, grad_bc + came, kept)
    mine = sum_blocks(after(total.astype(bf16), earlier), at)
    piece = mine.shape[0] // (2 * at.tp)
    line = mine.astype(f32).reshape(2, 2, 2, piece, total.shape[1])
    lower = at.t // 2 == 0
    went = at.over_far(jnp.where(lower, line[:, 1], line[:, 0]).astype(bf16)).astype(f32)
    line = jnp.where(lower, line[:, 0], line[:, 1]) + went
    lowest = at.t % 2 == 0
    went = at.over_z(jnp.where(lowest, line[:, 1], line[:, 0]).astype(bf16)).astype(f32)
    line = jnp.where(lowest, line[:, 0], line[:, 1]) + went
    mine = jnp.where(first, line[0], line[1])
    came = at.over_core(jnp.where(first, line[1], line[0]).astype(bf16)).astype(f32)
    return jnp.concatenate([jnp.where(first, mine, came), jnp.where(first, came, mine)], axis=1)


def sum_tensor(values, at):
    for bit in range(at.tp.bit_length() - 1):
        values = values + at.send(values, lambda d, t: (d, t ^ (1 << bit)))
    return values


def sum_data(values, at):
    for bit in range(at.dp.bit_length() - 1):
        values = values + at.send(values, lambda d, t: (d ^ (1 << bit), t))
    return values


def per_device(
    layer_in,
    teacher,
    lengths,
    input_gain,
    mixer_in_weight,
    step_weight,
    query_weight,
    shared_weight,
    conv_inner,
    conv_shared,
    step_bias,
    decay_log,
    skip_gain,
    inner_gain,
    mixer_out_weight,
    attn_out_weight,
    middle_gain,
    gate_up_weight,
    down_weight,
):
    f32 = jnp.float32
    bf16 = jnp.bfloat16
    contract_last = (((1,), (1,)), ((), ()))
    contract_first = (((0,), (0,)), ((), ()))
    at = Places()
    rows_here = layer_in.shape[0]
    slot_len = rows_here * at.tp
    local_heads = step_bias.shape[0]
    width = inner_gain.shape[0]
    head_dim = width // local_heads
    query_width = query_weight.shape[1]
    hidden_width = down_weight.shape[1]
    bc_width = conv_shared.shape[1]
    w_rows = step_weight.shape[0]

    seg = (
        lax.broadcasted_iota(jnp.int32, (width, WIDE), 0) // head_dim
        == lax.broadcasted_iota(jnp.int32, (width, WIDE), 1)
    ).astype(bf16)
    half = HD // 2
    freqs = jnp.exp(-jnp.log(ROPE_BASE) * 2.0 * jnp.arange(half, dtype=f32) / HD)
    angles = jnp.arange(slot_len).astype(f32)[:, None] * freqs[None, :]
    cosine, sine = jnp.cos(angles), jnp.sin(angles)
    cosine = jnp.concatenate([cosine, cosine], axis=1)
    sine = jnp.concatenate([-sine, sine], axis=1)
    quarters = jnp.arange(at.tp, dtype=jnp.int32)
    order = (at.c ^ (quarters // 2)) + 2 * (at.zq ^ (quarters % 2))

    in_pack = jnp.concatenate(
        [
            mixer_in_weight.reshape(w_rows, 2 * width),
            query_weight,
            step_weight,
            jnp.zeros((w_rows, WIDE - local_heads), bf16),
        ],
        axis=1,
    )
    out_pack = jnp.concatenate([mixer_out_weight, attn_out_weight], axis=1)
    column_params = jnp.concatenate(
        [conv_inner.reshape(-1), inner_gain, step_bias, decay_log, skip_gain]
    )
    params = jnp.pad(column_params, (0, -column_params.shape[0] % 1024)).reshape(-1, WIDE)
    in_all, out_pair, down_pair, act_all, x_low, _, params, proj, proj_shared, shared_all = front(
        in_pack, out_pack, down_weight, shared_weight, layer_in, input_gain, params, HD, at
    )
    column_params = params.reshape(-1)[: column_params.shape[0]]
    lane_params = jnp.concatenate(
        [
            column_params[: (KC + 1) * width].reshape(KC + 1, width),
            jnp.repeat(column_params[(KC + 1) * width + 2 * local_heads :], head_dim)[None],
            jnp.zeros((2, width), f32),
        ],
        axis=0,
    )
    head_rows = column_params[(KC + 1) * width :][: 2 * local_heads].reshape(2, local_heads)
    head_rows = jnp.concatenate([head_rows[:1], -jnp.exp(head_rows[1:])], axis=0)
    head_params = jnp.pad(head_rows, ((0, 6), (0, WIDE - local_heads)))
    def row_split(values):
        return [values[i * rows_here : (i + 1) * rows_here] for i in range(at.tp)]

    out_all = gather_blocks(out_pair, at)
    attn_low = attn_forward(order, proj, proj_shared, cosine, sine, query_width, width, bc_width)
    heads_all, y, states = mixer_forward(
        order, proj, proj_shared, attn_low, lane_params, conv_shared, head_params
    )
    seq_len = lax.dynamic_index_in_dim(lengths, at.slot, keepdims=False)
    positions = at.quarter * rows_here + jnp.arange(rows_here)
    live = (positions < seq_len).astype(f32)[:, None]
    ff_pair = pair_weight(gate_up_weight.reshape(w_rows, 2 * hidden_width), at)
    ff_all, mid_all, gate_low, up_low, hidden, grad_all, resid, error, layer_out, loss_part = middle(
        ff_pair, down_pair, heads_all, out_all, x_low, middle_gain, teacher, live, at
    )
    err_local = loss_part[0, 0]
    _, norm_mid_back = jax.vjp(rms_norm, resid, middle_gain)
    gate_up_all = ff_all[:, : 2 * hidden_width]
    down_all = ff_all[:, 2 * hidden_width :]
    gate_val, up_val = gate_low.astype(f32), up_low.astype(f32)
    sigmoid_gate = jax.nn.sigmoid(gate_val)

    def weight_grad(left, right):
        return lax.dot_general(left, right, contract_first, preferred_element_type=f32).astype(bf16)

    part_down = weight_grad(grad_all, hidden)
    grad_all, part_down = lax.optimization_barrier((grad_all, part_down))
    raw_down = sum_blocks(part_down, at)
    down_moves = send_settle(raw_down, at)
    grad_hidden = jnp.dot(grad_all, down_all, preferred_element_type=f32)
    grad_gate = grad_hidden * up_val * sigmoid_gate * (1.0 + gate_val * (1.0 - sigmoid_gate))
    grad_up = grad_hidden * gate_val * sigmoid_gate
    grad_gu = jnp.concatenate([grad_gate.astype(bf16), grad_up.astype(bf16)], axis=1)
    grad_mid_parts = [
        lax.dot_general(piece, gate_up_all, contract_last, preferred_element_type=f32)
        for piece in row_split(grad_gu)
    ]
    part_gate_up = weight_grad(mid_all, grad_gu)
    grad_mid = sum_rows(grad_mid_parts, at)
    grad_mid, part_gate_up = lax.optimization_barrier((grad_mid, part_gate_up))
    raw_gate_up = sum_blocks(part_gate_up, at)
    grad_resid_norm, grad_middle_gain = norm_mid_back(grad_mid)
    grad_resid = error + grad_resid_norm
    mix_grad_all = jnp.concatenate(share_rows(grad_resid.astype(bf16), at), axis=0)
    grad_heads = jnp.dot(mix_grad_all, out_all, preferred_element_type=f32)
    part_out = weight_grad(mix_grad_all, heads_all)
    grad_heads, part_out = lax.optimization_barrier((grad_heads, part_out))
    dq, dkv = attn_backward(
        order, proj, proj_shared, cosine, sine, grad_heads, query_width, width, bc_width
    )
    low_pack, low_shared, dlane, dconv, dhead = mixer_backward(
        order, proj, proj_shared, y, states, grad_heads, dq, dkv, lane_params, conv_shared,
        head_params, seg, query_width, down_moves[:2],
    )
    low_pack, low_shared, raw_gate_up, part_out = lax.optimization_barrier(
        (low_pack, low_shared, raw_gate_up, part_out)
    )
    raw_out = sum_blocks(part_out, at)
    column = at.column
    lanes_full = lax.dynamic_update_slice(
        jnp.zeros((KC + 1, DI), f32), dlane[: KC + 1], (0, column * width)
    )
    head_stack = jnp.concatenate(
        [dhead[:2, :local_heads], dlane[KC + 1].reshape(1, local_heads, head_dim).sum(2)], axis=0
    )
    heads_full = lax.dynamic_update_slice(
        jnp.zeros((3, H), f32), head_stack, (0, column * local_heads)
    )
    small = (
        jnp.zeros_like(input_gain),
        grad_middle_gain,
        lanes_full,
        dconv[:KC],
        heads_full,
        err_local,
    )
    flat = jnp.concatenate([part.reshape(-1) for part in small])
    padded = -(-flat.shape[0] // 1024) * 1024
    flat = jnp.pad(flat, (0, padded - flat.shape[0])).reshape(-1, WIDE)

    grad_down = end_settle(down_moves, at)
    part_in, part_bc, part_kv, grad_act, grad_gate_up = turn(
        low_pack, low_shared, act_all, in_all, shared_all, raw_gate_up, bc_width, at
    )
    grad_mix, grad_query, grad_step, grad_shared_weight, input_grad, flat, grad_out, grad_attn = back(
        part_in, part_bc, part_kv, grad_act, grad_resid, x_low, input_gain, flat, 0,
        raw_out, shared_weight.shape[0], width, at,
    )
    flat = flat.reshape(-1)
    sums = []
    start = 0
    for part in small:
        sums.append(flat[start : start + part.size].reshape(part.shape))
        start += part.size
    sum_input_gain, sum_middle_gain, sum_lanes, sum_convs, sum_heads, err_total = sums
    lanes_local = lax.dynamic_slice_in_dim(sum_lanes, at.t * width, width, 1)
    heads_local = lax.dynamic_slice_in_dim(sum_heads, at.t * local_heads, local_heads, 1)
    loss = err_total / jnp.sum(lengths).astype(f32)
    query_from = 2 * width
    step_from = query_from + query_width
    return (
        layer_out,
        loss,
        input_grad,
        sum_input_gain,
        grad_mix,
        grad_step[:, :local_heads],
        grad_query,
        grad_shared_weight,
        lanes_local[:KC],
        sum_convs,
        heads_local[0],
        heads_local[1],
        heads_local[2],
        lanes_local[KC],
        grad_out,
        grad_attn,
        sum_middle_gain,
        grad_gate_up,
        grad_down,
    )


def solution(mesh):
    placed = (
        P(("dp", "tensor"), None),
        P(("dp", "tensor"), None),
        P(),
        P(),
        P("dp", None, "tensor"),
        P("dp", "tensor"),
        P("dp", "tensor"),
        P(("dp", "tensor"), None),
        P(None, "tensor"),
        P(),
        P("tensor"),
        P("tensor"),
        P("tensor"),
        P("tensor"),
        P("dp", "tensor"),
        P("dp", "tensor"),
        P(),
        P("dp", None, "tensor"),
        P("dp", "tensor"),
    )
    return jax.shard_map(
        per_device,
        mesh=mesh,
        in_specs=placed,
        out_specs=(
            P(("dp", "tensor"), None),
            P(),
            P(("dp", "tensor"), None),
            P(),
            P("dp", None, "tensor"),
            P("dp", "tensor"),
            P("dp", "tensor"),
            P(("dp", "tensor"), None),
            P(None, "tensor"),
            P(),
            P("tensor"),
            P("tensor"),
            P("tensor"),
            P("tensor"),
            P("dp", "tensor"),
            P("dp", "tensor"),
            P(),
            P("dp", None, "tensor"),
            P("dp", "tensor"),
        ),
        check_vma=False,
    )
```

```python
import functools

import jax
import jax.numpy as jnp
from jax import lax
from jax.experimental import pallas as pl
from jax.experimental.pallas import tpu as pltpu
from jax.sharding import PartitionSpec as P

H = 48
KC = 4
QH = 8
KVH = 2
HD = 128
DI = 3072

EPS = 1e-05
ROPE_BASE = 100000000000.0


def rms_norm(values, gain):
    return values * lax.rsqrt(jnp.mean(values * values, axis=-1, keepdims=True) + EPS) * gain


def low_dot(left, right, dims):
    return lax.dot_general(left, right, (dims, ((), ())), preferred_element_type=jnp.float32)


NN = ((1,), (0,))
NT = ((1,), (1,))
TN = ((0,), (0,))
CHUNK = 128
ROWS = 256
WIDE = 128
FAR = -1e30


def exact_dot(ones, values, parts=3):
    total = None
    for _ in range(parts):
        part = values.astype(jnp.bfloat16)
        values = values - part.astype(jnp.float32)
        term = low_dot(ones, part, NN)
        total = term if total is None else total + term
    return total


def split_dot(values, ones, parts=2):
    total = None
    for _ in range(parts):
        part = values.astype(jnp.bfloat16)
        values = values - part.astype(jnp.float32)
        term = low_dot(part, ones, NN)
        total = term if total is None else total + term
    return total


def sigmoid(v):
    return 1.0 / (1.0 + jnp.exp(-v))


def softplus(v):
    return jnp.maximum(v, 0.0) + jnp.log1p(jnp.exp(-jnp.abs(v)))


def iota(shape, axis):
    return lax.broadcasted_iota(jnp.int32, shape, axis)


def spin(values, cosine, sine):
    return values * cosine + pltpu.roll(values, HD // 2, 1) * sine


def unspin(values, cosine, sine):
    return values * cosine - pltpu.roll(values, HD // 2, 1) * sine


def attn_probs(query_low, key_low, first_row, scale):
    scores = low_dot(query_low, key_low, NT) * scale
    rows, keys = scores.shape
    allowed = iota((rows, keys), 1) <= iota((rows, keys), 0) + first_row
    scores = jnp.where(allowed, scores, FAR)
    top = jnp.max(scores, axis=1, keepdims=True)
    weights = jnp.exp(scores - top)
    return weights / jnp.sum(weights, axis=1, keepdims=True)


def attn_fwd_body(order, q_ref, kv_ref, cos_ref, sin_ref, out_ref, key_s, value_s):
    bf16 = jnp.bfloat16
    step = pl.program_id(0)
    cosine, sine = cos_ref[...], sin_ref[...]
    rows = pl.ds(pl.multiple_of(step * ROWS, ROWS), ROWS)
    key_s[rows, :] = spin(kv_ref[:, :HD], cosine, sine).astype(bf16)
    value_s[rows, :] = kv_ref[:, HD:].astype(bf16)
    heads = q_ref.shape[1] // HD
    blocks = key_s.shape[0] // ROWS
    for block in range(blocks):

        @pl.when(step == block)
        def _(block=block):
            keys = (block + 1) * ROWS
            for head in range(heads):
                lanes = slice(head * HD, (head + 1) * HD)
                query = spin(q_ref[:, lanes], cosine, sine).astype(bf16)
                probs = attn_probs(query, key_s[:keys, :], block * ROWS, HD**-0.5)
                out_ref[:, lanes] = low_dot(
                    probs.astype(bf16), value_s[:keys, :], NN
                ).astype(bf16)


def attn_bwd_body(
    order, q_ref, kv_ref, cos_ref, sin_ref, grad_ref, all_cos, all_sin, dq_ref, dkv_ref,
    key_s, value_s, dkey_s, dvalue_s,
):
    bf16, f32 = jnp.bfloat16, jnp.float32
    step = pl.program_id(0)

    @pl.when(step == 0)
    def _():
        dkey_s[...] = jnp.zeros_like(dkey_s)
        dvalue_s[...] = jnp.zeros_like(dvalue_s)

    cosine, sine = cos_ref[...], sin_ref[...]
    rows = pl.ds(pl.multiple_of(step * ROWS, ROWS), ROWS)
    key_s[rows, :] = spin(kv_ref[:, :HD], cosine, sine).astype(bf16)
    value_s[rows, :] = kv_ref[:, HD:].astype(bf16)
    heads = q_ref.shape[1] // HD
    blocks = key_s.shape[0] // ROWS
    scale = HD**-0.5
    for block in range(blocks):

        @pl.when(step == block)
        def _(block=block):
            keys = (block + 1) * ROWS
            for head in range(heads):
                lanes = slice(head * HD, (head + 1) * HD)
                query = spin(q_ref[:, lanes], cosine, sine).astype(bf16)
                probs = attn_probs(query, key_s[:keys, :], block * ROWS, scale)
                grad = grad_ref[:, lanes].astype(bf16)
                dprobs = low_dot(grad, value_s[:keys, :], NT)
                dvalue_s[:keys, :] += low_dot(probs.astype(bf16), grad, TN)
                inner = jnp.sum(dprobs * probs, axis=1, keepdims=True)
                dscores = (probs * (dprobs - inner) * scale).astype(bf16)
                dquery = low_dot(dscores, key_s[:keys, :], NN)
                dkey_s[:keys, :] += low_dot(dscores, query, TN)
                dq_ref[:, lanes] = unspin(dquery, cosine, sine).astype(bf16)

    @pl.when(step == blocks - 1)
    def _():
        dkv_ref[:, :HD] = unspin(dkey_s[...], all_cos[...], all_sin[...]).astype(bf16)
        dkv_ref[:, HD:] = dvalue_s[...].astype(bf16)


def conv_taps(ext, taps, first, width):
    rows = ext.shape[0] - 8
    total = None
    for tap in range(width):
        at = 8 - (width - 1) + tap
        term = ext[at : at + rows, :] * taps[first + tap : first + tap + 1, :]
        total = term if total is None else total + term
    return total


def decays(steps, head_params, tri):
    shifted = steps + head_params[0:1, :]
    dt = softplus(shifted)
    la = dt * head_params[1:2, :]
    cum = exact_dot(tri, la)
    return shifted, dt, la, cum


def spread_lanes(values, pair, first):
    rows = values.shape[0]
    a = jnp.broadcast_to(values[:, 2 * pair : 2 * pair + 1], (rows, WIDE))
    b = jnp.broadcast_to(values[:, 2 * pair + 1 : 2 * pair + 2], (rows, WIDE))
    return a, b, jnp.where(first, a, b)


def mixer_fwd_body(
    order, gate_ref, inner_ref, step_ref, bc_ref, attn_ref, lane_ref, conv_ref, head_ref,
    out_ref, y_ref, state_ref, ext_s, extbc_s, state_s, x_s,
):
    bf16, f32 = jnp.bfloat16, jnp.float32
    step = pl.program_id(0)
    width = inner_ref.shape[1]
    states = bc_ref.shape[1] // 2

    @pl.when(step == 0)
    def _():
        ext_s[0:8, :] = jnp.zeros((8, width), f32)
        extbc_s[0:8, :] = jnp.zeros((8, 2 * states), f32)
        state_s[...] = jnp.zeros_like(state_s)

    ext_s[8:, :] = inner_ref[...]
    extbc_s[8:, :] = bc_ref[...]
    pre = conv_taps(ext_s, lane_ref, 0, KC)
    x_s[...] = pre * sigmoid(pre)
    pre = conv_taps(extbc_s, conv_ref, 0, KC)
    bc = (pre * sigmoid(pre)).astype(bf16)
    ext_s[0:8, :] = ext_s[ROWS : ROWS + 8, :]
    extbc_s[0:8, :] = extbc_s[ROWS : ROWS + 8, :]
    row, col = iota((CHUNK, CHUNK), 0), iota((CHUNK, CHUNK), 1)
    causal = row >= col
    tri = jnp.where(causal, 1.0, 0.0).astype(bf16)
    first = iota((CHUNK, WIDE), 1) < WIDE // 2
    for sub in range(ROWS // CHUNK):
        lo = sub * CHUNK
        b_low = bc[lo : lo + CHUNK, :states]
        c_low = bc[lo : lo + CHUNK, states:]
        _, dt, _, cum = decays(step_ref[lo : lo + CHUNK, :], head_ref, tri)
        cum_t = cum.T
        cross = low_dot(c_low, b_low, NT)
        state_low = state_s[...].astype(bf16)
        state_ref[sub] = state_low
        b_t = b_low.T
        for pair in range(width // WIDE):
            lanes = slice(pair * WIDE, (pair + 1) * WIDE)
            cum_a, cum_b, cum_p = spread_lanes(cum, pair, first)
            _, _, dt_p = spread_lanes(dt, pair, first)
            weights = []
            for wide, head in ((cum_a, 2 * pair), (cum_b, 2 * pair + 1)):
                gap = jnp.where(causal, wide - cum_t[head : head + 1, :], FAR)
                weights.append((cross * jnp.exp(gap)).astype(bf16))
            x = x_s[lo : lo + CHUNK, lanes]
            scaled = x * dt_p
            zero = jnp.zeros_like(scaled)
            stacked = jnp.concatenate(
                [jnp.where(first, scaled, zero), jnp.where(first, zero, scaled)], axis=0
            ).astype(bf16)
            y = low_dot(jnp.concatenate(weights, axis=1), stacked, NN)
            y = y + jnp.exp(cum_p) * low_dot(c_low, state_low[:, lanes], NN)
            y_ref[lo : lo + CHUNK, lanes] = y + lane_ref[5:6, lanes] * x
            last = cum_p[CHUNK - 1 : CHUNK, :]
            ends = (scaled * jnp.exp(last - cum_p)).astype(bf16)
            state_s[:, lanes] = state_s[:, lanes] * jnp.exp(last) + low_dot(b_t, ends, NN)
    gate = gate_ref[...]
    gated = y_ref[...] * (gate * sigmoid(gate))
    scale = lax.rsqrt(jnp.mean(gated * gated, axis=1, keepdims=True) + EPS)
    out_ref[:, :width] = (gated * scale * lane_ref[4:5, :]).astype(bf16)
    out_ref[:, width:] = attn_ref[...]


def mixer_bwd_body(
    order, gate_ref, inner_ref, before_ref, step_ref, bc_ref, bcbefore_ref, y_ref, state_ref,
    grad_ref, dq_ref, dkv_ref, lane_ref, conv_ref, head_ref, seg_ref, first_ref, second_ref,
    low_ref, lowsh_ref, dlane_ref, dconv_ref, dhead_ref,
    ext_s, extbc_s, pre_s, prebc_s, x_s, bc_s, g_s, dx_s, dbc_s, dpre_s, dprebc_s, dstate_s,
    z_s, rows_s,
):
    bf16, f32 = jnp.bfloat16, jnp.float32
    step = pl.program_id(0)
    blocks = pl.num_programs(0)
    width = inner_ref.shape[1]
    states = bc_ref.shape[1] // 2
    query_width = dq_ref.shape[1]

    @pl.when(step == 0)
    def _():
        dlane_ref[...] = jnp.zeros_like(dlane_ref)
        dconv_ref[...] = jnp.zeros_like(dconv_ref)
        dhead_ref[...] = jnp.zeros_like(dhead_ref)
        dstate_s[...] = jnp.zeros_like(dstate_s)
        dpre_s[ROWS:, :] = jnp.zeros((8, width), f32)
        dprebc_s[ROWS:, :] = jnp.zeros((8, 2 * states), f32)
        z_s[...] = jnp.zeros_like(z_s)
        rows_s[...] = jnp.zeros_like(rows_s)

    keep = jnp.where(step == blocks - 1, 0.0, 1.0)
    ext_s[0:8, :] = before_ref[...] * keep
    extbc_s[0:8, :] = bcbefore_ref[...] * keep
    ext_s[8:, :] = inner_ref[...]
    extbc_s[8:, :] = bc_ref[...]
    pre = conv_taps(ext_s, lane_ref, 0, KC)
    pre_s[...] = pre
    x_s[...] = pre * sigmoid(pre)
    pre = conv_taps(extbc_s, conv_ref, 0, KC)
    prebc_s[...] = pre
    bc_s[...] = (pre * sigmoid(pre)).astype(bf16)

    gate = gate_ref[...]
    sig = sigmoid(gate)
    gate_act = gate * sig
    y = y_ref[...]
    gated = y * gate_act
    scale = lax.rsqrt(jnp.mean(gated * gated, axis=1, keepdims=True) + EPS)
    grad = grad_ref[...]
    dlane_ref[4:5, :] += jnp.sum(grad * gated * scale, axis=0, keepdims=True)
    grad = grad * lane_ref[4:5, :]
    mean = jnp.mean(grad * gated, axis=1, keepdims=True)
    dgated = scale * grad - gated * (scale * scale * scale * mean)
    g_s[...] = dgated * gate_act
    low_ref[:, :width] = (dgated * y * sig * (1.0 + gate * (1.0 - sig))).astype(bf16)

    row, col = iota((CHUNK, CHUNK), 0), iota((CHUNK, CHUNK), 1)
    tri = jnp.where(row >= col, 1.0, 0.0).astype(bf16)
    tri_up = jnp.where(row <= col, 1.0, 0.0).astype(bf16)
    later = row <= col
    first = iota((CHUNK, WIDE), 1) < WIDE // 2
    last_row = iota((CHUNK, WIDE), 0) == CHUNK - 1
    for sub in reversed(range(ROWS // CHUNK)):
        lo = sub * CHUNK
        b_low = bc_s[lo : lo + CHUNK, :states]
        c_low = bc_s[lo : lo + CHUNK, states:]
        shifted, dt, la, cum = decays(step_ref[lo : lo + CHUNK, :], head_ref, tri)
        cum_t = cum.T
        cross_t = low_dot(b_low, c_low, NT)
        c_t = c_low.T
        state_low = state_ref[sub]
        dstate_low = dstate_s[...].astype(bf16)
        dcross_t = jnp.zeros((CHUNK, CHUNK), f32)
        db = jnp.zeros((CHUNK, states), f32)
        dc = jnp.zeros((CHUNK, states), f32)
        for pair in range(width // WIDE):
            lanes = slice(pair * WIDE, (pair + 1) * WIDE)
            cum_a, cum_b, cum_p = spread_lanes(cum, pair, first)
            _, _, dt_p = spread_lanes(dt, pair, first)
            x = x_s[lo : lo + CHUNK, lanes]
            g = g_s[lo : lo + CHUNK, lanes]
            scaled = x * dt_p
            scaled_low = scaled.astype(bf16)
            zero = jnp.zeros_like(g)
            g_stack = jnp.concatenate(
                [jnp.where(first, g, zero), jnp.where(first, zero, g)], axis=0
            ).astype(bf16)
            dweights_t = low_dot(scaled_low, g_stack, NT)
            weights_t = []
            for place, wide, head in ((0, cum_a, 2 * pair), (1, cum_b, 2 * pair + 1)):
                gap = jnp.where(later, cum_t[head : head + 1, :] - wide, FAR)
                grow = jnp.exp(gap)
                weight = (cross_t * grow).astype(bf16)
                weights_t.append(weight)
                dweight = dweights_t[:, place * CHUNK : (place + 1) * CHUNK]
                dcross_t = dcross_t + dweight * grow
                rows_s[head : head + 1, :] = jnp.sum(
                    dweight * weight.astype(f32), axis=0, keepdims=True
                )
            dx_in = low_dot(jnp.concatenate(weights_t, axis=1), g_stack, NN)
            grown = jnp.exp(cum_p)
            last = cum_p[CHUNK - 1 : CHUNK, :]
            tail = jnp.exp(last - cum_p)
            last = jnp.exp(last)
            dx_tail = tail * low_dot(b_low, dstate_low[:, lanes], NN)
            dscaled = dx_in + dx_tail
            g_grown = g * grown
            g_low = g_grown.astype(bf16)
            ends = (scaled * tail).astype(bf16)
            carried = low_dot(c_low, state_low[:, lanes], NN)
            dc = dc + low_dot(g_low, state_low[:, lanes], NT)
            db = db + low_dot(ends, dstate_low[:, lanes], NT)
            dstate = dstate_s[:, lanes]
            kept = jnp.sum(dstate * state_low[:, lanes].astype(f32), axis=0, keepdims=True) * last
            dstate_s[:, lanes] = dstate * last + low_dot(c_t, g_low, NN)
            tails = scaled * dx_tail
            z_s[0:CHUNK, lanes] = g_grown * carried - tails - scaled_low.astype(f32) * dx_in
            z_s[CHUNK : 2 * CHUNK, lanes] = dscaled * x
            z_s[2 * CHUNK : 2 * CHUNK + 1, lanes] = (
                jnp.sum(tails, axis=0, keepdims=True) + kept
            )
            dx_s[lo : lo + CHUNK, lanes] = dscaled * dt_p + lane_ref[5:6, lanes] * g
            dlane_ref[5:6, lanes] += jnp.sum(g * x, axis=0, keepdims=True)
        sums = split_dot(z_s[...], seg_ref[...])
        dcum = sums[0:CHUNK, :] + rows_s[...].T
        dcum = dcum + jnp.where(last_row, sums[2 * CHUNK : 2 * CHUNK + 1, :], 0.0)
        dla = exact_dot(tri_up, dcum)
        ddt = sums[CHUNK : 2 * CHUNK, :] + dla * head_ref[1:2, :]
        dsteps = ddt * sigmoid(shifted)
        dhead_ref[0:1, :] += jnp.sum(dsteps, axis=0, keepdims=True)
        dhead_ref[1:2, :] += jnp.sum(dla * la, axis=0, keepdims=True)
        low_ref[lo : lo + CHUNK, 2 * width + query_width :] = dsteps.astype(bf16)
        dcross_low = dcross_t.astype(bf16)
        dbc_s[lo : lo + CHUNK, :states] = db + low_dot(dcross_low, c_low, NN)
        dbc_s[lo : lo + CHUNK, states:] = dc + low_dot(dcross_low, b_low, TN)

    def conv_back(pre_ref, dact, dpre_ref, ext, taps, dtaps_ref):
        pre = pre_ref[...]
        sig = sigmoid(pre)
        dpre = dact * (sig * (1.0 + pre * (1.0 - sig)))
        dpre_ref[0:ROWS, :] = dpre
        total = None
        for tap in range(KC):
            ahead = KC - 1 - tap
            term = dpre_ref[ahead : ahead + ROWS, :] * taps[tap : tap + 1, :]
            total = term if total is None else total + term
            at = 8 - (KC - 1) + tap
            dtaps_ref[tap : tap + 1, :] += jnp.sum(
                dpre * ext[at : at + ROWS, :], axis=0, keepdims=True
            )
        dpre_ref[ROWS:, :] = dpre_ref[0:8, :]
        return total

    dinner = conv_back(pre_s, dx_s[...], dpre_s, ext_s, lane_ref, dlane_ref)
    low_ref[:, width : 2 * width] = dinner.astype(bf16)
    dbc = conv_back(prebc_s, dbc_s[...], dprebc_s, extbc_s, conv_ref, dconv_ref)
    lowsh_ref[:, : 2 * states] = dbc.astype(bf16)
    lowsh_ref[:, 2 * states :] = dkv_ref[...]
    low_ref[:, 2 * width : 2 * width + query_width] = dq_ref[...]


def block_at(rows, cols, col):
    return pl.BlockSpec((rows, cols), lambda i, order: (order[i], col))


def whole_at(shape):
    return pl.BlockSpec(shape, lambda i, order: (0,) * len(shape))


def kernel_params():
    return pltpu.CompilerParams(
        dimension_semantics=("arbitrary",), vmem_limit_bytes=56 * 1024 * 1024
    )


def attn_forward(order, proj, proj_shared, cosine, sine, query_width, width, bc_width):
    slot = proj.shape[0]
    scratch = [pltpu.VMEM((slot, HD), jnp.bfloat16)] * 2
    return pl.pallas_call(
        attn_fwd_body,
        grid_spec=pltpu.PrefetchScalarGridSpec(
            num_scalar_prefetch=1,
            grid=(slot // ROWS,),
            in_specs=[
                block_at(ROWS, query_width, 2 * width // query_width),
                block_at(ROWS, 2 * HD, bc_width // (2 * HD)),
                pl.BlockSpec((ROWS, HD), lambda i, order: (i, 0)),
                pl.BlockSpec((ROWS, HD), lambda i, order: (i, 0)),
            ],
            out_specs=block_at(ROWS, query_width, 0),
            scratch_shapes=scratch,
        ),
        out_shape=jax.ShapeDtypeStruct((slot, query_width), jnp.bfloat16),
        compiler_params=kernel_params(),
        cost_estimate=pl.CostEstimate(
            flops=slot * slot * query_width * 3,
            bytes_accessed=slot * 4 * (query_width + 4 * HD),
            transcendentals=slot * slot * query_width // HD,
        ),
    )(order, proj, proj_shared, cosine, sine)


def attn_backward(order, proj, proj_shared, cosine, sine, grad_heads, query_width, width, bc_width):
    slot = proj.shape[0]
    return pl.pallas_call(
        attn_bwd_body,
        grid_spec=pltpu.PrefetchScalarGridSpec(
            num_scalar_prefetch=1,
            grid=(slot // ROWS,),
            in_specs=[
                block_at(ROWS, query_width, 2 * width // query_width),
                block_at(ROWS, 2 * HD, bc_width // (2 * HD)),
                pl.BlockSpec((ROWS, HD), lambda i, order: (i, 0)),
                pl.BlockSpec((ROWS, HD), lambda i, order: (i, 0)),
                block_at(ROWS, query_width, width // query_width),
                whole_at((slot, HD)),
                whole_at((slot, HD)),
            ],
            out_specs=[block_at(ROWS, query_width, 0), whole_at((slot, 2 * HD))],
            scratch_shapes=[pltpu.VMEM((slot, HD), jnp.bfloat16)] * 2
            + [pltpu.VMEM((slot, HD), jnp.float32)] * 2,
        ),
        out_shape=[
            jax.ShapeDtypeStruct((slot, query_width), jnp.bfloat16),
            jax.ShapeDtypeStruct((slot, 2 * HD), jnp.bfloat16),
        ],
        compiler_params=kernel_params(),
        cost_estimate=pl.CostEstimate(
            flops=slot * slot * query_width * 8,
            bytes_accessed=slot * 4 * (2 * query_width + 6 * HD),
            transcendentals=slot * slot * query_width // HD,
        ),
    )(order, proj, proj_shared, cosine, sine, grad_heads, cosine, sine)


def mixer_forward(order, proj, proj_shared, attn_low, lane_params, conv_shared, head_params):
    slot = proj.shape[0]
    f32, bf16 = jnp.float32, jnp.bfloat16
    width = lane_params.shape[1]
    bc_width = conv_shared.shape[1]
    query_width = attn_low.shape[1]
    chunks = ROWS // CHUNK
    return pl.pallas_call(
        mixer_fwd_body,
        grid_spec=pltpu.PrefetchScalarGridSpec(
            num_scalar_prefetch=1,
            grid=(slot // ROWS,),
            in_specs=[
                block_at(ROWS, width, 0),
                block_at(ROWS, width, 1),
                block_at(ROWS, WIDE, (2 * width + query_width) // WIDE),
                block_at(ROWS, bc_width, 0),
                block_at(ROWS, query_width, 0),
                whole_at(lane_params.shape),
                whole_at(conv_shared.shape),
                whole_at(head_params.shape),
            ],
            out_specs=[
                block_at(ROWS, width + query_width, 0),
                pl.BlockSpec((ROWS, width), lambda i, order: (i, 0)),
                pl.BlockSpec((chunks, bc_width // 2, width), lambda i, order: (i, 0, 0)),
            ],
            scratch_shapes=[
                pltpu.VMEM((ROWS + 8, width), f32),
                pltpu.VMEM((ROWS + 8, bc_width), f32),
                pltpu.VMEM((bc_width // 2, width), f32),
                pltpu.VMEM((ROWS, width), f32),
            ],
        ),
        out_shape=[
            jax.ShapeDtypeStruct((slot, width + query_width), bf16),
            jax.ShapeDtypeStruct((slot, width), f32),
            jax.ShapeDtypeStruct((slot // CHUNK, bc_width // 2, width), bf16),
        ],
        compiler_params=kernel_params(),
        cost_estimate=pl.CostEstimate(
            flops=slot * width * bc_width * 8,
            bytes_accessed=slot * width * 20,
            transcendentals=slot * width * 8,
        ),
    )(order, proj, proj, proj, proj_shared, attn_low, lane_params, conv_shared, head_params)


def mixer_backward(
    order, proj, proj_shared, y, states, grad_heads, dq, dkv, lane_params, conv_shared,
    head_params, seg, query_width, moved,
):
    slot = proj.shape[0]
    f32, bf16 = jnp.float32, jnp.bfloat16
    width = lane_params.shape[1]
    bc_width = conv_shared.shape[1]
    blocks = slot // ROWS
    chunks = ROWS // CHUNK

    def back(rows, cols, col):
        return pl.BlockSpec((rows, cols), lambda i, order: (order[blocks - 1 - i], col))

    def straight(shape):
        return pl.BlockSpec(
            shape, lambda i, order: (blocks - 1 - i,) + (0,) * (len(shape) - 1)
        )

    def before(cols, col):
        return pl.BlockSpec(
            (8, cols),
            lambda i, order: (
                order[jnp.maximum(blocks - 2 - i, 0)] * (ROWS // 8) + ROWS // 8 - 1,
                col,
            ),
        )

    return pl.pallas_call(
        mixer_bwd_body,
        grid_spec=pltpu.PrefetchScalarGridSpec(
            num_scalar_prefetch=1,
            grid=(blocks,),
            in_specs=[
                back(ROWS, width, 0),
                back(ROWS, width, 1),
                before(width, 1),
                back(ROWS, WIDE, (2 * width + query_width) // WIDE),
                back(ROWS, bc_width, 0),
                before(bc_width, 0),
                straight((ROWS, width)),
                straight((chunks, bc_width // 2, width)),
                back(ROWS, width, 0),
                back(ROWS, query_width, 0),
                straight((ROWS, 2 * HD)),
                whole_at(lane_params.shape),
                whole_at(conv_shared.shape),
                whole_at(head_params.shape),
                whole_at(seg.shape),
                pl.BlockSpec(memory_space=pl.ANY),
                pl.BlockSpec(memory_space=pl.ANY),
            ],
            out_specs=[
                back(ROWS, 2 * width + query_width + WIDE, 0),
                back(ROWS, bc_width + 2 * HD, 0),
                whole_at((8, width)),
                whole_at((8, bc_width)),
                whole_at((8, WIDE)),
            ],
            scratch_shapes=[
                pltpu.VMEM((ROWS + 8, width), f32),
                pltpu.VMEM((ROWS + 8, bc_width), f32),
                pltpu.VMEM((ROWS, width), f32),
                pltpu.VMEM((ROWS, bc_width), f32),
                pltpu.VMEM((ROWS, width), f32),
                pltpu.VMEM((ROWS, bc_width), bf16),
                pltpu.VMEM((ROWS, width), f32),
                pltpu.VMEM((ROWS, width), f32),
                pltpu.VMEM((ROWS, bc_width), f32),
                pltpu.VMEM((ROWS + 8, width), f32),
                pltpu.VMEM((ROWS + 8, bc_width), f32),
                pltpu.VMEM((bc_width // 2, width), f32),
                pltpu.VMEM((2 * CHUNK + 8, width), f32),
                pltpu.VMEM((WIDE, CHUNK), f32),
            ],
        ),
        out_shape=[
            jax.ShapeDtypeStruct((slot, 2 * width + query_width + WIDE), bf16),
            jax.ShapeDtypeStruct((slot, bc_width + 2 * HD), bf16),
            jax.ShapeDtypeStruct((8, width), f32),
            jax.ShapeDtypeStruct((8, bc_width), f32),
            jax.ShapeDtypeStruct((8, WIDE), f32),
        ],
        compiler_params=kernel_params(),
        cost_estimate=pl.CostEstimate(
            flops=slot * width * bc_width * 20,
            bytes_accessed=slot * width * 40,
            transcendentals=slot * width * 16,
        ),
    )(
        order, proj, proj, proj, proj, proj_shared, proj_shared, y, states, grad_heads, dq, dkv,
        lane_params, conv_shared, head_params, seg, *moved,
    )


class Places:
    def __init__(self):
        self.dp = lax.axis_size("dp")
        self.tp = lax.axis_size("tensor")
        d = lax.axis_index("dp")
        t = lax.axis_index("tensor")
        self.d, self.t = d, t
        self.c = d % 2
        self.k = d // 2
        self.zq = t % 2
        self.home = self.c == t // 2
        self.quarter = 2 * self.c + self.zq
        self.column = self.zq + 2 * self.c
        self.slot = 2 * self.k + t // 2
        self.blocks = self.dp // 2
        self.bits = self.blocks.bit_length() - 1

    def pairs(self, where_to):
        out = []
        for d in range(self.dp):
            for t in range(self.tp):
                target = where_to(d, t)
                if target is not None:
                    out.append((d * self.tp + t, target[0] * self.tp + target[1]))
        return out

    def send(self, values, where_to):
        return lax.ppermute(values, ("dp", "tensor"), self.pairs(where_to))

    def over_core(self, values):
        return self.send(values, lambda d, t: (d ^ 1, t))

    def over_z(self, values):
        return self.send(values, lambda d, t: (d, t ^ 1))

    def over_far(self, values):
        return self.send(values, lambda d, t: (d, t ^ 2))

    def over_bit(self, values, bit):
        return self.send(values, lambda d, t: (d ^ (2 << bit), t))

    def swap_away(self, values):
        def where_to(d, t):
            if d % 2 == t // 2:
                return None
            return (d ^ 1, t ^ 2)

        return self.send(values, where_to)

    def column_out(self, values):
        def where_to(d, t):
            if d % 2 == t // 2:
                return (d, t ^ 2)
            return (d ^ 1, t)

        return self.send(values, where_to)

    def column_back(self, values):
        def where_to(d, t):
            if d % 2 == t // 2:
                return (d ^ 1, t)
            return (d, t ^ 2)

        return self.send(values, where_to)


def relocate(values, at):
    return jnp.where(at.home, values, at.swap_away(values))


MESH = pl.DeviceIdType.MESH


class Lanes:
    def __init__(self, blocks):
        d = lax.axis_index("dp")
        t = lax.axis_index("tensor")
        self.c = lax.rem(d, 2)
        self.k = lax.div(d, 2)
        self.d, self.t = d, t
        self.home = self.c == lax.div(t, 2)
        self.away = self.c != lax.div(t, 2)
        self.other = d + 1 - 2 * self.c
        self.near = t + 1 - 2 * lax.rem(t, 2)
        self.far = lax.rem(t + 2, 4)
        self.blocks = blocks
        self.bits = blocks.bit_length() - 1

    def block(self, place):
        value = self.k
        for bit in range(self.bits):
            if (place >> bit) & 1:
                value = value + (1 << bit) * (1 - 2 * lax.rem(lax.div(self.k, 1 << bit), 2))
        return value

    def across(self, bit):
        return (2 * self.block(1 << bit) + self.c, self.t)

    def greet(self):
        partners = [
            (self.other, self.t),
            (self.d, self.near),
            (self.d, self.far),
            (self.other, self.far),
        ] + [self.across(bit) for bit in range(self.bits)]
        barrier = pltpu.get_barrier_semaphore()
        for partner in partners:
            pl.semaphore_signal(barrier, inc=1, device_id=partner, device_id_type=MESH)
        pl.semaphore_wait(barrier, len(partners))


def remote(src, dst, send_sem, recv_sem, device):
    return pltpu.make_async_remote_copy(
        src_ref=src,
        dst_ref=dst,
        send_sem=send_sem,
        recv_sem=recv_sem,
        device_id=device,
        device_id_type=MESH,
    )


def onward(place, half, bits):
    if half == 0:
        return [bit for bit in range(bits) if place < (1 << bit)]
    return [bit for bit in reversed(range(bits)) if place % (2 << bit) == 0]


class Spread:
    def __init__(self, lanes, full, rows, chunks, send_sems, recv_sems, cols=slice(None), first=None, first_cols=None):
        self.lanes, self.full, self.rows, self.chunks = lanes, full, rows, chunks
        self.cols, self.first, self.first_cols = cols, first, first_cols
        self.piece = rows // chunks
        self.send_sems, self.recv_sems = send_sems, recv_sems

    def view(self, place, half, chunk):
        start = self.lanes.block(place) * (2 * self.rows) + half * self.rows + chunk * self.piece
        return self.full.at[pl.ds(pl.multiple_of(start, self.piece), self.piece), self.cols]

    def copy(self, place, half, chunk, bit):
        view = self.view(place, half, chunk)
        to = place | (1 << bit)
        source = view
        if place == 0 and self.first is not None:
            start = half * self.rows + chunk * self.piece
            source = self.first.at[pl.ds(start, self.piece), self.first_cols]
        return remote(
            source,
            view,
            self.send_sems.at[half, to, chunk],
            self.recv_sems.at[half, to, chunk],
            self.lanes.across(bit),
        )

    def give(self, place, half, chunk):
        for bit in onward(place, half, self.lanes.bits):
            self.copy(place, half, chunk, bit).start()

    def take(self, place, half, chunk):
        view = self.view(place, half, chunk)
        remote(
            view,
            view,
            self.send_sems.at[half, place, chunk],
            self.recv_sems.at[half, place, chunk],
            self.lanes.across(0),
        ).wait_recv()

    def pass_on(self, chunk):
        for half in range(2):
            places = range(1, self.lanes.blocks)
            if half == 1:
                key = lambda place: [-bit for bit in reversed(range(8)) if (place >> bit) & 1]
                places = sorted(places, key=key)
            for place in places:
                if onward(place, half, self.lanes.bits):
                    self.take(place, half, chunk)
                    self.give(place, half, chunk)

    def settle(self, place):
        for half in range(2):
            if not onward(place, half, self.lanes.bits):
                for chunk in range(self.chunks):
                    self.take(place, half, chunk)

    def sent(self, chunk):
        for half in range(2):
            for place in range(self.lanes.blocks):
                for bit in onward(place, half, self.lanes.bits):
                    self.copy(place, half, chunk, bit).wait_send()


def front_body(
    blocks, chunks, in_ref, out_ref, down_ref, shared_ref, x_ref, gain_ref, par_ref,
    full_ref, pair_ref, dpair_ref, act_ref, xr_ref, sh_ref, parr_ref, proj_ref, projsh_ref, shall_ref,
    x_s, act_s, home_sems, z_send, z_recv, o_sems, o_recv, send_sems, recv_sems, x_sems, a_send,
    a_recv, line_send, line_recv, sh_send, sh_recv, swap_send, swap_recv, par_sems,
    win_s, wsh_s, acc_s, w_sems, keep_sems, out_sems,
):
    lanes = Lanes(blocks)
    rows = in_ref.shape[0]
    piece = rows // chunks
    here = x_ref.shape[0]
    c, t = lanes.c, lanes.t
    lanes.greet()
    spread = Spread(lanes, full_ref, rows, chunks, send_sems, recv_sems)
    few, wide = shared_ref.shape
    side = wide // 2
    mine = pl.ds(pl.multiple_of(c * side, side), side)
    theirs = pl.ds(pl.multiple_of((1 - c) * side, side), side)

    def line_view(half, at_t, cols):
        start = lanes.k * (2 * rows) + half * rows + at_t * few
        return sh_ref.at[pl.ds(pl.multiple_of(start, few), few), cols]

    def line_own():
        return pltpu.make_async_copy(
            shared_ref.at[:, mine], line_view(c, t, mine), line_send.at[0]
        )

    def line_swap():
        return remote(
            shared_ref.at[:, theirs],
            line_view(c, t, theirs),
            line_send.at[1],
            line_recv.at[0],
            (lanes.other, t),
        )

    def line_swapped():
        view = line_view(1 - c, t, mine)
        return remote(view, view, line_send.at[1], line_recv.at[0], (lanes.other, t))

    def line_near(half, came):
        view = line_view(half, lanes.near if came else t, mine)
        return remote(
            view, view, line_send.at[2 + half], line_recv.at[1 + half], (lanes.d, lanes.near)
        )

    def line_far(half, near, came):
        at_t = lanes.near if near else t
        if came:
            at_t = lax.rem(at_t + 2, 4)
        view = line_view(half, at_t, mine)
        place = 2 * near + half
        return remote(
            view, view, line_send.at[4 + place], line_recv.at[3 + place], (lanes.d, lanes.far)
        )

    shared_spread = Spread(lanes, sh_ref, rows, 1, sh_send, sh_recv, mine)

    def swap_copy(place, half, came):
        start = lanes.block(place) * (2 * rows) + half * rows
        view = sh_ref.at[pl.ds(pl.multiple_of(start, rows), rows), theirs if came else mine]
        return remote(
            view, view, swap_send.at[half, place], swap_recv.at[half, place], (lanes.other, t)
        )

    def slot(chunk):
        start = lanes.k * (2 * rows) + c * rows + chunk * piece
        return full_ref.at[pl.ds(pl.multiple_of(start, piece), piece), :]

    def first_copy(chunk, device):
        return remote(
            in_ref.at[pl.ds(chunk * piece, piece), :],
            slot(chunk),
            z_send.at[0, chunk],
            z_recv.at[c, chunk],
            device,
        )

    def second_copy(chunk):
        return remote(
            in_ref.at[pl.ds(chunk * piece, piece), :],
            slot(chunk),
            z_send.at[1, chunk],
            z_recv.at[c, chunk],
            (lanes.other, lanes.far),
        )

    def own_copy(chunk):
        return pltpu.make_async_copy(
            in_ref.at[pl.ds(chunk * piece, piece), :], slot(chunk), home_sems.at[chunk]
        )

    riders = ((out_ref, pair_ref), (down_ref, dpair_ref))

    def out_slot(i):
        return riders[i][1].at[pl.ds(pl.multiple_of(c * rows, rows), rows), :]

    def out_first(i, device):
        return remote(riders[i][0], out_slot(i), o_sems.at[i, 0], o_recv.at[i, c], device)

    def out_second(i):
        return remote(
            riders[i][0], out_slot(i), o_sems.at[i, 1], o_recv.at[i, c], (lanes.other, lanes.far)
        )

    def out_own(i):
        return pltpu.make_async_copy(riders[i][0], out_slot(i), o_sems.at[i, 2])

    def out_came(i, half):
        view = riders[i][1].at[pl.ds(pl.multiple_of(half * rows, rows), rows), :]
        remote(view, view, o_sems.at[i, 0], o_recv.at[i, half], (lanes.other, t)).wait_recv()

    def x_away():
        return remote(x_ref, x_s, x_sems.at[0], x_sems.at[1], (lanes.other, lanes.far))

    def x_home():
        return pltpu.make_async_copy(x_ref, x_s, x_sems.at[2])

    def send_first(chunk):
        @pl.when(lanes.home)
        def _():
            own_copy(chunk).start()
            first_copy(chunk, (lanes.d, lanes.far)).start()

        @pl.when(lanes.away)
        def _():
            first_copy(chunk, (lanes.other, t)).start()
            second_copy(chunk).start()

    def z_view(half, chunk):
        start = lanes.k * (2 * rows) + half * rows + chunk * piece
        return full_ref.at[pl.ds(pl.multiple_of(start, piece), piece), :]

    def came(half, chunk):
        view = z_view(half, chunk)
        return remote(
            view, view, z_send.at[0, chunk], z_recv.at[half, chunk], (lanes.other, t)
        )

    def arrive_home(chunk):
        own_copy(chunk).wait()
        start = lanes.k * (2 * rows) + (1 - c) * rows + chunk * piece
        view = full_ref.at[pl.ds(pl.multiple_of(start, piece), piece), :]
        remote(
            view, view, z_send.at[0, chunk], z_recv.at[1 - c, chunk], (lanes.other, t)
        ).wait_recv()
        for half in range(2):
            spread.give(0, half, chunk)

    def arrive_away(chunk):
        for half in range(2):
            came(half, chunk).wait_recv()
        for half in range(2):
            spread.give(0, half, chunk)

    def arrive(chunk):
        @pl.when(lanes.home)
        def _():
            arrive_home(chunk)

        @pl.when(lanes.away)
        def _():
            arrive_away(chunk)

    block = 2 * rows

    def act_slot(index):
        return act_s.at[:, pl.ds(index * here, here), :]

    def act_far():
        return remote(
            act_slot(0), act_slot(2), a_send.at[0], a_recv.at[0], (lanes.d, lanes.near)
        )

    def act_core():
        return remote(act_slot(0), act_slot(1), a_send.at[1], a_recv.at[1], (lanes.other, t))

    def act_both():
        return remote(act_slot(2), act_slot(3), a_send.at[2], a_recv.at[2], (lanes.other, t))

    def norm():
        @pl.when(lanes.home)
        def _():
            x_home().wait()

        @pl.when(lanes.away)
        def _():
            x_away().wait_recv()

        @pl.loop(0, here // 32)
        def _(step):
            part = pl.ds(pl.multiple_of(step * 32, 32), 32)
            x = x_s[part, :].astype(jnp.float32)
            scale = lax.rsqrt(jnp.mean(x * x, axis=1, keepdims=True) + EPS)
            act = (x * scale * gain_ref[...]).astype(jnp.bfloat16)
            for index in range(blocks):
                act_s[index, part, :] = act[:, index * block : (index + 1) * block]

        act_far().start()
        act_core().start()
        pltpu.make_async_copy(x_s, xr_ref, x_sems.at[3]).start()

    def par_away():
        return remote(
            par_ref, parr_ref, par_sems.at[0], par_sems.at[1], (lanes.other, lanes.far)
        )

    @pl.when(lanes.home)
    def _():
        parr_ref[...] = par_ref[...]

    @pl.when(lanes.away)
    def _():
        par_away().start()

    early = list(range(max(chunks // 2, 1)))
    late = list(range(len(early), chunks))
    line_own().start()
    line_swap().start()
    for chunk in early:
        send_first(chunk)

    @pl.when(lanes.home)
    def _():
        x_home().start()

    @pl.when(lanes.away)
    def _():
        x_away().start()

    line_own().wait()
    line_swapped().wait_recv()
    for half in range(2):
        line_near(half, False).start()
    for chunk in early:
        arrive(chunk)
        if chunk:
            spread.pass_on(chunk - 1)
    for half in range(2):
        line_near(half, True).wait_recv()
    for near in range(2):
        for half in range(2):
            line_far(half, near, False).start()
    for chunk in late:
        send_first(chunk)
    spread.pass_on(early[-1])

    @pl.when(lanes.home)
    def _():
        for chunk in late:
            arrive_home(chunk)
            spread.pass_on(chunk)

    norm()

    for i in range(2):

        @pl.when(lanes.home)
        def _(i=i):
            out_first(i, (lanes.d, lanes.far)).start()
            out_own(i).start()

        @pl.when(lanes.away)
        def _(i=i):
            out_first(i, (lanes.other, t)).start()
            out_second(i).start()

    for near in range(2):
        for half in range(2):
            line_far(half, near, True).wait_recv()
    for half in range(2):
        shared_spread.give(0, half, 0)
        swap_copy(0, half, False).start()

    @pl.when(lanes.away)
    def _():
        for chunk in late:
            arrive_away(chunk)
            if chunk > late[0]:
                spread.pass_on(chunk - 1)

    shared_spread.pass_on(0)

    @pl.when(lanes.away)
    def _():
        for chunk in late[-1:]:
            spread.pass_on(chunk)

    for place in range(1, blocks):
        shared_spread.settle(place)
    for half in range(2):
        for place in range(1, blocks):
            swap_copy(place, half, False).start()

    width = full_ref.shape[1]
    narrow = wsh_s.shape[2]
    kv = (narrow - side) // 2

    def weight_copies(place, slot):
        start = lanes.block(place) * block
        view = pl.ds(pl.multiple_of(start, block), block)
        key = pl.ds(pl.multiple_of(side + c * kv, kv), kv)
        value = pl.ds(pl.multiple_of(side + 2 * kv + c * kv, kv), kv)
        return [
            pltpu.make_async_copy(src, dst, w_sems.at[slot, i])
            for i, (src, dst) in enumerate(
                (
                    (full_ref.at[view, :], win_s.at[slot]),
                    (sh_ref.at[view, pl.ds(0, side)], wsh_s.at[slot, :, pl.ds(0, side)]),
                    (sh_ref.at[view, key], wsh_s.at[slot, :, pl.ds(side, kv)]),
                    (sh_ref.at[view, value], wsh_s.at[slot, :, pl.ds(side + kv, kv)]),
                )
            )
        ]

    def shared_copy(place, slot):
        start = lanes.block(place) * block
        view = pl.ds(pl.multiple_of(start, block), block)
        return pltpu.make_async_copy(wsh_s.at[slot], shall_ref.at[view, :], keep_sems.at[slot])

    def fetch(place):
        if place:
            spread.settle(place)
        for half in range(2):
            swap_copy(place, half, True).wait_recv()
        if place >= 2:
            shared_copy(place - 2, place % 2).wait()
        for copy in weight_copies(place, place % 2):
            copy.start()

    def accumulate(place, first, last):
        slot = place % 2
        index = lanes.block(place)

        @pl.loop(first, last)
        def _(part):
            at_rows = pl.ds(pl.multiple_of(part * here, here), here)
            left = act_s[index, at_rows, :]
            for src, base in ((win_s, 0), (wsh_s, width)):
                total = src.shape[2]
                tile = total // 3
                for col in range(0, total, tile):
                    cols = slice(base + col, base + col + tile)
                    product = low_dot(left, src[slot, :, col : col + tile], NN)
                    if place:
                        product = product + acc_s[at_rows, cols]
                    acc_s[at_rows, cols] = product

    def out_copies(part):
        at_rows = pl.ds(part * here, here)
        return [
            pltpu.make_async_copy(
                acc_s.at[at_rows, pl.ds(0, width)], proj_ref.at[at_rows, :], out_sems.at[0, part]
            ),
            pltpu.make_async_copy(
                acc_s.at[at_rows, pl.ds(width, narrow)],
                projsh_ref.at[at_rows, :],
                out_sems.at[1, part],
            ),
        ]

    act_far().wait_recv()
    act_both().start()
    fetch(0)
    act_core().wait_recv()
    act_both().wait_recv()
    act_copies = [
        pltpu.make_async_copy(
            act_s.at[index],
            act_ref.at[:, pl.ds(index * block, block)],
            keep_sems.at[2 + index],
        )
        for index in range(blocks)
    ]
    for copy in act_copies:
        copy.start()
    for place in range(blocks):
        if place + 1 < blocks:
            fetch(place + 1)
        for copy in weight_copies(place, place % 2):
            copy.wait()
        shared_copy(place, place % 2).start()
        if place + 1 < blocks:
            accumulate(place, 0, 4)
        else:
            for part in range(4):
                accumulate(place, part, part + 1)
                for copy in out_copies(part):
                    copy.start()
    for place in range(max(blocks - 2, 0), blocks):
        shared_copy(place, place % 2).wait()
    for copy in act_copies:
        copy.wait()
    for chunk in range(chunks):
        spread.sent(chunk)
    shared_spread.sent(0)
    for half in range(2):
        for place in range(blocks):
            swap_copy(place, half, False).wait_send()
    line_swap().wait_send()
    for half in range(2):
        line_near(half, False).wait_send()
        for near in range(2):
            line_far(half, near, False).wait_send()
    act_far().wait_send()
    act_core().wait_send()
    act_both().wait_send()
    for part in range(4):
        for copy in out_copies(part):
            copy.wait()
    pltpu.make_async_copy(x_s, xr_ref, x_sems.at[3]).wait()

    @pl.when(lanes.home)
    def _():
        for chunk in range(chunks):
            first_copy(chunk, (lanes.d, lanes.far)).wait_send()
        for i in range(2):
            out_first(i, (lanes.d, lanes.far)).wait_send()
            out_own(i).wait()
            out_came(i, 1 - c)

    @pl.when(lanes.away)
    def _():
        par_away().wait_recv()
        par_away().wait_send()
        x_away().wait_send()
        for chunk in range(chunks):
            first_copy(chunk, (lanes.other, t)).wait_send()
            second_copy(chunk).wait_send()
        for i in range(2):
            out_first(i, (lanes.other, t)).wait_send()
            out_second(i).wait_send()
            for half in range(2):
                out_came(i, half)


def front(in_pack, out_pack, down, shared, layer_in, gain, params, kv_width, at):
    bf16 = jnp.bfloat16
    rows = in_pack.shape[0]
    blocks = at.blocks
    chunks = 4 if rows >= 256 else 1
    dma = pltpu.SemaphoreType.DMA
    anywhere = pl.BlockSpec(memory_space=pl.ANY)
    here, features = layer_in.shape
    total = 2 * blocks * rows
    narrow = shared.shape[1] // 2 + 2 * kv_width
    return pl.pallas_call(
        functools.partial(front_body, blocks, chunks),
        in_specs=[pl.BlockSpec(memory_space=pltpu.VMEM)] * 7,
        out_specs=[anywhere] * 6 + [pl.BlockSpec(memory_space=pltpu.VMEM)] + [anywhere] * 3,
        out_shape=[
            jax.ShapeDtypeStruct((total, in_pack.shape[1]), bf16),
            jax.ShapeDtypeStruct((2 * rows, out_pack.shape[1]), bf16),
            jax.ShapeDtypeStruct((2 * rows, down.shape[1]), bf16),
            jax.ShapeDtypeStruct((4 * here, features), bf16),
            jax.ShapeDtypeStruct((here, features), bf16),
            jax.ShapeDtypeStruct((total, shared.shape[1]), bf16),
            jax.ShapeDtypeStruct(params.shape, jnp.float32),
            jax.ShapeDtypeStruct((4 * here, in_pack.shape[1]), jnp.float32),
            jax.ShapeDtypeStruct((4 * here, narrow), jnp.float32),
            jax.ShapeDtypeStruct((total, narrow), bf16),
        ],
        scratch_shapes=[
            pltpu.VMEM((here, features), bf16),
            pltpu.VMEM((blocks, 4 * here, 2 * rows), bf16),
            dma((chunks,)),
            dma((2, chunks)),
            dma((2, chunks)),
            dma((2, 3)),
            dma((2, 2)),
            dma((2, blocks, chunks)),
            dma((2, blocks, chunks)),
            dma((4,)),
            dma((4,)),
            dma((3,)),
            dma((8,)),
            dma((7,)),
            dma((2, blocks, 1)),
            dma((2, blocks, 1)),
            dma((2, blocks)),
            dma((2, blocks)),
            dma((2,)),
            pltpu.VMEM((2, 2 * rows, in_pack.shape[1]), bf16),
            pltpu.VMEM((2, 2 * rows, narrow), bf16),
            pltpu.VMEM((4 * here, in_pack.shape[1] + narrow), jnp.float32),
            dma((2, 4)),
            dma((2 + blocks,)),
            dma((2, 4)),
        ],
        compiler_params=pltpu.CompilerParams(
            collective_id=1, has_side_effects=True, vmem_limit_bytes=52 * 1024 * 1024
        ),
        cost_estimate=pl.CostEstimate(
            flops=here * features * 8, bytes_accessed=300_000_000, transcendentals=0
        ),
    )(in_pack, out_pack, down, shared, layer_in, gain.reshape(1, -1), params)


class Stage:
    def __init__(self, lanes, pair, full, rows, cols, chunks, sems):
        pair_cols = slice(0, pair.shape[1])
        self.lanes, self.pair, self.full, self.rows, self.cols = lanes, pair, full, rows, cols
        self.chunks = chunks
        self.own_sem, ssem, rsem = sems
        self.spread = Spread(lanes, full, rows, chunks, ssem, rsem, cols, pair, pair_cols)

    def own(self):
        start = self.lanes.k * (2 * self.rows)
        view = self.full.at[pl.ds(pl.multiple_of(start, 2 * self.rows), 2 * self.rows), self.cols]
        return pltpu.make_async_copy(self.pair, view, self.own_sem.at[0])

    def give(self):
        for chunk in range(self.chunks):
            for half in range(2):
                self.spread.give(0, half, chunk)

    def settle(self, place):
        for half in range(2):
            if not onward(place, half, self.lanes.bits):
                for chunk in range(self.chunks):
                    self.spread.take(place, half, chunk)

    def finish(self):
        for chunk in range(self.chunks):
            for half in range(2):
                for place in range(self.lanes.blocks):
                    for bit in onward(place, half, self.lanes.bits):
                        self.spread.copy(place, half, chunk, bit).wait_send()


class Exchange:
    def __init__(self, lanes, work, own, sends, recvs, ssem, rsem):
        self.lanes, self.work, self.own = lanes, work, own
        self.both_s, self.core_s, self.pass_s = sends
        self.both_r, self.core_r, self.far_r = recvs
        self.ssem, self.rsem = ssem, rsem
        self.blocks, self.here, self.block = own.shape
        self.step = min(self.here, 64)

    def copies(self, index, place):
        core, near = (self.lanes.other, self.lanes.t), (self.lanes.d, self.lanes.near)
        table = (
            (self.both_s, self.both_r, core),
            (self.core_s, self.core_r, core),
            (self.pass_s, self.far_r, near),
        )

        def copy(kind):
            src, dst, device = table[kind]
            return remote(
                src.at[index], dst.at[index], self.ssem.at[kind, place], self.rsem.at[kind, place],
                device,
            )

        return copy

    def columns(self, place):
        return slice(place * self.block, (place + 1) * self.block)

    def rows(self, piece, i):
        start = piece * self.here + i * self.step
        return pl.ds(pl.multiple_of(start, self.step), self.step)

    def give(self, index, place, product):
        bf16 = jnp.bfloat16
        cols = self.columns(place)

        @pl.loop(0, 4)
        def _(piece):
            rows = pl.ds(pl.multiple_of(piece * self.here, self.here), self.here)
            self.work[rows, cols] = product(rows)

        @pl.loop(0, self.here // self.step)
        def _(i):
            part = self.rows(0, i)
            self.both_s[index, part, :] = self.work[self.rows(3, i), cols].astype(bf16)
            self.core_s[index, part, :] = self.work[self.rows(1, i), cols].astype(bf16)
            self.own[index, part, :] = self.work[part, cols]

        copy = self.copies(index, place)
        copy(0).start()
        copy(1).start()

    def pass_on(self, index, place):
        copy = self.copies(index, place)
        copy(0).wait_recv()
        cols = self.columns(place)

        @pl.loop(0, self.here // self.step)
        def _(i):
            part = self.rows(0, i)
            total = self.work[self.rows(2, i), cols] + self.both_r[index, part, :].astype(
                jnp.float32
            )
            self.pass_s[index, part, :] = total.astype(jnp.bfloat16)

        copy(2).start()

    def take(self, index, place):
        copy = self.copies(index, place)
        copy(1).wait_recv()
        copy(2).wait_recv()

    def total(self, index, rows):
        f32 = jnp.float32
        return (
            self.own[index, rows, :]
            + self.core_r[index, rows, :].astype(f32)
            + self.far_r[index, rows, :].astype(f32)
        )

    def finish(self, index, place):
        copy = self.copies(index, place)
        for kind in range(3):
            copy(kind).wait_send()


def middle_body(
    blocks, gu_chunks, down_chunks,
    pair_ref, dpair_ref, heads_ref, out_ref, teacher_ref, x_ref, gain_ref, live_ref,
    full_ref, mid_ref, gate_ref, up_ref, hidden_ref, grads_ref, resid_ref, error_ref, low_ref,
    loss_ref,
    wbuf, mid_s, acc_s, hid_s, gate_s, up_s, own_s, both_s, core_s, pass_s,
    both_r, core_r, far_r, both_q, core_q, far_q, err_s,
    w_sems, one_s, one_r, two_s, two_r, mid_ssem, mid_rsem, err_ssem, err_rsem, keep_sems,
    g_home, g_s, g_r, d_home, d_s, d_r, target_ref, t_sems, out_s,
):
    f32, bf16 = jnp.float32, jnp.bfloat16
    lanes = Lanes(blocks)
    rows = pair_ref.shape[0] // 2
    here = x_ref.shape[0]
    block = 2 * rows
    inner = heads_ref.shape[1]
    hidden_width = hid_s.shape[1]
    core_at = (lanes.other, lanes.t)
    near_at = (lanes.d, lanes.near)
    lanes.greet()
    gate_up = Stage(
        lanes, pair_ref, full_ref, rows, slice(0, 2 * hidden_width), gu_chunks,
        (g_home, g_s, g_r),
    )
    down = Stage(
        lanes, dpair_ref, full_ref, rows, slice(2 * hidden_width, 3 * hidden_width), down_chunks,
        (d_home, d_s, d_r),
    )

    def target_away():
        return remote(
            teacher_ref, target_ref, t_sems.at[0], t_sems.at[1], (lanes.other, lanes.far)
        )

    def target_home():
        return pltpu.make_async_copy(teacher_ref, target_ref, t_sems.at[2])

    sends = (both_s, core_s, pass_s)
    one = Exchange(lanes, acc_s, own_s, sends, (both_r, core_r, far_r), one_s, one_r)
    two = Exchange(lanes, acc_s, own_s, sends, (both_q, core_q, far_q), two_s, two_r)

    def load(src, slot, width, cols):
        return pltpu.make_async_copy(src, wbuf.at[slot, :, cols], w_sems.at[slot])

    def out_load(index):
        return load(
            out_ref.at[pl.ds(index * block, block), :], index % 2, inner, pl.ds(0, inner)
        )

    out_load(0).start()
    gate_up.give()
    gate_up.own().start()
    down.own().start()

    for index in range(blocks):
        if index + 1 < blocks:
            out_load(index + 1).start()
        out_load(index).wait()
        one.give(
            index,
            index,
            lambda rows: low_dot(heads_ref[rows, :], wbuf[index % 2, :, :inner], NT),
        )
    for index in range(blocks):
        one.pass_on(index, index)

    for chunk in range(gu_chunks):
        gate_up.spread.pass_on(chunk)
    down.give()

    for index in range(blocks):
        one.take(index, index)

    step = min(here, 32)

    def columns(index):
        return slice(index * block, (index + 1) * block)

    @pl.loop(0, here // step)
    def _(i):
        part = pl.ds(pl.multiple_of(i * step, step), step)
        total = jnp.zeros((step, 1), f32)
        for index in range(blocks):
            resid = x_ref[part, columns(index)].astype(f32) + one.total(index, part)
            resid_ref[part, columns(index)] = resid
            total = total + jnp.sum(resid * resid, axis=1, keepdims=True)
        scale = lax.rsqrt(total / (blocks * block) + EPS)
        for index in range(blocks):
            mid = resid_ref[part, columns(index)] * scale * gain_ref[:, columns(index)]
            mid_s[index, part, :] = mid.astype(bf16)

    def mid_view(slot):
        return mid_s.at[:, pl.ds(slot * here, here), :]

    def mid_near():
        return remote(mid_view(0), mid_view(2), mid_ssem.at[0], mid_rsem.at[0], near_at)

    def mid_core():
        return remote(mid_view(0), mid_view(1), mid_ssem.at[1], mid_rsem.at[1], core_at)

    def mid_both():
        return remote(mid_view(2), mid_view(3), mid_ssem.at[2], mid_rsem.at[2], core_at)

    mid_near().start()
    mid_core().start()

    @pl.when(lanes.home)
    def _():
        target_home().start()

    @pl.when(lanes.away)
    def _():
        target_away().start()

    def gu_load(place, slot):
        start = lanes.block(place) * block
        view = full_ref.at[pl.ds(pl.multiple_of(start, block), block), pl.ds(0, 2 * hidden_width)]
        return load(view, slot, 2 * hidden_width, pl.ds(0, 2 * hidden_width))

    def down_load(place, slot):
        start = lanes.block(place) * block
        view = full_ref.at[
            pl.ds(pl.multiple_of(start, block), block), pl.ds(2 * hidden_width, hidden_width)
        ]
        return load(view, slot, hidden_width, pl.ds(0, hidden_width))

    gate_up.own().wait()
    gu_load(0, 0).start()
    mid_near().wait_recv()
    mid_both().start()
    mid_core().wait_recv()

    wide = 2 * hidden_width
    tile = min(wide, 512)

    def accumulate(place, first, last):
        slot = place % 2
        index = lanes.block(place)

        @pl.loop(first, last)
        def _(piece):
            part = pl.ds(pl.multiple_of(piece * here, here), here)
            left = mid_s[index, part, :]
            for col in range(0, wide, tile):
                cols = slice(col, col + tile)
                product = low_dot(left, wbuf[slot, :, cols], NN)
                if place:
                    product = product + acc_s[part, cols]
                acc_s[part, cols] = product

    for place in range(blocks):
        if place + 1 < blocks:
            gate_up.settle(place + 1)
            gu_load(place + 1, (place + 1) % 2).start()
        gu_load(place, place % 2).wait()
        accumulate(place, 0, 3)
        if place == 0:
            mid_both().wait_recv()
        accumulate(place, 3, 4)
        if place < down_chunks:
            down.spread.pass_on(place)

    for chunk in range(blocks, down_chunks):
        down.spread.pass_on(chunk)

    down.own().wait()
    down_load(0, 0).start()

    @pl.loop(0, 4 * here // step)
    def _(i):
        part = pl.ds(pl.multiple_of(i * step, step), step)
        gate = acc_s[part, :hidden_width]
        up = acc_s[part, hidden_width : 2 * hidden_width]
        gate_s[part, :] = gate.astype(bf16)
        up_s[part, :] = up.astype(bf16)
        hid_s[part, :] = (gate * sigmoid(gate) * up).astype(bf16)

    kept = [
        pltpu.make_async_copy(hid_s, hidden_ref, keep_sems.at[0]),
        pltpu.make_async_copy(gate_s, gate_ref, keep_sems.at[1]),
        pltpu.make_async_copy(up_s, up_ref, keep_sems.at[2]),
    ] + [
        pltpu.make_async_copy(
            mid_s.at[index], mid_ref.at[:, pl.ds(index * block, block)], keep_sems.at[3 + index]
        )
        for index in range(blocks)
    ]
    for copy in kept:
        copy.start()
    for index in range(blocks):
        one.finish(index, index)

    for place in range(blocks):
        index = lanes.block(place)
        if place + 1 < blocks:
            down.settle(place + 1)
            down_load(place + 1, (place + 1) % 2).start()
        down_load(place, place % 2).wait()
        two.give(
            index,
            place,
            lambda rows: low_dot(hid_s[rows, :], wbuf[place % 2, :, :hidden_width], NT),
        )
        if place:
            two.pass_on(lanes.block(place - 1), place - 1)
    two.pass_on(lanes.block(blocks - 1), blocks - 1)
    for place in range(blocks):
        two.take(lanes.block(place), place)

    @pl.when(lanes.home)
    def _():
        target_home().wait()

    @pl.when(lanes.away)
    def _():
        target_away().wait_recv()
        target_away().wait_send()

    def output_part(i, loss):
        part = pl.ds(pl.multiple_of(i * step, step), step)
        live = live_ref[part, :]
        for index in range(blocks):
            cols = columns(index)
            outputs = resid_ref[part, cols] + two.total(index, part)
            out_s[part, cols] = outputs.astype(bf16)
            error = (outputs - target_ref[part, cols].astype(f32)) * live
            error_ref[part, cols] = error
            err_s[part, cols] = error.astype(bf16)
            loss = loss + jnp.sum(error * error)
        return loss

    loss = lax.fori_loop(0, here // step, output_part, jnp.zeros((), f32))
    loss_ref[...] = jnp.zeros((8, WIDE), f32) + 0.5 * loss

    def grads_view(slot):
        return grads_ref.at[pl.ds(slot * here, here), :]

    def err_near():
        return remote(err_s, grads_view(2), err_ssem.at[0], err_rsem.at[0], near_at)

    def err_core():
        return remote(err_s, grads_view(1), err_ssem.at[1], err_rsem.at[1], core_at)

    def err_both():
        return remote(grads_view(2), grads_view(3), err_ssem.at[2], err_rsem.at[2], core_at)

    own_err = pltpu.make_async_copy(err_s, grads_view(0), err_ssem.at[3])
    err_near().start()
    err_core().start()
    own_err.start()

    def out_home():
        return pltpu.make_async_copy(out_s, low_ref, t_sems.at[5])

    def out_away():
        return remote(out_s, low_ref, t_sems.at[3], t_sems.at[4], (lanes.other, lanes.far))

    @pl.when(lanes.home)
    def _():
        out_home().start()

    @pl.when(lanes.away)
    def _():
        out_away().start()

    for copy in kept:
        copy.wait()
    gate_up.finish()
    down.finish()
    for place in range(blocks):
        two.finish(lanes.block(place), place)
    for copy in (mid_near(), mid_core(), mid_both()):
        copy.wait_send()
    err_near().wait_recv()
    err_both().start()
    err_core().wait_recv()
    err_both().wait_recv()
    own_err.wait()

    @pl.when(lanes.home)
    def _():
        out_home().wait()

    @pl.when(lanes.away)
    def _():
        out_away().wait()

    for copy in (err_near(), err_core(), err_both()):
        copy.wait_send()


def middle(pair, down_pair, heads_all, out_all, x, gain, teacher, live, at):
    f32, bf16 = jnp.float32, jnp.bfloat16
    rows = pair.shape[0] // 2
    hidden_width = down_pair.shape[1]
    slot, inner = heads_all.shape
    here, features = x.shape
    blocks = at.blocks
    block = 2 * rows
    gu_chunks = 4 if rows >= 256 else 1
    down_chunks = 2 if rows >= 256 else 1
    dma = pltpu.SemaphoreType.DMA
    vmem = pl.BlockSpec(memory_space=pltpu.VMEM)
    anywhere = pl.BlockSpec(memory_space=pl.ANY)

    def stage_sems(chunks):
        return [dma((1,)), dma((2, blocks, chunks)), dma((2, blocks, chunks))]

    shape = jax.ShapeDtypeStruct
    buffers = [pltpu.VMEM((blocks, here, block), bf16)]
    return pl.pallas_call(
        functools.partial(middle_body, blocks, gu_chunks, down_chunks),
        in_specs=[vmem] * 3 + [anywhere, anywhere, vmem, vmem, vmem],
        out_specs=[anywhere] * 6 + [vmem] * 4,
        out_shape=[
            shape((features, 3 * hidden_width), bf16),
            shape((slot, features), bf16),
            shape((slot, hidden_width), bf16),
            shape((slot, hidden_width), bf16),
            shape((slot, hidden_width), bf16),
            shape((slot, features), bf16),
            shape((here, features), f32),
            shape((here, features), f32),
            shape((here, features), bf16),
            shape((8, WIDE), f32),
        ],
        scratch_shapes=[
            pltpu.VMEM((2, block, 2 * hidden_width), bf16),
            pltpu.VMEM((blocks, slot, block), bf16),
            pltpu.VMEM((slot, max(2 * hidden_width, features)), f32),
            pltpu.VMEM((slot, hidden_width), bf16),
            pltpu.VMEM((slot, hidden_width), bf16),
            pltpu.VMEM((slot, hidden_width), bf16),
            pltpu.VMEM((blocks, here, block), f32),
        ]
        + buffers * 9
        + [
            pltpu.VMEM((here, features), bf16),
            dma((2,)),
            dma((3, blocks)),
            dma((3, blocks)),
            dma((3, blocks)),
            dma((3, blocks)),
            dma((3,)),
            dma((3,)),
            dma((4,)),
            dma((3,)),
            dma((3 + blocks,)),
        ]
        + stage_sems(gu_chunks)
        + stage_sems(down_chunks)
        + [pltpu.VMEM((here, features), bf16), dma((6,)), pltpu.VMEM((here, features), bf16)],
        compiler_params=pltpu.CompilerParams(
            collective_id=3, has_side_effects=True, vmem_limit_bytes=58 * 1024 * 1024
        ),
        cost_estimate=pl.CostEstimate(
            flops=slot * features * hidden_width * 8, bytes_accessed=400_000_000, transcendentals=0
        ),
    )(
        pair, down_pair, heads_all, out_all, teacher, x, gain.reshape(1, -1), live,
    )


def turn_body(
    blocks, low_ref, lowsh_ref, act_ref, in_ref, sh_ref, rawgu_ref,
    part_ref, bc_ref, kv_ref, sum_ref, gu_ref,
    win_s, wsh_s, work_s, own_s, both_s, core_s, pass_s, both_r, core_r, far_r, stage_s,
    gu_r, w_sems, x_ssem, x_rsem, stage_sems, ff_ssem, ff_rsem,
):
    f32, bf16 = jnp.float32, jnp.bfloat16
    lanes = Lanes(blocks)
    c, t = lanes.c, lanes.t
    here = sum_ref.shape[0]
    rows = rawgu_ref.shape[0] // 2
    block = 2 * rows
    width = low_ref.shape[1]
    bc_width = bc_ref.shape[1]
    features = act_ref.shape[1]
    core_at, far_at, cross_at = (
        (lanes.other, t), (lanes.d, lanes.far), (lanes.other, lanes.far),
    )
    lanes.greet()

    def ff_copies(kind, half, device):
        view = pl.ds(pl.multiple_of(half * rows, rows), rows)
        return [
            remote(
                src.at[view, :], dst.at[kind], ff_ssem.at[kind, i], ff_rsem.at[kind, i], device
            )
            for i, (src, dst) in enumerate(((rawgu_ref, gu_r),))
        ]

    def first_home():
        return ff_copies(0, 1 - c, core_at)

    def first_away():
        return ff_copies(0, c, far_at)

    def second_away():
        return ff_copies(1, 1 - c, cross_at)

    def load(index):
        slot = index % 2
        view = pl.ds(index * block, block)
        return (
            pltpu.make_async_copy(in_ref.at[view, :], win_s.at[slot], w_sems.at[slot, 0]),
            pltpu.make_async_copy(sh_ref.at[view, :], wsh_s.at[slot], w_sems.at[slot, 1]),
        )

    for copy in load(0):
        copy.start()

    @pl.when(lanes.home)
    def _():
        for copy in first_home():
            copy.start()

    @pl.when(lanes.away)
    def _():
        for one, two in zip(first_away(), second_away()):
            one.start()
            two.start()

    exchange = Exchange(
        lanes, work_s, own_s, (both_s, core_s, pass_s), (both_r, core_r, far_r), x_ssem, x_rsem
    )
    for index in range(blocks):
        slot = index % 2
        if index + 1 < blocks:
            for copy in load(index + 1):
                copy.start()
        for copy in load(index):
            copy.wait()
        exchange.give(
            index,
            index,
            lambda part: low_dot(low_ref[part, :], win_s[slot], NT)
            + low_dot(lowsh_ref[part, :], wsh_s[slot], NT),
        )
        if index:
            exchange.pass_on(index - 1, index - 1)
    exchange.pass_on(blocks - 1, blocks - 1)

    tall = 256
    steps = features // tall

    def out_copies(i, slot):
        view = pl.ds(pl.multiple_of(i * tall, tall), tall)
        kv_from = width + bc_width
        return (
            pltpu.make_async_copy(
                stage_s.at[slot, :, :width], part_ref.at[view, :], stage_sems.at[slot, 0]
            ),
            pltpu.make_async_copy(
                stage_s.at[slot, :, width:kv_from], bc_ref.at[view, :], stage_sems.at[slot, 1]
            ),
            pltpu.make_async_copy(
                stage_s.at[slot, :, kv_from:], kv_ref.at[view, :], stage_sems.at[slot, 2]
            ),
        )

    @pl.loop(0, steps)
    def _(i):
        slot = lax.rem(i, 2)

        @pl.when(i >= 2)
        def _():
            for copy in out_copies(i - 2, slot):
                copy.wait()

        left = act_ref[:, pl.ds(pl.multiple_of(i * tall, tall), tall)].T
        for src, base in ((low_ref, 0), (lowsh_ref, width)):
            total = src.shape[1]
            tile = total // 3
            for col in range(0, total, tile):
                product = low_dot(left, src[:, col : col + tile], NN)
                stage_s[slot, :, base + col : base + col + tile] = product.astype(bf16)
        for copy in out_copies(i, slot):
            copy.start()

    for index in range(blocks):
        exchange.take(index, index)
    step = min(here, 32)

    @pl.loop(0, here // step)
    def _(i):
        part = pl.ds(pl.multiple_of(i * step, step), step)
        for index in range(blocks):
            sum_ref[part, index * block : (index + 1) * block] = exchange.total(index, part)

    for i in (steps - 2, steps - 1):
        for copy in out_copies(i, i % 2):
            copy.wait()
    for index in range(blocks):
        exchange.finish(index, index)
    for copy in first_home():
        copy.wait_recv()
    span = min(rows, 32)
    side_width = gu_ref.shape[2]

    @pl.when(lanes.home)
    def _():
        for copy in first_home():
            copy.wait_send()

        @pl.loop(0, rows // span)
        def _(i):
            part = pl.ds(pl.multiple_of(i * span, span), span)
            mine = pl.ds(pl.multiple_of(c * rows + i * span, span), span)
            for side in range(2):
                cols = slice(side * side_width, (side + 1) * side_width)
                total = rawgu_ref[mine, cols].astype(f32) + gu_r[0, part, cols].astype(f32)
                gu_ref[part, side, :] = total

    @pl.when(lanes.away)
    def _():
        for copy in second_away():
            copy.wait_recv()
        for copy in first_away() + second_away():
            copy.wait_send()

        @pl.loop(0, rows // span)
        def _(i):
            part = pl.ds(pl.multiple_of(i * span, span), span)
            for side in range(2):
                cols = slice(side * side_width, (side + 1) * side_width)
                total = gu_r[0, part, cols].astype(f32) + gu_r[1, part, cols].astype(f32)
                gu_ref[part, side, :] = total


def turn(low_pack, low_shared, act_all, in_all, shared_all, raw_gate_up, bc_width, at):
    f32, bf16 = jnp.float32, jnp.bfloat16
    slot, width = low_pack.shape
    shared_width = low_shared.shape[1]
    features = act_all.shape[1]
    here = slot // 4
    blocks = at.blocks
    rows = raw_gate_up.shape[0] // 2
    block = 2 * rows
    gu_width = raw_gate_up.shape[1]
    dma = pltpu.SemaphoreType.DMA
    vmem = pl.BlockSpec(memory_space=pltpu.VMEM)
    anywhere = pl.BlockSpec(memory_space=pl.ANY)
    shape = jax.ShapeDtypeStruct
    return pl.pallas_call(
        functools.partial(turn_body, blocks),
        in_specs=[vmem] * 3 + [anywhere] * 2 + [vmem],
        out_specs=[anywhere] * 3 + [vmem] * 2,
        out_shape=[
            shape((features, width), bf16),
            shape((features, bc_width), bf16),
            shape((features, shared_width - bc_width), bf16),
            shape((here, features), f32),
            shape((rows, 2, gu_width // 2), f32),
        ],
        scratch_shapes=[
            pltpu.VMEM((2, block, width), bf16),
            pltpu.VMEM((2, block, shared_width), bf16),
            pltpu.VMEM((slot, features), f32),
            pltpu.VMEM((blocks, here, block), f32),
        ]
        + [pltpu.VMEM((blocks, here, block), bf16)] * 6
        + [
            pltpu.VMEM((2, 256, width + shared_width), bf16),
            pltpu.VMEM((2, rows, gu_width), bf16),
            dma((2, 2)),
            dma((3, blocks)),
            dma((3, blocks)),
            dma((2, 3)),
            dma((2, 1)),
            dma((2, 1)),
        ],
        compiler_params=pltpu.CompilerParams(
            collective_id=4, has_side_effects=True, vmem_limit_bytes=58 * 1024 * 1024
        ),
        cost_estimate=pl.CostEstimate(
            flops=slot * features * width * 5, bytes_accessed=60_000_000, transcendentals=0
        ),
    )(low_pack, low_shared, act_all, in_all, shared_all, raw_gate_up)


class Collect:
    def __init__(self, lanes, part, rows, cols, send_s, recv_s, load_s, total_s, sems):
        self.lanes, self.part, self.rows, self.cols = lanes, part, rows, cols
        self.send_s, self.recv_s, self.load_s, self.total_s = send_s, recv_s, load_s, total_s
        self.send_sems, self.recv_sems, self.load_sems = sems
        self.loads = [
            (half, place)
            for half in range(2)
            for place in range(lanes.blocks)
            if onward(place, half, lanes.bits)
        ]

    def source(self, place, half, chunk):
        start = self.lanes.block(place) * (2 * self.rows) + half * self.rows
        return self.part.at[pl.ds(pl.multiple_of(start, self.rows), self.rows), self.cols[chunk]]

    def bit_of(self, place, half):
        bits = [bit for bit in range(self.lanes.bits) if (place >> bit) & 1]
        return bits[-1] if half == 0 else bits[0]

    def load(self, half, place):
        index = self.loads.index((half, place))
        start = self.lanes.block(place) * (2 * self.rows) + half * self.rows
        view = self.part.at[pl.ds(pl.multiple_of(start, self.rows), self.rows), :]
        return pltpu.make_async_copy(view, self.load_s.at[index], self.load_sems.at[index])

    def copy(self, place, half, chunk):
        if (half, place) in self.loads:
            source = self.send_s.at[self.loads.index((half, place)), :, self.cols[chunk]]
        else:
            source = self.source(place, half, chunk)
        return remote(
            source,
            self.recv_s.at[half, place - 1, :, self.cols[chunk]],
            self.send_sems.at[half, place, chunk],
            self.recv_sems.at[half, place, chunk],
            self.lanes.across(self.bit_of(place, half)),
        )

    def order(self, half):
        places = list(range(1, self.lanes.blocks))
        places.sort(key=lambda place: -len([b for b in range(8) if (place >> b) & 1]))
        return places

    def start(self):
        for half, place in self.loads:
            self.load(half, place).start()

    def direct(self, chunk):
        for half in range(2):
            for place in self.order(half):
                if (half, place) not in self.loads:
                    self.copy(place, half, chunk).start()

    def add(self, place, half, chunk):
        cols = self.cols[chunk]
        index = self.loads.index((half, place))
        total = self.load_s[index, :, cols].astype(jnp.float32)
        for bit in onward(place, half, self.lanes.bits):
            came = place | (1 << bit)
            self.copy(came, half, chunk).wait_recv()
            total = total + self.recv_s[half, came - 1, :, cols].astype(jnp.float32)
        return total

    def middle(self, chunk):
        for half in range(2):
            for place in self.order(half):
                if (half, place) in self.loads:
                    index = self.loads.index((half, place))
                    if chunk == 0:
                        self.load(half, place).wait()
                    total = self.add(place, half, chunk)
                    self.send_s[index, :, self.cols[chunk]] = total.astype(jnp.bfloat16)
                    self.copy(place, half, chunk).start()

    def last(self, chunk):
        for half in range(2):
            if chunk == 0:
                self.load(half, 0).wait()
            self.total_s[half, :, self.cols[chunk]] = self.add(0, half, chunk)

    def finish(self):
        for chunk in range(len(self.cols)):
            for half in range(2):
                for place in range(1, self.lanes.blocks):
                    self.copy(place, half, chunk).wait_send()


def back_body(
    blocks, in_cols, small_row, part_ref, bc_ref, kv_ref, act_ref,
    resid_ref, x_ref, gain_ref, small_ref, out_ref,
    gmix_ref, gquery_ref, gstep_ref, gsh_ref, gx_ref, sum_ref, gout_ref, gattn_ref,
    in_send, in_recv, in_load, in_total, settle_s, settle_r, sh_came, sh_part, sh_send, sh_recv,
    sh_load, sh_total, line_s, line_r, near_s, near_r, swap_s, swap_r,
    gx_s, gx_r, small_s, small_r,
    in_ssem, in_rsem, in_lsem, sh_ssem, sh_rsem, sh_lsem, set_ssem, set_rsem, misc_s, misc_r,
    small_ssem, small_rsem, out_r, out_ssem, out_rsem,
):
    f32, bf16 = jnp.float32, jnp.bfloat16
    lanes = Lanes(blocks)
    c, t = lanes.c, lanes.t
    rows = gquery_ref.shape[0]
    width = gmix_ref.shape[2]
    query_width = gquery_ref.shape[1]
    here = act_ref.shape[0]
    wide = bc_ref.shape[1]
    few = gsh_ref.shape[0]
    chunks = len(in_cols)
    step = min(here, 32)
    lanes.greet()
    core_at = (lanes.other, t)
    near_at = (lanes.d, lanes.near)
    far_at = (lanes.d, lanes.far)
    cross_at = (lanes.other, lanes.far)
    first = c == 0
    second = c == 1

    collect = Collect(
        lanes, part_ref, rows, in_cols, in_send, in_recv, in_load, in_total,
        (in_ssem, in_rsem, in_lsem),
    )
    shared = Collect(
        lanes, sh_part, rows, [slice(0, wide)], sh_send, sh_recv, sh_load, sh_total,
        (sh_ssem, sh_rsem, sh_lsem),
    )
    half_kv = kv_ref.shape[1] // 2

    def send_kv():
        return remote(
            kv_ref, sh_came.at[:, : 2 * half_kv], misc_s.at[2], misc_r.at[2], core_at
        )

    def send_bc():
        return remote(bc_ref, sh_came, misc_s.at[3], misc_r.at[3], core_at)

    def out_block(half):
        return out_ref.at[pl.ds(pl.multiple_of(half * rows, rows), rows), :]

    def out_first(half, device):
        return remote(out_block(half), out_r.at[0], out_ssem.at[0], out_rsem.at[0], device)

    def out_second():
        return remote(out_block(1 - c), out_r.at[1], out_ssem.at[1], out_rsem.at[1], cross_at)

    collect.start()
    for chunk in range(chunks):
        collect.direct(chunk)
    @pl.when(first)
    def _():
        send_kv().start()

    @pl.when(second)
    def _():
        send_bc().start()

    def send_x():
        return remote(gx_s, gx_r, misc_s.at[4], misc_r.at[4], cross_at)

    small_s[0] = small_ref[...]
    features = gain_ref.shape[1]

    def one_part(i, gains):
        view = pl.ds(pl.multiple_of(i * step, step), step)
        grad = act_ref[view, :]
        x = x_ref[view, :].astype(f32)
        scale = lax.rsqrt(jnp.mean(x * x, axis=1, keepdims=True) + EPS)
        gains = gains + jnp.sum(grad * (x * scale), axis=0, keepdims=True)
        grad = grad * gain_ref[...]
        mean = jnp.mean(grad * x, axis=1, keepdims=True)
        result = resid_ref[view, :] + scale * grad - x * (scale * scale * scale * mean)
        gx_ref[view, :] = result
        gx_s[view, :] = result.astype(bf16)
        return gains

    gains = lax.fori_loop(0, here // step, one_part, jnp.zeros((1, features), f32))
    for i in range(features // WIDE):
        small_s[0, small_row + i : small_row + i + 1, :] = gains[:, i * WIDE : (i + 1) * WIDE]

    stops = [far_at, near_at, core_at] + [lanes.across(bit) for bit in range(lanes.bits)]

    def send_small(index):
        return remote(
            small_s.at[index], small_r.at[index], small_ssem.at[index], small_rsem.at[index],
            stops[index],
        )

    def step_small(index):
        send_small(index).wait_recv()
        small_s[index + 1] = small_s[index] + small_r[index]
        if index + 1 < len(stops):
            send_small(index + 1).start()

    send_small(0).start()

    @pl.when(lanes.away)
    def _():
        send_x().start()

    @pl.when(lanes.home)
    def _():
        out_first(1 - c, core_at).start()

    @pl.when(lanes.away)
    def _():
        out_first(c, far_at).start()
        out_second().start()

    @pl.when(first)
    def _():
        send_bc().wait_recv()

        @pl.loop(0, bc_ref.shape[0] // 64)
        def _(i):
            view = pl.ds(pl.multiple_of(i * 64, 64), 64)
            total = bc_ref[view, :].astype(f32) + sh_came[view, :].astype(f32)
            sh_part[view, :] = total.astype(bf16)

    @pl.when(second)
    def _():
        send_kv().wait_recv()

        @pl.loop(0, bc_ref.shape[0] // 64)
        def _(i):
            view = pl.ds(pl.multiple_of(i * 64, 64), 64)
            for piece in range(2):
                kept = pl.ds(piece * half_kv, half_kv)
                sh_part[view, pl.ds(2 * piece * half_kv, half_kv)] = sh_came[view, kept]
                sh_part[view, pl.ds((2 * piece + 1) * half_kv, half_kv)] = kv_ref[view, kept]

    shared.start()
    for chunk in range(chunks):
        collect.middle(chunk)
    shared.direct(0)

    def send_first(chunk, device):
        cols = in_cols[chunk]
        return remote(
            settle_s.at[0, :, cols], settle_r.at[0, :, cols],
            set_ssem.at[0, chunk], set_rsem.at[0, chunk], device,
        )

    def send_second(chunk):
        cols = in_cols[chunk]
        return remote(
            settle_s.at[1, :, cols], settle_r.at[1, :, cols],
            set_ssem.at[1, chunk], set_rsem.at[1, chunk], cross_at,
        )

    for chunk in range(chunks):
        collect.last(chunk)
        cols = in_cols[chunk]

        @pl.when(lanes.home)
        def _(chunk=chunk, cols=cols):
            settle_s[0, :, cols] = in_total[1 - c, :, cols].astype(bf16)
            send_first(chunk, core_at).start()

        @pl.when(lanes.away)
        def _(chunk=chunk, cols=cols):
            settle_s[0, :, cols] = in_total[c, :, cols].astype(bf16)
            send_first(chunk, far_at).start()
            settle_s[1, :, cols] = in_total[1 - c, :, cols].astype(bf16)
            send_second(chunk).start()

        if chunk == 0:
            step_small(0)
            shared.middle(0)
        if chunk == 1:
            step_small(1)
    step_small(2)
    shared.last(0)

    t_high, t_low = lax.div(t, 2), lax.rem(t, 2)
    line = 2 * few

    def send_line():
        return remote(line_s, line_r, misc_s.at[5], misc_r.at[5], far_at)

    def send_near():
        return remote(near_s, near_r, misc_s.at[6], misc_r.at[6], near_at)

    def send_swap():
        return remote(swap_s, swap_r, misc_s.at[7], misc_r.at[7], core_at)

    theirs = pl.ds(pl.multiple_of((1 - t_high) * line, line), line)
    mine = pl.ds(pl.multiple_of(t_high * line, line), line)
    for half in range(2):
        line_s[half] = sh_total[half, theirs, :].astype(bf16)
    send_line().start()
    step_small(3)
    send_line().wait_recv()
    for half in range(2):
        sh_total[half, mine, :] = sh_total[half, mine, :] + line_r[half].astype(f32)
    theirs = pl.ds(pl.multiple_of(t_high * line + (1 - t_low) * few, few), few)
    mine = pl.ds(pl.multiple_of(t_high * line + t_low * few, few), few)
    for half in range(2):
        near_s[half] = sh_total[half, theirs, :].astype(bf16)
    send_near().start()
    for index in range(4, len(stops)):
        step_small(index)
    send_near().wait_recv()
    for half in range(2):
        sh_total[half, mine, :] = sh_total[half, mine, :] + near_r[half].astype(f32)
    swap_s[...] = sh_total[1 - c, mine, :].astype(bf16)
    send_swap().start()
    sum_ref[...] = small_s[len(stops)]

    bounds = [
        (0, gmix_ref.at[:, 0, :], width),
        (width, gmix_ref.at[:, 1, :], width),
        (2 * width, gquery_ref, query_width),
        (2 * width + query_width, gstep_ref, gstep_ref.shape[1]),
    ]

    def put_in(cols, other, kind):
        for start, dst, size in bounds:
            low, high = max(cols.start, start), min(cols.stop, start + size)
            if low < high:
                part = slice(low, high)
                total = settle_r[kind, :, part].astype(f32) + other(part)
                dst[:, low - start : high - start] = total

    for chunk in range(chunks):
        cols = in_cols[chunk]
        send_first(chunk, core_at).wait_recv()

        @pl.when(lanes.home)
        def _(chunk=chunk, cols=cols):
            put_in(cols, lambda part: in_total[c, :, part], 0)

        @pl.when(lanes.away)
        def _(chunk=chunk, cols=cols):
            send_second(chunk).wait_recv()
            put_in(cols, lambda part: settle_r[1, :, part].astype(f32), 0)

    out_first(0, core_at).wait_recv()

    @pl.when(lanes.home)
    def _():
        own_rows = pl.ds(pl.multiple_of(c * rows, rows), rows)
        gout_ref[...] = out_ref[own_rows, :width].astype(f32) + out_r[0, :, :width].astype(f32)
        gattn_ref[...] = out_ref[own_rows, width:].astype(f32) + out_r[0, :, width:].astype(f32)
        out_first(1 - c, core_at).wait_send()

    @pl.when(lanes.away)
    def _():
        out_second().wait_recv()
        gout_ref[...] = out_r[0, :, :width].astype(f32) + out_r[1, :, :width].astype(f32)
        gattn_ref[...] = out_r[0, :, width:].astype(f32) + out_r[1, :, width:].astype(f32)
        out_first(c, far_at).wait_send()
        out_second().wait_send()

    send_swap().wait_recv()

    @pl.when(first)
    def _():
        gsh_ref[:, :wide] = sh_total[0, mine, :]
        gsh_ref[:, wide:] = swap_r[...].astype(f32)

    @pl.when(second)
    def _():
        gsh_ref[:, :wide] = swap_r[...].astype(f32)
        gsh_ref[:, wide:] = sh_total[1, mine, :]

    @pl.when(lanes.away)
    def _():
        send_x().wait_recv()

        @pl.loop(0, here // step)
        def _(i):
            view = pl.ds(pl.multiple_of(i * step, step), step)
            gx_ref[view, :] = gx_r[view, :].astype(f32)

    collect.finish()
    shared.finish()

    @pl.when(first)
    def _():
        send_kv().wait_send()

    @pl.when(second)
    def _():
        send_bc().wait_send()

    for chunk in range(chunks):
        send_first(chunk, core_at).wait_send()

    @pl.when(lanes.away)
    def _():
        send_x().wait_send()
        for chunk in range(chunks):
            send_second(chunk).wait_send()

    for index in range(len(stops)):
        send_small(index).wait_send()
    send_line().wait_send()
    send_near().wait_send()
    send_swap().wait_send()


def back(part_in, bc, kv, grad_act, grad_resid, x, gain, small, small_row, raw_out, few, mixer_width, at):
    f32, bf16 = jnp.float32, jnp.bfloat16
    blocks = at.blocks
    features, width = part_in.shape
    query_width = width - 2 * mixer_width - WIDE
    rows = features // (2 * blocks)
    here = grad_act.shape[0]
    wide = bc.shape[1]
    cut = -(-width // (2 * WIDE)) * WIDE
    in_cols = [slice(0, cut), slice(cut, width)]
    chunks = len(in_cols)
    loads = sum(bool(onward(p, h, at.bits)) for h in range(2) for p in range(blocks))
    steps = 3 + at.bits
    dma = pltpu.SemaphoreType.DMA
    vmem = pl.BlockSpec(memory_space=pltpu.VMEM)
    anywhere = pl.BlockSpec(memory_space=pl.ANY)
    line = 2 * few
    return pl.pallas_call(
        functools.partial(back_body, blocks, in_cols, small_row),
        in_specs=[anywhere] + [vmem] * 8,
        out_specs=[vmem] * 8,
        out_shape=[
            jax.ShapeDtypeStruct((rows, 2, mixer_width), f32),
            jax.ShapeDtypeStruct((rows, query_width), f32),
            jax.ShapeDtypeStruct((rows, WIDE), f32),
            jax.ShapeDtypeStruct((few, 2 * wide), f32),
            jax.ShapeDtypeStruct((here, features), f32),
            jax.ShapeDtypeStruct(small.shape, f32),
            jax.ShapeDtypeStruct((rows, mixer_width), f32),
            jax.ShapeDtypeStruct((rows, raw_out.shape[1] - mixer_width), f32),
        ],
        scratch_shapes=[
            pltpu.VMEM((loads, rows, width), bf16),
            pltpu.VMEM((2, blocks - 1, rows, width), bf16),
            pltpu.VMEM((loads, rows, width), bf16),
            pltpu.VMEM((2, rows, width), f32),
            pltpu.VMEM((2, rows, width), bf16),
            pltpu.VMEM((2, rows, width), bf16),
            pltpu.VMEM((features, wide), bf16),
            pltpu.VMEM((features, wide), bf16),
            pltpu.VMEM((loads, rows, wide), bf16),
            pltpu.VMEM((2, blocks - 1, rows, wide), bf16),
            pltpu.VMEM((loads, rows, wide), bf16),
            pltpu.VMEM((2, rows, wide), f32),
            pltpu.VMEM((2, line, wide), bf16),
            pltpu.VMEM((2, line, wide), bf16),
            pltpu.VMEM((2, few, wide), bf16),
            pltpu.VMEM((2, few, wide), bf16),
            pltpu.VMEM((few, wide), bf16),
            pltpu.VMEM((few, wide), bf16),
            pltpu.VMEM((here, features), bf16),
            pltpu.VMEM((here, features), bf16),
            pltpu.VMEM((steps + 1,) + small.shape, f32),
            pltpu.VMEM((steps,) + small.shape, f32),
            dma((2, blocks, chunks)),
            dma((2, blocks, chunks)),
            dma((loads,)),
            dma((2, blocks, 1)),
            dma((2, blocks, 1)),
            dma((loads,)),
            dma((2, chunks)),
            dma((2, chunks)),
            dma((8,)),
            dma((8,)),
            dma((steps,)),
            dma((steps,)),
            pltpu.VMEM((2, rows, raw_out.shape[1]), bf16),
            dma((2,)),
            dma((2,)),
        ],
        compiler_params=pltpu.CompilerParams(
            collective_id=2, has_side_effects=True, vmem_limit_bytes=58 * 1024 * 1024
        ),
        cost_estimate=pl.CostEstimate(
            flops=here, bytes_accessed=here, transcendentals=0
        ),
    )(
        part_in, bc, kv, grad_act, grad_resid, x, gain.reshape(1, -1), small,
        raw_out,
    )


def after(values, *others):
    return lax.optimization_barrier((values,) + others)[0]


def share_rows(values, at):
    far = at.over_z(values)
    core = at.over_core(values)
    both = at.over_core(far)
    return (values, core, far, both)


def sum_rows(pieces, at):
    own, core, far, both = pieces
    bf16 = jnp.bfloat16
    from_both = at.over_core(both.astype(bf16))
    passed = (far + from_both.astype(jnp.float32)).astype(bf16)
    from_far = at.over_z(passed)
    from_core = at.over_core(core.astype(bf16))
    return own + from_core.astype(jnp.float32) + from_far.astype(jnp.float32)


def groups(at):
    return [[d for d in range(at.dp) if d % 2 == c] for c in range(2)]


def gather_blocks(block, at):
    return lax.all_gather(block, "dp", axis=0, tiled=True, axis_index_groups=groups(at))


def sum_blocks(values, at):
    return lax.psum_scatter(
        values, "dp", scatter_dimension=0, tiled=True, axis_index_groups=groups(at)
    )


def pair_up(own, other, at):
    first = at.c == 0
    return jnp.concatenate([jnp.where(first, own, other), jnp.where(first, other, own)], axis=0)


def pair_weight(shard, at):
    first_in = at.column_out(shard)
    second_in = at.swap_away(shard)
    own = jnp.where(at.home, shard, first_in)
    other = jnp.where(at.home, first_in, second_in)
    return pair_up(own, other, at)


def gather_weight(shard, at):
    return gather_blocks(pair_weight(shard, at), at)


def send_settle(mine, at):
    rows = mine.shape[0] // 2
    low, high = mine[:rows], mine[rows:]
    own = jnp.where(at.c == 0, low, high)
    other = jnp.where(at.c == 0, high, low)
    return at.column_back(jnp.where(at.home, other, own)), at.swap_away(other), own


def end_settle(moves, at):
    first_in, second_in, own = moves
    f32 = jnp.float32
    return first_in.astype(f32) + jnp.where(at.home, own, second_in).astype(f32)


def gather_shared(shard, at):
    rows, width = shard.shape
    half = width // 2
    mine = jnp.where(at.c == 0, shard[:, :half], shard[:, half:])
    theirs = jnp.where(at.c == 0, shard[:, half:], shard[:, :half])
    came = at.over_core(theirs)
    both = jnp.stack([jnp.where(at.c == 0, mine, came), jnp.where(at.c == 0, came, mine)])
    near = at.over_z(both)
    lowest = at.t % 2 == 0
    two = jnp.stack([jnp.where(lowest, both, near), jnp.where(lowest, near, both)], axis=1)
    far = at.over_far(two)
    lower = at.t // 2 == 0
    four = jnp.stack([jnp.where(lower, two, far), jnp.where(lower, far, two)], axis=1)
    part = gather_blocks(four.reshape(2 * rows * at.tp, half), at)
    other = at.over_core(part)
    return jnp.where(at.c == 0, part, other), jnp.where(at.c == 0, other, part)


def scatter_shared(grad_bc, grad_kv, earlier, at):
    f32, bf16 = jnp.float32, jnp.bfloat16
    first = at.c == 0
    bc_width = grad_bc.shape[1]
    going = jnp.where(
        first, jnp.pad(grad_kv, ((0, 0), (0, bc_width - grad_kv.shape[1]))), grad_bc
    )
    came = at.over_core(going.astype(bf16)).astype(f32)
    kept = jnp.concatenate(
        [came[:, :HD], grad_kv[:, :HD], came[:, HD : 2 * HD], grad_kv[:, HD:]], axis=1
    )
    total = jnp.where(first, grad_bc + came, kept)
    mine = sum_blocks(after(total.astype(bf16), earlier), at)
    piece = mine.shape[0] // (2 * at.tp)
    line = mine.astype(f32).reshape(2, 2, 2, piece, total.shape[1])
    lower = at.t // 2 == 0
    went = at.over_far(jnp.where(lower, line[:, 1], line[:, 0]).astype(bf16)).astype(f32)
    line = jnp.where(lower, line[:, 0], line[:, 1]) + went
    lowest = at.t % 2 == 0
    went = at.over_z(jnp.where(lowest, line[:, 1], line[:, 0]).astype(bf16)).astype(f32)
    line = jnp.where(lowest, line[:, 0], line[:, 1]) + went
    mine = jnp.where(first, line[0], line[1])
    came = at.over_core(jnp.where(first, line[1], line[0]).astype(bf16)).astype(f32)
    return jnp.concatenate([jnp.where(first, mine, came), jnp.where(first, came, mine)], axis=1)


def sum_tensor(values, at):
    for bit in range(at.tp.bit_length() - 1):
        values = values + at.send(values, lambda d, t: (d, t ^ (1 << bit)))
    return values


def sum_data(values, at):
    for bit in range(at.dp.bit_length() - 1):
        values = values + at.send(values, lambda d, t: (d ^ (1 << bit), t))
    return values


def per_device(
    layer_in,
    teacher,
    lengths,
    input_gain,
    mixer_in_weight,
    step_weight,
    query_weight,
    shared_weight,
    conv_inner,
    conv_shared,
    step_bias,
    decay_log,
    skip_gain,
    inner_gain,
    mixer_out_weight,
    attn_out_weight,
    middle_gain,
    gate_up_weight,
    down_weight,
):
    f32 = jnp.float32
    bf16 = jnp.bfloat16
    contract_last = (((1,), (1,)), ((), ()))
    contract_first = (((0,), (0,)), ((), ()))
    at = Places()
    rows_here = layer_in.shape[0]
    slot_len = rows_here * at.tp
    local_heads = step_bias.shape[0]
    width = inner_gain.shape[0]
    head_dim = width // local_heads
    query_width = query_weight.shape[1]
    hidden_width = down_weight.shape[1]
    bc_width = conv_shared.shape[1]
    w_rows = step_weight.shape[0]

    seg = (
        lax.broadcasted_iota(jnp.int32, (width, WIDE), 0) // head_dim
        == lax.broadcasted_iota(jnp.int32, (width, WIDE), 1)
    ).astype(bf16)
    half = HD // 2
    freqs = jnp.exp(-jnp.log(ROPE_BASE) * 2.0 * jnp.arange(half, dtype=f32) / HD)
    angles = jnp.arange(slot_len).astype(f32)[:, None] * freqs[None, :]
    cosine, sine = jnp.cos(angles), jnp.sin(angles)
    cosine = jnp.concatenate([cosine, cosine], axis=1)
    sine = jnp.concatenate([-sine, sine], axis=1)
    quarters = jnp.arange(at.tp, dtype=jnp.int32)
    order = (at.c ^ (quarters // 2)) + 2 * (at.zq ^ (quarters % 2))

    in_pack = jnp.concatenate(
        [
            mixer_in_weight.reshape(w_rows, 2 * width),
            query_weight,
            step_weight,
            jnp.zeros((w_rows, WIDE - local_heads), bf16),
        ],
        axis=1,
    )
    out_pack = jnp.concatenate([mixer_out_weight, attn_out_weight], axis=1)
    column_params = jnp.concatenate(
        [conv_inner.reshape(-1), inner_gain, step_bias, decay_log, skip_gain]
    )
    params = jnp.pad(column_params, (0, -column_params.shape[0] % 1024)).reshape(-1, WIDE)
    in_all, out_pair, down_pair, act_all, x_low, _, params, proj, proj_shared, shared_all = front(
        in_pack, out_pack, down_weight, shared_weight, layer_in, input_gain, params, HD, at
    )
    column_params = params.reshape(-1)[: column_params.shape[0]]
    lane_params = jnp.concatenate(
        [
            column_params[: (KC + 1) * width].reshape(KC + 1, width),
            jnp.repeat(column_params[(KC + 1) * width + 2 * local_heads :], head_dim)[None],
            jnp.zeros((2, width), f32),
        ],
        axis=0,
    )
    head_rows = column_params[(KC + 1) * width :][: 2 * local_heads].reshape(2, local_heads)
    head_rows = jnp.concatenate([head_rows[:1], -jnp.exp(head_rows[1:])], axis=0)
    head_params = jnp.pad(head_rows, ((0, 6), (0, WIDE - local_heads)))
    def row_split(values):
        return [values[i * rows_here : (i + 1) * rows_here] for i in range(at.tp)]

    out_all = gather_blocks(out_pair, at)
    attn_low = attn_forward(order, proj, proj_shared, cosine, sine, query_width, width, bc_width)
    heads_all, y, states = mixer_forward(
        order, proj, proj_shared, attn_low, lane_params, conv_shared, head_params
    )
    seq_len = lax.dynamic_index_in_dim(lengths, at.slot, keepdims=False)
    positions = at.quarter * rows_here + jnp.arange(rows_here)
    live = (positions < seq_len).astype(f32)[:, None]
    ff_pair = pair_weight(gate_up_weight.reshape(w_rows, 2 * hidden_width), at)
    ff_all, mid_all, gate_low, up_low, hidden, grad_all, resid, error, layer_out, loss_part = middle(
        ff_pair, down_pair, heads_all, out_all, x_low, middle_gain, teacher, live, at
    )
    err_local = loss_part[0, 0]
    _, norm_mid_back = jax.vjp(rms_norm, resid, middle_gain)
    gate_up_all = ff_all[:, : 2 * hidden_width]
    down_all = ff_all[:, 2 * hidden_width :]
    gate_val, up_val = gate_low.astype(f32), up_low.astype(f32)
    sigmoid_gate = jax.nn.sigmoid(gate_val)

    def weight_grad(left, right):
        return lax.dot_general(left, right, contract_first, preferred_element_type=f32).astype(bf16)

    part_down = weight_grad(grad_all, hidden)
    grad_all, part_down = lax.optimization_barrier((grad_all, part_down))
    raw_down = sum_blocks(part_down, at)
    down_moves = send_settle(raw_down, at)
    grad_hidden = jnp.dot(grad_all, down_all, preferred_element_type=f32)
    grad_gate = grad_hidden * up_val * sigmoid_gate * (1.0 + gate_val * (1.0 - sigmoid_gate))
    grad_up = grad_hidden * gate_val * sigmoid_gate
    grad_gu = jnp.concatenate([grad_gate.astype(bf16), grad_up.astype(bf16)], axis=1)
    grad_mid_parts = [
        lax.dot_general(piece, gate_up_all, contract_last, preferred_element_type=f32)
        for piece in row_split(grad_gu)
    ]
    part_gate_up = weight_grad(mid_all, grad_gu)
    grad_mid = sum_rows(grad_mid_parts, at)
    grad_mid, part_gate_up = lax.optimization_barrier((grad_mid, part_gate_up))
    raw_gate_up = sum_blocks(part_gate_up, at)
    grad_resid_norm, grad_middle_gain = norm_mid_back(grad_mid)
    grad_resid = error + grad_resid_norm
    mix_grad_all = jnp.concatenate(share_rows(grad_resid.astype(bf16), at), axis=0)
    grad_heads = jnp.dot(mix_grad_all, out_all, preferred_element_type=f32)
    part_out = weight_grad(mix_grad_all, heads_all)
    grad_heads, part_out = lax.optimization_barrier((grad_heads, part_out))
    dq, dkv = attn_backward(
        order, proj, proj_shared, cosine, sine, grad_heads, query_width, width, bc_width
    )
    low_pack, low_shared, dlane, dconv, dhead = mixer_backward(
        order, proj, proj_shared, y, states, grad_heads, dq, dkv, lane_params, conv_shared,
        head_params, seg, query_width, down_moves[:2],
    )
    low_pack, low_shared, raw_gate_up, part_out = lax.optimization_barrier(
        (low_pack, low_shared, raw_gate_up, part_out)
    )
    raw_out = sum_blocks(part_out, at)
    column = at.column
    lanes_full = lax.dynamic_update_slice(
        jnp.zeros((KC + 1, DI), f32), dlane[: KC + 1], (0, column * width)
    )
    head_stack = jnp.concatenate(
        [dhead[:2, :local_heads], dlane[KC + 1].reshape(1, local_heads, head_dim).sum(2)], axis=0
    )
    heads_full = lax.dynamic_update_slice(
        jnp.zeros((3, H), f32), head_stack, (0, column * local_heads)
    )
    small = (
        jnp.zeros_like(input_gain),
        grad_middle_gain,
        lanes_full,
        dconv[:KC],
        heads_full,
        err_local,
    )
    flat = jnp.concatenate([part.reshape(-1) for part in small])
    padded = -(-flat.shape[0] // 1024) * 1024
    flat = jnp.pad(flat, (0, padded - flat.shape[0])).reshape(-1, WIDE)

    grad_down = end_settle(down_moves, at)
    part_in, part_bc, part_kv, grad_act, grad_gate_up = turn(
        low_pack, low_shared, act_all, in_all, shared_all, raw_gate_up, bc_width, at
    )
    grad_mix, grad_query, grad_step, grad_shared_weight, input_grad, flat, grad_out, grad_attn = back(
        part_in, part_bc, part_kv, grad_act, grad_resid, x_low, input_gain, flat, 0,
        raw_out, shared_weight.shape[0], width, at,
    )
    flat = flat.reshape(-1)
    sums = []
    start = 0
    for part in small:
        sums.append(flat[start : start + part.size].reshape(part.shape))
        start += part.size
    sum_input_gain, sum_middle_gain, sum_lanes, sum_convs, sum_heads, err_total = sums
    lanes_local = lax.dynamic_slice_in_dim(sum_lanes, at.t * width, width, 1)
    heads_local = lax.dynamic_slice_in_dim(sum_heads, at.t * local_heads, local_heads, 1)
    loss = err_total / jnp.sum(lengths).astype(f32)
    query_from = 2 * width
    step_from = query_from + query_width
    return (
        layer_out,
        loss,
        input_grad,
        sum_input_gain,
        grad_mix,
        grad_step[:, :local_heads],
        grad_query,
        grad_shared_weight,
        lanes_local[:KC],
        sum_convs,
        heads_local[0],
        heads_local[1],
        heads_local[2],
        lanes_local[KC],
        grad_out,
        grad_attn,
        sum_middle_gain,
        grad_gate_up,
        grad_down,
    )


def solution(mesh):
    placed = (
        P(("dp", "tensor"), None),
        P(("dp", "tensor"), None),
        P(),
        P(),
        P("dp", None, "tensor"),
        P("dp", "tensor"),
        P("dp", "tensor"),
        P(("dp", "tensor"), None),
        P(None, "tensor"),
        P(),
        P("tensor"),
        P("tensor"),
        P("tensor"),
        P("tensor"),
        P("dp", "tensor"),
        P("dp", "tensor"),
        P(),
        P("dp", None, "tensor"),
        P("dp", "tensor"),
    )
    return jax.shard_map(
        per_device,
        mesh=mesh,
        in_specs=placed,
        out_specs=(
            P(("dp", "tensor"), None),
            P(),
            P(("dp", "tensor"), None),
            P(),
            P("dp", None, "tensor"),
            P("dp", "tensor"),
            P("dp", "tensor"),
            P(("dp", "tensor"), None),
            P(None, "tensor"),
            P(),
            P("tensor"),
            P("tensor"),
            P("tensor"),
            P("tensor"),
            P("dp", "tensor"),
            P("dp", "tensor"),
            P(),
            P("dp", None, "tensor"),
            P("dp", "tensor"),
        ),
        check_vma=False,
    )
```
